32 devices in a mesh: blk: 16 (over z, y, core), grp: 2 (over x).
Axes of the slice: x: 2, y: 2, z: 4, core: 2. Of those that a mesh axis runs over, the one named last changes fastest.
Arguments:
- frames: float32 [6144, 1024], P(('blk', 'grp')), may hold values from -6 to 6
- lengths: int32 [12], replicated, may hold values from 1 to 4096, 6144 in all
- norm1_gain: float32 [1024], replicated, may hold values from 0.5 to 1.5
- w_query: bfloat16 [1024, 1024], replicated, may hold values from -0.1875 to 0.1875
- w_key: bfloat16 [1024, 1024], replicated, may hold values from -0.1875 to 0.1875
- w_value: bfloat16 [1024, 1024], replicated, may hold values from -0.1875 to 0.1875
- w_out: bfloat16 [1024, 1024], replicated, may hold values from -1.5 to 1.5
- norm2_gain: float32 [1024], replicated, may hold values from 0.5 to 1.5
- w_up: bfloat16 [1024, 4096], replicated, may hold values from -0.1875 to 0.1875
- b_up: float32 [4096], replicated, may hold values from -3 to 3
- w_down: bfloat16 [4096, 1024], replicated, may hold values from -0.09375 to 0.09375
- b_down: float32 [1024], replicated, may hold values from -3 to 3
- cotangent: float32 [6144, 1024], P(('blk', 'grp')), may hold values from -6 to 6
Outputs:
- layer_out: float32 [6144, 1024], P(('blk', 'grp'))
- frames_grad: float32 [6144, 1024], P(('blk', 'grp'))
- norm1_gain_grad: float32 [1024], P(('blk', 'grp'))
- w_query_grad: float32 [1024, 1024], P(('blk', 'grp'))
- w_key_grad: float32 [1024, 1024], P(('blk', 'grp'))
- w_value_grad: float32 [1024, 1024], P(('blk', 'grp'))
- w_out_grad: float32 [1024, 1024], P(('blk', 'grp'))
- norm2_gain_grad: float32 [1024], P(('blk', 'grp'))
- w_up_grad: float32 [1024, 4096], P(('blk', 'grp'))
- b_up_grad: float32 [4096], P(('blk', 'grp'))
- w_down_grad: float32 [4096, 1024], P(('blk', 'grp'))
- b_down_grad: float32 [1024], P(('blk', 'grp'))
The draws below stay inside these ranges and needn't reach their ends.
Inputs may be any that keep to these rules, and one draw needn't show every extreme that they name: The lengths sum to 6144; the longest item has exactly 4096 frames.
All inputs are finite; a program needn't handle non-finite values.
Results may differ from the reference program's by a relative error of at most 0.012.
Values may be sent and summed in bfloat16 or wider, within the bound.
A program may use at most 192 MiB of HBM per device.

```python
import math
import jax
import jax.numpy as jnp
import numpy as np
from jax import lax

D = 1024
HEAD_DIM = 64
FF = 4096
ITEM_MAX = 4096
TOKENS = 6144
ITEMS = 12


def strengthened(result, own_key, source, target, shards_of, factor):
    def block_of(position):
        return (jnp.arange(result.shape[position]) // (result.shape[position] // shards_of)).reshape((-1,) + (1,) * (result.ndim - 1 - position))

    first = jax.random.permutation(own_key, shards_of)[block_of(target)]
    second = (block_of(target) + shards_of // 2) % shards_of
    return jnp.where((block_of(source) == first) | (block_of(source) == second), factor * result, result)


def steps_of(key, extent, cuts, least, largest):
    level, own = 1.0, jax.random.fold_in(key, 6)
    for dim, shards_of in cuts:
        heights = jnp.exp(jax.random.uniform(jax.random.fold_in(own, dim), (shards_of,), jnp.float32, least / len(cuts), largest / len(cuts)))
        level = level * jnp.repeat(heights, extent[dim] // shards_of).reshape([-1 if axis == dim else 1 for axis in range(len(extent))])
    return level


def profile(count, total, limit, slope):
    loads = [(1 << 20) // math.isqrt(rank ** slope) + 1 for rank in range(2, count + 1)]
    surplus, holding = total - limit - (count - 1), [1] * (count - 1)
    while surplus > 0:
        candidates = [i for i in range(count - 1) if holding[i] < limit]
        mass, left = sum([loads[i] for i in candidates]), surplus
        for i in candidates:
            addition = min(limit - holding[i], max(1, left * loads[i] // mass), surplus)
            holding[i] = holding[i] + addition
            surplus = surplus - addition
    return np.array([limit] + holding)


def ragged_sizes(rng, amount, total, limit, skew):
    if amount == 2:
        one = jax.random.randint(rng, (), max(1, total - limit), min(limit, total - 1) + 1)
        return jnp.stack([one, total - one])
    sizes = jnp.asarray(profile(amount, total, limit, skew), jnp.int32)
    pairs = (amount - 1) // 2
    giver, sink = sizes[1:1 + 2 * pairs:2], sizes[2:2 + 2 * pairs:2]
    slack = jnp.minimum(giver - 1, limit - sink)
    moved = jax.random.randint(jax.random.fold_in(rng, 1), (pairs,), 0, 1 << 20) % (slack + 1)
    sizes = sizes.at[1:1 + 2 * pairs:2].set(giver - moved).at[2:2 + 2 * pairs:2].set(sink + moved)
    return sizes[jax.random.permutation(jax.random.fold_in(rng, 2), amount)]


def bell_draw(own_key, shape, spread, most, pieces=(), kind=jnp.bfloat16):
    factor_of = steps_of(own_key, shape, pieces, -0.22, 0.18) if pieces else 1.0
    values = jax.random.normal(own_key, shape, jnp.float32) * spread * factor_of
    return jnp.minimum(jnp.maximum(values, -most), most).astype(kind)


def gaussian_with(rng, dims, width, bound, split, heavy, held_as=jnp.bfloat16):
    values = width * jax.random.normal(rng, dims, jnp.float32)
    if split:
        values = values * steps_of(rng, dims, split, -0.22, 0.18)
    return jnp.clip(strengthened(values, jax.random.fold_in(rng, 3), *heavy), -bound, bound).astype(held_as)


def setup_inputs(seed: int = 0) -> dict:
    splits = jax.random.split(jax.random.key(seed), 14)
    frames = gaussian_with(splits[0], (TOKENS, D), 1.0, 6.0, ((0, 32),), (0, 1, 32, 2.75), jnp.float32)
    lengths = ragged_sizes(splits[1], ITEMS, TOKENS, ITEM_MAX, 2).astype(jnp.int32)
    norm1_gain = jnp.clip(1.0 + 0.1 * jax.random.normal(splits[2], (D,), jnp.float32), 0.5, 1.5)
    w_query = bell_draw(splits[3], (D, D), D ** -0.5, 0.1875)
    w_key = bell_draw(splits[4], (D, D), D ** -0.5, 0.1875)
    w_value = bell_draw(splits[5], (D, D), D ** -0.5, 0.1875)
    w_out = bell_draw(splits[6], (D, D), (D // 64) ** -0.5, 1.5)
    norm2_gain = jnp.clip(1.0 + 0.1 * jax.random.normal(splits[7], (D,), jnp.float32), 0.5, 1.5)
    w_up = bell_draw(splits[8], (D, FF), D ** -0.5, 0.1875)
    b_up = bell_draw(splits[9], (FF,), 0.5, 3.0, (), jnp.float32)
    w_down = bell_draw(splits[10], (FF, D), FF ** -0.5, 0.09375)
    b_down = bell_draw(splits[11], (D,), 0.5, 3.0, (), jnp.float32)
    cotangent = bell_draw(splits[12], (TOKENS, D), 1.0, 6.0, ((0, 32),), jnp.float32)
    return {"frames": frames, "lengths": lengths, "norm1_gain": norm1_gain, "w_query": w_query, "w_key": w_key, "w_value": w_value, "w_out": w_out, "norm2_gain": norm2_gain, "w_up": w_up, "b_up": b_up, "w_down": w_down, "b_down": b_down, "cotangent": cotangent}


EPSILON = 1e-05
MASKED = -1e+30
SCALING = 0.125

@jax.custom_vjp
def low(v):
    return lax.optimization_barrier(v.astype(jnp.bfloat16)).astype(jnp.float32)

@jax.custom_vjp
def low_back(v):
    return v

def low_keep(v):
    return (low(v), None)

def low_pass(kept, grad):
    return (grad,)

def back_keep(v):
    return (v, None)

def back_low(kept, grad):
    return (low(grad),)
low.defvjp(low_keep, low_pass)
low_back.defvjp(back_keep, back_low)

def rms_norm(values, gain):
    return values * lax.rsqrt(lax.optimization_barrier(jnp.mean(values * values, axis=-1, keepdims=True)) + EPSILON) * gain

def matmul(left, right):
    return jnp.dot(left, right, precision=lax.Precision.HIGHEST, preferred_element_type=jnp.float32)

def item_starts(lengths):
    ends = jnp.cumsum(lengths).astype(jnp.int32)
    offsets = (ends - lengths).astype(jnp.int32)
    positions = jnp.arange(TOKENS, dtype=jnp.int32)
    which = lax.optimization_barrier(jnp.sum((ends[None, :] <= positions[:, None]).astype(jnp.int32), axis=1))
    return jnp.take(offsets, which).astype(jnp.int32)

def attention(queries, keys, values, starts):
    heads = D // HEAD_DIM
    block = min(512, TOKENS)
    count = TOKENS // block
    window = ITEM_MAX + block
    padded_keys = jnp.concatenate([jnp.zeros((ITEM_MAX, D), keys.dtype), keys], axis=0)
    padded_values = jnp.concatenate([jnp.zeros((ITEM_MAX, D), values.dtype), values], axis=0)

    def one_block(block_index):
        first = (block_index * block).astype(jnp.int32)
        query_rows = lax.dynamic_slice_in_dim(queries, first, block, 0).reshape(block, heads, HEAD_DIM)
        key_rows = lax.dynamic_slice_in_dim(padded_keys, first, window, 0).reshape(window, heads, HEAD_DIM)
        value_rows = lax.dynamic_slice_in_dim(padded_values, first, window, 0).reshape(window, heads, HEAD_DIM)
        query_pos = first + jnp.arange(block, dtype=jnp.int32)
        key_pos = first - ITEM_MAX + jnp.arange(window, dtype=jnp.int32)
        query_start = lax.dynamic_slice_in_dim(starts, first, block, 0)
        live = (key_pos[None, :] >= query_start[:, None]) & (key_pos[None, :] <= query_pos[:, None])
        scores = low_back(jnp.einsum('qhd,khd->hqk', query_rows, key_rows, precision=lax.Precision.HIGHEST) * SCALING)
        scores = jnp.where(live[None], scores, MASKED)
        probs = low(jax.nn.softmax(scores, axis=-1))
        mixed = jnp.einsum('hqk,khd->qhd', probs, value_rows, precision=lax.Precision.HIGHEST)
        return mixed.reshape(block, D)
    blocks = lax.map(jax.checkpoint(one_block), jnp.arange(count, dtype=jnp.int32))
    return blocks.reshape(TOKENS, D)

def layer(frames, norm1_gain, w_query, w_key, w_value, w_out, norm2_gain, w_up, b_up, w_down, b_down, starts):
    act1 = low(rms_norm(frames, norm1_gain))
    queries = low(low_back(matmul(act1, w_query)))
    keys = low(low_back(matmul(act1, w_key)))
    values = low(low_back(matmul(act1, w_value)))
    mixed = low(low_back(attention(queries, keys, values, starts)))
    middle = frames + low_back(matmul(mixed, w_out))
    act2 = low(rms_norm(middle, norm2_gain))
    before = low_back(matmul(act2, w_up) + b_up)
    hidden = low(jax.nn.gelu(before, approximate=False))
    return middle + low_back(matmul(hidden, w_down) + b_down)

def reference(frames, lengths, norm1_gain, w_query, w_key, w_value, w_out, norm2_gain, w_up, b_up, w_down, b_down, cotangent):
    starts = item_starts(lengths)
    params = (frames, norm1_gain, w_query.astype(jnp.float32), w_key.astype(jnp.float32), w_value.astype(jnp.float32), w_out.astype(jnp.float32), norm2_gain, w_up.astype(jnp.float32), b_up, w_down.astype(jnp.float32), b_down)

    def forward(p_frames, p_gain1, p_query, p_key, p_value, p_out, p_gain2, p_up, p_bup, p_down, p_bdown):
        return layer(p_frames, p_gain1, p_query, p_key, p_value, p_out, p_gain2, p_up, p_bup, p_down, p_bdown, starts)
    output, pullback = jax.vjp(forward, *params)
    grads = pullback(cotangent)
    return (output, grads[0], grads[1], grads[2], grads[3], grads[4], grads[5], grads[6], grads[7], grads[8], grads[9], grads[10])
```

```python
import functools

import jax
import jax.numpy as jnp
import numpy as np
from jax import lax
from jax.experimental import pallas as pl
from jax.experimental.pallas import tpu as pltpu
from jax.sharding import PartitionSpec as P

HEAD_DIM = 64
ITEM_MAX = 4096


EPSILON = 1e-05
MASKED = -1e30
SCALING = 0.125


def shortened(array):

    def short(part):
        return part.astype(jnp.bfloat16) if part.dtype == jnp.float32 else part

    return jax.tree.map(short, array)


def passed_along(block, axis, distance):
    devices = range(lax.axis_size(axis))
    route = [(i - distance, i) for i in devices if i - distance in devices]
    return lax.ppermute(block, axis, route)


def rms_norm(values, gain):
    return values * lax.rsqrt(jnp.mean(values * values, axis=-1, keepdims=True) + EPSILON) * gain


def gelu_exact(values):
    return jax.nn.gelu(values, approximate=False)


def item_starts(lengths, positions):
    ends = jnp.cumsum(lengths)
    offsets = ends - lengths
    before = offsets[None, :] <= positions[:, None]
    return jnp.max(jnp.where(before, offsets[None, :], 0), axis=1)


def live_mask(query_pos, query_start, key_first, key_count):
    key_pos = key_first + jnp.arange(key_count, dtype=jnp.int32)
    return (key_pos[None, :] >= query_start[:, None]) & (key_pos[None, :] <= query_pos[:, None])


def split_heads(matrix):
    return matrix.reshape(matrix.shape[0], matrix.shape[1] // HEAD_DIM, HEAD_DIM)


def merge_heads(tensor):
    return tensor.reshape(tensor.shape[0], tensor.shape[1] * tensor.shape[2])


def scores_of(queries3, keys_block, mask):
    raw = jnp.einsum(
        "qhd,khd->hqk", queries3, split_heads(keys_block), preferred_element_type=jnp.float32
    )
    return jnp.where(mask[None], raw * SCALING, MASKED)


def left_dot(left, right):
    return lax.dot_general(
        left, right, (((0,), (0,)), ((), ())), preferred_element_type=jnp.float32
    )


def right_dot(left, right):
    return lax.dot_general(
        left, right, (((1,), (1,)), ((), ())), preferred_element_type=jnp.float32
    )


def grad_parts(queries3, grad_out3, log_total, delta, keys_block, values_block, mask):
    probs = jnp.exp(scores_of(queries3, keys_block, mask) - log_total[:, :, None])
    grad_probs = jnp.einsum(
        "qhd,khd->hqk", grad_out3, split_heads(values_block), preferred_element_type=jnp.float32
    )
    grad_scores = (probs * (grad_probs - delta[:, :, None])).astype(jnp.bfloat16)
    return (probs.astype(jnp.bfloat16), grad_scores)


def key_terms(queries3, grad_out3, probs_low, grad_scores):
    grad_keys = jnp.einsum(
        "hqk,qhd->khd", grad_scores, queries3, preferred_element_type=jnp.float32
    )
    grad_values = jnp.einsum(
        "hqk,qhd->khd", probs_low, grad_out3, preferred_element_type=jnp.float32
    )
    return (merge_heads(grad_keys), merge_heads(grad_values))


def query_term(grad_scores, keys_block):
    return jnp.einsum(
        "hqk,khd->qhd", grad_scores, split_heads(keys_block), preferred_element_type=jnp.float32
    )


def shards_ring(
    frames,
    lengths,
    norm1_gain,
    w_query,
    w_key,
    w_value,
    w_out,
    norm2_gain,
    w_up,
    b_up,
    w_down,
    b_down,
    cotangent,
):
    row_count = frames.shape[0]
    width = frames.shape[1]
    heads = width // HEAD_DIM
    groups = lax.axis_size("grp")
    block_rows = row_count * groups
    span = (ITEM_MAX + block_rows - 2) // block_rows
    blk_index = lax.axis_index("blk")
    sub_index = lax.axis_index("grp")
    block_first = blk_index * block_rows
    query_pos = block_first + sub_index * row_count + jnp.arange(row_count, dtype=jnp.int32)
    query_start = item_starts(lengths, query_pos)
    back_steps = jnp.arange(span + 1, dtype=jnp.int32)
    normed1, norm1_back = jax.vjp(rms_norm, frames, norm1_gain)
    act1 = normed1.astype(jnp.bfloat16)
    queries = jnp.dot(act1, w_query, preferred_element_type=jnp.float32).astype(jnp.bfloat16)
    keys_own = jnp.dot(act1, w_key, preferred_element_type=jnp.float32).astype(jnp.bfloat16)
    values_own = jnp.dot(act1, w_value, preferred_element_type=jnp.float32).astype(jnp.bfloat16)
    queries3 = split_heads(queries)
    block_keys, block_values = (
        lax.all_gather(keys_own, "grp", axis=0, tiled=True),
        lax.all_gather(values_own, "grp", axis=0, tiled=True),
    )

    def cycle_step(carry, unused_input):
        moved = jax.tree.map(
            lambda part, own: part.astype(own.dtype),
            passed_along(shortened(carry), "blk", 1),
            carry,
        )
        return (moved, moved)

    unused_last, far_blocks = lax.scan(cycle_step, (block_keys, block_values), None, length=span)
    keys_all = jnp.concatenate([block_keys[None], far_blocks[0]], axis=0)
    values_all = jnp.concatenate([block_values[None], far_blocks[1]], axis=0)

    def mask_for(back):
        return live_mask(query_pos, query_start, block_first - back * block_rows, block_rows)

    def total_step(carry, inputs):
        run_max, run_sum = carry
        keys_block, back = inputs
        scores = scores_of(queries3, keys_block, mask_for(back))
        new_max = jnp.maximum(run_max, jnp.max(scores, axis=-1))
        run_sum = run_sum * jnp.exp(run_max - new_max) + jnp.sum(
            jnp.exp(scores - new_max[:, :, None]), axis=-1
        )
        return ((new_max, run_sum), None)

    start_max = jnp.full((heads, row_count), MASKED, jnp.float32)
    start_sum = jnp.zeros((heads, row_count), jnp.float32)
    (top_max, top_sum), unused_out = lax.scan(
        total_step, (start_max, start_sum), (keys_all, back_steps)
    )
    log_total = top_max + jnp.log(top_sum)

    def mix_step(total, inputs):
        keys_block, values_block, back = inputs
        probs = jnp.exp(
            scores_of(queries3, keys_block, mask_for(back)) - log_total[:, :, None]
        ).astype(jnp.bfloat16)
        return (
            total
            + jnp.einsum(
                "hqk,khd->qhd", probs, split_heads(values_block), preferred_element_type=jnp.float32
            ),
            None,
        )

    zero_query = jnp.zeros((row_count, heads, HEAD_DIM), jnp.float32)
    mixed_sum, unused_out = lax.scan(mix_step, zero_query, (keys_all, values_all, back_steps))
    mixed = merge_heads(mixed_sum).astype(jnp.bfloat16)
    middle = frames + jnp.dot(mixed, w_out, preferred_element_type=jnp.float32)
    normed2, norm2_back = jax.vjp(rms_norm, middle, norm2_gain)
    act2 = normed2.astype(jnp.bfloat16)
    before = jnp.dot(act2, w_up, preferred_element_type=jnp.float32) + b_up
    activated, gelu_back = jax.vjp(gelu_exact, before)
    hidden = activated.astype(jnp.bfloat16)
    layer_out = middle + jnp.dot(hidden, w_down, preferred_element_type=jnp.float32) + b_down
    grad_low = cotangent.astype(jnp.bfloat16)
    b_down_grad = jnp.sum(grad_low.astype(jnp.float32), axis=0)
    w_down_grad = left_dot(hidden, grad_low)
    grad_before = gelu_back(right_dot(grad_low, w_down))[0].astype(jnp.bfloat16)
    b_up_grad = jnp.sum(grad_before.astype(jnp.float32), axis=0)
    w_up_grad = left_dot(act2, grad_before)
    grad_mid_norm, norm2_gain_grad = norm2_back(right_dot(grad_before, w_up))
    grad_middle = cotangent + grad_mid_norm
    grad_attn = grad_middle.astype(jnp.bfloat16)
    w_out_grad = left_dot(mixed, grad_attn)
    grad_mixed = right_dot(grad_attn, w_out).astype(jnp.bfloat16)
    grad_out3 = split_heads(grad_mixed)

    def delta_step(total, inputs):
        keys_block, values_block, back = inputs
        probs = jnp.exp(scores_of(queries3, keys_block, mask_for(back)) - log_total[:, :, None])
        grad_probs = jnp.einsum(
            "qhd,khd->hqk", grad_out3, split_heads(values_block), preferred_element_type=jnp.float32
        )
        return (total + jnp.sum(probs * grad_probs, axis=-1), None)

    delta, unused_out = lax.scan(
        delta_step, jnp.zeros((heads, row_count), jnp.float32), (keys_all, values_all, back_steps)
    )
    zero_block = jnp.zeros((block_rows, width), jnp.float32)

    def return_step(carry, inputs):
        grad_q, travel = carry
        keys_block, values_block, back = inputs
        probs_low, grad_scores = grad_parts(
            queries3, grad_out3, log_total, delta, keys_block, values_block, mask_for(back)
        )
        grad_keys, grad_values = key_terms(queries3, grad_out3, probs_low, grad_scores)
        moved = (
            passed_along((travel[0] + grad_keys).astype(jnp.bfloat16), "blk", -1).astype(
                jnp.float32
            ),
            passed_along((travel[1] + grad_values).astype(jnp.bfloat16), "blk", -1).astype(
                jnp.float32
            ),
        )
        return ((grad_q + query_term(grad_scores, keys_block), moved), None)

    (grad_q, travel), unused_out = lax.scan(
        return_step,
        (zero_query, (zero_block, zero_block)),
        (far_blocks[0], far_blocks[1], back_steps[1:]),
        reverse=True,
    )
    probs_low, grad_scores = grad_parts(
        queries3, grad_out3, log_total, delta, block_keys, block_values, mask_for(0)
    )
    grad_keys, grad_values = key_terms(queries3, grad_out3, probs_low, grad_scores)
    grad_q = grad_q + query_term(grad_scores, block_keys)
    block_grad_keys = travel[0] + grad_keys
    block_grad_values = travel[1] + grad_values
    grad_keys_rows, grad_values_rows = (
        lax.psum_scatter(
            block_grad_keys.astype(jnp.bfloat16), "grp", scatter_dimension=0, tiled=True
        ).astype(jnp.float32),
        lax.psum_scatter(
            block_grad_values.astype(jnp.bfloat16), "grp", scatter_dimension=0, tiled=True
        ).astype(jnp.float32),
    )
    grad_keys_low = (grad_keys_rows * SCALING).astype(jnp.bfloat16)
    grad_values_low = grad_values_rows.astype(jnp.bfloat16)
    grad_queries_low = (merge_heads(grad_q) * SCALING).astype(jnp.bfloat16)
    w_query_grad = left_dot(act1, grad_queries_low)
    w_key_grad = left_dot(act1, grad_keys_low)
    w_value_grad = left_dot(act1, grad_values_low)
    grad_act1 = (
        right_dot(grad_queries_low, w_query)
        + right_dot(grad_keys_low, w_key)
        + right_dot(grad_values_low, w_value)
    )
    grad_frames_norm, norm1_gain_grad = norm1_back(grad_act1)
    frames_grad = grad_middle + grad_frames_norm
    shares = (
        lax.psum_scatter(norm1_gain_grad, ("blk", "grp"), scatter_dimension=0, tiled=True),
        lax.psum_scatter(w_query_grad, ("blk", "grp"), scatter_dimension=0, tiled=True),
        lax.psum_scatter(w_key_grad, ("blk", "grp"), scatter_dimension=0, tiled=True),
        lax.psum_scatter(w_value_grad, ("blk", "grp"), scatter_dimension=0, tiled=True),
        lax.psum_scatter(w_out_grad, ("blk", "grp"), scatter_dimension=0, tiled=True),
        lax.psum_scatter(norm2_gain_grad, ("blk", "grp"), scatter_dimension=0, tiled=True),
        lax.psum_scatter(w_up_grad, ("blk", "grp"), scatter_dimension=0, tiled=True),
        lax.psum_scatter(b_up_grad, ("blk", "grp"), scatter_dimension=0, tiled=True),
        lax.psum_scatter(w_down_grad, ("blk", "grp"), scatter_dimension=0, tiled=True),
        lax.psum_scatter(b_down_grad, ("blk", "grp"), scatter_dimension=0, tiled=True),
    )
    return (
        layer_out,
        frames_grad,
        shares[0],
        shares[1],
        shares[2],
        shares[3],
        shares[4],
        shares[5],
        shares[6],
        shares[7],
        shares[8],
        shares[9],
    )


def solution_ring(mesh):
    placed = (
        P(("blk", "grp"), None),
        P(),
        P(),
        P(),
        P(),
        P(),
        P(),
        P(),
        P(),
        P(),
        P(),
        P(),
        P(("blk", "grp"), None),
    )
    return jax.shard_map(
        shards_ring,
        mesh=mesh,
        in_specs=placed,
        out_specs=(
            P(("blk", "grp"), None),
            P(("blk", "grp"), None),
            P(("blk", "grp")),
            P(("blk", "grp"), None),
            P(("blk", "grp"), None),
            P(("blk", "grp"), None),
            P(("blk", "grp"), None),
            P(("blk", "grp")),
            P(("blk", "grp"), None),
            P(("blk", "grp")),
            P(("blk", "grp"), None),
            P(("blk", "grp")),
        ),
        check_vma=False,
    )


LOG2E = 1.4426950408889634
F32, BF16 = jnp.float32, jnp.bfloat16


def nt_dot(a, b):
    return lax.dot_general(a, b, (((1,), (1,)), ((), ())), preferred_element_type=F32)


def nn_dot(a, b):
    return lax.dot_general(a, b, (((1,), (0,)), ((), ())), preferred_element_type=F32)


def low_lanes(shape):
    return lax.broadcasted_iota(jnp.int32, shape, 1) < 64


def pack_kernel(half, frames_ref, gain_ref, wq_ref, wk_ref, wv_ref, kv_ref, q_ref, act_ref):
    @pl.when(pl.program_id(0) == 0)
    def _():
        x = frames_ref[...]
        r = lax.rsqrt(jnp.mean(x * x, axis=-1, keepdims=True) + EPSILON)
        act_ref[...] = (x * r * gain_ref[...]).astype(BF16)

    act = act_ref[...]
    q = nn_dot(act, wq_ref[...]).astype(BF16).astype(F32) * 0.125
    k = nn_dot(act, wk_ref[...])
    v = nn_dot(act, wv_ref[...])
    rows = q.shape[0]
    low = low_lanes((rows, 128))
    low_h = low_lanes((half // 2, 128))
    for p in range(q.shape[1] // 128):
        at = slice(p * 128, (p + 1) * 128)
        k2, v2, q2 = k[:, at], v[:, at], q[:, at]
        kv_a = jnp.where(low, k2, pltpu.roll(v2, 64, 1)).astype(BF16)
        kv_b = jnp.where(low, pltpu.roll(k2, 64, 1), v2).astype(BF16)
        for s in range(2):
            span = slice(s * half, (s + 1) * half)
            kv_ref[2 * p, s] = kv_a[span]
            kv_ref[2 * p + 1, s] = kv_b[span]
            top = q2[s * half : s * half + half // 2]
            bot = q2[s * half + half // 2 : (s + 1) * half]
            q_ref[2 * p, s] = jnp.where(low_h, top, pltpu.roll(bot, 64, 1)).astype(BF16)
            q_ref[2 * p + 1, s] = jnp.where(low_h, pltpu.roll(top, 64, 1), bot).astype(BF16)


def project_and_pack(frames, gain, w_query, w_key, w_value):
    rows, width = frames.shape
    heads, half, step = width // 64, rows // 2, 256
    w_spec = pl.BlockSpec((width, step), lambda i: (0, i))
    whole = lambda i: (0, 0)
    return pl.pallas_call(
        functools.partial(pack_kernel, half),
        grid=(width // step,),
        in_specs=[pl.BlockSpec((rows, width), whole), pl.BlockSpec((1, width), whole), w_spec, w_spec, w_spec],
        out_specs=[
            pl.BlockSpec((step // 64, 2, half, 128), lambda i: (i, 0, 0, 0)),
            pl.BlockSpec((step // 64, 2, half // 2, 128), lambda i: (i, 0, 0, 0)),
            pl.BlockSpec((rows, width), whole),
        ],
        out_shape=[
            jax.ShapeDtypeStruct((heads, 2, half, 128), BF16),
            jax.ShapeDtypeStruct((heads, 2, half // 2, 128), BF16),
            jax.ShapeDtypeStruct((rows, width), BF16),
        ],
        compiler_params=pltpu.CompilerParams(vmem_limit_bytes=40 << 20),
        name="project_and_pack",
    )(frames, gain.reshape(1, width), w_query, w_key, w_value)


def block_bounds(len_ref, items, qpos, first, last, key_block):
    off = jnp.int32(0)
    start = jnp.zeros(qpos.shape, jnp.int32)
    s_first, s_last = jnp.int32(0), jnp.int32(0)
    for i in range(items):
        start = jnp.where(qpos >= off, off, start)
        s_first = jnp.where(first >= off, off, s_first)
        s_last = jnp.where(last >= off, off, s_last)
        off = off + len_ref[i]
    lo, hi = s_first // key_block, last // key_block + 1
    f0 = jnp.clip((s_last + key_block - 1) // key_block, lo, hi)
    f1 = jnp.clip((first + 1) // key_block, f0, hi)
    return start, lo, f0, f1, hi


def query_ends(i, chunks, half, core):
    first = i * chunks * 2 * half + core * half
    return first, first + (chunks - 1) * 2 * half + half - 1


def spread(packed, low, to_high):
    f = packed.astype(F32)
    other = pltpu.roll(f, 64, 1)
    zero = jnp.zeros_like(f)
    if to_high:
        return jnp.where(low, zero, other).astype(BF16), jnp.where(low, zero, f).astype(BF16)
    return jnp.where(low, f, zero).astype(BF16), jnp.where(low, other, zero).astype(BF16)


def mix_kernel(
    items, chunks, key_block,
    len_ref, core_ref, kv_ref, qp_ref, qpos_ref,
    out_t_ref, lse_ref, out_ref,
    kv_t, qz, acc, m_ref, l_ref,
):
    i = pl.program_id(0)
    half = 2 * qp_ref.shape[1]
    n = chunks * half
    core = core_ref[0]

    @pl.when(i == 0)
    def _():
        for c in range(kv_ref.shape[0] // 512):
            at = slice(c * 512, (c + 1) * 512)
            kv_t[:, at] = kv_ref[at, :].astype(F32).T.astype(BF16)

    low = low_lanes((half // 2, 128))
    for c in range(chunks):
        a, b = spread(qp_ref[c], low, False)
        qz[c * half : c * half + half // 2] = a
        qz[c * half + half // 2 : (c + 1) * half] = b
    qpos = qpos_ref[...] + core * half
    first, last = query_ends(i, chunks, half, core)
    start, lo, f0, f1, hi = block_bounds(len_ref, items, qpos, first, last, key_block)
    acc[...] = jnp.zeros_like(acc)
    m_ref[...] = jnp.full_like(m_ref, MASKED)
    l_ref[...] = jnp.zeros_like(l_ref)

    def step(j, masked):
        at = pl.ds(pl.multiple_of(j * key_block, key_block), key_block)
        s = nt_dot(kv_ref[at, :], qz[...]) * LOG2E
        if masked:
            kpos = j * key_block + lax.broadcasted_iota(jnp.int32, (key_block, 1), 0)
            s = jnp.where((kpos >= start) & (kpos <= qpos), s, MASKED)
        m_old = m_ref[...]
        m_new = jnp.maximum(m_old, jnp.max(s, axis=0, keepdims=True))
        p = jnp.exp2(s - m_new)
        alpha = jnp.exp2(m_old - m_new)
        m_ref[...] = m_new
        l_ref[...] = l_ref[...] * alpha + jnp.sum(p, axis=0, keepdims=True)
        acc[...] = acc[...] * alpha + nn_dot(kv_t[64:, at], p.astype(BF16))

    lax.fori_loop(lo, f0, lambda j, c: (step(j, True), c)[1], 0)
    lax.fori_loop(f0, f1, lambda j, c: (step(j, False), c)[1], 0)
    lax.fori_loop(f1, hi, lambda j, c: (step(j, True), c)[1], 0)
    out_t = acc[...] / l_ref[...]
    out_t_ref[...] = out_t
    lse_ref[...] = m_ref[...] + jnp.log2(l_ref[...])
    doubled = jnp.concatenate([out_t, out_t], axis=0).T
    for c in range(chunks):
        a = doubled[c * half : c * half + half // 2]
        b = doubled[c * half + half // 2 : (c + 1) * half]
        out_ref[c] = jnp.where(low, a, b).astype(BF16)


def mix(lengths, core, kv, qp, qpos, chunks=4, key_block=768):
    total = kv.shape[0]
    n_src, quarter = qp.shape[0], qp.shape[1]
    half = 2 * quarter
    n = chunks * half
    whole = lambda i, *_: (0, 0)
    return pl.pallas_call(
        functools.partial(mix_kernel, lengths.shape[0], chunks, key_block),
        grid_spec=pltpu.PrefetchScalarGridSpec(
            num_scalar_prefetch=2,
            grid=(n_src // chunks,),
            in_specs=[
                pl.BlockSpec((total, 128), whole),
                pl.BlockSpec((chunks, quarter, 128), lambda i, *_: (i, 0, 0)),
                pl.BlockSpec((1, n), lambda i, *_: (0, i)),
            ],
            out_specs=[
                pl.BlockSpec((64, n), lambda i, *_: (0, i)),
                pl.BlockSpec((1, n), lambda i, *_: (0, i)),
                pl.BlockSpec((chunks, quarter, 128), lambda i, *_: (i, 0, 0)),
            ],
            scratch_shapes=[
                pltpu.VMEM((128, total), BF16),
                pltpu.VMEM((n, 128), BF16),
                pltpu.VMEM((64, n), F32),
                pltpu.VMEM((1, n), F32),
                pltpu.VMEM((1, n), F32),
            ],
        ),
        out_shape=[
            jax.ShapeDtypeStruct((64, n_src * half), F32),
            jax.ShapeDtypeStruct((1, n_src * half), F32),
            jax.ShapeDtypeStruct((n_src, quarter, 128), BF16),
        ],
        compiler_params=pltpu.CompilerParams(vmem_limit_bytes=40 << 20),
        name="mix",
    )(lengths, core, kv, qp, qpos)


def back_kernel(
    items, chunks, key_block,
    len_ref, core_ref, kv_ref, qp_ref, dp_ref, qpos_ref, out_t_ref, lse_ref,
    dkv_ref, dq_ref,
    kv_t, qd, dq_acc,
):
    i = pl.program_id(0)
    half = 2 * qp_ref.shape[1]
    n = chunks * half
    core = core_ref[0]

    @pl.when(i == 0)
    def _():
        for c in range(kv_ref.shape[0] // 512):
            at = slice(c * 512, (c + 1) * 512)
            kv_t[:, at] = kv_ref[at, :].astype(F32).T.astype(BF16)
        dkv_ref[...] = jnp.zeros_like(dkv_ref)

    low = low_lanes((half // 2, 128))
    for c in range(chunks):
        a, b = spread(qp_ref[c], low, False)
        qd[c * half : c * half + half // 2] = a
        qd[c * half + half // 2 : (c + 1) * half] = b
        a, b = spread(dp_ref[c], low, True)
        qd[n + c * half : n + c * half + half // 2] = a
        qd[n + c * half + half // 2 : n + (c + 1) * half] = b
    do_t = qd[n:, :].astype(F32).T[64:]
    delta = jnp.sum(do_t * out_t_ref[...], axis=0, keepdims=True)
    lse = lse_ref[...]
    qpos = qpos_ref[...] + core * half
    first, last = query_ends(i, chunks, half, core)
    start, lo, f0, f1, hi = block_bounds(len_ref, items, qpos, first, last, key_block)
    dq_acc[...] = jnp.zeros_like(dq_acc)

    def step(j, masked):
        at = pl.ds(pl.multiple_of(j * key_block, key_block), key_block)
        both = nt_dot(kv_ref[at, :], qd[...])
        s = both[:, :n] * LOG2E
        if masked:
            kpos = j * key_block + lax.broadcasted_iota(jnp.int32, (key_block, 1), 0)
            s = jnp.where((kpos >= start) & (kpos <= qpos), s, MASKED)
        p = jnp.exp2(s - lse)
        ds = (p * (both[:, n:] - delta)).astype(BF16)
        dq_acc[...] += nn_dot(kv_t[:64, at], ds)
        dkv_ref[at, :] += nn_dot(ds, qd[:n, :]) + nn_dot(p.astype(BF16), qd[n:, :])

    lax.fori_loop(lo, f0, lambda j, c: (step(j, True), c)[1], 0)
    lax.fori_loop(f0, f1, lambda j, c: (step(j, False), c)[1], 0)
    lax.fori_loop(f1, hi, lambda j, c: (step(j, True), c)[1], 0)
    dq_t = dq_acc[...] * 0.125
    doubled = jnp.concatenate([dq_t, dq_t], axis=0).T
    for c in range(chunks):
        a = doubled[c * half : c * half + half // 2]
        b = doubled[c * half + half // 2 : (c + 1) * half]
        dq_ref[c] = jnp.where(low, a, b).astype(BF16)


def mix_back(lengths, core, kv, qp, dp, qpos, out_t, lse, chunks=4, key_block=768):
    total = kv.shape[0]
    n_src, quarter = qp.shape[0], qp.shape[1]
    half = 2 * quarter
    n = chunks * half
    whole = lambda i, *_: (0, 0)
    rows = lambda i, *_: (0, i)
    blocks = pl.BlockSpec((chunks, quarter, 128), lambda i, *_: (i, 0, 0))
    return pl.pallas_call(
        functools.partial(back_kernel, lengths.shape[0], chunks, key_block),
        grid_spec=pltpu.PrefetchScalarGridSpec(
            num_scalar_prefetch=2,
            grid=(n_src // chunks,),
            in_specs=[
                pl.BlockSpec((total, 128), whole),
                blocks,
                blocks,
                pl.BlockSpec((1, n), rows),
                pl.BlockSpec((64, n), rows),
                pl.BlockSpec((1, n), rows),
            ],
            out_specs=[pl.BlockSpec((total, 128), whole), blocks],
            scratch_shapes=[
                pltpu.VMEM((128, total), BF16),
                pltpu.VMEM((2 * n, 128), BF16),
                pltpu.VMEM((64, n), F32),
            ],
        ),
        out_shape=[
            jax.ShapeDtypeStruct((total, 128), F32),
            jax.ShapeDtypeStruct((n_src, quarter, 128), BF16),
        ],
        compiler_params=pltpu.CompilerParams(vmem_limit_bytes=48 << 20),
        name="mix_back",
    )(lengths, core, kv, qp, dp, qpos, out_t, lse)


def packed_positions(n_src, half):
    j = np.arange(n_src * half)
    return ((j // half) * 2 * half + j % half).astype(np.int32)[None]


MESH = pl.DeviceIdType.MESH
ALL = ("blk", "grp")


def place(index):
    return {"blk": lax.div(index, 2), "grp": lax.rem(index, 2)}


def head_of(index):
    blk, grp = lax.div(index, 2), lax.rem(index, 2)
    return lax.div(blk, 2) * 2 + grp, lax.rem(blk, 2)


def own_index():
    return lax.axis_index("blk") * 2 + lax.axis_index("grp")


def greet_all(me, n):
    barrier = pltpu.get_barrier_semaphore()

    @pl.loop(1, n)
    def _(i):
        pl.semaphore_signal(barrier, inc=1, device_id=place(lax.rem(me + i, n)), device_id_type=MESH)

    pl.semaphore_wait(barrier, n - 1)


def remote(src, dst, send_sem, recv_sem, device):
    return pltpu.make_async_remote_copy(
        src_ref=src, dst_ref=dst, send_sem=send_sem, recv_sem=recv_sem, device_id=device, device_id_type=MESH
    )


def to_heads_kernel(n, kv_in, q_in, kv_out, q_out, send, recv, local, pair):
    me = own_index()
    head, core = head_of(me)
    greet_all(me, n)

    def copies(i, src):
        other = lax.rem(me + i, n)
        h, c = head_of(other)
        kv_at = core if src is not me else c
        return (
            remote(kv_in.at[h, c], kv_out.at[src, kv_at], send.at[0, i], recv.at[0, src], place(other)),
            remote(q_in.at[h, c], q_out.at[src], send.at[1, i], recv.at[1, src], place(other)),
        )

    @pl.loop(1, n)
    def _(i):
        for copy in copies(i, me):
            copy.start()

    own = (
        pltpu.make_async_copy(kv_in.at[head, core], kv_out.at[me, core], local.at[0]),
        pltpu.make_async_copy(q_in.at[head, core], q_out.at[me], local.at[1]),
    )
    for copy in own:
        copy.start()
    for copy in own:
        copy.wait()

    @pl.loop(1, n)
    def _(i):
        for copy in copies(i, lax.rem(me + i, n)):
            copy.wait()

    sibling = {"blk": lax.axis_index("blk") + 1 - 2 * core, "grp": lax.axis_index("grp")}
    swap = remote(kv_out.at[:, core], kv_out.at[:, core], pair.at[0], pair.at[1], sibling)
    swap.start()
    swap.wait()


def to_heads(kv, q, n):
    half = kv.shape[2]
    anywhere = pl.BlockSpec(memory_space=pl.ANY)
    return pl.pallas_call(
        functools.partial(to_heads_kernel, n),
        in_specs=[anywhere] * 2,
        out_specs=[anywhere] * 2,
        out_shape=[
            jax.ShapeDtypeStruct((n, 2, half, 128), BF16),
            jax.ShapeDtypeStruct((n, half // 2, 128), BF16),
        ],
        scratch_shapes=[
            pltpu.SemaphoreType.DMA((2, n)),
            pltpu.SemaphoreType.DMA((2, n)),
            pltpu.SemaphoreType.DMA((2,)),
            pltpu.SemaphoreType.DMA((2,)),
        ],
        compiler_params=pltpu.CompilerParams(collective_id=0, has_side_effects=True),
        name="to_heads",
    )(kv, q)


def exchange_kernel(n, x_in, x_out, send, recv, local):
    me = own_index()
    greet_all(me, n)

    def copy_with(i, src):
        other = lax.rem(me + i, n)
        return remote(x_in.at[other], x_out.at[src], send.at[i], recv.at[src], place(other))

    @pl.loop(1, n)
    def _(i):
        copy_with(i, me).start()

    own = pltpu.make_async_copy(x_in.at[me], x_out.at[me], local)
    own.start()
    own.wait()

    @pl.loop(1, n)
    def _(i):
        copy_with(i, lax.rem(me + i, n)).wait()


def exchange(x, n, collective_id):
    anywhere = pl.BlockSpec(memory_space=pl.ANY)
    return pl.pallas_call(
        functools.partial(exchange_kernel, n),
        in_specs=[anywhere],
        out_specs=anywhere,
        out_shape=jax.ShapeDtypeStruct(x.shape, x.dtype),
        scratch_shapes=[
            pltpu.SemaphoreType.DMA((n,)),
            pltpu.SemaphoreType.DMA((n,)),
            pltpu.SemaphoreType.DMA,
        ],
        compiler_params=pltpu.CompilerParams(collective_id=collective_id, has_side_effects=True),
        name="exchange",
    )(x)


def from_heads_kernel(n, dkv_in, dq_in, dkv_out, dq_out, theirs, total, send, recv, local, pair):
    me = own_index()
    head, core = head_of(me)
    greet_all(me, n)
    sibling = {"blk": lax.axis_index("blk") + 1 - 2 * core, "grp": lax.axis_index("grp")}
    swap = remote(dkv_in.at[:, 1 - core], theirs, pair.at[0], pair.at[1], sibling)
    swap.start()

    def dq_copy(i, src):
        other = lax.rem(me + i, n)
        return remote(dq_in.at[other], dq_out.at[src], send.at[1, i], recv.at[1, src], place(other))

    def dkv_copy(i, src):
        other = lax.rem(me + i, n)
        return remote(total.at[other], dkv_out.at[src], send.at[0, i], recv.at[0, src], place(other))

    @pl.loop(1, n)
    def _(i):
        dq_copy(i, me).start()

    own_q = pltpu.make_async_copy(dq_in.at[me], dq_out.at[me], local.at[1])
    own_q.start()
    swap.wait()

    def add(j):
        total[j] = (dkv_in[j, core] + theirs[j]).astype(BF16)

    @pl.loop(1, n)
    def _(i):
        add(lax.rem(me + i, n))
        dkv_copy(i, me).start()

    add(me)
    own = pltpu.make_async_copy(total.at[me], dkv_out.at[me], local.at[0])
    own.start()
    own.wait()
    own_q.wait()

    @pl.loop(1, n)
    def _(i):
        src = lax.rem(me + i, n)
        dkv_copy(i, src).wait()
        dq_copy(i, src).wait()


def from_heads(dkv, dq, n):
    half = dkv.shape[2]
    anywhere = pl.BlockSpec(memory_space=pl.ANY)
    return pl.pallas_call(
        functools.partial(from_heads_kernel, n),
        in_specs=[pl.BlockSpec(memory_space=pltpu.VMEM), anywhere],
        out_specs=[anywhere] * 2,
        out_shape=[
            jax.ShapeDtypeStruct((n, half, 128), BF16),
            jax.ShapeDtypeStruct(dq.shape, BF16),
        ],
        scratch_shapes=[
            pltpu.VMEM((n, half, 128), F32),
            pltpu.VMEM((n, half, 128), BF16),
            pltpu.SemaphoreType.DMA((2, n)),
            pltpu.SemaphoreType.DMA((2, n)),
            pltpu.SemaphoreType.DMA((2,)),
            pltpu.SemaphoreType.DMA((2,)),
        ],
        compiler_params=pltpu.CompilerParams(
            collective_id=1, has_side_effects=True, vmem_limit_bytes=24 << 20
        ),
        name="from_heads",
    )(dkv, dq)


def flipped(x, axis):
    if axis == "x":
        return lax.ppermute(x, "grp", [(0, 1), (1, 0)])
    bit = {"core": 1, "y": 2, "z0": 4, "z1": 8}[axis]
    return lax.ppermute(x, "blk", [(i, i ^ bit) for i in range(lax.axis_size("blk"))])


def bit_of(axis):
    if axis == "x":
        return lax.axis_index("grp")
    bit = {"core": 1, "y": 2, "z0": 4, "z1": 8}[axis]
    return lax.rem(lax.div(lax.axis_index("blk"), bit), 2)


def pick(x, dim, index):
    return lax.dynamic_index_in_dim(x, index, dim, keepdims=False)


def scattered_sum(x, order):
    dims = ["z1", "z0", "y", "x"]
    total = x
    for axis in order:
        mine, at = bit_of(axis), dims.index(axis)
        got = flipped(pick(total, at, 1 - mine), axis)
        total = pick(total, at, mine).astype(F32) + got.astype(F32)
        dims.remove(axis)
        if dims:
            total = total.astype(BF16)
    return total


def halves(x, core, per_device):
    parts = x.reshape(x.shape[0], 8, 2, 2 * per_device)
    take = lambda c: pick(parts, 2, c).reshape(x.shape[0], 16 * per_device)
    return take(core), take(1 - core)


def both(x):
    return jnp.concatenate([x, flipped(x, "core")], axis=0)


def row_gradients(left, right, core, per_device):
    mine, others = halves(left, core, per_device)
    lefts = jnp.concatenate([mine, flipped(others, "core")], axis=0)
    grad = left_dot(lefts, right).astype(BF16)
    return grad.reshape(2, 2, 2, 2, per_device, grad.shape[1])


def unpacked(blocks, rows):
    parts = blocks.reshape(8, 2, 2, rows // 4, 2, 64)
    return parts.transpose(1, 4, 3, 0, 2, 5).reshape(rows, 1024)


def shards_heads(
    frames, lengths, norm1_gain, w_query, w_key, w_value, w_out, norm2_gain, w_up, b_up, w_down, b_down, cotangent
):
    rows, width = frames.shape
    n = lax.axis_size("blk") * lax.axis_size("grp")
    half = rows // 2
    core = bit_of("core")
    core_word = core.astype(jnp.int32).reshape(1)
    qpos = jnp.asarray(packed_positions(n, half))

    kv_blocks, q_blocks, act1 = project_and_pack(frames, norm1_gain, w_query, w_key, w_value)
    kv, q = to_heads(kv_blocks, q_blocks, n)
    kv_rows = kv.reshape(n * rows, 128)
    out_t, lse, out_blocks = mix(lengths, core_word, kv_rows, q, qpos)
    mixed = unpacked(exchange(out_blocks, n, 2), rows)

    middle = frames + jnp.dot(mixed, w_out, preferred_element_type=F32)
    normed2, norm2_back = jax.vjp(rms_norm, middle, norm2_gain)
    act2 = normed2.astype(BF16)
    before = jnp.dot(act2, w_up, preferred_element_type=F32) + b_up
    activated, gelu_back = jax.vjp(gelu_exact, before)
    hidden = activated.astype(BF16)
    layer_out = middle + jnp.dot(hidden, w_down, preferred_element_type=F32) + b_down
    grad_low = cotangent.astype(BF16)
    b_down_grad = jnp.sum(grad_low.astype(F32), axis=0)
    grad_before = gelu_back(right_dot(grad_low, w_down))[0].astype(BF16)
    b_up_grad = jnp.sum(grad_before.astype(F32), axis=0)
    grad_mid_norm, norm2_gain_grad = norm2_back(right_dot(grad_before, w_up))
    grad_middle = cotangent + grad_mid_norm
    grad_attn = grad_middle.astype(BF16)
    grad_mixed = right_dot(grad_attn, w_out).astype(BF16)

    grad_blocks = exchange(to_blocks(grad_mixed), n, 3)
    dkv, dq = mix_back(lengths, core_word, kv_rows, q, grad_blocks, qpos, out_t, lse)

    grads_low = both(grad_low)
    w_down_part = row_gradients(hidden, grads_low, core, 128)
    w_up_part = row_gradients(act2, both(grad_before), core, 32)
    w_out_part = row_gradients(mixed, both(grad_attn), core, 32)
    w_down_grad = scattered_sum(w_down_part, ("x", "y", "z0", "z1"))
    w_up_grad = scattered_sum(w_up_part, ("y", "x", "z0", "z1"))
    w_out_grad = scattered_sum(w_out_part, ("x", "y", "z0", "z1"))

    dkv_blocks, dq_blocks = from_heads(dkv.reshape(n, 2, half, 128), dq, n)
    grad_queries = unpacked(dq_blocks, rows)
    grad_kv = dkv_blocks.reshape(8, 2, 2, half, 2, 64).transpose(4, 1, 3, 0, 2, 5).reshape(2, rows, width)
    grad_keys, grad_values = grad_kv[0], grad_kv[1]
    grad_act1 = right_dot(grad_queries, w_query) + right_dot(grad_keys, w_key) + right_dot(grad_values, w_value)
    unused_out, norm1_back = jax.vjp(rms_norm, frames, norm1_gain)
    grad_frames_norm, norm1_gain_grad = norm1_back(grad_act1)
    frames_grad = grad_middle + grad_frames_norm

    qkv = both(jnp.concatenate([grad_queries, grad_keys, grad_values], axis=1))
    qkv_part = row_gradients(act1, qkv, core, 32)
    w_query_grad = scattered_sum(qkv_part[..., :width], ("x", "y", "z0", "z1"))
    w_key_grad = scattered_sum(qkv_part[..., width : 2 * width], ("y", "x", "z0", "z1"))
    w_value_grad = scattered_sum(qkv_part[..., 2 * width :], ("x", "y", "z0", "z1"))

    small = jnp.concatenate(
        [
            norm1_gain_grad.reshape(n, -1),
            norm2_gain_grad.reshape(n, -1),
            b_down_grad.reshape(n, -1),
            b_up_grad.reshape(n, -1),
        ],
        axis=1,
    )
    part = width // n
    small = jnp.pad(small, ((0, 0), (0, 1024 - small.shape[1]))).reshape(n, 8, 128)
    small = jnp.sum(exchange(small, n, 4), axis=0).reshape(1024)
    return (
        layer_out,
        frames_grad,
        small[:part],
        w_query_grad,
        w_key_grad,
        w_value_grad,
        w_out_grad,
        small[part : 2 * part],
        w_up_grad,
        small[3 * part : 3 * part + b_up.shape[0] // n],
        w_down_grad,
        small[2 * part : 3 * part],
    )


def to_blocks(grad_mixed):
    rows = grad_mixed.shape[0]
    parts = grad_mixed.reshape(2, 2, rows // 4, 8, 2, 64)
    return parts.transpose(3, 0, 4, 2, 1, 5).reshape(32, rows // 4, 128)


def solution(mesh):
    if mesh.shape["blk"] != 16 or mesh.shape["grp"] != 2:
        return solution_ring(mesh)
    split = P(ALL, None)
    return jax.shard_map(
        shards_heads,
        mesh=mesh,
        in_specs=(split, P(), P(), P(), P(), P(), P(), P(), P(), P(), P(), P(), split),
        out_specs=(split, split, P(ALL), split, split, split, split, P(ALL), split, P(ALL), split, P(ALL)),
        check_vma=False,
    )
```

```python
import functools

import jax
import jax.numpy as jnp
import numpy as np
from jax import lax
from jax.experimental import pallas as pl
from jax.experimental.pallas import tpu as pltpu
from jax.sharding import PartitionSpec as P

HEAD_DIM = 64
ITEM_MAX = 4096


EPSILON = 1e-05
MASKED = -1e30
SCALING = 0.125


def shortened(array):

    def short(part):
        return part.astype(jnp.bfloat16) if part.dtype == jnp.float32 else part

    return jax.tree.map(short, array)


def passed_along(block, axis, distance):
    devices = range(lax.axis_size(axis))
    route = [(i - distance, i) for i in devices if i - distance in devices]
    return lax.ppermute(block, axis, route)


def rms_norm(values, gain):
    return values * lax.rsqrt(jnp.mean(values * values, axis=-1, keepdims=True) + EPSILON) * gain


def gelu_exact(values):
    return jax.nn.gelu(values, approximate=False)


def item_starts(lengths, positions):
    ends = jnp.cumsum(lengths)
    offsets = ends - lengths
    before = offsets[None, :] <= positions[:, None]
    return jnp.max(jnp.where(before, offsets[None, :], 0), axis=1)


def live_mask(query_pos, query_start, key_first, key_count):
    key_pos = key_first + jnp.arange(key_count, dtype=jnp.int32)
    return (key_pos[None, :] >= query_start[:, None]) & (key_pos[None, :] <= query_pos[:, None])


def split_heads(matrix):
    return matrix.reshape(matrix.shape[0], matrix.shape[1] // HEAD_DIM, HEAD_DIM)


def merge_heads(tensor):
    return tensor.reshape(tensor.shape[0], tensor.shape[1] * tensor.shape[2])


def scores_of(queries3, keys_block, mask):
    raw = jnp.einsum(
        "qhd,khd->hqk", queries3, split_heads(keys_block), preferred_element_type=jnp.float32
    )
    return jnp.where(mask[None], raw * SCALING, MASKED)


def left_dot(left, right):
    return lax.dot_general(
        left, right, (((0,), (0,)), ((), ())), preferred_element_type=jnp.float32
    )


def right_dot(left, right):
    return lax.dot_general(
        left, right, (((1,), (1,)), ((), ())), preferred_element_type=jnp.float32
    )


def grad_parts(queries3, grad_out3, log_total, delta, keys_block, values_block, mask):
    probs = jnp.exp(scores_of(queries3, keys_block, mask) - log_total[:, :, None])
    grad_probs = jnp.einsum(
        "qhd,khd->hqk", grad_out3, split_heads(values_block), preferred_element_type=jnp.float32
    )
    grad_scores = (probs * (grad_probs - delta[:, :, None])).astype(jnp.bfloat16)
    return (probs.astype(jnp.bfloat16), grad_scores)


def key_terms(queries3, grad_out3, probs_low, grad_scores):
    grad_keys = jnp.einsum(
        "hqk,qhd->khd", grad_scores, queries3, preferred_element_type=jnp.float32
    )
    grad_values = jnp.einsum(
        "hqk,qhd->khd", probs_low, grad_out3, preferred_element_type=jnp.float32
    )
    return (merge_heads(grad_keys), merge_heads(grad_values))


def query_term(grad_scores, keys_block):
    return jnp.einsum(
        "hqk,khd->qhd", grad_scores, split_heads(keys_block), preferred_element_type=jnp.float32
    )


def shards_ring(
    frames,
    lengths,
    norm1_gain,
    w_query,
    w_key,
    w_value,
    w_out,
    norm2_gain,
    w_up,
    b_up,
    w_down,
    b_down,
    cotangent,
):
    row_count = frames.shape[0]
    width = frames.shape[1]
    heads = width // HEAD_DIM
    groups = lax.axis_size("grp")
    block_rows = row_count * groups
    span = (ITEM_MAX + block_rows - 2) // block_rows
    blk_index = lax.axis_index("blk")
    sub_index = lax.axis_index("grp")
    block_first = blk_index * block_rows
    query_pos = block_first + sub_index * row_count + jnp.arange(row_count, dtype=jnp.int32)
    query_start = item_starts(lengths, query_pos)
    back_steps = jnp.arange(span + 1, dtype=jnp.int32)
    normed1, norm1_back = jax.vjp(rms_norm, frames, norm1_gain)
    act1 = normed1.astype(jnp.bfloat16)
    queries = jnp.dot(act1, w_query, preferred_element_type=jnp.float32).astype(jnp.bfloat16)
    keys_own = jnp.dot(act1, w_key, preferred_element_type=jnp.float32).astype(jnp.bfloat16)
    values_own = jnp.dot(act1, w_value, preferred_element_type=jnp.float32).astype(jnp.bfloat16)
    queries3 = split_heads(queries)
    block_keys, block_values = (
        lax.all_gather(keys_own, "grp", axis=0, tiled=True),
        lax.all_gather(values_own, "grp", axis=0, tiled=True),
    )

    def cycle_step(carry, unused_input):
        moved = jax.tree.map(
            lambda part, own: part.astype(own.dtype),
            passed_along(shortened(carry), "blk", 1),
            carry,
        )
        return (moved, moved)

    unused_last, far_blocks = lax.scan(cycle_step, (block_keys, block_values), None, length=span)
    keys_all = jnp.concatenate([block_keys[None], far_blocks[0]], axis=0)
    values_all = jnp.concatenate([block_values[None], far_blocks[1]], axis=0)

    def mask_for(back):
        return live_mask(query_pos, query_start, block_first - back * block_rows, block_rows)

    def total_step(carry, inputs):
        run_max, run_sum = carry
        keys_block, back = inputs
        scores = scores_of(queries3, keys_block, mask_for(back))
        new_max = jnp.maximum(run_max, jnp.max(scores, axis=-1))
        run_sum = run_sum * jnp.exp(run_max - new_max) + jnp.sum(
            jnp.exp(scores - new_max[:, :, None]), axis=-1
        )
        return ((new_max, run_sum), None)

    start_max = jnp.full((heads, row_count), MASKED, jnp.float32)
    start_sum = jnp.zeros((heads, row_count), jnp.float32)
    (top_max, top_sum), unused_out = lax.scan(
        total_step, (start_max, start_sum), (keys_all, back_steps)
    )
    log_total = top_max + jnp.log(top_sum)

    def mix_step(total, inputs):
        keys_block, values_block, back = inputs
        probs = jnp.exp(
            scores_of(queries3, keys_block, mask_for(back)) - log_total[:, :, None]
        ).astype(jnp.bfloat16)
        return (
            total
            + jnp.einsum(
                "hqk,khd->qhd", probs, split_heads(values_block), preferred_element_type=jnp.float32
            ),
            None,
        )

    zero_query = jnp.zeros((row_count, heads, HEAD_DIM), jnp.float32)
    mixed_sum, unused_out = lax.scan(mix_step, zero_query, (keys_all, values_all, back_steps))
    mixed = merge_heads(mixed_sum).astype(jnp.bfloat16)
    middle = frames + jnp.dot(mixed, w_out, preferred_element_type=jnp.float32)
    normed2, norm2_back = jax.vjp(rms_norm, middle, norm2_gain)
    act2 = normed2.astype(jnp.bfloat16)
    before = jnp.dot(act2, w_up, preferred_element_type=jnp.float32) + b_up
    activated, gelu_back = jax.vjp(gelu_exact, before)
    hidden = activated.astype(jnp.bfloat16)
    layer_out = middle + jnp.dot(hidden, w_down, preferred_element_type=jnp.float32) + b_down
    grad_low = cotangent.astype(jnp.bfloat16)
    b_down_grad = jnp.sum(grad_low.astype(jnp.float32), axis=0)
    w_down_grad = left_dot(hidden, grad_low)
    grad_before = gelu_back(right_dot(grad_low, w_down))[0].astype(jnp.bfloat16)
    b_up_grad = jnp.sum(grad_before.astype(jnp.float32), axis=0)
    w_up_grad = left_dot(act2, grad_before)
    grad_mid_norm, norm2_gain_grad = norm2_back(right_dot(grad_before, w_up))
    grad_middle = cotangent + grad_mid_norm
    grad_attn = grad_middle.astype(jnp.bfloat16)
    w_out_grad = left_dot(mixed, grad_attn)
    grad_mixed = right_dot(grad_attn, w_out).astype(jnp.bfloat16)
    grad_out3 = split_heads(grad_mixed)

    def delta_step(total, inputs):
        keys_block, values_block, back = inputs
        probs = jnp.exp(scores_of(queries3, keys_block, mask_for(back)) - log_total[:, :, None])
        grad_probs = jnp.einsum(
            "qhd,khd->hqk", grad_out3, split_heads(values_block), preferred_element_type=jnp.float32
        )
        return (total + jnp.sum(probs * grad_probs, axis=-1), None)

    delta, unused_out = lax.scan(
        delta_step, jnp.zeros((heads, row_count), jnp.float32), (keys_all, values_all, back_steps)
    )
    zero_block = jnp.zeros((block_rows, width), jnp.float32)

    def return_step(carry, inputs):
        grad_q, travel = carry
        keys_block, values_block, back = inputs
        probs_low, grad_scores = grad_parts(
            queries3, grad_out3, log_total, delta, keys_block, values_block, mask_for(back)
        )
        grad_keys, grad_values = key_terms(queries3, grad_out3, probs_low, grad_scores)
        moved = (
            passed_along((travel[0] + grad_keys).astype(jnp.bfloat16), "blk", -1).astype(
                jnp.float32
            ),
            passed_along((travel[1] + grad_values).astype(jnp.bfloat16), "blk", -1).astype(
                jnp.float32
            ),
        )
        return ((grad_q + query_term(grad_scores, keys_block), moved), None)

    (grad_q, travel), unused_out = lax.scan(
        return_step,
        (zero_query, (zero_block, zero_block)),
        (far_blocks[0], far_blocks[1], back_steps[1:]),
        reverse=True,
    )
    probs_low, grad_scores = grad_parts(
        queries3, grad_out3, log_total, delta, block_keys, block_values, mask_for(0)
    )
    grad_keys, grad_values = key_terms(queries3, grad_out3, probs_low, grad_scores)
    grad_q = grad_q + query_term(grad_scores, block_keys)
    block_grad_keys = travel[0] + grad_keys
    block_grad_values = travel[1] + grad_values
    grad_keys_rows, grad_values_rows = (
        lax.psum_scatter(
            block_grad_keys.astype(jnp.bfloat16), "grp", scatter_dimension=0, tiled=True
        ).astype(jnp.float32),
        lax.psum_scatter(
            block_grad_values.astype(jnp.bfloat16), "grp", scatter_dimension=0, tiled=True
        ).astype(jnp.float32),
    )
    grad_keys_low = (grad_keys_rows * SCALING).astype(jnp.bfloat16)
    grad_values_low = grad_values_rows.astype(jnp.bfloat16)
    grad_queries_low = (merge_heads(grad_q) * SCALING).astype(jnp.bfloat16)
    w_query_grad = left_dot(act1, grad_queries_low)
    w_key_grad = left_dot(act1, grad_keys_low)
    w_value_grad = left_dot(act1, grad_values_low)
    grad_act1 = (
        right_dot(grad_queries_low, w_query)
        + right_dot(grad_keys_low, w_key)
        + right_dot(grad_values_low, w_value)
    )
    grad_frames_norm, norm1_gain_grad = norm1_back(grad_act1)
    frames_grad = grad_middle + grad_frames_norm
    shares = (
        lax.psum_scatter(norm1_gain_grad, ("blk", "grp"), scatter_dimension=0, tiled=True),
        lax.psum_scatter(w_query_grad, ("blk", "grp"), scatter_dimension=0, tiled=True),
        lax.psum_scatter(w_key_grad, ("blk", "grp"), scatter_dimension=0, tiled=True),
        lax.psum_scatter(w_value_grad, ("blk", "grp"), scatter_dimension=0, tiled=True),
        lax.psum_scatter(w_out_grad, ("blk", "grp"), scatter_dimension=0, tiled=True),
        lax.psum_scatter(norm2_gain_grad, ("blk", "grp"), scatter_dimension=0, tiled=True),
        lax.psum_scatter(w_up_grad, ("blk", "grp"), scatter_dimension=0, tiled=True),
        lax.psum_scatter(b_up_grad, ("blk", "grp"), scatter_dimension=0, tiled=True),
        lax.psum_scatter(w_down_grad, ("blk", "grp"), scatter_dimension=0, tiled=True),
        lax.psum_scatter(b_down_grad, ("blk", "grp"), scatter_dimension=0, tiled=True),
    )
    return (
        layer_out,
        frames_grad,
        shares[0],
        shares[1],
        shares[2],
        shares[3],
        shares[4],
        shares[5],
        shares[6],
        shares[7],
        shares[8],
        shares[9],
    )


def solution_ring(mesh):
    placed = (
        P(("blk", "grp"), None),
        P(),
        P(),
        P(),
        P(),
        P(),
        P(),
        P(),
        P(),
        P(),
        P(),
        P(),
        P(("blk", "grp"), None),
    )
    return jax.shard_map(
        shards_ring,
        mesh=mesh,
        in_specs=placed,
        out_specs=(
            P(("blk", "grp"), None),
            P(("blk", "grp"), None),
            P(("blk", "grp")),
            P(("blk", "grp"), None),
            P(("blk", "grp"), None),
            P(("blk", "grp"), None),
            P(("blk", "grp"), None),
            P(("blk", "grp")),
            P(("blk", "grp"), None),
            P(("blk", "grp")),
            P(("blk", "grp"), None),
            P(("blk", "grp")),
        ),
        check_vma=False,
    )


LOG2E = 1.4426950408889634
F32, BF16 = jnp.float32, jnp.bfloat16


def nt_dot(a, b):
    return lax.dot_general(a, b, (((1,), (1,)), ((), ())), preferred_element_type=F32)


def nn_dot(a, b):
    return lax.dot_general(a, b, (((1,), (0,)), ((), ())), preferred_element_type=F32)


def low_lanes(shape):
    return lax.broadcasted_iota(jnp.int32, shape, 1) < 64


def pair_low(a, b, low):
    return jnp.where(low, a, pltpu.roll(b, 64, 1))


def pair_high(a, b, low):
    return jnp.where(low, pltpu.roll(a, 64, 1), b)


def store_halves(ref, x):
    low = low_lanes((x.shape[0], 128))
    for p in range(x.shape[1] // 256):
        a, b = x[:, p * 256 : p * 256 + 128], x[:, p * 256 + 128 : (p + 1) * 256]
        ref[0, :, p * 128 : (p + 1) * 128] = pair_low(a, b, low).astype(BF16)
        ref[1, :, p * 128 : (p + 1) * 128] = pair_high(a, b, low).astype(BF16)


def pack_kernel(half, frames_ref, gain_ref, wq_ref, wk_ref, wv_ref, kv_ref, q_ref, halves_ref, act_ref):
    @pl.when(pl.program_id(0) == 0)
    def _():
        x = frames_ref[...]
        r = lax.rsqrt(jnp.mean(x * x, axis=-1, keepdims=True) + EPSILON)
        normed = x * r * gain_ref[...]
        act_ref[...] = normed.astype(BF16)
        store_halves(halves_ref, normed)

    act = act_ref[...]
    q = nn_dot(act, wq_ref[...]).astype(BF16).astype(F32) * 0.125
    k = nn_dot(act, wk_ref[...])
    v = nn_dot(act, wv_ref[...])
    rows = q.shape[0]
    low = low_lanes((rows, 128))
    low_h = low_lanes((half // 2, 128))
    for p in range(q.shape[1] // 128):
        at = slice(p * 128, (p + 1) * 128)
        k2, v2, q2 = k[:, at], v[:, at], q[:, at]
        kv_a = jnp.where(low, k2, pltpu.roll(v2, 64, 1)).astype(BF16)
        kv_b = jnp.where(low, pltpu.roll(k2, 64, 1), v2).astype(BF16)
        for s in range(2):
            span = slice(s * half, (s + 1) * half)
            kv_ref[2 * p, s] = kv_a[span]
            kv_ref[2 * p + 1, s] = kv_b[span]
            top = q2[s * half : s * half + half // 2]
            bot = q2[s * half + half // 2 : (s + 1) * half]
            q_ref[2 * p, s] = jnp.where(low_h, top, pltpu.roll(bot, 64, 1)).astype(BF16)
            q_ref[2 * p + 1, s] = jnp.where(low_h, pltpu.roll(top, 64, 1), bot).astype(BF16)


def project_and_pack(frames, gain, w_query, w_key, w_value):
    rows, width = frames.shape
    heads, half, step = width // 64, rows // 2, 256
    w_spec = pl.BlockSpec((width, step), lambda i: (0, i))
    whole = lambda i: (0, 0)
    return pl.pallas_call(
        functools.partial(pack_kernel, half),
        grid=(width // step,),
        in_specs=[pl.BlockSpec((rows, width), whole), pl.BlockSpec((1, width), whole), w_spec, w_spec, w_spec],
        out_specs=[
            pl.BlockSpec((step // 64, 2, half, 128), lambda i: (i, 0, 0, 0)),
            pl.BlockSpec((step // 64, 2, half // 2, 128), lambda i: (i, 0, 0, 0)),
            pl.BlockSpec((2, rows, width // 2), lambda i: (0, 0, 0)),
        ],
        out_shape=[
            jax.ShapeDtypeStruct((heads, 2, half, 128), BF16),
            jax.ShapeDtypeStruct((heads, 2, half // 2, 128), BF16),
            jax.ShapeDtypeStruct((2, rows, width // 2), BF16),
        ],
        scratch_shapes=[pltpu.VMEM((rows, width), BF16)],
        compiler_params=pltpu.CompilerParams(vmem_limit_bytes=40 << 20),
        name="project_and_pack",
    )(frames, gain.reshape(1, width), w_query, w_key, w_value)


def block_bounds(len_ref, items, qpos, first, last, key_block):
    off = jnp.int32(0)
    start = jnp.zeros(qpos.shape, jnp.int32)
    s_first, s_last = jnp.int32(0), jnp.int32(0)
    for i in range(items):
        start = jnp.where(qpos >= off, off, start)
        s_first = jnp.where(first >= off, off, s_first)
        s_last = jnp.where(last >= off, off, s_last)
        off = off + len_ref[i]
    lo, hi = s_first // key_block, last // key_block + 1
    f0 = jnp.clip((s_last + key_block - 1) // key_block, lo, hi)
    f1 = jnp.clip((first + 1) // key_block, f0, hi)
    return start, lo, f0, f1, hi


def query_ends(i, chunks, half, core):
    first = i * chunks * 2 * half + core * half
    return first, first + (chunks - 1) * 2 * half + half - 1


def spread(packed, low, to_high):
    f = packed.astype(F32)
    other = pltpu.roll(f, 64, 1)
    zero = jnp.zeros_like(f)
    if to_high:
        return jnp.where(low, zero, other).astype(BF16), jnp.where(low, zero, f).astype(BF16)
    return jnp.where(low, f, zero).astype(BF16), jnp.where(low, other, zero).astype(BF16)


def mix_kernel(
    items, chunks, key_block,
    len_ref, core_ref, kv_ref, qp_ref, qpos_ref,
    out_t_ref, lse_ref, out_ref,
    kv_t, qz, acc, m_ref, l_ref,
):
    i = pl.program_id(0)
    half = 2 * qp_ref.shape[1]
    n = chunks * half
    core = core_ref[0]

    @pl.when(i == 0)
    def _():
        for c in range(kv_ref.shape[0] // 512):
            at = slice(c * 512, (c + 1) * 512)
            kv_t[:, at] = kv_ref[at, :].astype(F32).T.astype(BF16)

    low = low_lanes((half // 2, 128))
    for c in range(chunks):
        a, b = spread(qp_ref[c], low, False)
        qz[c * half : c * half + half // 2] = a
        qz[c * half + half // 2 : (c + 1) * half] = b
    qpos = qpos_ref[...] + core * half
    first, last = query_ends(i, chunks, half, core)
    start, lo, f0, f1, hi = block_bounds(len_ref, items, qpos, first, last, key_block)
    acc[...] = jnp.zeros_like(acc)
    m_ref[...] = jnp.full_like(m_ref, MASKED)
    l_ref[...] = jnp.zeros_like(l_ref)

    def step(j, masked):
        at = pl.ds(pl.multiple_of(j * key_block, key_block), key_block)
        s = nt_dot(kv_ref[at, :], qz[...]) * LOG2E
        if masked:
            kpos = j * key_block + lax.broadcasted_iota(jnp.int32, (key_block, 1), 0)
            s = jnp.where((kpos >= start) & (kpos <= qpos), s, MASKED)
        m_old = m_ref[...]
        m_new = jnp.maximum(m_old, jnp.max(s, axis=0, keepdims=True))
        p = jnp.exp2(s - m_new)
        alpha = jnp.exp2(m_old - m_new)
        m_ref[...] = m_new
        l_ref[...] = l_ref[...] * alpha + jnp.sum(p, axis=0, keepdims=True)
        acc[...] = acc[...] * alpha + nn_dot(kv_t[64:, at], p.astype(BF16))

    lax.fori_loop(lo, f0, lambda j, c: (step(j, True), c)[1], 0)
    lax.fori_loop(f0, f1, lambda j, c: (step(j, False), c)[1], 0)
    lax.fori_loop(f1, hi, lambda j, c: (step(j, True), c)[1], 0)
    out_t = acc[...] / l_ref[...]
    out_t_ref[...] = out_t
    lse_ref[...] = m_ref[...] + jnp.log2(l_ref[...])
    doubled = jnp.concatenate([out_t, out_t], axis=0).T
    for c in range(chunks):
        a = doubled[c * half : c * half + half // 2]
        b = doubled[c * half + half // 2 : (c + 1) * half]
        out_ref[c] = jnp.where(low, a, b).astype(BF16)


def mix(lengths, core, kv, qp, qpos, chunks=4, key_block=768):
    total = kv.shape[0]
    n_src, quarter = qp.shape[0], qp.shape[1]
    half = 2 * quarter
    n = chunks * half
    whole = lambda i, *_: (0, 0)
    return pl.pallas_call(
        functools.partial(mix_kernel, lengths.shape[0], chunks, key_block),
        grid_spec=pltpu.PrefetchScalarGridSpec(
            num_scalar_prefetch=2,
            grid=(n_src // chunks,),
            in_specs=[
                pl.BlockSpec((total, 128), whole),
                pl.BlockSpec((chunks, quarter, 128), lambda i, *_: (i, 0, 0)),
                pl.BlockSpec((1, n), lambda i, *_: (0, i)),
            ],
            out_specs=[
                pl.BlockSpec((64, n), lambda i, *_: (0, i)),
                pl.BlockSpec((1, n), lambda i, *_: (0, i)),
                pl.BlockSpec((chunks, quarter, 128), lambda i, *_: (i, 0, 0)),
            ],
            scratch_shapes=[
                pltpu.VMEM((128, total), BF16),
                pltpu.VMEM((n, 128), BF16),
                pltpu.VMEM((64, n), F32),
                pltpu.VMEM((1, n), F32),
                pltpu.VMEM((1, n), F32),
            ],
        ),
        out_shape=[
            jax.ShapeDtypeStruct((64, n_src * half), F32),
            jax.ShapeDtypeStruct((1, n_src * half), F32),
            jax.ShapeDtypeStruct((n_src, quarter, 128), BF16),
        ],
        compiler_params=pltpu.CompilerParams(vmem_limit_bytes=32 << 20),
        cost_estimate=pl.CostEstimate(flops=25_000_000_000, bytes_accessed=8 << 20, transcendentals=0),
        name="mix",
    )(lengths, core, kv, qp, qpos)


def back_kernel(
    items, chunks, key_block,
    len_ref, core_ref, kv_ref, qp_ref, dp_ref, qpos_ref, out_t_ref, lse_ref,
    dkv_ref, dq_ref,
    kv_t, qd, dq_acc,
):
    i = pl.program_id(0)
    half = 2 * qp_ref.shape[1]
    n = chunks * half
    core = core_ref[0]

    @pl.when(i == 0)
    def _():
        for c in range(kv_ref.shape[0] // 512):
            at = slice(c * 512, (c + 1) * 512)
            kv_t[:, at] = kv_ref[at, :].astype(F32).T.astype(BF16)
        dkv_ref[...] = jnp.zeros_like(dkv_ref)

    low = low_lanes((half // 2, 128))
    for c in range(chunks):
        a, b = spread(qp_ref[c], low, False)
        qd[c * half : c * half + half // 2] = a
        qd[c * half + half // 2 : (c + 1) * half] = b
        a, b = spread(dp_ref[c], low, True)
        qd[n + c * half : n + c * half + half // 2] = a
        qd[n + c * half + half // 2 : n + (c + 1) * half] = b
    do_t = qd[n:, :].astype(F32).T[64:]
    delta = jnp.sum(do_t * out_t_ref[...], axis=0, keepdims=True)
    lse = lse_ref[...]
    qpos = qpos_ref[...] + core * half
    first, last = query_ends(i, chunks, half, core)
    start, lo, f0, f1, hi = block_bounds(len_ref, items, qpos, first, last, key_block)
    dq_acc[...] = jnp.zeros_like(dq_acc)

    def step(j, masked):
        at = pl.ds(pl.multiple_of(j * key_block, key_block), key_block)
        both = nt_dot(kv_ref[at, :], qd[...])
        s = both[:, :n] * LOG2E
        if masked:
            kpos = j * key_block + lax.broadcasted_iota(jnp.int32, (key_block, 1), 0)
            s = jnp.where((kpos >= start) & (kpos <= qpos), s, MASKED)
        p = jnp.exp2(s - lse)
        ds = (p * (both[:, n:] - delta)).astype(BF16)
        dq_acc[...] += nn_dot(kv_t[:64, at], ds)
        dkv_ref[at, :] += nn_dot(ds, qd[:n, :]) + nn_dot(p.astype(BF16), qd[n:, :])

    lax.fori_loop(lo, f0, lambda j, c: (step(j, True), c)[1], 0)
    lax.fori_loop(f0, f1, lambda j, c: (step(j, False), c)[1], 0)
    lax.fori_loop(f1, hi, lambda j, c: (step(j, True), c)[1], 0)
    dq_t = dq_acc[...] * 0.125
    doubled = jnp.concatenate([dq_t, dq_t], axis=0).T
    for c in range(chunks):
        a = doubled[c * half : c * half + half // 2]
        b = doubled[c * half + half // 2 : (c + 1) * half]
        dq_ref[c] = jnp.where(low, a, b).astype(BF16)


def mix_back(lengths, core, kv, qp, dp, qpos, out_t, lse, chunks=4, key_block=768):
    total = kv.shape[0]
    n_src, quarter = qp.shape[0], qp.shape[1]
    half = 2 * quarter
    n = chunks * half
    whole = lambda i, *_: (0, 0)
    rows = lambda i, *_: (0, i)
    blocks = pl.BlockSpec((chunks, quarter, 128), lambda i, *_: (i, 0, 0))
    return pl.pallas_call(
        functools.partial(back_kernel, lengths.shape[0], chunks, key_block),
        grid_spec=pltpu.PrefetchScalarGridSpec(
            num_scalar_prefetch=2,
            grid=(n_src // chunks,),
            in_specs=[
                pl.BlockSpec((total, 128), whole),
                blocks,
                blocks,
                pl.BlockSpec((1, n), rows),
                pl.BlockSpec((64, n), rows),
                pl.BlockSpec((1, n), rows),
            ],
            out_specs=[pl.BlockSpec((total, 128), whole), blocks],
            scratch_shapes=[
                pltpu.VMEM((128, total), BF16),
                pltpu.VMEM((2 * n, 128), BF16),
                pltpu.VMEM((64, n), F32),
            ],
        ),
        out_shape=[
            jax.ShapeDtypeStruct((total, 128), F32),
            jax.ShapeDtypeStruct((n_src, quarter, 128), BF16),
        ],
        compiler_params=pltpu.CompilerParams(vmem_limit_bytes=32 << 20),
        cost_estimate=pl.CostEstimate(flops=40_000_000_000, bytes_accessed=8 << 20, transcendentals=0),
        name="mix_back",
    )(lengths, core, kv, qp, dp, qpos, out_t, lse)


def packed_positions(n_src, half):
    j = np.arange(n_src * half)
    return ((j // half) * 2 * half + j % half).astype(np.int32)[None]


def feed_kernel(
    blocks_ref, frames_ref, cot_ref, w_out_ref, gain_ref, w_up_ref, b_up_ref, w_down_ref, b_down_ref,
    out_ref, grad_mid_ref, grad_blocks_ref, hidden_ref, grad_before_ref, act2_ref, mixed_ref, low_ref, attn_ref,
    gain_grad_ref, b_up_grad_ref, b_down_grad_ref,
    mixed, act2, act_grad,
):
    i = pl.program_id(0)
    rows = frames_ref.shape[0]
    quarter = rows // 4
    low_q = low_lanes((quarter, 128))

    @pl.when(i == 0)
    def _():
        for zy in range(8):
            for s in range(2):
                a = blocks_ref[(zy * 2 + s) * 2].astype(F32)
                b = blocks_ref[(zy * 2 + s) * 2 + 1].astype(F32)
                at = slice(zy * 128, (zy + 1) * 128)
                first = 2 * s * quarter
                mixed[first : first + quarter, at] = pair_low(a, b, low_q)
                mixed[first + quarter : first + 2 * quarter, at] = pair_high(a, b, low_q)
        store_halves(mixed_ref, mixed[...])
        middle = frames_ref[...] + nn_dot(mixed[...].astype(BF16), w_out_ref[...])
        r = lax.rsqrt(jnp.mean(middle * middle, axis=-1, keepdims=True) + EPSILON)
        normed = middle * r * gain_ref[...]
        act2[...] = normed.astype(BF16)
        store_halves(act2_ref, normed)
        grad_mid_ref[...] = middle
        out_ref[...] = middle + b_down_ref[...]
        grad_low = cot_ref[...].astype(BF16)
        low_ref[...] = grad_low
        b_down_grad_ref[...] = jnp.sum(grad_low.astype(F32), axis=0, keepdims=True)
        act_grad[...] = jnp.zeros_like(act_grad)

    before = nn_dot(act2[...], w_up_ref[...]) + b_up_ref[...]
    cdf = 0.5 + 0.5 * lax.erf(before * 0.7071067811865476)
    pdf = jnp.exp(-0.5 * before * before) * 0.3989422804014327
    hidden = (before * cdf).astype(BF16)
    step = hidden.shape[1] // 2
    hidden_ref[0] = hidden[:, :step]
    hidden_ref[1] = hidden[:, step:]
    out_ref[...] += nn_dot(hidden, w_down_ref[...])
    grad_before = (nt_dot(low_ref[...], w_down_ref[...]) * (cdf + before * pdf)).astype(BF16)
    grad_before_ref[...] = grad_before
    b_up_grad_ref[...] = jnp.sum(grad_before.astype(F32), axis=0, keepdims=True)
    act_grad[...] += nt_dot(grad_before, w_up_ref[...])

    @pl.when(i == pl.num_programs(0) - 1)
    def _():
        middle = grad_mid_ref[...]
        r = lax.rsqrt(jnp.mean(middle * middle, axis=-1, keepdims=True) + EPSILON)
        n = middle * r
        g = act_grad[...]
        gain_grad_ref[...] = jnp.sum(g * n, axis=0, keepdims=True)
        g = g * gain_ref[...]
        grad_mid = cot_ref[...] + r * (g - n * jnp.mean(g * n, axis=-1, keepdims=True))
        grad_mid_ref[...] = grad_mid
        grad_attn = grad_mid.astype(BF16)
        attn_ref[...] = grad_attn
        grad_mixed = nt_dot(grad_attn, w_out_ref[...])
        for zy in range(8):
            for s in range(2):
                at = slice(zy * 128, (zy + 1) * 128)
                first = 2 * s * quarter
                a = grad_mixed[first : first + quarter, at]
                b = grad_mixed[first + quarter : first + 2 * quarter, at]
                grad_blocks_ref[(zy * 2 + s) * 2] = pair_low(a, b, low_q).astype(BF16)
                grad_blocks_ref[(zy * 2 + s) * 2 + 1] = pair_high(a, b, low_q).astype(BF16)


def feed(blocks, frames, cotangent, w_out, gain, w_up, b_up, w_down, b_down):
    rows, width = frames.shape
    ff = w_up.shape[1]
    steps = 8
    step = ff // steps
    fixed = lambda *shape: pl.BlockSpec(shape, lambda i: (0,) * len(shape))
    columns = lambda *shape: pl.BlockSpec(shape, lambda i: (0,) * (len(shape) - 1) + (i,))
    shape = jax.ShapeDtypeStruct
    return pl.pallas_call(
        feed_kernel,
        grid=(steps,),
        in_specs=[
            fixed(*blocks.shape),
            fixed(rows, width),
            fixed(rows, width),
            fixed(width, width),
            fixed(1, width),
            columns(width, step),
            columns(1, step),
            pl.BlockSpec((step, width), lambda i: (i, 0)),
            fixed(1, width),
        ],
        out_specs=[
            fixed(rows, width),
            fixed(rows, width),
            fixed(*blocks.shape),
            columns(2, rows, step // 2),
            columns(rows, step),
            fixed(2, rows, width // 2),
            fixed(2, rows, width // 2),
            fixed(rows, width),
            fixed(rows, width),
            fixed(1, width),
            columns(1, step),
            fixed(1, width),
        ],
        out_shape=[
            shape((rows, width), F32),
            shape((rows, width), F32),
            shape(blocks.shape, BF16),
            shape((2, rows, ff // 2), BF16),
            shape((rows, ff), BF16),
            shape((2, rows, width // 2), BF16),
            shape((2, rows, width // 2), BF16),
            shape((rows, width), BF16),
            shape((rows, width), BF16),
            shape((1, width), F32),
            shape((1, ff), F32),
            shape((1, width), F32),
        ],
        scratch_shapes=[
            pltpu.VMEM((rows, width), F32),
            pltpu.VMEM((rows, width), BF16),
            pltpu.VMEM((rows, width), F32),
        ],
        compiler_params=pltpu.CompilerParams(vmem_limit_bytes=40 << 20),
        name="feed",
    )(
        blocks, frames, cotangent, w_out, gain.reshape(1, width), w_up, b_up.reshape(1, ff), w_down,
        b_down.reshape(1, width),
    )


def input_grad_kernel(
    dkv_ref, dq_ref, frames_ref, grad_mid_ref, gain_ref, wq_ref, wk_ref, wv_ref, gain2_grad_ref, b_up_grad_ref,
    b_down_grad_ref, grads_ref, out_ref, small_ref,
):
    rows, width = frames_ref.shape
    quarter = rows // 4
    low_q, low_h = low_lanes((quarter, 128)), low_lanes((2 * quarter, 128))
    for zy in range(8):
        for s in range(2):
            j = (zy * 2 + s) * 2
            first = 2 * s * quarter
            a, b = dq_ref[j].astype(F32), dq_ref[j + 1].astype(F32)
            at = slice(zy * 128, (zy + 1) * 128)
            grads_ref[first : first + quarter, at] = pair_low(a, b, low_q).astype(BF16)
            grads_ref[first + quarter : first + 2 * quarter, at] = pair_high(a, b, low_q).astype(BF16)
            a, b = dkv_ref[j].astype(F32), dkv_ref[j + 1].astype(F32)
            at = slice(width + zy * 128, width + (zy + 1) * 128)
            grads_ref[first : first + 2 * quarter, at] = pair_low(a, b, low_h).astype(BF16)
            at = slice(2 * width + zy * 128, 2 * width + (zy + 1) * 128)
            grads_ref[first : first + 2 * quarter, at] = pair_high(a, b, low_h).astype(BF16)
    g = nt_dot(grads_ref[:, :width], wq_ref[...])
    g += nt_dot(grads_ref[:, width : 2 * width], wk_ref[...])
    g += nt_dot(grads_ref[:, 2 * width :], wv_ref[...])
    x = frames_ref[...]
    r = lax.rsqrt(jnp.mean(x * x, axis=-1, keepdims=True) + EPSILON)
    n = x * r
    gain_grad = jnp.sum(g * n, axis=0, keepdims=True)
    small_ref[...] = jnp.zeros_like(small_ref)
    for d in range(small_ref.shape[0]):
        at = slice(d // 4 * 128, (d // 4 + 1) * 128)
        small_ref[d, 0:1] = gain_grad[:, at]
        small_ref[d, 1:2] = gain2_grad_ref[:, at]
        small_ref[d, 2:3] = b_down_grad_ref[:, at]
        small_ref[d, 3:4] = b_up_grad_ref[:, d * 128 : (d + 1) * 128]
    g = g * gain_ref[...]
    out_ref[...] = grad_mid_ref[...] + r * (g - n * jnp.mean(g * n, axis=-1, keepdims=True))


def input_grad(dkv, dq, frames, grad_mid, gain, w_query, w_key, w_value, gain2_grad, b_up_grad, b_down_grad):
    rows, width = frames.shape
    shape = jax.ShapeDtypeStruct
    return pl.pallas_call(
        input_grad_kernel,
        in_specs=[pl.BlockSpec(memory_space=pltpu.VMEM)] * 11,
        out_specs=[pl.BlockSpec(memory_space=pltpu.VMEM)] * 3,
        out_shape=[shape((rows, 3 * width), BF16), shape((rows, width), F32), shape((32, 8, 128), F32)],
        compiler_params=pltpu.CompilerParams(vmem_limit_bytes=24 << 20),
        name="input_grad",
    )(
        dkv, dq, frames, grad_mid, gain.reshape(1, width), w_query, w_key, w_value, gain2_grad, b_up_grad, b_down_grad
    )


MESH = pl.DeviceIdType.MESH
ALL = ("blk", "grp")


def place(index):
    return {"blk": lax.div(index, 2), "grp": lax.rem(index, 2)}


def head_of(index):
    blk, grp = lax.div(index, 2), lax.rem(index, 2)
    return lax.div(blk, 2) * 2 + grp, lax.rem(blk, 2)


def own_index():
    return lax.axis_index("blk") * 2 + lax.axis_index("grp")


def greet_all(me, n):
    barrier = pltpu.get_barrier_semaphore()

    @pl.loop(1, n)
    def _(i):
        pl.semaphore_signal(barrier, inc=1, device_id=place(lax.rem(me + i, n)), device_id_type=MESH)

    pl.semaphore_wait(barrier, n - 1)


def remote(src, dst, send_sem, recv_sem, device):
    return pltpu.make_async_remote_copy(
        src_ref=src, dst_ref=dst, send_sem=send_sem, recv_sem=recv_sem, device_id=device, device_id_type=MESH
    )


def to_heads_kernel(n, kv_in, q_in, kv_out, q_out, send, recv, local, pair):
    me = own_index()
    head, core = head_of(me)
    greet_all(me, n)

    def copies(i, src):
        other = lax.rem(me + i, n)
        h, c = head_of(other)
        kv_at = core if src is not me else c
        return (
            remote(kv_in.at[h, c], kv_out.at[src, kv_at], send.at[0, i], recv.at[0, src], place(other)),
            remote(q_in.at[h, c], q_out.at[src], send.at[1, i], recv.at[1, src], place(other)),
        )

    @pl.loop(1, n)
    def _(i):
        for copy in copies(i, me):
            copy.start()

    own = (
        pltpu.make_async_copy(kv_in.at[head, core], kv_out.at[me, core], local.at[0]),
        pltpu.make_async_copy(q_in.at[head, core], q_out.at[me], local.at[1]),
    )
    for copy in own:
        copy.start()
    for copy in own:
        copy.wait()

    @pl.loop(1, n)
    def _(i):
        for copy in copies(i, lax.rem(me + i, n)):
            copy.wait()

    sibling = {"blk": lax.axis_index("blk") + 1 - 2 * core, "grp": lax.axis_index("grp")}
    swap = remote(kv_out.at[:, core], kv_out.at[:, core], pair.at[0], pair.at[1], sibling)
    swap.start()
    swap.wait()


def to_heads(kv, q, n):
    half = kv.shape[2]
    anywhere = pl.BlockSpec(memory_space=pl.ANY)
    return pl.pallas_call(
        functools.partial(to_heads_kernel, n),
        in_specs=[anywhere] * 2,
        out_specs=[anywhere] * 2,
        out_shape=[
            jax.ShapeDtypeStruct((n, 2, half, 128), BF16),
            jax.ShapeDtypeStruct((n, half // 2, 128), BF16),
        ],
        scratch_shapes=[
            pltpu.SemaphoreType.DMA((2, n)),
            pltpu.SemaphoreType.DMA((2, n)),
            pltpu.SemaphoreType.DMA((2,)),
            pltpu.SemaphoreType.DMA((2,)),
        ],
        compiler_params=pltpu.CompilerParams(collective_id=0, has_side_effects=True),
        name="to_heads",
    )(kv, q)


def exchange_kernel(n, x_in, x_out, send, recv, local):
    me = own_index()
    greet_all(me, n)

    def copy_with(i, src):
        other = lax.rem(me + i, n)
        return remote(x_in.at[other], x_out.at[src], send.at[i], recv.at[src], place(other))

    @pl.loop(1, n)
    def _(i):
        copy_with(i, me).start()

    own = pltpu.make_async_copy(x_in.at[me], x_out.at[me], local)
    own.start()
    own.wait()

    @pl.loop(1, n)
    def _(i):
        copy_with(i, lax.rem(me + i, n)).wait()


def exchange(x, n, collective_id):
    anywhere = pl.BlockSpec(memory_space=pl.ANY)
    return pl.pallas_call(
        functools.partial(exchange_kernel, n),
        in_specs=[anywhere],
        out_specs=anywhere,
        out_shape=jax.ShapeDtypeStruct(x.shape, x.dtype),
        scratch_shapes=[
            pltpu.SemaphoreType.DMA((n,)),
            pltpu.SemaphoreType.DMA((n,)),
            pltpu.SemaphoreType.DMA,
        ],
        compiler_params=pltpu.CompilerParams(collective_id=collective_id, has_side_effects=True),
        name="exchange",
    )(x)


def from_heads_kernel(n, dkv_in, dq_in, dkv_out, dq_out, theirs, total, send, recv, local, pair):
    me = own_index()
    head, core = head_of(me)
    greet_all(me, n)
    sibling = {"blk": lax.axis_index("blk") + 1 - 2 * core, "grp": lax.axis_index("grp")}
    swap = remote(dkv_in.at[:, 1 - core], theirs, pair.at[0], pair.at[1], sibling)
    swap.start()

    def dq_copy(i, src):
        other = lax.rem(me + i, n)
        return remote(dq_in.at[other], dq_out.at[src], send.at[1, i], recv.at[1, src], place(other))

    def dkv_copy(i, src):
        other = lax.rem(me + i, n)
        return remote(total.at[other], dkv_out.at[src], send.at[0, i], recv.at[0, src], place(other))

    @pl.loop(1, n)
    def _(i):
        dq_copy(i, me).start()

    own_q = pltpu.make_async_copy(dq_in.at[me], dq_out.at[me], local.at[1])
    own_q.start()
    swap.wait()

    def add(j):
        total[j] = (dkv_in[j, core] + theirs[j]).astype(BF16)

    @pl.loop(1, n)
    def _(i):
        add(lax.rem(me + i, n))
        dkv_copy(i, me).start()

    add(me)
    own = pltpu.make_async_copy(total.at[me], dkv_out.at[me], local.at[0])
    own.start()
    own.wait()
    own_q.wait()

    @pl.loop(1, n)
    def _(i):
        src = lax.rem(me + i, n)
        dkv_copy(i, src).wait()
        dq_copy(i, src).wait()


def from_heads(dkv, dq, n):
    half = dkv.shape[2]
    anywhere = pl.BlockSpec(memory_space=pl.ANY)
    return pl.pallas_call(
        functools.partial(from_heads_kernel, n),
        in_specs=[pl.BlockSpec(memory_space=pltpu.VMEM), anywhere],
        out_specs=[anywhere] * 2,
        out_shape=[
            jax.ShapeDtypeStruct((n, half, 128), BF16),
            jax.ShapeDtypeStruct(dq.shape, BF16),
        ],
        scratch_shapes=[
            pltpu.VMEM((n, half, 128), F32),
            pltpu.VMEM((n, half, 128), BF16),
            pltpu.SemaphoreType.DMA((2, n)),
            pltpu.SemaphoreType.DMA((2, n)),
            pltpu.SemaphoreType.DMA((2,)),
            pltpu.SemaphoreType.DMA((2,)),
        ],
        compiler_params=pltpu.CompilerParams(
            collective_id=1, has_side_effects=True, vmem_limit_bytes=24 << 20
        ),
        name="from_heads",
    )(dkv, dq)


BITS = {"core": 1, "y": 2, "z0": 4, "z1": 8}


def flipped(x, axis):
    if axis == "x":
        return lax.ppermute(x, "grp", [(0, 1), (1, 0)])
    return lax.ppermute(x, "blk", [(i, i ^ BITS[axis]) for i in range(lax.axis_size("blk"))])


def bit_of(axis):
    if axis == "x":
        return lax.axis_index("grp")
    return lax.rem(lax.div(lax.axis_index("blk"), BITS[axis]), 2)


def sibling_of(core):
    return {"blk": lax.axis_index("blk") + 1 - 2 * core, "grp": lax.axis_index("grp")}


def across(axis):
    blk, grp = lax.axis_index("blk"), lax.axis_index("grp")
    if axis == "x":
        return {"blk": blk, "grp": 1 - grp}
    bit = BITS[axis]
    return {"blk": blk + bit - 2 * bit * bit_of(axis), "grp": grp}


def tn_dot(a, b):
    return lax.dot_general(a, b, (((0,), (0,)), ((), ())), preferred_element_type=F32)


def share_kernel(
    n, blocks_in, hidden, grad_before, act2, mixed, low, attn,
    blocks_out, keep_a, send_a, keep_b, send_b, keep_c, send_c,
    hidden2, before2, act2_2, mixed2, low2, attn2, tile, send, recv, local, pair_send, pair_recv,
):
    me = own_index()
    head, core = head_of(me)
    rows = low.shape[0]
    greet_all(me, n)
    sibling = sibling_of(core)
    theirs = pl.ds(rows, rows)
    pairs = [
        remote(src, dst.at[theirs], pair_send.at[k], pair_recv.at[k], sibling)
        for k, (src, dst) in enumerate(
            (
                (low, low2),
                (hidden.at[1 - core], hidden2),
                (act2.at[1 - core], act2_2),
                (grad_before, before2),
                (mixed.at[1 - core], mixed2),
                (attn, attn2),
            )
        )
    ]
    for copy in pairs:
        copy.start()

    def copy_with(i, src):
        other = lax.rem(me + i, n)
        return remote(blocks_in.at[other], blocks_out.at[src], send.at[i], recv.at[src], place(other))

    @pl.loop(1, n)
    def _(i):
        copy_with(i, me).start()

    own = pltpu.make_async_copy(blocks_in.at[me], blocks_out.at[me], local)
    own.start()
    low2[:rows] = low[...]
    hidden2[:rows] = hidden[core]
    act2_2[:rows] = act2[core]
    before2[:rows] = grad_before[...]
    mixed2[:rows] = mixed[core]
    attn2[:rows] = attn[...]

    x_mine, y_mine, z_mine = bit_of("x"), bit_of("y"), bit_of("z0")

    def put(keep, away, mine, bit, at, row, value):
        @pl.when(mine == bit)
        def _():
            keep[at, row : row + value.shape[0]] = value

        @pl.when(mine != bit)
        def _():
            away[at, row : row + value.shape[0]] = value

    pairs[0].wait()
    pairs[1].wait()

    @pl.loop(0, 8)
    def _(zy):
        columns = pl.ds(pl.multiple_of(zy * 256, 256), 256)
        value = tn_dot(hidden2[:, columns], low2[...]).astype(BF16)
        z1, z0, y = lax.div(zy, 4), lax.rem(lax.div(zy, 2), 2), lax.rem(zy, 2)
        for x in range(2):
            put(keep_a, send_a, x_mine, x, zy, 0, value[x * 128 : x * 128 + 96])
            put(keep_c, send_c, z_mine, z0, (z1 * 2 + y) * 2 + x, 0, value[x * 128 + 96 : (x + 1) * 128])

    def spread_rows(left, right, slab, to_b, row):
        tile[...] = tn_dot(left[...], right[:, slab * 1024 : (slab + 1) * 1024]).astype(BF16)

        @pl.loop(0, 16)
        def _(j):
            value = tile[pl.ds(pl.multiple_of(j * 32, 32), 32)]
            z1, z0 = lax.div(j, 8), lax.rem(lax.div(j, 4), 2)
            y, x = lax.rem(lax.div(j, 2), 2), lax.rem(j, 2)
            if to_b:
                put(keep_b, send_b, y_mine, y, (z1 * 2 + z0) * 2 + x, row, value)
            else:
                put(keep_c, send_c, z_mine, z0, (z1 * 2 + y) * 2 + x, row, value)

    pairs[2].wait()
    pairs[3].wait()
    for slab in range(3):
        spread_rows(act2_2, before2, slab, True, 32 * slab)
    spread_rows(act2_2, before2, 3, False, 32)
    pairs[4].wait()
    pairs[5].wait()
    spread_rows(mixed2, attn2, 0, False, 64)
    own.wait()

    @pl.loop(1, n)
    def _(i):
        copy_with(i, lax.rem(me + i, n)).wait()


def share(blocks, hidden, grad_before, act2, mixed, low, attn, n):
    rows, width = low.shape
    vmem = pl.BlockSpec(memory_space=pltpu.VMEM)
    shape = jax.ShapeDtypeStruct
    return pl.pallas_call(
        functools.partial(share_kernel, n),
        in_specs=[vmem] * 7,
        out_specs=[vmem] * 7,
        out_shape=[shape(blocks.shape, BF16)] + [shape((8, 96, width), BF16)] * 6,
        scratch_shapes=[
            pltpu.VMEM((2 * rows, hidden.shape[2]), BF16),
            pltpu.VMEM((2 * rows, grad_before.shape[1]), BF16),
            pltpu.VMEM((2 * rows, width // 2), BF16),
            pltpu.VMEM((2 * rows, width // 2), BF16),
            pltpu.VMEM((2 * rows, width), BF16),
            pltpu.VMEM((2 * rows, width), BF16),
            pltpu.VMEM((width // 2, 1024), BF16),
            pltpu.SemaphoreType.DMA((n,)),
            pltpu.SemaphoreType.DMA((n,)),
            pltpu.SemaphoreType.DMA,
            pltpu.SemaphoreType.DMA((6,)),
            pltpu.SemaphoreType.DMA((6,)),
        ],
        compiler_params=pltpu.CompilerParams(
            collective_id=3, has_side_effects=True, vmem_limit_bytes=40 << 20
        ),
        name="share",
    )(blocks, hidden, grad_before, act2, mixed, low, attn)


class Part:
    def __init__(self, total, dims, order, landing, send, recv):
        self.view, self.dims, self.order = total, list(dims), list(order)
        self.landing, self.send, self.recv = landing, send, recv
        self.stage, self.copy, self.kept = 0, None, None

    def start(self):
        axis = self.order[self.stage]
        at, mine = self.dims.index(axis), bit_of(axis)
        ahead = (slice(None),) * at
        self.copy = remote(
            self.view.at[ahead + (1 - mine,)],
            self.landing[self.stage],
            self.send.at[self.stage],
            self.recv.at[self.stage],
            across(axis),
        )
        self.copy.start()
        self.kept = self.view.at[ahead + (mine,)]
        self.dims.remove(axis)
        self.stage += 1

    def finish(self):
        self.copy.wait()
        got, kept = self.landing[self.stage - 1], self.kept
        lead = len(self.dims)

        @pl.loop(0, 2**lead)
        def _(k):
            at = tuple(lax.rem(lax.div(k, 2**d), 2) for d in reversed(range(lead)))
            kept[at] = (kept[at].astype(F32) + got[at].astype(F32)).astype(BF16)

        self.view = kept

    def last(self):
        self.copy.wait()
        return self.kept[...].astype(F32) + self.landing[self.stage - 1][...].astype(F32)


def gather_kernel(
    n, act1, qkv, keep_a, got_a, keep_b, got_b, keep_c, got_c, small_in,
    q_out, k_out, v_out, o_out, up_out, down_out, small_out,
    act1_2, qkv2, sum_a, sum_b, sum_c, sum_q, sum_k, sum_v,
    a2, a3, a4, b2, b3, b4, c2, c3, c4,
    q1, q2, q3, q4, k1, k2, k3, k4, v1, v2, v3, v4, small_all,
    send, recv, small_send, small_recv, pair_send, pair_recv,
):
    me = own_index()
    head, core = head_of(me)
    rows, width = qkv.shape[0], qkv.shape[1] // 3
    greet_all(me, n)
    sibling = sibling_of(core)
    theirs = pl.ds(rows, rows)
    pairs = [
        remote(act1.at[1 - core], act1_2.at[theirs], pair_send.at[0], pair_recv.at[0], sibling),
        remote(qkv, qkv2.at[theirs], pair_send.at[1], pair_recv.at[1], sibling),
    ]
    for copy in pairs:
        copy.start()
    sums = [sum_a, sum_b, sum_c, sum_q, sum_k, sum_v]
    dims = [("z1", "z0", "y"), ("z1", "z0", "x"), ("z1", "y", "x")] + [("z1", "z0", "y", "x")] * 3
    orders = [
        ("y", "z0", "z1"), ("z0", "x", "z1"), ("x", "y", "z1"),
        ("x", "y", "z0", "z1"), ("y", "z0", "x", "z1"), ("z0", "x", "y", "z1"),
    ]
    landings = [(a2, a3, a4), (b2, b3, b4), (c2, c3, c4), (q1, q2, q3, q4), (k1, k2, k3, k4), (v1, v2, v3, v4)]
    parts = [
        Part(total, names, order, landing, send.at[k], recv.at[k])
        for k, (total, names, order, landing) in enumerate(zip(sums, dims, orders, landings))
    ]
    for part, total, keep, got in zip(parts, sums, (keep_a, keep_b, keep_c), (got_a, got_b, got_c)):

        @pl.loop(0, 8)
        def _(k):
            at = (lax.div(k, 4), lax.rem(lax.div(k, 2), 2), lax.rem(k, 2))
            total[at] = (keep[k].astype(F32) + got[k].astype(F32)).astype(BF16)

        part.start()

    def small_copy(i, src):
        other = lax.rem(me + i, n)
        return remote(small_in.at[other], small_all.at[src], small_send.at[i], small_recv.at[src], place(other))

    @pl.loop(1, n)
    def _(i):
        small_copy(i, me).start()

    act1_2[:rows] = act1[core]
    qkv2[:rows] = qkv[...]
    for copy in pairs:
        copy.wait()
    for k in range(3):
        value = tn_dot(act1_2[...], qkv2[:, k * width : (k + 1) * width]).astype(BF16)
        for j in range(16):
            sums[3 + k][j // 8, j // 4 % 2, j // 2 % 2, j % 2] = value[j * 32 : (j + 1) * 32]
        parts[3 + k].start()

    for turn in range(2):
        for part in parts:
            part.finish()
            part.start()
    for part in parts[3:]:
        part.finish()
        part.start()
    small_all[me] = small_in[me]

    @pl.loop(1, n)
    def _(i):
        small_copy(i, lax.rem(me + i, n)).wait()

    small_out[...] = jnp.sum(small_all[...], axis=0)
    down_out[:96] = parts[0].last()
    value = parts[1].last()
    for slab in range(3):
        up_out[:, slab * 1024 : (slab + 1) * 1024] = value[slab * 32 : (slab + 1) * 32]
    value = parts[2].last()
    down_out[96:] = value[:32]
    up_out[:, 3072:] = value[32:64]
    o_out[...] = value[64:]
    q_out[...] = parts[3].last()
    k_out[...] = parts[4].last()
    v_out[...] = parts[5].last()


def gather(act1, qkv, keeps, gots, small, n):
    rows, width = qkv.shape[0], qkv.shape[1] // 3
    vmem = pl.BlockSpec(memory_space=pltpu.VMEM)
    shape = jax.ShapeDtypeStruct
    thin, wide = (32, width), (96, width)
    buffers = [pltpu.VMEM((2, 2, 2, *wide), BF16)] * 3 + [pltpu.VMEM((2, 2, 2, 2, *thin), BF16)] * 3
    buffers += [pltpu.VMEM((2,) * k + wide, BF16) for k in (2, 1, 0)] * 3
    buffers += [pltpu.VMEM((2,) * k + thin, BF16) for k in (3, 2, 1, 0)] * 3
    return pl.pallas_call(
        functools.partial(gather_kernel, n),
        in_specs=[vmem] * 9,
        out_specs=[vmem] * 7,
        out_shape=[shape(thin, F32)] * 4 + [shape((32, 4 * width), F32), shape((128, width), F32), shape((8, 128), F32)],
        scratch_shapes=[
            pltpu.VMEM((2 * rows, width // 2), BF16),
            pltpu.VMEM((2 * rows, 3 * width), BF16),
            *buffers,
            pltpu.VMEM((n, 8, 128), F32),
            pltpu.SemaphoreType.DMA((6, 4)),
            pltpu.SemaphoreType.DMA((6, 4)),
            pltpu.SemaphoreType.DMA((n,)),
            pltpu.SemaphoreType.DMA((n,)),
            pltpu.SemaphoreType.DMA((2,)),
            pltpu.SemaphoreType.DMA((2,)),
        ],
        compiler_params=pltpu.CompilerParams(
            collective_id=4, has_side_effects=True, vmem_limit_bytes=40 << 20
        ),
        name="gather",
    )(act1, qkv, keeps[0], gots[0], keeps[1], gots[1], keeps[2], gots[2], small)


def shards_heads(
    frames, lengths, norm1_gain, w_query, w_key, w_value, w_out, norm2_gain, w_up, b_up, w_down, b_down, cotangent
):
    rows, width = frames.shape
    n = lax.axis_size("blk") * lax.axis_size("grp")
    half = rows // 2
    core_word = bit_of("core").astype(jnp.int32).reshape(1)
    qpos = jnp.asarray(packed_positions(n, half))

    kv_blocks, q_blocks, act1 = project_and_pack(frames, norm1_gain, w_query, w_key, w_value)
    kv, q = to_heads(kv_blocks, q_blocks, n)
    kv_rows = kv.reshape(n * rows, 128)
    out_t, lse, out_blocks = mix(lengths, core_word, kv_rows, q, qpos)
    mixed_blocks = exchange(out_blocks, n, 2)
    (
        layer_out, grad_middle, grad_blocks, hidden, grad_before, act2, mixed, grad_low, grad_attn,
        norm2_gain_grad, b_up_grad, b_down_grad,
    ) = feed(mixed_blocks, frames, cotangent, w_out, norm2_gain, w_up, b_up, w_down, b_down)

    grad_blocks, *parts = share(grad_blocks, hidden, grad_before, act2, mixed, grad_low, grad_attn, n)
    keeps = parts[0::2]
    gots = [flipped(part, axis) for part, axis in zip(parts[1::2], ("x", "y", "z0"))]
    dkv, dq = mix_back(lengths, core_word, kv_rows, q, grad_blocks, qpos, out_t, lse)

    dkv_blocks, dq_blocks = from_heads(dkv.reshape(n, 2, half, 128), dq, n)
    qkv, frames_grad, small = input_grad(
        dkv_blocks, dq_blocks, frames, grad_middle, norm1_gain, w_query, w_key, w_value,
        norm2_gain_grad, b_up_grad, b_down_grad,
    )
    w_query_grad, w_key_grad, w_value_grad, w_out_grad, w_up_grad, w_down_grad, small = gather(
        act1, qkv, keeps, gots, small, n
    )
    part = width // n
    turn = lax.rem(own_index(), 128 // part) * part
    vectors = lax.dynamic_slice(small, (0, turn), (3, part))
    return (
        layer_out,
        frames_grad,
        vectors[0],
        w_query_grad,
        w_key_grad,
        w_value_grad,
        w_out_grad,
        vectors[1],
        w_up_grad,
        small[3],
        w_down_grad,
        vectors[2],
    )


def solution(mesh):
    if mesh.shape["blk"] != 16 or mesh.shape["grp"] != 2:
        return solution_ring(mesh)
    split = P(ALL, None)
    return jax.shard_map(
        shards_heads,
        mesh=mesh,
        in_specs=(split, P(), P(), P(), P(), P(), P(), P(), P(), P(), P(), P(), split),
        out_specs=(split, split, P(ALL), split, split, split, split, P(ALL), split, P(ALL), split, P(ALL)),
        check_vma=False,
    )
```

```python
import functools

import jax
import jax.numpy as jnp
import numpy as np
from jax import lax
from jax.experimental import pallas as pl
from jax.experimental.pallas import tpu as pltpu
from jax.sharding import PartitionSpec as P

HEAD_DIM = 64
ITEM_MAX = 4096


EPSILON = 1e-05
MASKED = -1e30
SCALING = 0.125


def shortened(array):

    def short(part):
        return part.astype(jnp.bfloat16) if part.dtype == jnp.float32 else part

    return jax.tree.map(short, array)


def passed_along(block, axis, distance):
    devices = range(lax.axis_size(axis))
    route = [(i - distance, i) for i in devices if i - distance in devices]
    return lax.ppermute(block, axis, route)


def rms_norm(values, gain):
    return values * lax.rsqrt(jnp.mean(values * values, axis=-1, keepdims=True) + EPSILON) * gain


def gelu_exact(values):
    return jax.nn.gelu(values, approximate=False)


def item_starts(lengths, positions):
    ends = jnp.cumsum(lengths)
    offsets = ends - lengths
    before = offsets[None, :] <= positions[:, None]
    return jnp.max(jnp.where(before, offsets[None, :], 0), axis=1)


def live_mask(query_pos, query_start, key_first, key_count):
    key_pos = key_first + jnp.arange(key_count, dtype=jnp.int32)
    return (key_pos[None, :] >= query_start[:, None]) & (key_pos[None, :] <= query_pos[:, None])


def split_heads(matrix):
    return matrix.reshape(matrix.shape[0], matrix.shape[1] // HEAD_DIM, HEAD_DIM)


def merge_heads(tensor):
    return tensor.reshape(tensor.shape[0], tensor.shape[1] * tensor.shape[2])


def scores_of(queries3, keys_block, mask):
    raw = jnp.einsum(
        "qhd,khd->hqk", queries3, split_heads(keys_block), preferred_element_type=jnp.float32
    )
    return jnp.where(mask[None], raw * SCALING, MASKED)


def left_dot(left, right):
    return lax.dot_general(
        left, right, (((0,), (0,)), ((), ())), preferred_element_type=jnp.float32
    )


def right_dot(left, right):
    return lax.dot_general(
        left, right, (((1,), (1,)), ((), ())), preferred_element_type=jnp.float32
    )


def grad_parts(queries3, grad_out3, log_total, delta, keys_block, values_block, mask):
    probs = jnp.exp(scores_of(queries3, keys_block, mask) - log_total[:, :, None])
    grad_probs = jnp.einsum(
        "qhd,khd->hqk", grad_out3, split_heads(values_block), preferred_element_type=jnp.float32
    )
    grad_scores = (probs * (grad_probs - delta[:, :, None])).astype(jnp.bfloat16)
    return (probs.astype(jnp.bfloat16), grad_scores)


def key_terms(queries3, grad_out3, probs_low, grad_scores):
    grad_keys = jnp.einsum(
        "hqk,qhd->khd", grad_scores, queries3, preferred_element_type=jnp.float32
    )
    grad_values = jnp.einsum(
        "hqk,qhd->khd", probs_low, grad_out3, preferred_element_type=jnp.float32
    )
    return (merge_heads(grad_keys), merge_heads(grad_values))


def query_term(grad_scores, keys_block):
    return jnp.einsum(
        "hqk,khd->qhd", grad_scores, split_heads(keys_block), preferred_element_type=jnp.float32
    )


def shards_ring(
    frames,
    lengths,
    norm1_gain,
    w_query,
    w_key,
    w_value,
    w_out,
    norm2_gain,
    w_up,
    b_up,
    w_down,
    b_down,
    cotangent,
):
    row_count = frames.shape[0]
    width = frames.shape[1]
    heads = width // HEAD_DIM
    groups = lax.axis_size("grp")
    block_rows = row_count * groups
    span = (ITEM_MAX + block_rows - 2) // block_rows
    blk_index = lax.axis_index("blk")
    sub_index = lax.axis_index("grp")
    block_first = blk_index * block_rows
    query_pos = block_first + sub_index * row_count + jnp.arange(row_count, dtype=jnp.int32)
    query_start = item_starts(lengths, query_pos)
    back_steps = jnp.arange(span + 1, dtype=jnp.int32)
    normed1, norm1_back = jax.vjp(rms_norm, frames, norm1_gain)
    act1 = normed1.astype(jnp.bfloat16)
    queries = jnp.dot(act1, w_query, preferred_element_type=jnp.float32).astype(jnp.bfloat16)
    keys_own = jnp.dot(act1, w_key, preferred_element_type=jnp.float32).astype(jnp.bfloat16)
    values_own = jnp.dot(act1, w_value, preferred_element_type=jnp.float32).astype(jnp.bfloat16)
    queries3 = split_heads(queries)
    block_keys, block_values = (
        lax.all_gather(keys_own, "grp", axis=0, tiled=True),
        lax.all_gather(values_own, "grp", axis=0, tiled=True),
    )

    def cycle_step(carry, unused_input):
        moved = jax.tree.map(
            lambda part, own: part.astype(own.dtype),
            passed_along(shortened(carry), "blk", 1),
            carry,
        )
        return (moved, moved)

    unused_last, far_blocks = lax.scan(cycle_step, (block_keys, block_values), None, length=span)
    keys_all = jnp.concatenate([block_keys[None], far_blocks[0]], axis=0)
    values_all = jnp.concatenate([block_values[None], far_blocks[1]], axis=0)

    def mask_for(back):
        return live_mask(query_pos, query_start, block_first - back * block_rows, block_rows)

    def total_step(carry, inputs):
        run_max, run_sum = carry
        keys_block, back = inputs
        scores = scores_of(queries3, keys_block, mask_for(back))
        new_max = jnp.maximum(run_max, jnp.max(scores, axis=-1))
        run_sum = run_sum * jnp.exp(run_max - new_max) + jnp.sum(
            jnp.exp(scores - new_max[:, :, None]), axis=-1
        )
        return ((new_max, run_sum), None)

    start_max = jnp.full((heads, row_count), MASKED, jnp.float32)
    start_sum = jnp.zeros((heads, row_count), jnp.float32)
    (top_max, top_sum), unused_out = lax.scan(
        total_step, (start_max, start_sum), (keys_all, back_steps)
    )
    log_total = top_max + jnp.log(top_sum)

    def mix_step(total, inputs):
        keys_block, values_block, back = inputs
        probs = jnp.exp(
            scores_of(queries3, keys_block, mask_for(back)) - log_total[:, :, None]
        ).astype(jnp.bfloat16)
        return (
            total
            + jnp.einsum(
                "hqk,khd->qhd", probs, split_heads(values_block), preferred_element_type=jnp.float32
            ),
            None,
        )

    zero_query = jnp.zeros((row_count, heads, HEAD_DIM), jnp.float32)
    mixed_sum, unused_out = lax.scan(mix_step, zero_query, (keys_all, values_all, back_steps))
    mixed = merge_heads(mixed_sum).astype(jnp.bfloat16)
    middle = frames + jnp.dot(mixed, w_out, preferred_element_type=jnp.float32)
    normed2, norm2_back = jax.vjp(rms_norm, middle, norm2_gain)
    act2 = normed2.astype(jnp.bfloat16)
    before = jnp.dot(act2, w_up, preferred_element_type=jnp.float32) + b_up
    activated, gelu_back = jax.vjp(gelu_exact, before)
    hidden = activated.astype(jnp.bfloat16)
    layer_out = middle + jnp.dot(hidden, w_down, preferred_element_type=jnp.float32) + b_down
    grad_low = cotangent.astype(jnp.bfloat16)
    b_down_grad = jnp.sum(grad_low.astype(jnp.float32), axis=0)
    w_down_grad = left_dot(hidden, grad_low)
    grad_before = gelu_back(right_dot(grad_low, w_down))[0].astype(jnp.bfloat16)
    b_up_grad = jnp.sum(grad_before.astype(jnp.float32), axis=0)
    w_up_grad = left_dot(act2, grad_before)
    grad_mid_norm, norm2_gain_grad = norm2_back(right_dot(grad_before, w_up))
    grad_middle = cotangent + grad_mid_norm
    grad_attn = grad_middle.astype(jnp.bfloat16)
    w_out_grad = left_dot(mixed, grad_attn)
    grad_mixed = right_dot(grad_attn, w_out).astype(jnp.bfloat16)
    grad_out3 = split_heads(grad_mixed)

    def delta_step(total, inputs):
        keys_block, values_block, back = inputs
        probs = jnp.exp(scores_of(queries3, keys_block, mask_for(back)) - log_total[:, :, None])
        grad_probs = jnp.einsum(
            "qhd,khd->hqk", grad_out3, split_heads(values_block), preferred_element_type=jnp.float32
        )
        return (total + jnp.sum(probs * grad_probs, axis=-1), None)

    delta, unused_out = lax.scan(
        delta_step, jnp.zeros((heads, row_count), jnp.float32), (keys_all, values_all, back_steps)
    )
    zero_block = jnp.zeros((block_rows, width), jnp.float32)

    def return_step(carry, inputs):
        grad_q, travel = carry
        keys_block, values_block, back = inputs
        probs_low, grad_scores = grad_parts(
            queries3, grad_out3, log_total, delta, keys_block, values_block, mask_for(back)
        )
        grad_keys, grad_values = key_terms(queries3, grad_out3, probs_low, grad_scores)
        moved = (
            passed_along((travel[0] + grad_keys).astype(jnp.bfloat16), "blk", -1).astype(
                jnp.float32
            ),
            passed_along((travel[1] + grad_values).astype(jnp.bfloat16), "blk", -1).astype(
                jnp.float32
            ),
        )
        return ((grad_q + query_term(grad_scores, keys_block), moved), None)

    (grad_q, travel), unused_out = lax.scan(
        return_step,
        (zero_query, (zero_block, zero_block)),
        (far_blocks[0], far_blocks[1], back_steps[1:]),
        reverse=True,
    )
    probs_low, grad_scores = grad_parts(
        queries3, grad_out3, log_total, delta, block_keys, block_values, mask_for(0)
    )
    grad_keys, grad_values = key_terms(queries3, grad_out3, probs_low, grad_scores)
    grad_q = grad_q + query_term(grad_scores, block_keys)
    block_grad_keys = travel[0] + grad_keys
    block_grad_values = travel[1] + grad_values
    grad_keys_rows, grad_values_rows = (
        lax.psum_scatter(
            block_grad_keys.astype(jnp.bfloat16), "grp", scatter_dimension=0, tiled=True
        ).astype(jnp.float32),
        lax.psum_scatter(
            block_grad_values.astype(jnp.bfloat16), "grp", scatter_dimension=0, tiled=True
        ).astype(jnp.float32),
    )
    grad_keys_low = (grad_keys_rows * SCALING).astype(jnp.bfloat16)
    grad_values_low = grad_values_rows.astype(jnp.bfloat16)
    grad_queries_low = (merge_heads(grad_q) * SCALING).astype(jnp.bfloat16)
    w_query_grad = left_dot(act1, grad_queries_low)
    w_key_grad = left_dot(act1, grad_keys_low)
    w_value_grad = left_dot(act1, grad_values_low)
    grad_act1 = (
        right_dot(grad_queries_low, w_query)
        + right_dot(grad_keys_low, w_key)
        + right_dot(grad_values_low, w_value)
    )
    grad_frames_norm, norm1_gain_grad = norm1_back(grad_act1)
    frames_grad = grad_middle + grad_frames_norm
    shares = (
        lax.psum_scatter(norm1_gain_grad, ("blk", "grp"), scatter_dimension=0, tiled=True),
        lax.psum_scatter(w_query_grad, ("blk", "grp"), scatter_dimension=0, tiled=True),
        lax.psum_scatter(w_key_grad, ("blk", "grp"), scatter_dimension=0, tiled=True),
        lax.psum_scatter(w_value_grad, ("blk", "grp"), scatter_dimension=0, tiled=True),
        lax.psum_scatter(w_out_grad, ("blk", "grp"), scatter_dimension=0, tiled=True),
        lax.psum_scatter(norm2_gain_grad, ("blk", "grp"), scatter_dimension=0, tiled=True),
        lax.psum_scatter(w_up_grad, ("blk", "grp"), scatter_dimension=0, tiled=True),
        lax.psum_scatter(b_up_grad, ("blk", "grp"), scatter_dimension=0, tiled=True),
        lax.psum_scatter(w_down_grad, ("blk", "grp"), scatter_dimension=0, tiled=True),
        lax.psum_scatter(b_down_grad, ("blk", "grp"), scatter_dimension=0, tiled=True),
    )
    return (
        layer_out,
        frames_grad,
        shares[0],
        shares[1],
        shares[2],
        shares[3],
        shares[4],
        shares[5],
        shares[6],
        shares[7],
        shares[8],
        shares[9],
    )


def solution_ring(mesh):
    placed = (
        P(("blk", "grp"), None),
        P(),
        P(),
        P(),
        P(),
        P(),
        P(),
        P(),
        P(),
        P(),
        P(),
        P(),
        P(("blk", "grp"), None),
    )
    return jax.shard_map(
        shards_ring,
        mesh=mesh,
        in_specs=placed,
        out_specs=(
            P(("blk", "grp"), None),
            P(("blk", "grp"), None),
            P(("blk", "grp")),
            P(("blk", "grp"), None),
            P(("blk", "grp"), None),
            P(("blk", "grp"), None),
            P(("blk", "grp"), None),
            P(("blk", "grp")),
            P(("blk", "grp"), None),
            P(("blk", "grp")),
            P(("blk", "grp"), None),
            P(("blk", "grp")),
        ),
        check_vma=False,
    )


LOG2E = 1.4426950408889634
F32, BF16 = jnp.float32, jnp.bfloat16


def nt_dot(a, b):
    return lax.dot_general(a, b, (((1,), (1,)), ((), ())), preferred_element_type=F32)


def nn_dot(a, b):
    return lax.dot_general(a, b, (((1,), (0,)), ((), ())), preferred_element_type=F32)


def low_lanes(shape):
    return lax.broadcasted_iota(jnp.int32, shape, 1) < 64


def pair_low(a, b, low):
    return jnp.where(low, a, pltpu.roll(b, 64, 1))


def pair_high(a, b, low):
    return jnp.where(low, pltpu.roll(a, 64, 1), b)


def store_halves(ref, x):
    low = low_lanes((x.shape[0], 128))
    for p in range(x.shape[1] // 256):
        a, b = x[:, p * 256 : p * 256 + 128], x[:, p * 256 + 128 : (p + 1) * 256]
        ref[0, :, p * 128 : (p + 1) * 128] = pair_low(a, b, low).astype(BF16)
        ref[1, :, p * 128 : (p + 1) * 128] = pair_high(a, b, low).astype(BF16)


def block_bounds(len_ref, items, qpos, first, last, key_block):
    off = jnp.int32(0)
    start = jnp.zeros(qpos.shape, jnp.int32)
    s_first, s_last = jnp.int32(0), jnp.int32(0)
    for i in range(items):
        start = jnp.where(qpos >= off, off, start)
        s_first = jnp.where(first >= off, off, s_first)
        s_last = jnp.where(last >= off, off, s_last)
        off = off + len_ref[i]
    lo, hi = s_first // key_block, last // key_block + 1
    f0 = jnp.clip((s_last + key_block - 1) // key_block, lo, hi)
    f1 = jnp.clip((first + 1) // key_block, f0, hi)
    return start, lo, f0, f1, hi


def query_ends(i, chunks, half, core):
    first = i * chunks * 2 * half + core * half
    return first, first + (chunks - 1) * 2 * half + half - 1


def spread(packed, low, to_high):
    f = packed.astype(F32)
    other = pltpu.roll(f, 64, 1)
    zero = jnp.zeros_like(f)
    if to_high:
        return jnp.where(low, zero, other).astype(BF16), jnp.where(low, zero, f).astype(BF16)
    return jnp.where(low, f, zero).astype(BF16), jnp.where(low, other, zero).astype(BF16)


def mix_kernel(
    items, chunks, key_block,
    len_ref, core_ref, kv_ref, qp_ref, qpos_ref,
    out_t_ref, lse_ref, out_ref,
    kv_t, qz, acc, m_ref, l_ref,
):
    i = pl.program_id(0)
    half = 2 * qp_ref.shape[1]
    n = chunks * half
    core = core_ref[0]

    @pl.when(i == 0)
    def _():
        for c in range(kv_ref.shape[0] // 512):
            at = slice(c * 512, (c + 1) * 512)
            kv_t[:, at] = kv_ref[at, :].astype(F32).T.astype(BF16)

    low = low_lanes((half // 2, 128))
    for c in range(chunks):
        a, b = spread(qp_ref[c], low, False)
        qz[c * half : c * half + half // 2] = a
        qz[c * half + half // 2 : (c + 1) * half] = b
    qpos = qpos_ref[...] + core * half
    first, last = query_ends(i, chunks, half, core)
    start, lo, f0, f1, hi = block_bounds(len_ref, items, qpos, first, last, key_block)
    acc[...] = jnp.zeros_like(acc)
    m_ref[...] = jnp.full_like(m_ref, MASKED)
    l_ref[...] = jnp.zeros_like(l_ref)

    def step(j, masked):
        at = pl.ds(pl.multiple_of(j * key_block, key_block), key_block)
        s = nt_dot(kv_ref[at, :], qz[...]) * LOG2E
        if masked:
            kpos = j * key_block + lax.broadcasted_iota(jnp.int32, (key_block, 1), 0)
            s = jnp.where((kpos >= start) & (kpos <= qpos), s, MASKED)
        m_old = m_ref[...]
        m_new = jnp.maximum(m_old, jnp.max(s, axis=0, keepdims=True))
        p = jnp.exp2(s - m_new)
        alpha = jnp.exp2(m_old - m_new)
        m_ref[...] = m_new
        l_ref[...] = l_ref[...] * alpha + jnp.sum(p, axis=0, keepdims=True)
        acc[...] = acc[...] * alpha + nn_dot(kv_t[64:, at], p.astype(BF16))

    lax.fori_loop(lo, f0, lambda j, c: (step(j, True), c)[1], 0)
    lax.fori_loop(f0, f1, lambda j, c: (step(j, False), c)[1], 0)
    lax.fori_loop(f1, hi, lambda j, c: (step(j, True), c)[1], 0)
    out_t = acc[...] / l_ref[...]
    out_t_ref[...] = out_t
    lse_ref[...] = m_ref[...] + jnp.log2(l_ref[...])
    doubled = jnp.concatenate([out_t, out_t], axis=0).T
    for c in range(chunks):
        a = doubled[c * half : c * half + half // 2]
        b = doubled[c * half + half // 2 : (c + 1) * half]
        out_ref[c] = jnp.where(low, a, b).astype(BF16)


def mix(lengths, core, kv, qp, qpos, chunks=4, key_block=768):
    total = kv.shape[0]
    n_src, quarter = qp.shape[0], qp.shape[1]
    half = 2 * quarter
    n = chunks * half
    whole = lambda i, *_: (0, 0)
    return pl.pallas_call(
        functools.partial(mix_kernel, lengths.shape[0], chunks, key_block),
        grid_spec=pltpu.PrefetchScalarGridSpec(
            num_scalar_prefetch=2,
            grid=(n_src // chunks,),
            in_specs=[
                pl.BlockSpec((total, 128), whole),
                pl.BlockSpec((chunks, quarter, 128), lambda i, *_: (i, 0, 0)),
                pl.BlockSpec((1, n), lambda i, *_: (0, i)),
            ],
            out_specs=[
                pl.BlockSpec((64, n), lambda i, *_: (0, i)),
                pl.BlockSpec((1, n), lambda i, *_: (0, i)),
                pl.BlockSpec((chunks, quarter, 128), lambda i, *_: (i, 0, 0)),
            ],
            scratch_shapes=[
                pltpu.VMEM((128, total), BF16),
                pltpu.VMEM((n, 128), BF16),
                pltpu.VMEM((64, n), F32),
                pltpu.VMEM((1, n), F32),
                pltpu.VMEM((1, n), F32),
            ],
        ),
        out_shape=[
            jax.ShapeDtypeStruct((64, n_src * half), F32),
            jax.ShapeDtypeStruct((1, n_src * half), F32),
            jax.ShapeDtypeStruct((n_src, quarter, 128), BF16),
        ],
        compiler_params=pltpu.CompilerParams(vmem_limit_bytes=32 << 20),
        cost_estimate=pl.CostEstimate(flops=25_000_000_000, bytes_accessed=8 << 20, transcendentals=0),
        name="mix",
    )(lengths, core, kv, qp, qpos)


def back_kernel(
    items, chunks, key_block,
    len_ref, core_ref, kv_ref, qp_ref, dp_ref, qpos_ref, out_t_ref, lse_ref,
    dkv_ref, dq_ref,
    kv_t, qd, dq_acc,
):
    i = pl.program_id(0)
    half = 2 * qp_ref.shape[1]
    n = chunks * half
    core = core_ref[0]

    @pl.when(i == 0)
    def _():
        for c in range(kv_ref.shape[0] // 512):
            at = slice(c * 512, (c + 1) * 512)
            kv_t[:, at] = kv_ref[at, :].astype(F32).T.astype(BF16)
        dkv_ref[...] = jnp.zeros_like(dkv_ref)

    low = low_lanes((half // 2, 128))
    for c in range(chunks):
        a, b = spread(qp_ref[c], low, False)
        qd[c * half : c * half + half // 2] = a
        qd[c * half + half // 2 : (c + 1) * half] = b
        a, b = spread(dp_ref[c], low, True)
        qd[n + c * half : n + c * half + half // 2] = a
        qd[n + c * half + half // 2 : n + (c + 1) * half] = b
    do_t = qd[n:, :].astype(F32).T[64:]
    delta = jnp.sum(do_t * out_t_ref[...], axis=0, keepdims=True)
    lse = lse_ref[...]
    qpos = qpos_ref[...] + core * half
    first, last = query_ends(i, chunks, half, core)
    start, lo, f0, f1, hi = block_bounds(len_ref, items, qpos, first, last, key_block)
    dq_acc[...] = jnp.zeros_like(dq_acc)

    def step(j, masked):
        at = pl.ds(pl.multiple_of(j * key_block, key_block), key_block)
        both = nt_dot(kv_ref[at, :], qd[...])
        s = both[:, :n] * LOG2E
        if masked:
            kpos = j * key_block + lax.broadcasted_iota(jnp.int32, (key_block, 1), 0)
            s = jnp.where((kpos >= start) & (kpos <= qpos), s, MASKED)
        p = jnp.exp2(s - lse)
        ds = (p * (both[:, n:] - delta)).astype(BF16)
        dq_acc[...] += nn_dot(kv_t[:64, at], ds)
        dkv_ref[at, :] += nn_dot(ds, qd[:n, :]) + nn_dot(p.astype(BF16), qd[n:, :])

    lax.fori_loop(lo, f0, lambda j, c: (step(j, True), c)[1], 0)
    lax.fori_loop(f0, f1, lambda j, c: (step(j, False), c)[1], 0)
    lax.fori_loop(f1, hi, lambda j, c: (step(j, True), c)[1], 0)
    dq_t = dq_acc[...] * 0.125
    doubled = jnp.concatenate([dq_t, dq_t], axis=0).T
    for c in range(chunks):
        a = doubled[c * half : c * half + half // 2]
        b = doubled[c * half + half // 2 : (c + 1) * half]
        dq_ref[c] = jnp.where(low, a, b).astype(BF16)


def mix_back(lengths, core, kv, qp, dp, qpos, out_t, lse, chunks=4, key_block=768):
    total = kv.shape[0]
    n_src, quarter = qp.shape[0], qp.shape[1]
    half = 2 * quarter
    n = chunks * half
    whole = lambda i, *_: (0, 0)
    rows = lambda i, *_: (0, i)
    blocks = pl.BlockSpec((chunks, quarter, 128), lambda i, *_: (i, 0, 0))
    return pl.pallas_call(
        functools.partial(back_kernel, lengths.shape[0], chunks, key_block),
        grid_spec=pltpu.PrefetchScalarGridSpec(
            num_scalar_prefetch=2,
            grid=(n_src // chunks,),
            in_specs=[
                pl.BlockSpec((total, 128), whole),
                blocks,
                blocks,
                pl.BlockSpec((1, n), rows),
                pl.BlockSpec((64, n), rows),
                pl.BlockSpec((1, n), rows),
            ],
            out_specs=[pl.BlockSpec((total, 128), whole), blocks],
            scratch_shapes=[
                pltpu.VMEM((128, total), BF16),
                pltpu.VMEM((2 * n, 128), BF16),
                pltpu.VMEM((64, n), F32),
            ],
        ),
        out_shape=[
            jax.ShapeDtypeStruct((total, 128), F32),
            jax.ShapeDtypeStruct((n_src, quarter, 128), BF16),
        ],
        compiler_params=pltpu.CompilerParams(vmem_limit_bytes=32 << 20),
        cost_estimate=pl.CostEstimate(flops=40_000_000_000, bytes_accessed=8 << 20, transcendentals=0),
        name="mix_back",
    )(lengths, core, kv, qp, dp, qpos, out_t, lse)


def packed_positions(n_src, half):
    j = np.arange(n_src * half)
    return ((j // half) * 2 * half + j % half).astype(np.int32)[None]


def feed_kernel(
    blocks_ref, frames_ref, cot_ref, w_out_ref, gain_ref, w_up_ref, b_up_ref, w_down_ref, b_down_ref,
    out_ref, grad_mid_ref, grad_blocks_ref, hidden_ref, grad_before_ref, act2_ref, mixed_ref, low_ref, attn_ref,
    gain_grad_ref, b_up_grad_ref, b_down_grad_ref,
    mixed, act2, act_grad,
):
    i = pl.program_id(0)
    rows = frames_ref.shape[0]
    quarter = rows // 4
    low_q = low_lanes((quarter, 128))

    @pl.when(i == 0)
    def _():
        for zy in range(8):
            for s in range(2):
                a = blocks_ref[(zy * 2 + s) * 2].astype(F32)
                b = blocks_ref[(zy * 2 + s) * 2 + 1].astype(F32)
                at = slice(zy * 128, (zy + 1) * 128)
                first = 2 * s * quarter
                mixed[first : first + quarter, at] = pair_low(a, b, low_q)
                mixed[first + quarter : first + 2 * quarter, at] = pair_high(a, b, low_q)
        store_halves(mixed_ref, mixed[...])
        middle = frames_ref[...] + nn_dot(mixed[...].astype(BF16), w_out_ref[...])
        r = lax.rsqrt(jnp.mean(middle * middle, axis=-1, keepdims=True) + EPSILON)
        normed = middle * r * gain_ref[...]
        act2[...] = normed.astype(BF16)
        store_halves(act2_ref, normed)
        grad_mid_ref[...] = middle
        out_ref[...] = middle + b_down_ref[...]
        grad_low = cot_ref[...].astype(BF16)
        low_ref[...] = grad_low
        b_down_grad_ref[...] = jnp.sum(grad_low.astype(F32), axis=0, keepdims=True)
        act_grad[...] = jnp.zeros_like(act_grad)

    before = nn_dot(act2[...], w_up_ref[...]) + b_up_ref[...]
    cdf = 0.5 + 0.5 * lax.erf(before * 0.7071067811865476)
    pdf = jnp.exp(-0.5 * before * before) * 0.3989422804014327
    hidden = (before * cdf).astype(BF16)
    step = hidden.shape[1] // 2
    hidden_ref[0] = hidden[:, :step]
    hidden_ref[1] = hidden[:, step:]
    out_ref[...] += nn_dot(hidden, w_down_ref[...])
    grad_before = (nt_dot(low_ref[...], w_down_ref[...]) * (cdf + before * pdf)).astype(BF16)
    grad_before_ref[...] = grad_before
    b_up_grad_ref[...] = jnp.sum(grad_before.astype(F32), axis=0, keepdims=True)
    act_grad[...] += nt_dot(grad_before, w_up_ref[...])

    @pl.when(i == pl.num_programs(0) - 1)
    def _():
        middle = grad_mid_ref[...]
        r = lax.rsqrt(jnp.mean(middle * middle, axis=-1, keepdims=True) + EPSILON)
        n = middle * r
        g = act_grad[...]
        gain_grad_ref[...] = jnp.sum(g * n, axis=0, keepdims=True)
        g = g * gain_ref[...]
        grad_mid = cot_ref[...] + r * (g - n * jnp.mean(g * n, axis=-1, keepdims=True))
        grad_mid_ref[...] = grad_mid
        grad_attn = grad_mid.astype(BF16)
        attn_ref[...] = grad_attn
        grad_mixed = nt_dot(grad_attn, w_out_ref[...])
        for zy in range(8):
            for s in range(2):
                at = slice(zy * 128, (zy + 1) * 128)
                first = 2 * s * quarter
                a = grad_mixed[first : first + quarter, at]
                b = grad_mixed[first + quarter : first + 2 * quarter, at]
                grad_blocks_ref[(zy * 2 + s) * 2] = pair_low(a, b, low_q).astype(BF16)
                grad_blocks_ref[(zy * 2 + s) * 2 + 1] = pair_high(a, b, low_q).astype(BF16)


def feed(blocks, frames, cotangent, w_out, gain, w_up, b_up, w_down, b_down):
    rows, width = frames.shape
    ff = w_up.shape[1]
    steps = 8
    step = ff // steps
    fixed = lambda *shape: pl.BlockSpec(shape, lambda i: (0,) * len(shape))
    columns = lambda *shape: pl.BlockSpec(shape, lambda i: (0,) * (len(shape) - 1) + (i,))
    shape = jax.ShapeDtypeStruct
    return pl.pallas_call(
        feed_kernel,
        grid=(steps,),
        in_specs=[
            fixed(*blocks.shape),
            fixed(rows, width),
            fixed(rows, width),
            fixed(width, width),
            fixed(1, width),
            columns(width, step),
            columns(1, step),
            pl.BlockSpec((step, width), lambda i: (i, 0)),
            fixed(1, width),
        ],
        out_specs=[
            fixed(rows, width),
            fixed(rows, width),
            fixed(*blocks.shape),
            columns(2, rows, step // 2),
            columns(rows, step),
            fixed(2, rows, width // 2),
            fixed(2, rows, width // 2),
            fixed(rows, width),
            fixed(rows, width),
            fixed(1, width),
            columns(1, step),
            fixed(1, width),
        ],
        out_shape=[
            shape((rows, width), F32),
            shape((rows, width), F32),
            shape(blocks.shape, BF16),
            shape((2, rows, ff // 2), BF16),
            shape((rows, ff), BF16),
            shape((2, rows, width // 2), BF16),
            shape((2, rows, width // 2), BF16),
            shape((rows, width), BF16),
            shape((rows, width), BF16),
            shape((1, width), F32),
            shape((1, ff), F32),
            shape((1, width), F32),
        ],
        scratch_shapes=[
            pltpu.VMEM((rows, width), F32),
            pltpu.VMEM((rows, width), BF16),
            pltpu.VMEM((rows, width), F32),
        ],
        compiler_params=pltpu.CompilerParams(vmem_limit_bytes=28 << 20),
        name="feed",
    )(
        blocks, frames, cotangent, w_out, gain.reshape(1, width), w_up, b_up.reshape(1, ff), w_down,
        b_down.reshape(1, width),
    )


MESH = pl.DeviceIdType.MESH
ALL = ("blk", "grp")


def in_hbm(*arrays):
    return [pltpu.with_memory_space_constraint(x, pltpu.HBM) for x in arrays]


def in_vmem(*arrays):
    return [pltpu.with_memory_space_constraint(x, pltpu.VMEM) for x in arrays]


def place(index):
    return {"blk": lax.div(index, 2), "grp": lax.rem(index, 2)}


def head_of(index):
    blk, grp = lax.div(index, 2), lax.rem(index, 2)
    return lax.div(blk, 2) * 2 + grp, lax.rem(blk, 2)


def own_index():
    return lax.axis_index("blk") * 2 + lax.axis_index("grp")


def sibling_of(core):
    return {"blk": lax.axis_index("blk") + 1 - 2 * core, "grp": lax.axis_index("grp")}


def greet_all(me, n):
    barrier = pltpu.get_barrier_semaphore()

    @pl.loop(1, n)
    def _(i):
        pl.semaphore_signal(barrier, inc=1, device_id=place(lax.rem(me + i, n)), device_id_type=MESH)

    pl.semaphore_wait(barrier, n - 1)


def remote(src, dst, send_sem, recv_sem, device):
    return pltpu.make_async_remote_copy(
        src_ref=src, dst_ref=dst, send_sem=send_sem, recv_sem=recv_sem, device_id=device, device_id_type=MESH
    )


def to_heads_kernel(
    n, gain, frames_in, wq_in, wk_in, wv_in, kv_out, q_out, halves,
    frames, act, wq, wk, wv, kv_own, q_own, send, recv, local, pair,
):
    me = own_index()
    head, core = head_of(me)
    rows, width = frames.shape
    half = rows // 2
    weights = [
        pltpu.make_async_copy(src, dst, local.at[k])
        for k, (src, dst) in enumerate(((frames_in, frames), (wq_in, wq), (wk_in, wk), (wv_in, wv)))
    ]
    for copy in weights:
        copy.start()
    greet_all(me, n)
    weights[0].wait()
    x = frames[...]
    r = lax.rsqrt(jnp.mean(x * x, axis=-1, keepdims=True) + EPSILON)
    normed = x * r * gain[...]
    act[...] = normed.astype(BF16)
    store_halves(halves, normed)
    for copy in weights[1:]:
        copy.wait()

    def copies(other, src):
        h, c = head_of(other)
        kv_at = core if src is not me else c
        return (
            remote(kv_own.at[h, c], kv_out.at[src, kv_at], send.at[0, other], recv.at[0, src], place(other)),
            remote(q_own.at[h, c], q_out.at[src], send.at[1, other], recv.at[1, src], place(other)),
        )

    low = low_lanes((rows, 128))
    low_h = low_lanes((half // 2, 128))
    groups = width // 256

    @pl.loop(0, groups)
    def _(i):
        group = lax.rem(lax.div(me, n // groups) + 1 + i, groups)
        columns = pl.ds(pl.multiple_of(group * 256, 256), 256)
        q = nn_dot(act[...], wq[:, columns]).astype(BF16).astype(F32) * 0.125
        k = nn_dot(act[...], wk[:, columns])
        v = nn_dot(act[...], wv[:, columns])
        for p in range(2):
            at = slice(p * 128, (p + 1) * 128)
            k2, v2, q2 = k[:, at], v[:, at], q[:, at]
            kv_a = pair_low(k2, v2, low).astype(BF16)
            kv_b = pair_high(k2, v2, low).astype(BF16)
            h = group * 4 + 2 * p
            for s in range(2):
                span = slice(s * half, (s + 1) * half)
                kv_own[h, s] = kv_a[span]
                kv_own[h + 1, s] = kv_b[span]
                top = q2[s * half : s * half + half // 2]
                bot = q2[s * half + half // 2 : (s + 1) * half]
                q_own[h, s] = pair_low(top, bot, low_h).astype(BF16)
                q_own[h + 1, s] = pair_high(top, bot, low_h).astype(BF16)

        @pl.loop(0, n // groups)
        def _(j):
            other = group * (n // groups) + j

            @pl.when(other != me)
            def _():
                for copy in copies(other, me):
                    copy.start()

    kv_out[me, core] = kv_own[head, core]
    q_out[me] = q_own[head, core]

    @pl.loop(1, n)
    def _(i):
        other = lax.rem(me + i, n)
        for copy in copies(other, other):
            copy.wait()

    swap = remote(kv_out.at[:, core], kv_out.at[:, core], pair.at[0], pair.at[1], sibling_of(core))
    swap.start()
    swap.wait()


def to_heads(frames, gain, w_query, w_key, w_value, n):
    rows, width = frames.shape
    half = rows // 2
    vmem = pl.BlockSpec(memory_space=pltpu.VMEM)
    hbm = pl.BlockSpec(memory_space=pltpu.HBM)
    return pl.pallas_call(
        functools.partial(to_heads_kernel, n),
        in_specs=[vmem] + [hbm] * 4,
        out_specs=[vmem] * 3,
        out_shape=[
            jax.ShapeDtypeStruct((n, 2, half, 128), BF16),
            jax.ShapeDtypeStruct((n, half // 2, 128), BF16),
            jax.ShapeDtypeStruct((2, rows, width // 2), BF16),
        ],
        scratch_shapes=[
            pltpu.VMEM((rows, width), F32),
            pltpu.VMEM((rows, width), BF16),
            pltpu.VMEM((width, width), BF16),
            pltpu.VMEM((width, width), BF16),
            pltpu.VMEM((width, width), BF16),
            pltpu.VMEM((width // 64, 2, half, 128), BF16),
            pltpu.VMEM((width // 64, 2, half // 2, 128), BF16),
            pltpu.SemaphoreType.DMA((2, n)),
            pltpu.SemaphoreType.DMA((2, n)),
            pltpu.SemaphoreType.DMA((4,)),
            pltpu.SemaphoreType.DMA((2,)),
        ],
        compiler_params=pltpu.CompilerParams(
            collective_id=0, has_side_effects=True, vmem_limit_bytes=16 << 20
        ),
        name="to_heads",
    )(gain.reshape(1, width), *in_hbm(frames, w_query, w_key, w_value))


def exchange_kernel(n, x_in, x_out, send, recv, local):
    me = own_index()
    greet_all(me, n)

    def copy_with(i, src):
        other = lax.rem(me + i, n)
        return remote(x_in.at[other], x_out.at[src], send.at[i], recv.at[src], place(other))

    @pl.loop(1, n)
    def _(i):
        copy_with(i, me).start()

    own = pltpu.make_async_copy(x_in.at[me], x_out.at[me], local)
    own.start()
    own.wait()

    @pl.loop(1, n)
    def _(i):
        copy_with(i, lax.rem(me + i, n)).wait()


def exchange(x, n, collective_id):
    vmem = pl.BlockSpec(memory_space=pltpu.VMEM)
    return pl.pallas_call(
        functools.partial(exchange_kernel, n),
        in_specs=[vmem],
        out_specs=vmem,
        out_shape=jax.ShapeDtypeStruct(x.shape, x.dtype),
        scratch_shapes=[
            pltpu.SemaphoreType.DMA((n,)),
            pltpu.SemaphoreType.DMA((n,)),
            pltpu.SemaphoreType.DMA,
        ],
        compiler_params=pltpu.CompilerParams(collective_id=collective_id, has_side_effects=True, vmem_limit_bytes=8 << 20),
        name="exchange",
    )(x)


BITS = {"core": 1, "y": 2, "z0": 4, "z1": 8}


def flipped(x, axis):
    if axis == "x":
        return lax.ppermute(x, "grp", [(0, 1), (1, 0)])
    return lax.ppermute(x, "blk", [(i, i ^ BITS[axis]) for i in range(lax.axis_size("blk"))])


def bit_of(axis):
    if axis == "x":
        return lax.axis_index("grp")
    return lax.rem(lax.div(lax.axis_index("blk"), BITS[axis]), 2)


def across(axis):
    blk, grp = lax.axis_index("blk"), lax.axis_index("grp")
    if axis == "x":
        return {"blk": blk, "grp": 1 - grp}
    bit = BITS[axis]
    return {"blk": blk + bit - 2 * bit * bit_of(axis), "grp": grp}


def tn_dot(a, b):
    return lax.dot_general(a, b, (((0,), (0,)), ((), ())), preferred_element_type=F32)


def share_kernel(
    n, blocks_in, hidden, grad_before, act2, mixed, low, attn,
    blocks_out, keep_a_out, send_a_out, keep_b_out, send_b_out, keep_c_out, send_c_out,
    keep_a, send_a, keep_b, send_b, keep_c, send_c, hidden2, before2, act2_2, mixed2, low2, attn2, tile, send, recv, local, out, pair_send, pair_recv,
):
    me = own_index()
    head, core = head_of(me)
    rows = low.shape[0]
    greet_all(me, n)
    sibling = sibling_of(core)
    theirs = pl.ds(rows, rows)
    pairs = [
        remote(src, dst.at[theirs], pair_send.at[k], pair_recv.at[k], sibling)
        for k, (src, dst) in enumerate(
            (
                (low, low2),
                (hidden.at[1 - core], hidden2),
                (act2.at[1 - core], act2_2),
                (grad_before, before2),
                (mixed.at[1 - core], mixed2),
                (attn, attn2),
            )
        )
    ]
    for copy in pairs:
        copy.start()

    def copy_with(i, src):
        other = lax.rem(me + i, n)
        return remote(blocks_in.at[other], blocks_out.at[src], send.at[i], recv.at[src], place(other))

    @pl.loop(1, n)
    def _(i):
        copy_with(i, me).start()

    own = pltpu.make_async_copy(blocks_in.at[me], blocks_out.at[me], local)
    own.start()
    low2[:rows] = low[...]
    hidden2[:rows] = hidden[core]
    act2_2[:rows] = act2[core]
    before2[:rows] = grad_before[...]
    mixed2[:rows] = mixed[core]
    attn2[:rows] = attn[...]

    x_mine, y_mine, z_mine = bit_of("x"), bit_of("y"), bit_of("z0")

    def put(keep, away, mine, bit, at, row, value):
        @pl.when(mine == bit)
        def _():
            keep[at, row : row + value.shape[0]] = value

        @pl.when(mine != bit)
        def _():
            away[at, row : row + value.shape[0]] = value

    flushes = []

    def flush(src, dst):
        flushes.append(pltpu.make_async_copy(src, dst, out.at[len(flushes)]))
        flushes[-1].start()

    pairs[0].wait()
    pairs[1].wait()

    @pl.loop(0, 8)
    def _(zy):
        columns = pl.ds(pl.multiple_of(zy * 256, 256), 256)
        value = tn_dot(hidden2[:, columns], low2[...]).astype(BF16)
        z1, z0, y = lax.div(zy, 4), lax.rem(lax.div(zy, 2), 2), lax.rem(zy, 2)
        for x in range(2):
            put(keep_a, send_a, x_mine, x, zy, 0, value[x * 128 : x * 128 + 96])
            put(keep_c, send_c, z_mine, z0, (z1 * 2 + y) * 2 + x, 0, value[x * 128 + 96 : (x + 1) * 128])

    def spread_rows(left, right, slab, to_b, row):
        tile[...] = tn_dot(left[...], right[:, slab * 1024 : (slab + 1) * 1024]).astype(BF16)

        @pl.loop(0, 16)
        def _(j):
            value = tile[pl.ds(pl.multiple_of(j * 32, 32), 32)]
            z1, z0 = lax.div(j, 8), lax.rem(lax.div(j, 4), 2)
            y, x = lax.rem(lax.div(j, 2), 2), lax.rem(j, 2)
            if to_b:
                put(keep_b, send_b, y_mine, y, (z1 * 2 + z0) * 2 + x, row, value)
            else:
                put(keep_c, send_c, z_mine, z0, (z1 * 2 + y) * 2 + x, row, value)

    flush(keep_a, keep_a_out)
    flush(send_a, send_a_out)
    pairs[2].wait()
    pairs[3].wait()
    for slab in range(3):
        spread_rows(act2_2, before2, slab, True, 32 * slab)
    flush(keep_b, keep_b_out)
    flush(send_b, send_b_out)
    spread_rows(act2_2, before2, 3, False, 32)
    pairs[4].wait()
    pairs[5].wait()
    spread_rows(mixed2, attn2, 0, False, 64)
    flush(keep_c, keep_c_out)
    flush(send_c, send_c_out)
    own.wait()

    @pl.loop(1, n)
    def _(i):
        copy_with(i, lax.rem(me + i, n)).wait()

    for copy in flushes:
        copy.wait()


def share(blocks, hidden, grad_before, act2, mixed, low, attn, n):
    rows, width = low.shape
    vmem = pl.BlockSpec(memory_space=pltpu.VMEM)
    hbm = pl.BlockSpec(memory_space=pltpu.HBM)
    shape = jax.ShapeDtypeStruct
    return pl.pallas_call(
        functools.partial(share_kernel, n),
        in_specs=[vmem] * 7,
        out_specs=[vmem] + [hbm] * 6,
        out_shape=[shape(blocks.shape, BF16)] + [pltpu.HBM((8, 96, width), BF16)] * 6,
        scratch_shapes=[
            *[pltpu.VMEM((8, 96, width), BF16)] * 6,
            pltpu.VMEM((2 * rows, hidden.shape[2]), BF16),
            pltpu.VMEM((2 * rows, grad_before.shape[1]), BF16),
            pltpu.VMEM((2 * rows, width // 2), BF16),
            pltpu.VMEM((2 * rows, width // 2), BF16),
            pltpu.VMEM((2 * rows, width), BF16),
            pltpu.VMEM((2 * rows, width), BF16),
            pltpu.VMEM((width // 2, 1024), BF16),
            pltpu.SemaphoreType.DMA((n,)),
            pltpu.SemaphoreType.DMA((n,)),
            pltpu.SemaphoreType.DMA,
            pltpu.SemaphoreType.DMA((6,)),
            pltpu.SemaphoreType.DMA((6,)),
            pltpu.SemaphoreType.DMA((6,)),
        ],
        compiler_params=pltpu.CompilerParams(
            collective_id=3, has_side_effects=True, vmem_limit_bytes=26 << 20
        ),
        name="share",
    )(blocks, hidden, grad_before, act2, mixed, low, attn)


class Part:
    def __init__(self, total, dims, order, landing, send, recv):
        self.view, self.dims, self.order = total, list(dims), list(order)
        self.landing, self.send, self.recv = landing, send, recv
        self.stage, self.copy, self.kept = 0, None, None

    def start(self):
        axis = self.order[self.stage]
        at, mine = self.dims.index(axis), bit_of(axis)
        ahead = (slice(None),) * at
        self.copy = remote(
            self.view.at[ahead + (1 - mine,)],
            self.landing[self.stage],
            self.send.at[self.stage],
            self.recv.at[self.stage],
            across(axis),
        )
        self.copy.start()
        self.kept = self.view.at[ahead + (mine,)]
        self.dims.remove(axis)
        self.stage += 1

    def finish(self):
        self.copy.wait()
        got, kept = self.landing[self.stage - 1], self.kept
        lead = len(self.dims)

        @pl.loop(0, 2**lead)
        def _(k):
            at = tuple(lax.rem(lax.div(k, 2**d), 2) for d in reversed(range(lead)))
            kept[at] = (kept[at].astype(F32) + got[at].astype(F32)).astype(BF16)

        self.view = kept

    def last(self):
        self.copy.wait()
        return self.kept[...].astype(F32) + self.landing[self.stage - 1][...].astype(F32)


def finish_kernel(
    n, dkv_in, dq_in, gain, gain2_grad, b_up_grad, b_down_grad, act1, frames_in, grad_mid_in, wq_in, wk_in, wv_in,
    keep_a, got_a, keep_b, got_b, keep_c, got_c,
    frames_out, q_out, k_out, v_out, o_out, up_out, down_out, small_out,
    theirs, total, dkv_all, dq_all, frames, grad_mid, wq, wk, wv, small_in, new_a, new_b, new_c,
    act1_2, qkv2, sum_a, sum_b, sum_c, sum_q, sum_k, sum_v,
    a2, a3, a4, b2, b3, b4, c2, c3, c4,
    q1, q2, q3, q4, k1, k2, k3, k4, v1, v2, v3, v4, small_all,
    send, recv, dq_send, dq_recv, dkv_send, dkv_recv, small_send, small_recv, pair_send, pair_recv, local,
):
    me = own_index()
    head, core = head_of(me)
    rows, width = frames.shape
    quarter = rows // 4
    sums = [sum_a, sum_b, sum_c, sum_q, sum_k, sum_v]
    news = [new_a, new_b, new_c]
    fetches = [
        pltpu.make_async_copy(src, dst, local.at[k])
        for k, (src, dst) in enumerate(
            (
                (keep_a, sum_a), (got_a, new_a), (keep_b, sum_b), (got_b, new_b), (keep_c, sum_c), (got_c, new_c),
                (wq_in, wq), (wk_in, wk), (wv_in, wv), (frames_in, frames), (grad_mid_in, grad_mid),
            )
        )
    ]
    for copy in fetches:
        copy.start()
    greet_all(me, n)
    sibling = sibling_of(core)
    swap = remote(dkv_in.at[:, 1 - core], theirs, pair_send.at[0], pair_recv.at[0], sibling)
    swap.start()
    act1_copy = remote(act1.at[1 - core], act1_2.at[pl.ds(rows, rows)], pair_send.at[1], pair_recv.at[1], sibling)

    def to_all(src_ref, dst_ref, sends, recvs):
        def copy_with(i, src):
            other = lax.rem(me + i, n)
            return remote(src_ref.at[other], dst_ref.at[src], sends.at[i], recvs.at[src], place(other))

        return copy_with

    dq_copy = to_all(dq_in, dq_all, dq_send, dq_recv)
    dkv_copy = to_all(total, dkv_all, dkv_send, dkv_recv)
    small_copy = to_all(small_in, small_all, small_send, small_recv)

    @pl.loop(1, n)
    def _(i):
        dq_copy(i, me).start()

    swap.wait()

    def add(j):
        return (dkv_in[j, core] + theirs[j]).astype(BF16)

    @pl.loop(1, n)
    def _(i):
        other = lax.rem(me + i, n)
        total[other] = add(other)
        dkv_copy(i, me).start()

    dkv_all[me] = add(me)
    dq_all[me] = dq_in[me]
    act1_copy.start()
    dims = [("z1", "z0", "y"), ("z1", "z0", "x"), ("z1", "y", "x")] + [("z1", "z0", "y", "x")] * 3
    orders = [
        ("y", "z0", "z1"), ("z0", "x", "z1"), ("x", "y", "z1"),
        ("x", "y", "z0", "z1"), ("y", "z0", "x", "z1"), ("z0", "x", "y", "z1"),
    ]
    landings = [(a2, a3, a4), (b2, b3, b4), (c2, c3, c4), (q1, q2, q3, q4), (k1, k2, k3, k4), (v1, v2, v3, v4)]
    parts = [
        Part(whole, names, order, landing, send.at[k], recv.at[k])
        for k, (whole, names, order, landing) in enumerate(zip(sums, dims, orders, landings))
    ]
    for k in range(3):
        whole, new = sums[k], news[k]
        fetches[2 * k].wait()
        fetches[2 * k + 1].wait()

        @pl.loop(0, 8)
        def _(k):
            at = (lax.div(k, 4), lax.rem(lax.div(k, 2), 2), lax.rem(k, 2))
            whole[at] = (whole[at].astype(F32) + new[at].astype(F32)).astype(BF16)

        parts[k].start()

    act1_own = pltpu.make_async_copy(act1.at[core], act1_2.at[pl.ds(0, rows)], local.at[11])
    act1_own.start()

    @pl.loop(1, n)
    def _(i):
        src = lax.rem(me + i, n)
        dq_copy(i, src).wait()
        dkv_copy(i, src).wait()

    for part in parts[:3]:
        part.finish()
        part.start()
    low_q, low_h = low_lanes((quarter, 128)), low_lanes((2 * quarter, 128))
    for zy in range(8):
        for s in range(2):
            j = (zy * 2 + s) * 2
            first = 2 * s * quarter
            a, b = dq_all[j].astype(F32), dq_all[j + 1].astype(F32)
            at = slice(zy * 128, (zy + 1) * 128)
            qkv2[first : first + quarter, at] = pair_low(a, b, low_q).astype(BF16)
            qkv2[first + quarter : first + 2 * quarter, at] = pair_high(a, b, low_q).astype(BF16)
            a, b = dkv_all[j].astype(F32), dkv_all[j + 1].astype(F32)
            at = slice(width + zy * 128, width + (zy + 1) * 128)
            qkv2[first : first + 2 * quarter, at] = pair_low(a, b, low_h).astype(BF16)
            at = slice(2 * width + zy * 128, 2 * width + (zy + 1) * 128)
            qkv2[first : first + 2 * quarter, at] = pair_high(a, b, low_h).astype(BF16)
    pair = remote(qkv2.at[pl.ds(0, rows)], qkv2.at[pl.ds(rows, rows)], pair_send.at[2], pair_recv.at[2], sibling)
    pair.start()

    for copy in fetches[6:]:
        copy.wait()
    g = nt_dot(qkv2[:rows, :width], wq[...])
    g += nt_dot(qkv2[:rows, width : 2 * width], wk[...])
    g += nt_dot(qkv2[:rows, 2 * width :], wv[...])
    act1_copy.wait()
    act1_own.wait()
    pair.wait()
    for k in range(3):
        value = tn_dot(act1_2[...], qkv2[:, k * width : (k + 1) * width]).astype(BF16)
        for j in range(16):
            sums[3 + k][j // 8, j // 4 % 2, j // 2 % 2, j % 2] = value[j * 32 : (j + 1) * 32]
        parts[3 + k].start()
    for part in parts[:3]:
        part.finish()
        part.start()

    x = frames[...]
    r = lax.rsqrt(jnp.mean(x * x, axis=-1, keepdims=True) + EPSILON)
    norm = x * r
    gain_grad = jnp.sum(g * norm, axis=0, keepdims=True)
    small_in[...] = jnp.zeros_like(small_in)
    for d in range(n):
        at = slice(d // 4 * 128, (d // 4 + 1) * 128)
        small_in[d, 0:1] = gain_grad[:, at]
        small_in[d, 1:2] = gain2_grad[:, at]
        small_in[d, 2:3] = b_down_grad[:, at]
        small_in[d, 3:4] = b_up_grad[:, d * 128 : (d + 1) * 128]

    @pl.loop(1, n)
    def _(i):
        small_copy(i, me).start()

    g = g * gain[...]
    frames_out[...] = grad_mid[...] + r * (g - norm * jnp.mean(g * norm, axis=-1, keepdims=True))
    small_all[me] = small_in[me]

    for part in parts[3:] * 3:
        part.finish()
        part.start()

    @pl.loop(1, n)
    def _(i):
        small_copy(i, lax.rem(me + i, n)).wait()

    small_out[...] = jnp.sum(small_all[...], axis=0)
    down_out[:96] = parts[0].last()
    value = parts[1].last()
    for slab in range(3):
        up_out[:, slab * 1024 : (slab + 1) * 1024] = value[slab * 32 : (slab + 1) * 32]
    value = parts[2].last()
    down_out[96:] = value[:32]
    up_out[:, 3072:] = value[32:64]
    o_out[...] = value[64:]
    q_out[...] = parts[3].last()
    k_out[...] = parts[4].last()
    v_out[...] = parts[5].last()


def finish(dkv, dq, act1, frames, grad_mid, gain, gain2_grad, b_up_grad, b_down_grad, weights, keeps, gots, n):
    rows, width = frames.shape
    parts = [x.reshape(2, 2, 2, *x.shape[1:]) for pair in zip(keeps, gots) for x in pair]
    half = dkv.shape[2]
    vmem = pl.BlockSpec(memory_space=pltpu.VMEM)
    hbm = pl.BlockSpec(memory_space=pltpu.HBM)
    shape = jax.ShapeDtypeStruct
    thin, wide = (32, width), (96, width)
    buffers = [pltpu.VMEM((2, 2, 2, *wide), BF16)] * 3 + [pltpu.VMEM((2, 2, 2, 2, *thin), BF16)] * 3
    buffers += [pltpu.VMEM((2,) * k + wide, BF16) for k in (2, 1, 0)] * 3
    buffers += [pltpu.VMEM((2,) * k + thin, BF16) for k in (3, 2, 1, 0)] * 3
    over_devices = [pltpu.SemaphoreType.DMA((n,))] * 6
    return pl.pallas_call(
        functools.partial(finish_kernel, n),
        in_specs=[vmem] * 6 + [hbm] * 12,
        out_specs=[vmem] * 8,
        out_shape=[shape((rows, width), F32)]
        + [shape(thin, F32)] * 4
        + [shape((32, 4 * width), F32), shape((128, width), F32), shape((8, 128), F32)],
        scratch_shapes=[
            pltpu.VMEM((n, half, 128), F32),
            pltpu.VMEM((n, half, 128), BF16),
            pltpu.VMEM((n, half, 128), BF16),
            pltpu.VMEM((n, half // 2, 128), BF16),
            pltpu.VMEM((rows, width), F32),
            pltpu.VMEM((rows, width), F32),
            pltpu.VMEM((width, width), BF16),
            pltpu.VMEM((width, width), BF16),
            pltpu.VMEM((width, width), BF16),
            pltpu.VMEM((n, 8, 128), F32),
            *[pltpu.VMEM((2, 2, 2, *wide), BF16)] * 3,
            pltpu.VMEM((2 * rows, width // 2), BF16),
            pltpu.VMEM((2 * rows, 3 * width), BF16),
            *buffers,
            pltpu.VMEM((n, 8, 128), F32),
            pltpu.SemaphoreType.DMA((6, 4)),
            pltpu.SemaphoreType.DMA((6, 4)),
            *over_devices,
            pltpu.SemaphoreType.DMA((3,)),
            pltpu.SemaphoreType.DMA((3,)),
            pltpu.SemaphoreType.DMA((12,)),
        ],
        compiler_params=pltpu.CompilerParams(
            collective_id=4, has_side_effects=True, vmem_limit_bytes=42 << 20
        ),
        name="finish",
    )(
        *in_vmem(dkv, dq), gain.reshape(1, width), gain2_grad, b_up_grad, b_down_grad,
        *in_hbm(act1, frames, grad_mid, *weights, *parts),
    )


def shards_heads(
    frames, lengths, norm1_gain, w_query, w_key, w_value, w_out, norm2_gain, w_up, b_up, w_down, b_down, cotangent
):
    rows, width = frames.shape
    n = lax.axis_size("blk") * lax.axis_size("grp")
    half = rows // 2
    core_word = bit_of("core").astype(jnp.int32).reshape(1)
    qpos = jnp.asarray(packed_positions(n, half))

    kv, q, act1 = to_heads(frames, norm1_gain, w_query, w_key, w_value, n)
    kv_rows = kv.reshape(n * rows, 128)
    out_t, lse, out_blocks = mix(lengths, core_word, kv_rows, q, qpos)
    mixed_blocks = exchange(out_blocks, n, 2)
    (
        layer_out, grad_middle, grad_blocks, hidden, grad_before, act2, mixed, grad_low, grad_attn,
        norm2_gain_grad, b_up_grad, b_down_grad,
    ) = feed(mixed_blocks, frames, cotangent, w_out, norm2_gain, w_up, b_up, w_down, b_down)

    grad_blocks, *parts = share(grad_blocks, hidden, grad_before, act2, mixed, grad_low, grad_attn, n)
    keeps = parts[0::2]
    gots = [flipped(part, axis) for part, axis in zip(parts[1::2], ("x", "y", "z0"))]
    dkv, dq = mix_back(lengths, core_word, kv_rows, q, grad_blocks, qpos, out_t, lse)

    frames_grad, w_query_grad, w_key_grad, w_value_grad, w_out_grad, w_up_grad, w_down_grad, small = finish(
        dkv.reshape(n, 2, half, 128), dq, act1, frames, grad_middle, norm1_gain, norm2_gain_grad, b_up_grad,
        b_down_grad, (w_query, w_key, w_value), keeps, gots, n,
    )
    part = width // n
    turn = lax.rem(own_index(), 128 // part) * part
    vectors = lax.dynamic_slice(small, (0, turn), (3, part))
    return (
        layer_out,
        frames_grad,
        vectors[0],
        w_query_grad,
        w_key_grad,
        w_value_grad,
        w_out_grad,
        vectors[1],
        w_up_grad,
        small[3],
        w_down_grad,
        vectors[2],
    )


def solution(mesh):
    if mesh.shape["blk"] != 16 or mesh.shape["grp"] != 2:
        return solution_ring(mesh)
    split = P(ALL, None)
    return jax.shard_map(
        shards_heads,
        mesh=mesh,
        in_specs=(split, P(), P(), P(), P(), P(), P(), P(), P(), P(), P(), P(), split),
        out_specs=(split, split, P(ALL), split, split, split, split, P(ALL), split, P(ALL), split, P(ALL)),
        check_vma=False,
    )
```

```python
import functools

import jax
import jax.numpy as jnp
import numpy as np
from jax import lax
from jax.experimental import pallas as pl
from jax.experimental.pallas import tpu as pltpu
from jax.sharding import PartitionSpec as P

HEAD_DIM = 64
ITEM_MAX = 4096


EPSILON = 1e-05
MASKED = -1e30
SCALING = 0.125


def shortened(array):

    def short(part):
        return part.astype(jnp.bfloat16) if part.dtype == jnp.float32 else part

    return jax.tree.map(short, array)


def passed_along(block, axis, distance):
    devices = range(lax.axis_size(axis))
    route = [(i - distance, i) for i in devices if i - distance in devices]
    return lax.ppermute(block, axis, route)


def rms_norm(values, gain):
    return values * lax.rsqrt(jnp.mean(values * values, axis=-1, keepdims=True) + EPSILON) * gain


def gelu_exact(values):
    return jax.nn.gelu(values, approximate=False)


def item_starts(lengths, positions):
    ends = jnp.cumsum(lengths)
    offsets = ends - lengths
    before = offsets[None, :] <= positions[:, None]
    return jnp.max(jnp.where(before, offsets[None, :], 0), axis=1)


def live_mask(query_pos, query_start, key_first, key_count):
    key_pos = key_first + jnp.arange(key_count, dtype=jnp.int32)
    return (key_pos[None, :] >= query_start[:, None]) & (key_pos[None, :] <= query_pos[:, None])


def split_heads(matrix):
    return matrix.reshape(matrix.shape[0], matrix.shape[1] // HEAD_DIM, HEAD_DIM)


def merge_heads(tensor):
    return tensor.reshape(tensor.shape[0], tensor.shape[1] * tensor.shape[2])


def scores_of(queries3, keys_block, mask):
    raw = jnp.einsum(
        "qhd,khd->hqk", queries3, split_heads(keys_block), preferred_element_type=jnp.float32
    )
    return jnp.where(mask[None], raw * SCALING, MASKED)


def left_dot(left, right):
    return lax.dot_general(
        left, right, (((0,), (0,)), ((), ())), preferred_element_type=jnp.float32
    )


def right_dot(left, right):
    return lax.dot_general(
        left, right, (((1,), (1,)), ((), ())), preferred_element_type=jnp.float32
    )


def grad_parts(queries3, grad_out3, log_total, delta, keys_block, values_block, mask):
    probs = jnp.exp(scores_of(queries3, keys_block, mask) - log_total[:, :, None])
    grad_probs = jnp.einsum(
        "qhd,khd->hqk", grad_out3, split_heads(values_block), preferred_element_type=jnp.float32
    )
    grad_scores = (probs * (grad_probs - delta[:, :, None])).astype(jnp.bfloat16)
    return (probs.astype(jnp.bfloat16), grad_scores)


def key_terms(queries3, grad_out3, probs_low, grad_scores):
    grad_keys = jnp.einsum(
        "hqk,qhd->khd", grad_scores, queries3, preferred_element_type=jnp.float32
    )
    grad_values = jnp.einsum(
        "hqk,qhd->khd", probs_low, grad_out3, preferred_element_type=jnp.float32
    )
    return (merge_heads(grad_keys), merge_heads(grad_values))


def query_term(grad_scores, keys_block):
    return jnp.einsum(
        "hqk,khd->qhd", grad_scores, split_heads(keys_block), preferred_element_type=jnp.float32
    )


def shards_ring(
    frames,
    lengths,
    norm1_gain,
    w_query,
    w_key,
    w_value,
    w_out,
    norm2_gain,
    w_up,
    b_up,
    w_down,
    b_down,
    cotangent,
):
    row_count = frames.shape[0]
    width = frames.shape[1]
    heads = width // HEAD_DIM
    groups = lax.axis_size("grp")
    block_rows = row_count * groups
    span = (ITEM_MAX + block_rows - 2) // block_rows
    blk_index = lax.axis_index("blk")
    sub_index = lax.axis_index("grp")
    block_first = blk_index * block_rows
    query_pos = block_first + sub_index * row_count + jnp.arange(row_count, dtype=jnp.int32)
    query_start = item_starts(lengths, query_pos)
    back_steps = jnp.arange(span + 1, dtype=jnp.int32)
    normed1, norm1_back = jax.vjp(rms_norm, frames, norm1_gain)
    act1 = normed1.astype(jnp.bfloat16)
    queries = jnp.dot(act1, w_query, preferred_element_type=jnp.float32).astype(jnp.bfloat16)
    keys_own = jnp.dot(act1, w_key, preferred_element_type=jnp.float32).astype(jnp.bfloat16)
    values_own = jnp.dot(act1, w_value, preferred_element_type=jnp.float32).astype(jnp.bfloat16)
    queries3 = split_heads(queries)
    block_keys, block_values = (
        lax.all_gather(keys_own, "grp", axis=0, tiled=True),
        lax.all_gather(values_own, "grp", axis=0, tiled=True),
    )

    def cycle_step(carry, unused_input):
        moved = jax.tree.map(
            lambda part, own: part.astype(own.dtype),
            passed_along(shortened(carry), "blk", 1),
            carry,
        )
        return (moved, moved)

    unused_last, far_blocks = lax.scan(cycle_step, (block_keys, block_values), None, length=span)
    keys_all = jnp.concatenate([block_keys[None], far_blocks[0]], axis=0)
    values_all = jnp.concatenate([block_values[None], far_blocks[1]], axis=0)

    def mask_for(back):
        return live_mask(query_pos, query_start, block_first - back * block_rows, block_rows)

    def total_step(carry, inputs):
        run_max, run_sum = carry
        keys_block, back = inputs
        scores = scores_of(queries3, keys_block, mask_for(back))
        new_max = jnp.maximum(run_max, jnp.max(scores, axis=-1))
        run_sum = run_sum * jnp.exp(run_max - new_max) + jnp.sum(
            jnp.exp(scores - new_max[:, :, None]), axis=-1
        )
        return ((new_max, run_sum), None)

    start_max = jnp.full((heads, row_count), MASKED, jnp.float32)
    start_sum = jnp.zeros((heads, row_count), jnp.float32)
    (top_max, top_sum), unused_out = lax.scan(
        total_step, (start_max, start_sum), (keys_all, back_steps)
    )
    log_total = top_max + jnp.log(top_sum)

    def mix_step(total, inputs):
        keys_block, values_block, back = inputs
        probs = jnp.exp(
            scores_of(queries3, keys_block, mask_for(back)) - log_total[:, :, None]
        ).astype(jnp.bfloat16)
        return (
            total
            + jnp.einsum(
                "hqk,khd->qhd", probs, split_heads(values_block), preferred_element_type=jnp.float32
            ),
            None,
        )

    zero_query = jnp.zeros((row_count, heads, HEAD_DIM), jnp.float32)
    mixed_sum, unused_out = lax.scan(mix_step, zero_query, (keys_all, values_all, back_steps))
    mixed = merge_heads(mixed_sum).astype(jnp.bfloat16)
    middle = frames + jnp.dot(mixed, w_out, preferred_element_type=jnp.float32)
    normed2, norm2_back = jax.vjp(rms_norm, middle, norm2_gain)
    act2 = normed2.astype(jnp.bfloat16)
    before = jnp.dot(act2, w_up, preferred_element_type=jnp.float32) + b_up
    activated, gelu_back = jax.vjp(gelu_exact, before)
    hidden = activated.astype(jnp.bfloat16)
    layer_out = middle + jnp.dot(hidden, w_down, preferred_element_type=jnp.float32) + b_down
    grad_low = cotangent.astype(jnp.bfloat16)
    b_down_grad = jnp.sum(grad_low.astype(jnp.float32), axis=0)
    w_down_grad = left_dot(hidden, grad_low)
    grad_before = gelu_back(right_dot(grad_low, w_down))[0].astype(jnp.bfloat16)
    b_up_grad = jnp.sum(grad_before.astype(jnp.float32), axis=0)
    w_up_grad = left_dot(act2, grad_before)
    grad_mid_norm, norm2_gain_grad = norm2_back(right_dot(grad_before, w_up))
    grad_middle = cotangent + grad_mid_norm
    grad_attn = grad_middle.astype(jnp.bfloat16)
    w_out_grad = left_dot(mixed, grad_attn)
    grad_mixed = right_dot(grad_attn, w_out).astype(jnp.bfloat16)
    grad_out3 = split_heads(grad_mixed)

    def delta_step(total, inputs):
        keys_block, values_block, back = inputs
        probs = jnp.exp(scores_of(queries3, keys_block, mask_for(back)) - log_total[:, :, None])
        grad_probs = jnp.einsum(
            "qhd,khd->hqk", grad_out3, split_heads(values_block), preferred_element_type=jnp.float32
        )
        return (total + jnp.sum(probs * grad_probs, axis=-1), None)

    delta, unused_out = lax.scan(
        delta_step, jnp.zeros((heads, row_count), jnp.float32), (keys_all, values_all, back_steps)
    )
    zero_block = jnp.zeros((block_rows, width), jnp.float32)

    def return_step(carry, inputs):
        grad_q, travel = carry
        keys_block, values_block, back = inputs
        probs_low, grad_scores = grad_parts(
            queries3, grad_out3, log_total, delta, keys_block, values_block, mask_for(back)
        )
        grad_keys, grad_values = key_terms(queries3, grad_out3, probs_low, grad_scores)
        moved = (
            passed_along((travel[0] + grad_keys).astype(jnp.bfloat16), "blk", -1).astype(
                jnp.float32
            ),
            passed_along((travel[1] + grad_values).astype(jnp.bfloat16), "blk", -1).astype(
                jnp.float32
            ),
        )
        return ((grad_q + query_term(grad_scores, keys_block), moved), None)

    (grad_q, travel), unused_out = lax.scan(
        return_step,
        (zero_query, (zero_block, zero_block)),
        (far_blocks[0], far_blocks[1], back_steps[1:]),
        reverse=True,
    )
    probs_low, grad_scores = grad_parts(
        queries3, grad_out3, log_total, delta, block_keys, block_values, mask_for(0)
    )
    grad_keys, grad_values = key_terms(queries3, grad_out3, probs_low, grad_scores)
    grad_q = grad_q + query_term(grad_scores, block_keys)
    block_grad_keys = travel[0] + grad_keys
    block_grad_values = travel[1] + grad_values
    grad_keys_rows, grad_values_rows = (
        lax.psum_scatter(
            block_grad_keys.astype(jnp.bfloat16), "grp", scatter_dimension=0, tiled=True
        ).astype(jnp.float32),
        lax.psum_scatter(
            block_grad_values.astype(jnp.bfloat16), "grp", scatter_dimension=0, tiled=True
        ).astype(jnp.float32),
    )
    grad_keys_low = (grad_keys_rows * SCALING).astype(jnp.bfloat16)
    grad_values_low = grad_values_rows.astype(jnp.bfloat16)
    grad_queries_low = (merge_heads(grad_q) * SCALING).astype(jnp.bfloat16)
    w_query_grad = left_dot(act1, grad_queries_low)
    w_key_grad = left_dot(act1, grad_keys_low)
    w_value_grad = left_dot(act1, grad_values_low)
    grad_act1 = (
        right_dot(grad_queries_low, w_query)
        + right_dot(grad_keys_low, w_key)
        + right_dot(grad_values_low, w_value)
    )
    grad_frames_norm, norm1_gain_grad = norm1_back(grad_act1)
    frames_grad = grad_middle + grad_frames_norm
    shares = (
        lax.psum_scatter(norm1_gain_grad, ("blk", "grp"), scatter_dimension=0, tiled=True),
        lax.psum_scatter(w_query_grad, ("blk", "grp"), scatter_dimension=0, tiled=True),
        lax.psum_scatter(w_key_grad, ("blk", "grp"), scatter_dimension=0, tiled=True),
        lax.psum_scatter(w_value_grad, ("blk", "grp"), scatter_dimension=0, tiled=True),
        lax.psum_scatter(w_out_grad, ("blk", "grp"), scatter_dimension=0, tiled=True),
        lax.psum_scatter(norm2_gain_grad, ("blk", "grp"), scatter_dimension=0, tiled=True),
        lax.psum_scatter(w_up_grad, ("blk", "grp"), scatter_dimension=0, tiled=True),
        lax.psum_scatter(b_up_grad, ("blk", "grp"), scatter_dimension=0, tiled=True),
        lax.psum_scatter(w_down_grad, ("blk", "grp"), scatter_dimension=0, tiled=True),
        lax.psum_scatter(b_down_grad, ("blk", "grp"), scatter_dimension=0, tiled=True),
    )
    return (
        layer_out,
        frames_grad,
        shares[0],
        shares[1],
        shares[2],
        shares[3],
        shares[4],
        shares[5],
        shares[6],
        shares[7],
        shares[8],
        shares[9],
    )


def solution_ring(mesh):
    placed = (
        P(("blk", "grp"), None),
        P(),
        P(),
        P(),
        P(),
        P(),
        P(),
        P(),
        P(),
        P(),
        P(),
        P(),
        P(("blk", "grp"), None),
    )
    return jax.shard_map(
        shards_ring,
        mesh=mesh,
        in_specs=placed,
        out_specs=(
            P(("blk", "grp"), None),
            P(("blk", "grp"), None),
            P(("blk", "grp")),
            P(("blk", "grp"), None),
            P(("blk", "grp"), None),
            P(("blk", "grp"), None),
            P(("blk", "grp"), None),
            P(("blk", "grp")),
            P(("blk", "grp"), None),
            P(("blk", "grp")),
            P(("blk", "grp"), None),
            P(("blk", "grp")),
        ),
        check_vma=False,
    )


LOG2E = 1.4426950408889634
F32, BF16 = jnp.float32, jnp.bfloat16


def nt_dot(a, b):
    return lax.dot_general(a, b, (((1,), (1,)), ((), ())), preferred_element_type=F32)


def nn_dot(a, b):
    return lax.dot_general(a, b, (((1,), (0,)), ((), ())), preferred_element_type=F32)


def low_lanes(shape):
    return lax.broadcasted_iota(jnp.int32, shape, 1) < 64


def pair_low(a, b, low):
    return jnp.where(low, a, pltpu.roll(b, 64, 1))


def pair_high(a, b, low):
    return jnp.where(low, pltpu.roll(a, 64, 1), b)


def store_halves(ref, x):
    low = low_lanes((x.shape[0], 128))
    for p in range(x.shape[1] // 256):
        a, b = x[:, p * 256 : p * 256 + 128], x[:, p * 256 + 128 : (p + 1) * 256]
        ref[0, :, p * 128 : (p + 1) * 128] = pair_low(a, b, low).astype(BF16)
        ref[1, :, p * 128 : (p + 1) * 128] = pair_high(a, b, low).astype(BF16)


def block_bounds(len_ref, items, qpos, first, last, key_block):
    off = jnp.int32(0)
    start = jnp.zeros(qpos.shape, jnp.int32)
    s_first, s_last = jnp.int32(0), jnp.int32(0)
    for i in range(items):
        start = jnp.where(qpos >= off, off, start)
        s_first = jnp.where(first >= off, off, s_first)
        s_last = jnp.where(last >= off, off, s_last)
        off = off + len_ref[i]
    lo, hi = s_first // key_block, last // key_block + 1
    f0 = jnp.clip((s_last + key_block - 1) // key_block, lo, hi)
    f1 = jnp.clip((first + 1) // key_block, f0, hi)
    return start, lo, f0, f1, hi


def query_ends(i, chunks, half, core):
    first = i * chunks * 2 * half + core * half
    return first, first + (chunks - 1) * 2 * half + half - 1


def spread(packed, low, to_high):
    f = packed.astype(F32)
    other = pltpu.roll(f, 64, 1)
    zero = jnp.zeros_like(f)
    if to_high:
        return jnp.where(low, zero, other).astype(BF16), jnp.where(low, zero, f).astype(BF16)
    return jnp.where(low, f, zero).astype(BF16), jnp.where(low, other, zero).astype(BF16)


def mix_kernel(
    items, chunks, key_block,
    len_ref, core_ref, kv_ref, qp_ref, qpos_ref,
    out_t_ref, lse_ref, out_ref,
    kv_t, qz, acc, m_ref, l_ref,
):
    i = pl.program_id(0)
    half = 2 * qp_ref.shape[1]
    n = chunks * half
    core = core_ref[0]

    @pl.when(i == 0)
    def _():
        for c in range(kv_ref.shape[0] // 512):
            at = slice(c * 512, (c + 1) * 512)
            kv_t[:, at] = kv_ref[at, :].astype(F32).T.astype(BF16)

    low = low_lanes((half // 2, 128))
    for c in range(chunks):
        a, b = spread(qp_ref[c], low, False)
        qz[c * half : c * half + half // 2] = a
        qz[c * half + half // 2 : (c + 1) * half] = b
    qpos = qpos_ref[...] + core * half
    first, last = query_ends(i, chunks, half, core)
    start, lo, f0, f1, hi = block_bounds(len_ref, items, qpos, first, last, key_block)
    acc[...] = jnp.zeros_like(acc)
    m_ref[...] = jnp.full_like(m_ref, MASKED)
    l_ref[...] = jnp.zeros_like(l_ref)

    def step(j, masked):
        at = pl.ds(pl.multiple_of(j * key_block, key_block), key_block)
        s = nt_dot(kv_ref[at, :], qz[...]) * LOG2E
        if masked:
            kpos = j * key_block + lax.broadcasted_iota(jnp.int32, (key_block, 1), 0)
            s = jnp.where((kpos >= start) & (kpos <= qpos), s, MASKED)
        m_old = m_ref[...]
        m_new = jnp.maximum(m_old, jnp.max(s, axis=0, keepdims=True))
        p = jnp.exp2(s - m_new)
        alpha = jnp.exp2(m_old - m_new)
        m_ref[...] = m_new
        l_ref[...] = l_ref[...] * alpha + jnp.sum(p, axis=0, keepdims=True)
        acc[...] = acc[...] * alpha + nn_dot(kv_t[64:, at], p.astype(BF16))

    lax.fori_loop(lo, f0, lambda j, c: (step(j, True), c)[1], 0)
    lax.fori_loop(f0, f1, lambda j, c: (step(j, False), c)[1], 0)
    lax.fori_loop(f1, hi, lambda j, c: (step(j, True), c)[1], 0)
    out_t = acc[...] / l_ref[...]
    out_t_ref[...] = out_t
    lse_ref[...] = m_ref[...] + jnp.log2(l_ref[...])
    doubled = jnp.concatenate([out_t, out_t], axis=0).T
    for c in range(chunks):
        a = doubled[c * half : c * half + half // 2]
        b = doubled[c * half + half // 2 : (c + 1) * half]
        out_ref[c] = jnp.where(low, a, b).astype(BF16)


def mix(lengths, core, kv, qp, qpos, chunks=4, key_block=768):
    total = kv.shape[0]
    n_src, quarter = qp.shape[0], qp.shape[1]
    half = 2 * quarter
    n = chunks * half
    whole = lambda i, *_: (0, 0)
    return pl.pallas_call(
        functools.partial(mix_kernel, lengths.shape[0], chunks, key_block),
        grid_spec=pltpu.PrefetchScalarGridSpec(
            num_scalar_prefetch=2,
            grid=(n_src // chunks,),
            in_specs=[
                pl.BlockSpec((total, 128), whole),
                pl.BlockSpec((chunks, quarter, 128), lambda i, *_: (i, 0, 0)),
                pl.BlockSpec((1, n), lambda i, *_: (0, i)),
            ],
            out_specs=[
                pl.BlockSpec((64, n), lambda i, *_: (0, i)),
                pl.BlockSpec((1, n), lambda i, *_: (0, i)),
                pl.BlockSpec((chunks, quarter, 128), lambda i, *_: (i, 0, 0)),
            ],
            scratch_shapes=[
                pltpu.VMEM((128, total), BF16),
                pltpu.VMEM((n, 128), BF16),
                pltpu.VMEM((64, n), F32),
                pltpu.VMEM((1, n), F32),
                pltpu.VMEM((1, n), F32),
            ],
        ),
        out_shape=[
            jax.ShapeDtypeStruct((64, n_src * half), F32),
            jax.ShapeDtypeStruct((1, n_src * half), F32),
            jax.ShapeDtypeStruct((n_src, quarter, 128), BF16),
        ],
        compiler_params=pltpu.CompilerParams(vmem_limit_bytes=22 << 20),
        cost_estimate=pl.CostEstimate(flops=25_000_000_000, bytes_accessed=8 << 20, transcendentals=0),
        name="mix",
    )(lengths, core, kv, qp, qpos)


def back_kernel(
    items, chunks, key_block,
    len_ref, core_ref, kv_ref, qp_ref, dp_ref, qpos_ref, out_t_ref, lse_ref,
    dkv_ref, dq_ref,
    kv_t, qd, dq_acc,
):
    i = pl.program_id(0)
    half = 2 * qp_ref.shape[1]
    n = chunks * half
    core = core_ref[0]

    @pl.when(i == 0)
    def _():
        for c in range(kv_ref.shape[0] // 512):
            at = slice(c * 512, (c + 1) * 512)
            kv_t[:, at] = kv_ref[at, :].astype(F32).T.astype(BF16)
        dkv_ref[...] = jnp.zeros_like(dkv_ref)

    low = low_lanes((half // 2, 128))
    for c in range(chunks):
        a, b = spread(qp_ref[c], low, False)
        qd[c * half : c * half + half // 2] = a
        qd[c * half + half // 2 : (c + 1) * half] = b
        a, b = spread(dp_ref[c], low, True)
        qd[n + c * half : n + c * half + half // 2] = a
        qd[n + c * half + half // 2 : n + (c + 1) * half] = b
    do_t = qd[n:, :].astype(F32).T[64:]
    delta = jnp.sum(do_t * out_t_ref[...], axis=0, keepdims=True)
    lse = lse_ref[...]
    qpos = qpos_ref[...] + core * half
    first, last = query_ends(i, chunks, half, core)
    start, lo, f0, f1, hi = block_bounds(len_ref, items, qpos, first, last, key_block)
    dq_acc[...] = jnp.zeros_like(dq_acc)

    def step(j, masked):
        at = pl.ds(pl.multiple_of(j * key_block, key_block), key_block)
        both = nt_dot(kv_ref[at, :], qd[...])
        s = both[:, :n] * LOG2E
        if masked:
            kpos = j * key_block + lax.broadcasted_iota(jnp.int32, (key_block, 1), 0)
            s = jnp.where((kpos >= start) & (kpos <= qpos), s, MASKED)
        p = jnp.exp2(s - lse)
        ds = (p * (both[:, n:] - delta)).astype(BF16)
        dq_acc[...] += nn_dot(kv_t[:64, at], ds)
        dkv_ref[at, :] += nn_dot(ds, qd[:n, :]) + nn_dot(p.astype(BF16), qd[n:, :])

    lax.fori_loop(lo, f0, lambda j, c: (step(j, True), c)[1], 0)
    lax.fori_loop(f0, f1, lambda j, c: (step(j, False), c)[1], 0)
    lax.fori_loop(f1, hi, lambda j, c: (step(j, True), c)[1], 0)
    dq_t = dq_acc[...] * 0.125
    doubled = jnp.concatenate([dq_t, dq_t], axis=0).T
    for c in range(chunks):
        a = doubled[c * half : c * half + half // 2]
        b = doubled[c * half + half // 2 : (c + 1) * half]
        dq_ref[c] = jnp.where(low, a, b).astype(BF16)


def mix_back(lengths, core, kv, qp, dp, qpos, out_t, lse, chunks=4, key_block=768):
    total = kv.shape[0]
    n_src, quarter = qp.shape[0], qp.shape[1]
    half = 2 * quarter
    n = chunks * half
    whole = lambda i, *_: (0, 0)
    rows = lambda i, *_: (0, i)
    blocks = pl.BlockSpec((chunks, quarter, 128), lambda i, *_: (i, 0, 0))
    return pl.pallas_call(
        functools.partial(back_kernel, lengths.shape[0], chunks, key_block),
        grid_spec=pltpu.PrefetchScalarGridSpec(
            num_scalar_prefetch=2,
            grid=(n_src // chunks,),
            in_specs=[
                pl.BlockSpec((total, 128), whole),
                blocks,
                blocks,
                pl.BlockSpec((1, n), rows),
                pl.BlockSpec((64, n), rows),
                pl.BlockSpec((1, n), rows),
            ],
            out_specs=[pl.BlockSpec((total, 128), whole), blocks],
            scratch_shapes=[
                pltpu.VMEM((128, total), BF16),
                pltpu.VMEM((2 * n, 128), BF16),
                pltpu.VMEM((64, n), F32),
            ],
        ),
        out_shape=[
            jax.ShapeDtypeStruct((total, 128), F32),
            jax.ShapeDtypeStruct((n_src, quarter, 128), BF16),
        ],
        compiler_params=pltpu.CompilerParams(vmem_limit_bytes=22 << 20),
        cost_estimate=pl.CostEstimate(flops=40_000_000_000, bytes_accessed=8 << 20, transcendentals=0),
        name="mix_back",
    )(lengths, core, kv, qp, dp, qpos, out_t, lse)


def packed_positions(n_src, half):
    j = np.arange(n_src * half)
    return ((j // half) * 2 * half + j % half).astype(np.int32)[None]


def feed_kernel(
    blocks_ref, frames_ref, cot_ref, w_out_ref, gain_ref, w_up_ref, b_up_ref, w_down_ref, b_down_ref,
    out_ref, grad_mid_ref, grad_blocks_ref, hidden_ref, grad_before_ref, act2_ref, mixed_ref, low_ref, attn_ref,
    gain_grad_ref, b_up_grad_ref, b_down_grad_ref,
    mixed, act2, act_grad,
):
    i = pl.program_id(0)
    rows = frames_ref.shape[0]
    quarter = rows // 4
    low_q = low_lanes((quarter, 128))

    @pl.when(i == 0)
    def _():
        for zy in range(8):
            for s in range(2):
                a = blocks_ref[(zy * 2 + s) * 2].astype(F32)
                b = blocks_ref[(zy * 2 + s) * 2 + 1].astype(F32)
                at = slice(zy * 128, (zy + 1) * 128)
                first = 2 * s * quarter
                mixed[first : first + quarter, at] = pair_low(a, b, low_q)
                mixed[first + quarter : first + 2 * quarter, at] = pair_high(a, b, low_q)
        store_halves(mixed_ref, mixed[...])
        middle = frames_ref[...] + nn_dot(mixed[...].astype(BF16), w_out_ref[...])
        r = lax.rsqrt(jnp.mean(middle * middle, axis=-1, keepdims=True) + EPSILON)
        normed = middle * r * gain_ref[...]
        act2[...] = normed.astype(BF16)
        store_halves(act2_ref, normed)
        grad_mid_ref[...] = middle
        out_ref[...] = middle + b_down_ref[...]
        grad_low = cot_ref[...].astype(BF16)
        low_ref[...] = grad_low
        b_down_grad_ref[...] = jnp.sum(grad_low.astype(F32), axis=0, keepdims=True)
        act_grad[...] = jnp.zeros_like(act_grad)

    before = nn_dot(act2[...], w_up_ref[...]) + b_up_ref[...]
    cdf = 0.5 + 0.5 * lax.erf(before * 0.7071067811865476)
    pdf = jnp.exp(-0.5 * before * before) * 0.3989422804014327
    hidden = (before * cdf).astype(BF16)
    step = hidden.shape[1] // 2
    hidden_ref[0] = hidden[:, :step]
    hidden_ref[1] = hidden[:, step:]
    out_ref[...] += nn_dot(hidden, w_down_ref[...])
    grad_before = (nt_dot(low_ref[...], w_down_ref[...]) * (cdf + before * pdf)).astype(BF16)
    grad_before_ref[...] = grad_before
    b_up_grad_ref[...] = jnp.sum(grad_before.astype(F32), axis=0, keepdims=True)
    act_grad[...] += nt_dot(grad_before, w_up_ref[...])

    @pl.when(i == pl.num_programs(0) - 1)
    def _():
        middle = grad_mid_ref[...]
        r = lax.rsqrt(jnp.mean(middle * middle, axis=-1, keepdims=True) + EPSILON)
        n = middle * r
        g = act_grad[...]
        gain_grad_ref[...] = jnp.sum(g * n, axis=0, keepdims=True)
        g = g * gain_ref[...]
        grad_mid = cot_ref[...] + r * (g - n * jnp.mean(g * n, axis=-1, keepdims=True))
        grad_mid_ref[...] = grad_mid
        grad_attn = grad_mid.astype(BF16)
        attn_ref[...] = grad_attn
        grad_mixed = nt_dot(grad_attn, w_out_ref[...])
        for zy in range(8):
            for s in range(2):
                at = slice(zy * 128, (zy + 1) * 128)
                first = 2 * s * quarter
                a = grad_mixed[first : first + quarter, at]
                b = grad_mixed[first + quarter : first + 2 * quarter, at]
                grad_blocks_ref[(zy * 2 + s) * 2] = pair_low(a, b, low_q).astype(BF16)
                grad_blocks_ref[(zy * 2 + s) * 2 + 1] = pair_high(a, b, low_q).astype(BF16)


def feed(blocks, frames, cotangent, w_out, gain, w_up, b_up, w_down, b_down):
    rows, width = frames.shape
    ff = w_up.shape[1]
    steps = 8
    step = ff // steps
    fixed = lambda *shape: pl.BlockSpec(shape, lambda i: (0,) * len(shape))
    columns = lambda *shape: pl.BlockSpec(shape, lambda i: (0,) * (len(shape) - 1) + (i,))
    shape = jax.ShapeDtypeStruct
    return pl.pallas_call(
        feed_kernel,
        grid=(steps,),
        in_specs=[
            fixed(*blocks.shape),
            fixed(rows, width),
            fixed(rows, width),
            fixed(width, width),
            fixed(1, width),
            columns(width, step),
            columns(1, step),
            pl.BlockSpec((step, width), lambda i: (i, 0)),
            fixed(1, width),
        ],
        out_specs=[
            fixed(rows, width),
            fixed(rows, width),
            fixed(*blocks.shape),
            columns(2, rows, step // 2),
            columns(rows, step),
            fixed(2, rows, width // 2),
            fixed(2, rows, width // 2),
            fixed(rows, width),
            fixed(rows, width),
            fixed(1, width),
            columns(1, step),
            fixed(1, width),
        ],
        out_shape=[
            shape((rows, width), F32),
            shape((rows, width), F32),
            shape(blocks.shape, BF16),
            shape((2, rows, ff // 2), BF16),
            shape((rows, ff), BF16),
            shape((2, rows, width // 2), BF16),
            shape((2, rows, width // 2), BF16),
            shape((rows, width), BF16),
            shape((rows, width), BF16),
            shape((1, width), F32),
            shape((1, ff), F32),
            shape((1, width), F32),
        ],
        scratch_shapes=[
            pltpu.VMEM((rows, width), F32),
            pltpu.VMEM((rows, width), BF16),
            pltpu.VMEM((rows, width), F32),
        ],
        compiler_params=pltpu.CompilerParams(vmem_limit_bytes=28 << 20),
        name="feed",
    )(
        blocks, frames, cotangent, w_out, gain.reshape(1, width), w_up, b_up.reshape(1, ff), w_down,
        b_down.reshape(1, width),
    )


MESH = pl.DeviceIdType.MESH
ALL = ("blk", "grp")


def in_hbm(*arrays):
    return [pltpu.with_memory_space_constraint(x, pltpu.HBM) for x in arrays]


def in_vmem(*arrays):
    return [pltpu.with_memory_space_constraint(x, pltpu.VMEM) for x in arrays]


def place(index):
    return {"blk": lax.div(index, 2), "grp": lax.rem(index, 2)}


def head_of(index):
    blk, grp = lax.div(index, 2), lax.rem(index, 2)
    return lax.div(blk, 2) * 2 + grp, lax.rem(blk, 2)


def own_index():
    return lax.axis_index("blk") * 2 + lax.axis_index("grp")


def sibling_of(core):
    return {"blk": lax.axis_index("blk") + 1 - 2 * core, "grp": lax.axis_index("grp")}


def greet_all(me, n):
    barrier = pltpu.get_barrier_semaphore()

    @pl.loop(1, n)
    def _(i):
        pl.semaphore_signal(barrier, inc=1, device_id=place(lax.rem(me + i, n)), device_id_type=MESH)

    pl.semaphore_wait(barrier, n - 1)


def remote(src, dst, send_sem, recv_sem, device):
    return pltpu.make_async_remote_copy(
        src_ref=src, dst_ref=dst, send_sem=send_sem, recv_sem=recv_sem, device_id=device, device_id_type=MESH
    )


def to_heads_kernel(
    n, gain_in, frames_in, wq_in, wk_in, wv_in, kv_out, q_out, halves_out,
    gain, frames, act, halves, wq, wk, wv, kv_own, q_own, send, recv, local, pair,
):
    me = own_index()
    head, core = head_of(me)
    rows, width = frames.shape
    half = rows // 2
    weights = [
        pltpu.make_async_copy(src, dst, local.at[k])
        for k, (src, dst) in enumerate(
            ((gain_in, gain), (frames_in, frames), (wq_in, wq), (wk_in, wk), (wv_in, wv), (halves, halves_out))
        )
    ]
    for copy in weights[:5]:
        copy.start()
    greet_all(me, n)
    weights[0].wait()
    weights[1].wait()
    x = frames[...]
    r = lax.rsqrt(jnp.mean(x * x, axis=-1, keepdims=True) + EPSILON)
    normed = x * r * gain[...]
    act[...] = normed.astype(BF16)
    store_halves(halves, normed)
    weights[5].start()
    for copy in weights[2:5]:
        copy.wait()

    def copies(other, src):
        h, c = head_of(other)
        kv_at = core if src is not me else c
        return (
            remote(kv_own.at[h, c], kv_out.at[src, kv_at], send.at[0, other], recv.at[0, src], place(other)),
            remote(q_own.at[h, c], q_out.at[src], send.at[1, other], recv.at[1, src], place(other)),
        )

    low = low_lanes((rows, 128))
    low_h = low_lanes((half // 2, 128))
    groups = width // 256

    @pl.loop(0, groups)
    def _(i):
        group = lax.rem(lax.div(me, n // groups) + 1 + i, groups)
        columns = pl.ds(pl.multiple_of(group * 256, 256), 256)
        q = nn_dot(act[...], wq[:, columns]).astype(BF16).astype(F32) * 0.125
        k = nn_dot(act[...], wk[:, columns])
        v = nn_dot(act[...], wv[:, columns])
        for p in range(2):
            at = slice(p * 128, (p + 1) * 128)
            k2, v2, q2 = k[:, at], v[:, at], q[:, at]
            kv_a = pair_low(k2, v2, low).astype(BF16)
            kv_b = pair_high(k2, v2, low).astype(BF16)
            h = group * 4 + 2 * p
            for s in range(2):
                span = slice(s * half, (s + 1) * half)
                kv_own[h, s] = kv_a[span]
                kv_own[h + 1, s] = kv_b[span]
                top = q2[s * half : s * half + half // 2]
                bot = q2[s * half + half // 2 : (s + 1) * half]
                q_own[h, s] = pair_low(top, bot, low_h).astype(BF16)
                q_own[h + 1, s] = pair_high(top, bot, low_h).astype(BF16)

        @pl.loop(0, n // groups)
        def _(j):
            other = group * (n // groups) + j

            @pl.when(other != me)
            def _():
                for copy in copies(other, me):
                    copy.start()

    kv_out[me, core] = kv_own[head, core]
    q_out[me] = q_own[head, core]

    plane = n // groups
    swaps = []
    for t in range(groups):
        first = pl.multiple_of(lax.rem(lax.div(me, plane) + groups - 1 - t, groups) * plane, plane)

        @pl.loop(0, plane)
        def _(j):
            @pl.when(first + j != me)
            def _():
                for copy in copies(first + j, first + j):
                    copy.wait()

        at = pl.ds(first, plane)
        swap = remote(kv_out.at[at, core], kv_out.at[at, core], pair.at[0, t], pair.at[1, t], sibling_of(core))
        swap.start()
        swaps.append(swap)
    weights[5].wait()
    for swap in swaps:
        swap.wait()


def to_heads(frames, gain, w_query, w_key, w_value, n):
    rows, width = frames.shape
    half = rows // 2
    vmem = pl.BlockSpec(memory_space=pltpu.VMEM)
    hbm = pl.BlockSpec(memory_space=pltpu.HBM)
    return pl.pallas_call(
        functools.partial(to_heads_kernel, n),
        in_specs=[hbm] * 5,
        out_specs=[vmem, vmem, hbm],
        out_shape=[
            jax.ShapeDtypeStruct((n, 2, half, 128), BF16),
            jax.ShapeDtypeStruct((n, half // 2, 128), BF16),
            pltpu.HBM((2, rows, width // 2), BF16),
        ],
        scratch_shapes=[
            pltpu.VMEM((1, width), F32),
            pltpu.VMEM((rows, width), F32),
            pltpu.VMEM((rows, width), BF16),
            pltpu.VMEM((2, rows, width // 2), BF16),
            pltpu.VMEM((width, width), BF16),
            pltpu.VMEM((width, width), BF16),
            pltpu.VMEM((width, width), BF16),
            pltpu.VMEM((width // 64, 2, half, 128), BF16),
            pltpu.VMEM((width // 64, 2, half // 2, 128), BF16),
            pltpu.SemaphoreType.DMA((2, n)),
            pltpu.SemaphoreType.DMA((2, n)),
            pltpu.SemaphoreType.DMA((6,)),
            pltpu.SemaphoreType.DMA((2, 4)),
        ],
        compiler_params=pltpu.CompilerParams(
            collective_id=0, has_side_effects=True, vmem_limit_bytes=16 << 20
        ),
        name="to_heads",
    )(*in_hbm(gain.reshape(1, width), frames, w_query, w_key, w_value))


def exchange_kernel(n, x_in, x_out, send, recv, local):
    me = own_index()
    greet_all(me, n)

    def copy_with(i, src):
        other = lax.rem(me + i, n)
        return remote(x_in.at[other], x_out.at[src], send.at[i], recv.at[src], place(other))

    @pl.loop(1, n)
    def _(i):
        copy_with(i, me).start()

    own = pltpu.make_async_copy(x_in.at[me], x_out.at[me], local)
    own.start()
    own.wait()

    @pl.loop(1, n)
    def _(i):
        copy_with(i, lax.rem(me + i, n)).wait()


def exchange(x, n, collective_id):
    vmem = pl.BlockSpec(memory_space=pltpu.VMEM)
    return pl.pallas_call(
        functools.partial(exchange_kernel, n),
        in_specs=[vmem],
        out_specs=vmem,
        out_shape=pltpu.VMEM(x.shape, x.dtype),
        scratch_shapes=[
            pltpu.SemaphoreType.DMA((n,)),
            pltpu.SemaphoreType.DMA((n,)),
            pltpu.SemaphoreType.DMA,
        ],
        compiler_params=pltpu.CompilerParams(collective_id=collective_id, has_side_effects=True, vmem_limit_bytes=8 << 20),
        name="exchange",
    )(*in_vmem(x))


BITS = {"core": 1, "y": 2, "z0": 4, "z1": 8}


def flipped(x, axis):
    if axis == "x":
        return lax.ppermute(x, "grp", [(0, 1), (1, 0)])
    return lax.ppermute(x, "blk", [(i, i ^ BITS[axis]) for i in range(lax.axis_size("blk"))])


def bit_of(axis):
    if axis == "x":
        return lax.axis_index("grp")
    return lax.rem(lax.div(lax.axis_index("blk"), BITS[axis]), 2)


def across(axis):
    blk, grp = lax.axis_index("blk"), lax.axis_index("grp")
    if axis == "x":
        return {"blk": blk, "grp": 1 - grp}
    bit = BITS[axis]
    return {"blk": blk + bit - 2 * bit * bit_of(axis), "grp": grp}


def tn_dot(a, b):
    return lax.dot_general(a, b, (((0,), (0,)), ((), ())), preferred_element_type=F32)


def share_kernel(
    n, blocks_in, hidden, grad_before, act2, mixed, low, attn,
    blocks_out, keep_a_out, send_a_out, keep_b_out, send_b_out, keep_c_out, send_c_out,
    keep_a, send_a, keep_b, send_b, keep_c, send_c, hidden2, before2, act2_2, mixed2, low2, attn2, tile, send, recv, local, out, pair_send, pair_recv,
):
    me = own_index()
    head, core = head_of(me)
    rows = low.shape[0]
    greet_all(me, n)
    sibling = sibling_of(core)
    theirs = pl.ds(rows, rows)
    pairs = [
        remote(src, dst.at[theirs], pair_send.at[k], pair_recv.at[k], sibling)
        for k, (src, dst) in enumerate(
            (
                (low, low2),
                (hidden.at[1 - core], hidden2),
                (act2.at[1 - core], act2_2),
                (grad_before, before2),
                (mixed.at[1 - core], mixed2),
                (attn, attn2),
            )
        )
    ]
    for copy in pairs:
        copy.start()

    def copy_with(i, src):
        other = lax.rem(me + i, n)
        return remote(blocks_in.at[other], blocks_out.at[src], send.at[i], recv.at[src], place(other))

    @pl.loop(1, n)
    def _(i):
        copy_with(i, me).start()

    own = pltpu.make_async_copy(blocks_in.at[me], blocks_out.at[me], local)
    own.start()
    low2[:rows] = low[...]
    hidden2[:rows] = hidden[core]
    act2_2[:rows] = act2[core]
    before2[:rows] = grad_before[...]
    mixed2[:rows] = mixed[core]
    attn2[:rows] = attn[...]

    x_mine, y_mine, z_mine = bit_of("x"), bit_of("y"), bit_of("z0")

    def put(keep, away, mine, bit, at, row, value):
        @pl.when(mine == bit)
        def _():
            keep[at, row : row + value.shape[0]] = value

        @pl.when(mine != bit)
        def _():
            away[at, row : row + value.shape[0]] = value

    flushes = []

    def flush(src, dst):
        flushes.append(pltpu.make_async_copy(src, dst, out.at[len(flushes)]))
        flushes[-1].start()

    pairs[0].wait()
    pairs[1].wait()

    @pl.loop(0, 8)
    def _(zy):
        columns = pl.ds(pl.multiple_of(zy * 256, 256), 256)
        value = tn_dot(hidden2[:, columns], low2[...]).astype(BF16)
        z1, z0, y = lax.div(zy, 4), lax.rem(lax.div(zy, 2), 2), lax.rem(zy, 2)
        for x in range(2):
            put(keep_a, send_a, x_mine, x, zy, 0, value[x * 128 : x * 128 + 96])
            put(keep_c, send_c, z_mine, z0, (z1 * 2 + y) * 2 + x, 0, value[x * 128 + 96 : (x + 1) * 128])

    def spread_rows(left, right, slab, to_b, row):
        tile[...] = tn_dot(left[...], right[:, slab * 1024 : (slab + 1) * 1024]).astype(BF16)

        @pl.loop(0, 16)
        def _(j):
            value = tile[pl.ds(pl.multiple_of(j * 32, 32), 32)]
            z1, z0 = lax.div(j, 8), lax.rem(lax.div(j, 4), 2)
            y, x = lax.rem(lax.div(j, 2), 2), lax.rem(j, 2)
            if to_b:
                put(keep_b, send_b, y_mine, y, (z1 * 2 + z0) * 2 + x, row, value)
            else:
                put(keep_c, send_c, z_mine, z0, (z1 * 2 + y) * 2 + x, row, value)

    flush(keep_a, keep_a_out)
    flush(send_a, send_a_out)
    pairs[2].wait()
    pairs[3].wait()
    for slab in range(3):
        spread_rows(act2_2, before2, slab, True, 32 * slab)
    flush(keep_b, keep_b_out)
    flush(send_b, send_b_out)
    spread_rows(act2_2, before2, 3, False, 32)
    pairs[4].wait()
    pairs[5].wait()
    spread_rows(mixed2, attn2, 0, False, 64)
    flush(keep_c, keep_c_out)
    flush(send_c, send_c_out)
    own.wait()

    @pl.loop(1, n)
    def _(i):
        copy_with(i, lax.rem(me + i, n)).wait()

    for copy in flushes:
        copy.wait()


def share(blocks, hidden, grad_before, act2, mixed, low, attn, n):
    rows, width = low.shape
    vmem = pl.BlockSpec(memory_space=pltpu.VMEM)
    hbm = pl.BlockSpec(memory_space=pltpu.HBM)
    shape = jax.ShapeDtypeStruct
    return pl.pallas_call(
        functools.partial(share_kernel, n),
        in_specs=[vmem] * 7,
        out_specs=[vmem] + [hbm] * 6,
        out_shape=[pltpu.VMEM(blocks.shape, BF16)] + [pltpu.HBM((8, 96, width), BF16)] * 6,
        scratch_shapes=[
            *[pltpu.VMEM((8, 96, width), BF16)] * 6,
            pltpu.VMEM((2 * rows, hidden.shape[2]), BF16),
            pltpu.VMEM((2 * rows, grad_before.shape[1]), BF16),
            pltpu.VMEM((2 * rows, width // 2), BF16),
            pltpu.VMEM((2 * rows, width // 2), BF16),
            pltpu.VMEM((2 * rows, width), BF16),
            pltpu.VMEM((2 * rows, width), BF16),
            pltpu.VMEM((width // 2, 1024), BF16),
            pltpu.SemaphoreType.DMA((n,)),
            pltpu.SemaphoreType.DMA((n,)),
            pltpu.SemaphoreType.DMA,
            pltpu.SemaphoreType.DMA((6,)),
            pltpu.SemaphoreType.DMA((6,)),
            pltpu.SemaphoreType.DMA((6,)),
        ],
        compiler_params=pltpu.CompilerParams(
            collective_id=3, has_side_effects=True, vmem_limit_bytes=26 << 20
        ),
        name="share",
    )(blocks, hidden, grad_before, act2, mixed, low, attn)


class Part:
    def __init__(self, total, dims, order, landing, send, recv):
        self.view, self.dims, self.order = total, list(dims), list(order)
        self.landing, self.send, self.recv = landing, send, recv
        self.stage, self.copy, self.kept = 0, None, None

    def start(self):
        axis = self.order[self.stage]
        at, mine = self.dims.index(axis), bit_of(axis)
        ahead = (slice(None),) * at
        self.copy = remote(
            self.view.at[ahead + (1 - mine,)],
            self.landing[self.stage],
            self.send.at[self.stage],
            self.recv.at[self.stage],
            across(axis),
        )
        self.copy.start()
        self.kept = self.view.at[ahead + (mine,)]
        self.dims.remove(axis)
        self.stage += 1

    def finish(self):
        self.copy.wait()
        got, kept = self.landing[self.stage - 1], self.kept
        lead = len(self.dims)

        @pl.loop(0, 2**lead)
        def _(k):
            at = tuple(lax.rem(lax.div(k, 2**d), 2) for d in reversed(range(lead)))
            kept[at] = (kept[at].astype(F32) + got[at].astype(F32)).astype(BF16)

        self.view = kept

    def last(self):
        self.copy.wait()
        return self.kept[...].astype(F32) + self.landing[self.stage - 1][...].astype(F32)


def finish_kernel(
    n, dkv_in, dq_in, gain2_grad, b_up_grad, b_down_grad,
    gain_in, act1, frames_in, grad_mid_in, wq_in, wk_in, wv_in, keep_a, keep_b, keep_c, got_a, got_b, got_c,
    frames_out, q_out, k_out, v_out, o_out, up_out, down_out, small_out,
    theirs, total, dkv_all, dq_all, gain, frames, grad_mid, wq, wk, wv, small_in, new_a, new_b, new_c,
    act1_2, qkv2, sum_a, sum_b, sum_c, sum_q, sum_k, sum_v,
    a2, a3, a4, b2, b3, b4, c2, c3, c4,
    q1, q2, q3, q4, k1, k2, k3, k4, v1, v2, v3, v4, small_all,
    early_send, early_recv, send, recv, dq_send, dq_recv, dkv_send, dkv_recv, small_send, small_recv, pair_send, pair_recv, local,
):
    me = own_index()
    head, core = head_of(me)
    rows, width = frames.shape
    quarter = rows // 4
    sums = [sum_a, sum_b, sum_c, sum_q, sum_k, sum_v]
    news = [new_a, new_b, new_c]
    fetches = [
        pltpu.make_async_copy(src, dst, local.at[k])
        for k, (src, dst) in enumerate(
            (
                (keep_a, sum_a), (got_a, new_a), (keep_b, sum_b), (got_b, new_b), (keep_c, sum_c), (got_c, new_c),
                (wq_in, wq), (wk_in, wk), (wv_in, wv), (gain_in, gain), (frames_in, frames), (grad_mid_in, grad_mid),
            )
        )
    ]
    for copy in fetches:
        copy.start()
    greet_all(me, n)
    sibling = sibling_of(core)
    swap = remote(dkv_in.at[:, 1 - core], theirs, pair_send.at[0], pair_recv.at[0], sibling)
    swap.start()
    act1_copy = remote(act1.at[1 - core], act1_2.at[pl.ds(rows, rows)], pair_send.at[1], pair_recv.at[1], sibling)

    def to_all(src_ref, dst_ref, sends, recvs):
        def copy_with(i, src):
            other = lax.rem(me + i, n)
            return remote(src_ref.at[other], dst_ref.at[src], sends.at[i], recvs.at[src], place(other))

        return copy_with

    dq_copy = to_all(dq_in, dq_all, dq_send, dq_recv)
    dkv_copy = to_all(total, dkv_all, dkv_send, dkv_recv)
    small_copy = to_all(small_in, small_all, small_send, small_recv)

    @pl.loop(1, n)
    def _(i):
        dq_copy(i, me).start()

    swap.wait()

    def add(j):
        return (dkv_in[j, core] + theirs[j]).astype(BF16)

    @pl.loop(1, n)
    def _(i):
        other = lax.rem(me + i, n)
        total[other] = add(other)
        dkv_copy(i, me).start()

    dkv_all[me] = add(me)
    dq_all[me] = dq_in[me]
    act1_copy.start()
    order = ("x", "y", "z0", "z1"), ("y", "z0", "x", "z1"), ("z0", "x", "y", "z1")
    landings = (q1, q2, q3, q4), (k1, k2, k3, k4), (v1, v2, v3, v4)
    late = [Part(sums[3 + k], ("z1", "z0", "y", "x"), order[k], landings[k], send.at[k], recv.at[k]) for k in range(3)]
    dims = ("z1", "z0", "y"), ("z1", "z0", "x"), ("z1", "y", "x")
    order = ("y", "z0", "z1"), ("z0", "x", "z1"), ("x", "y", "z1")
    landings = (a2, a3, a4), (b2, b3, b4), (c2, c3, c4)
    waves = []
    for u in range(3):
        band = slice(32 * u, 32 * u + 32)
        wave = []
        for k in range(3):
            wave.append(
                Part(
                    sums[k].at[:, :, :, band],
                    dims[k],
                    order[k],
                    [ref.at[(slice(None),) * lead + (band,)] for lead, ref in zip((2, 1, 0), landings[k])],
                    early_send.at[u, k],
                    early_recv.at[u, k],
                )
            )
        waves.append(wave)

    for u, wave in enumerate(waves):
        for k, part in enumerate(wave):
            whole, new = sums[k], news[k]
            if u == 0:
                fetches[2 * k].wait()
                fetches[2 * k + 1].wait()

            @pl.loop(0, 8)
            def _(j):
                at = (lax.div(j, 4), lax.rem(lax.div(j, 2), 2), lax.rem(j, 2), slice(32 * u, 32 * u + 32))
                whole[at] = (whole[at].astype(F32) + new[at].astype(F32)).astype(BF16)

            part.start()

    def advance(parts):
        for part in parts:
            part.finish()
            part.start()

    act1_own = pltpu.make_async_copy(act1.at[core], act1_2.at[pl.ds(0, rows)], local.at[12])
    act1_own.start()

    @pl.loop(1, n)
    def _(i):
        dq_copy(i, lax.rem(me + i, n)).wait()

    advance(waves[0])
    advance(waves[1])

    @pl.loop(1, n)
    def _(i):
        dkv_copy(i, lax.rem(me + i, n)).wait()

    advance(waves[0])
    advance(waves[2])
    low_q, low_h = low_lanes((quarter, 128)), low_lanes((2 * quarter, 128))
    for zy in range(8):
        for s in range(2):
            j = (zy * 2 + s) * 2
            first = 2 * s * quarter
            a, b = dq_all[j].astype(F32), dq_all[j + 1].astype(F32)
            at = slice(zy * 128, (zy + 1) * 128)
            qkv2[first : first + quarter, at] = pair_low(a, b, low_q).astype(BF16)
            qkv2[first + quarter : first + 2 * quarter, at] = pair_high(a, b, low_q).astype(BF16)
            a, b = dkv_all[j].astype(F32), dkv_all[j + 1].astype(F32)
            at = slice(width + zy * 128, width + (zy + 1) * 128)
            qkv2[first : first + 2 * quarter, at] = pair_low(a, b, low_h).astype(BF16)
            at = slice(2 * width + zy * 128, 2 * width + (zy + 1) * 128)
            qkv2[first : first + 2 * quarter, at] = pair_high(a, b, low_h).astype(BF16)
    pair = remote(qkv2.at[pl.ds(0, rows)], qkv2.at[pl.ds(rows, rows)], pair_send.at[2], pair_recv.at[2], sibling)
    pair.start()
    advance(waves[1])

    for copy in fetches[6:]:
        copy.wait()
    g = nt_dot(qkv2[:rows, :width], wq[...])
    g += nt_dot(qkv2[:rows, width : 2 * width], wk[...])
    g += nt_dot(qkv2[:rows, 2 * width :], wv[...])
    act1_copy.wait()
    act1_own.wait()
    pair.wait()
    for k in range(3):
        value = tn_dot(act1_2[...], qkv2[:, k * width : (k + 1) * width]).astype(BF16)
        for j in range(16):
            sums[3 + k][j // 8, j // 4 % 2, j // 2 % 2, j % 2] = value[j * 32 : (j + 1) * 32]
        late[k].start()

    advance(waves[2])

    x = frames[...]
    r = lax.rsqrt(jnp.mean(x * x, axis=-1, keepdims=True) + EPSILON)
    norm = x * r
    gain_grad = jnp.sum(g * norm, axis=0, keepdims=True)
    small_in[...] = jnp.zeros_like(small_in)
    for d in range(n):
        at = slice(d // 4 * 128, (d // 4 + 1) * 128)
        small_in[d, 0:1] = gain_grad[:, at]
        small_in[d, 1:2] = gain2_grad[:, at]
        small_in[d, 2:3] = b_down_grad[:, at]
        small_in[d, 3:4] = b_up_grad[:, d * 128 : (d + 1) * 128]

    @pl.loop(1, n)
    def _(i):
        small_copy(i, me).start()

    g = g * gain[...]
    frames_out[...] = grad_mid[...] + r * (g - norm * jnp.mean(g * norm, axis=-1, keepdims=True))
    small_all[me] = small_in[me]

    advance(late * 3)

    @pl.loop(1, n)
    def _(i):
        small_copy(i, lax.rem(me + i, n)).wait()

    small_out[...] = jnp.sum(small_all[...], axis=0)
    for u, wave in enumerate(waves):
        down_out[32 * u : 32 * u + 32] = wave[0].last()
        up_out[:, 1024 * u : 1024 * u + 1024] = wave[1].last()
    down_out[96:] = waves[0][2].last()
    up_out[:, 3072:] = waves[1][2].last()
    o_out[...] = waves[2][2].last()
    q_out[...] = late[0].last()
    k_out[...] = late[1].last()
    v_out[...] = late[2].last()


def finish(dkv, dq, act1, frames, grad_mid, gain, gain2_grad, b_up_grad, b_down_grad, weights, keeps, gots, n):
    rows, width = frames.shape
    keeps, gots = [[x.reshape(2, 2, 2, *x.shape[1:]) for x in xs] for xs in (keeps, gots)]
    half = dkv.shape[2]
    vmem = pl.BlockSpec(memory_space=pltpu.VMEM)
    hbm = pl.BlockSpec(memory_space=pltpu.HBM)
    shape = jax.ShapeDtypeStruct
    thin, wide = (32, width), (96, width)
    buffers = [pltpu.VMEM((2, 2, 2, *wide), BF16)] * 3 + [pltpu.VMEM((2, 2, 2, 2, *thin), BF16)] * 3
    buffers += [pltpu.VMEM((2,) * k + wide, BF16) for k in (2, 1, 0)] * 3
    buffers += [pltpu.VMEM((2,) * k + thin, BF16) for k in (3, 2, 1, 0)] * 3
    over_devices = [pltpu.SemaphoreType.DMA((n,))] * 6
    return pl.pallas_call(
        functools.partial(finish_kernel, n),
        in_specs=[vmem] * 5 + [hbm] * 13,
        out_specs=[vmem] * 8,
        out_shape=[pltpu.VMEM((rows, width), F32)]
        + [pltpu.VMEM(thin, F32)] * 4
        + [pltpu.VMEM((32, 4 * width), F32), pltpu.VMEM((128, width), F32), shape((8, 128), F32)],
        scratch_shapes=[
            pltpu.VMEM((n, half, 128), F32),
            pltpu.VMEM((n, half, 128), BF16),
            pltpu.VMEM((n, half, 128), BF16),
            pltpu.VMEM((n, half // 2, 128), BF16),
            pltpu.VMEM((1, width), F32),
            pltpu.VMEM((rows, width), F32),
            pltpu.VMEM((rows, width), F32),
            pltpu.VMEM((width, width), BF16),
            pltpu.VMEM((width, width), BF16),
            pltpu.VMEM((width, width), BF16),
            pltpu.VMEM((n, 8, 128), F32),
            *[pltpu.VMEM((2, 2, 2, *wide), BF16)] * 3,
            pltpu.VMEM((2 * rows, width // 2), BF16),
            pltpu.VMEM((2 * rows, 3 * width), BF16),
            *buffers,
            pltpu.VMEM((n, 8, 128), F32),
            pltpu.SemaphoreType.DMA((3, 3, 3)),
            pltpu.SemaphoreType.DMA((3, 3, 3)),
            pltpu.SemaphoreType.DMA((3, 4)),
            pltpu.SemaphoreType.DMA((3, 4)),
            *over_devices,
            pltpu.SemaphoreType.DMA((3,)),
            pltpu.SemaphoreType.DMA((3,)),
            pltpu.SemaphoreType.DMA((13,)),
        ],
        compiler_params=pltpu.CompilerParams(
            collective_id=4, has_side_effects=True, vmem_limit_bytes=40 << 20
        ),
        name="finish",
    )(
        *in_vmem(dkv, dq), gain2_grad, b_up_grad, b_down_grad,
        *in_hbm(gain.reshape(1, width), act1, frames, grad_mid, *weights, *keeps, *gots),
    )


def emit_kernel(n, *refs):
    sems = refs[-1]
    copies = [pltpu.make_async_copy(refs[k], refs[n + k], sems.at[k]) for k in range(n)]
    for copy in copies:
        copy.start()
    for copy in copies:
        copy.wait()


def emit(*arrays):
    n = len(arrays)
    return pl.pallas_call(
        functools.partial(emit_kernel, n),
        in_specs=[pl.BlockSpec(memory_space=pltpu.VMEM)] * n,
        out_specs=[pl.BlockSpec(memory_space=pltpu.HBM)] * n,
        out_shape=[pltpu.HBM(x.shape, x.dtype) for x in arrays],
        scratch_shapes=[pltpu.SemaphoreType.DMA((n,))],
        compiler_params=pltpu.CompilerParams(vmem_limit_bytes=8 << 20),
        name="emit",
    )(*in_vmem(*arrays))


def shards_heads(
    frames, lengths, norm1_gain, w_query, w_key, w_value, w_out, norm2_gain, w_up, b_up, w_down, b_down, cotangent
):
    rows, width = frames.shape
    n = lax.axis_size("blk") * lax.axis_size("grp")
    half = rows // 2
    core_word = bit_of("core").astype(jnp.int32).reshape(1)
    qpos = jnp.asarray(packed_positions(n, half))

    kv, q, act1 = to_heads(frames, norm1_gain, w_query, w_key, w_value, n)
    kv_rows = kv.reshape(n * rows, 128)
    out_t, lse, out_blocks = mix(lengths, core_word, kv_rows, q, qpos)
    mixed_blocks = exchange(out_blocks, n, 2)
    (
        layer_out, grad_middle, grad_blocks, hidden, grad_before, act2, mixed, grad_low, grad_attn,
        norm2_gain_grad, b_up_grad, b_down_grad,
    ) = feed(mixed_blocks, frames, cotangent, w_out, norm2_gain, w_up, b_up, w_down, b_down)
    grad_blocks, *parts = share(grad_blocks, hidden, grad_before, act2, mixed, grad_low, grad_attn, n)
    keeps = parts[0::2]
    gots = [flipped(part, axis) for part, axis in zip(parts[1::2], ("x", "y", "z0"))]
    dkv, dq = mix_back(lengths, core_word, kv_rows, q, *in_vmem(grad_blocks), qpos, out_t, lse)

    frames_grad, w_query_grad, w_key_grad, w_value_grad, w_out_grad, w_up_grad, w_down_grad, small = finish(
        dkv.reshape(n, 2, half, 128), dq, act1, frames, grad_middle, norm1_gain, norm2_gain_grad, b_up_grad,
        b_down_grad, (w_query, w_key, w_value), keeps, gots, n,
    )
    (
        layer_out, frames_grad, w_query_grad, w_key_grad, w_value_grad, w_out_grad, w_up_grad, w_down_grad
    ) = emit(
        layer_out, frames_grad, w_query_grad, w_key_grad, w_value_grad, w_out_grad, w_up_grad, w_down_grad
    )
    part = width // n
    turn = lax.rem(own_index(), 128 // part) * part
    vectors = lax.dynamic_slice(small, (0, turn), (3, part))
    return (
        layer_out,
        frames_grad,
        vectors[0],
        w_query_grad,
        w_key_grad,
        w_value_grad,
        w_out_grad,
        vectors[1],
        w_up_grad,
        small[3],
        w_down_grad,
        vectors[2],
    )


def solution(mesh):
    if mesh.shape["blk"] != 16 or mesh.shape["grp"] != 2:
        return solution_ring(mesh)
    split = P(ALL, None)
    return jax.shard_map(
        shards_heads,
        mesh=mesh,
        in_specs=(split, P(), P(), P(), P(), P(), P(), P(), P(), P(), P(), P(), split),
        out_specs=(split, split, P(ALL), split, split, split, split, P(ALL), split, P(ALL), split, P(ALL)),
        check_vma=False,
    )
```

```python
import functools

import jax
import jax.numpy as jnp
import numpy as np
from jax import lax
from jax.experimental import pallas as pl
from jax.experimental.pallas import tpu as pltpu
from jax.sharding import PartitionSpec as P

HEAD_DIM = 64
ITEM_MAX = 4096


EPSILON = 1e-05
MASKED = -1e30
SCALING = 0.125


def shortened(array):

    def short(part):
        return part.astype(jnp.bfloat16) if part.dtype == jnp.float32 else part

    return jax.tree.map(short, array)


def passed_along(block, axis, distance):
    devices = range(lax.axis_size(axis))
    route = [(i - distance, i) for i in devices if i - distance in devices]
    return lax.ppermute(block, axis, route)


def rms_norm(values, gain):
    return values * lax.rsqrt(jnp.mean(values * values, axis=-1, keepdims=True) + EPSILON) * gain


def gelu_exact(values):
    return jax.nn.gelu(values, approximate=False)


def item_starts(lengths, positions):
    ends = jnp.cumsum(lengths)
    offsets = ends - lengths
    before = offsets[None, :] <= positions[:, None]
    return jnp.max(jnp.where(before, offsets[None, :], 0), axis=1)


def live_mask(query_pos, query_start, key_first, key_count):
    key_pos = key_first + jnp.arange(key_count, dtype=jnp.int32)
    return (key_pos[None, :] >= query_start[:, None]) & (key_pos[None, :] <= query_pos[:, None])


def split_heads(matrix):
    return matrix.reshape(matrix.shape[0], matrix.shape[1] // HEAD_DIM, HEAD_DIM)


def merge_heads(tensor):
    return tensor.reshape(tensor.shape[0], tensor.shape[1] * tensor.shape[2])


def scores_of(queries3, keys_block, mask):
    raw = jnp.einsum(
        "qhd,khd->hqk", queries3, split_heads(keys_block), preferred_element_type=jnp.float32
    )
    return jnp.where(mask[None], raw * SCALING, MASKED)


def left_dot(left, right):
    return lax.dot_general(
        left, right, (((0,), (0,)), ((), ())), preferred_element_type=jnp.float32
    )


def right_dot(left, right):
    return lax.dot_general(
        left, right, (((1,), (1,)), ((), ())), preferred_element_type=jnp.float32
    )


def grad_parts(queries3, grad_out3, log_total, delta, keys_block, values_block, mask):
    probs = jnp.exp(scores_of(queries3, keys_block, mask) - log_total[:, :, None])
    grad_probs = jnp.einsum(
        "qhd,khd->hqk", grad_out3, split_heads(values_block), preferred_element_type=jnp.float32
    )
    grad_scores = (probs * (grad_probs - delta[:, :, None])).astype(jnp.bfloat16)
    return (probs.astype(jnp.bfloat16), grad_scores)


def key_terms(queries3, grad_out3, probs_low, grad_scores):
    grad_keys = jnp.einsum(
        "hqk,qhd->khd", grad_scores, queries3, preferred_element_type=jnp.float32
    )
    grad_values = jnp.einsum(
        "hqk,qhd->khd", probs_low, grad_out3, preferred_element_type=jnp.float32
    )
    return (merge_heads(grad_keys), merge_heads(grad_values))


def query_term(grad_scores, keys_block):
    return jnp.einsum(
        "hqk,khd->qhd", grad_scores, split_heads(keys_block), preferred_element_type=jnp.float32
    )


def shards_ring(
    frames,
    lengths,
    norm1_gain,
    w_query,
    w_key,
    w_value,
    w_out,
    norm2_gain,
    w_up,
    b_up,
    w_down,
    b_down,
    cotangent,
):
    row_count = frames.shape[0]
    width = frames.shape[1]
    heads = width // HEAD_DIM
    groups = lax.axis_size("grp")
    block_rows = row_count * groups
    span = (ITEM_MAX + block_rows - 2) // block_rows
    blk_index = lax.axis_index("blk")
    sub_index = lax.axis_index("grp")
    block_first = blk_index * block_rows
    query_pos = block_first + sub_index * row_count + jnp.arange(row_count, dtype=jnp.int32)
    query_start = item_starts(lengths, query_pos)
    back_steps = jnp.arange(span + 1, dtype=jnp.int32)
    normed1, norm1_back = jax.vjp(rms_norm, frames, norm1_gain)
    act1 = normed1.astype(jnp.bfloat16)
    queries = jnp.dot(act1, w_query, preferred_element_type=jnp.float32).astype(jnp.bfloat16)
    keys_own = jnp.dot(act1, w_key, preferred_element_type=jnp.float32).astype(jnp.bfloat16)
    values_own = jnp.dot(act1, w_value, preferred_element_type=jnp.float32).astype(jnp.bfloat16)
    queries3 = split_heads(queries)
    block_keys, block_values = (
        lax.all_gather(keys_own, "grp", axis=0, tiled=True),
        lax.all_gather(values_own, "grp", axis=0, tiled=True),
    )

    def cycle_step(carry, unused_input):
        moved = jax.tree.map(
            lambda part, own: part.astype(own.dtype),
            passed_along(shortened(carry), "blk", 1),
            carry,
        )
        return (moved, moved)

    unused_last, far_blocks = lax.scan(cycle_step, (block_keys, block_values), None, length=span)
    keys_all = jnp.concatenate([block_keys[None], far_blocks[0]], axis=0)
    values_all = jnp.concatenate([block_values[None], far_blocks[1]], axis=0)

    def mask_for(back):
        return live_mask(query_pos, query_start, block_first - back * block_rows, block_rows)

    def total_step(carry, inputs):
        run_max, run_sum = carry
        keys_block, back = inputs
        scores = scores_of(queries3, keys_block, mask_for(back))
        new_max = jnp.maximum(run_max, jnp.max(scores, axis=-1))
        run_sum = run_sum * jnp.exp(run_max - new_max) + jnp.sum(
            jnp.exp(scores - new_max[:, :, None]), axis=-1
        )
        return ((new_max, run_sum), None)

    start_max = jnp.full((heads, row_count), MASKED, jnp.float32)
    start_sum = jnp.zeros((heads, row_count), jnp.float32)
    (top_max, top_sum), unused_out = lax.scan(
        total_step, (start_max, start_sum), (keys_all, back_steps)
    )
    log_total = top_max + jnp.log(top_sum)

    def mix_step(total, inputs):
        keys_block, values_block, back = inputs
        probs = jnp.exp(
            scores_of(queries3, keys_block, mask_for(back)) - log_total[:, :, None]
        ).astype(jnp.bfloat16)
        return (
            total
            + jnp.einsum(
                "hqk,khd->qhd", probs, split_heads(values_block), preferred_element_type=jnp.float32
            ),
            None,
        )

    zero_query = jnp.zeros((row_count, heads, HEAD_DIM), jnp.float32)
    mixed_sum, unused_out = lax.scan(mix_step, zero_query, (keys_all, values_all, back_steps))
    mixed = merge_heads(mixed_sum).astype(jnp.bfloat16)
    middle = frames + jnp.dot(mixed, w_out, preferred_element_type=jnp.float32)
    normed2, norm2_back = jax.vjp(rms_norm, middle, norm2_gain)
    act2 = normed2.astype(jnp.bfloat16)
    before = jnp.dot(act2, w_up, preferred_element_type=jnp.float32) + b_up
    activated, gelu_back = jax.vjp(gelu_exact, before)
    hidden = activated.astype(jnp.bfloat16)
    layer_out = middle + jnp.dot(hidden, w_down, preferred_element_type=jnp.float32) + b_down
    grad_low = cotangent.astype(jnp.bfloat16)
    b_down_grad = jnp.sum(grad_low.astype(jnp.float32), axis=0)
    w_down_grad = left_dot(hidden, grad_low)
    grad_before = gelu_back(right_dot(grad_low, w_down))[0].astype(jnp.bfloat16)
    b_up_grad = jnp.sum(grad_before.astype(jnp.float32), axis=0)
    w_up_grad = left_dot(act2, grad_before)
    grad_mid_norm, norm2_gain_grad = norm2_back(right_dot(grad_before, w_up))
    grad_middle = cotangent + grad_mid_norm
    grad_attn = grad_middle.astype(jnp.bfloat16)
    w_out_grad = left_dot(mixed, grad_attn)
    grad_mixed = right_dot(grad_attn, w_out).astype(jnp.bfloat16)
    grad_out3 = split_heads(grad_mixed)

    def delta_step(total, inputs):
        keys_block, values_block, back = inputs
        probs = jnp.exp(scores_of(queries3, keys_block, mask_for(back)) - log_total[:, :, None])
        grad_probs = jnp.einsum(
            "qhd,khd->hqk", grad_out3, split_heads(values_block), preferred_element_type=jnp.float32
        )
        return (total + jnp.sum(probs * grad_probs, axis=-1), None)

    delta, unused_out = lax.scan(
        delta_step, jnp.zeros((heads, row_count), jnp.float32), (keys_all, values_all, back_steps)
    )
    zero_block = jnp.zeros((block_rows, width), jnp.float32)

    def return_step(carry, inputs):
        grad_q, travel = carry
        keys_block, values_block, back = inputs
        probs_low, grad_scores = grad_parts(
            queries3, grad_out3, log_total, delta, keys_block, values_block, mask_for(back)
        )
        grad_keys, grad_values = key_terms(queries3, grad_out3, probs_low, grad_scores)
        moved = (
            passed_along((travel[0] + grad_keys).astype(jnp.bfloat16), "blk", -1).astype(
                jnp.float32
            ),
            passed_along((travel[1] + grad_values).astype(jnp.bfloat16), "blk", -1).astype(
                jnp.float32
            ),
        )
        return ((grad_q + query_term(grad_scores, keys_block), moved), None)

    (grad_q, travel), unused_out = lax.scan(
        return_step,
        (zero_query, (zero_block, zero_block)),
        (far_blocks[0], far_blocks[1], back_steps[1:]),
        reverse=True,
    )
    probs_low, grad_scores = grad_parts(
        queries3, grad_out3, log_total, delta, block_keys, block_values, mask_for(0)
    )
    grad_keys, grad_values = key_terms(queries3, grad_out3, probs_low, grad_scores)
    grad_q = grad_q + query_term(grad_scores, block_keys)
    block_grad_keys = travel[0] + grad_keys
    block_grad_values = travel[1] + grad_values
    grad_keys_rows, grad_values_rows = (
        lax.psum_scatter(
            block_grad_keys.astype(jnp.bfloat16), "grp", scatter_dimension=0, tiled=True
        ).astype(jnp.float32),
        lax.psum_scatter(
            block_grad_values.astype(jnp.bfloat16), "grp", scatter_dimension=0, tiled=True
        ).astype(jnp.float32),
    )
    grad_keys_low = (grad_keys_rows * SCALING).astype(jnp.bfloat16)
    grad_values_low = grad_values_rows.astype(jnp.bfloat16)
    grad_queries_low = (merge_heads(grad_q) * SCALING).astype(jnp.bfloat16)
    w_query_grad = left_dot(act1, grad_queries_low)
    w_key_grad = left_dot(act1, grad_keys_low)
    w_value_grad = left_dot(act1, grad_values_low)
    grad_act1 = (
        right_dot(grad_queries_low, w_query)
        + right_dot(grad_keys_low, w_key)
        + right_dot(grad_values_low, w_value)
    )
    grad_frames_norm, norm1_gain_grad = norm1_back(grad_act1)
    frames_grad = grad_middle + grad_frames_norm
    shares = (
        lax.psum_scatter(norm1_gain_grad, ("blk", "grp"), scatter_dimension=0, tiled=True),
        lax.psum_scatter(w_query_grad, ("blk", "grp"), scatter_dimension=0, tiled=True),
        lax.psum_scatter(w_key_grad, ("blk", "grp"), scatter_dimension=0, tiled=True),
        lax.psum_scatter(w_value_grad, ("blk", "grp"), scatter_dimension=0, tiled=True),
        lax.psum_scatter(w_out_grad, ("blk", "grp"), scatter_dimension=0, tiled=True),
        lax.psum_scatter(norm2_gain_grad, ("blk", "grp"), scatter_dimension=0, tiled=True),
        lax.psum_scatter(w_up_grad, ("blk", "grp"), scatter_dimension=0, tiled=True),
        lax.psum_scatter(b_up_grad, ("blk", "grp"), scatter_dimension=0, tiled=True),
        lax.psum_scatter(w_down_grad, ("blk", "grp"), scatter_dimension=0, tiled=True),
        lax.psum_scatter(b_down_grad, ("blk", "grp"), scatter_dimension=0, tiled=True),
    )
    return (
        layer_out,
        frames_grad,
        shares[0],
        shares[1],
        shares[2],
        shares[3],
        shares[4],
        shares[5],
        shares[6],
        shares[7],
        shares[8],
        shares[9],
    )


def solution_ring(mesh):
    placed = (
        P(("blk", "grp"), None),
        P(),
        P(),
        P(),
        P(),
        P(),
        P(),
        P(),
        P(),
        P(),
        P(),
        P(),
        P(("blk", "grp"), None),
    )
    return jax.shard_map(
        shards_ring,
        mesh=mesh,
        in_specs=placed,
        out_specs=(
            P(("blk", "grp"), None),
            P(("blk", "grp"), None),
            P(("blk", "grp")),
            P(("blk", "grp"), None),
            P(("blk", "grp"), None),
            P(("blk", "grp"), None),
            P(("blk", "grp"), None),
            P(("blk", "grp")),
            P(("blk", "grp"), None),
            P(("blk", "grp")),
            P(("blk", "grp"), None),
            P(("blk", "grp")),
        ),
        check_vma=False,
    )


LOG2E = 1.4426950408889634
F32, BF16 = jnp.float32, jnp.bfloat16


def nt_dot(a, b):
    return lax.dot_general(a, b, (((1,), (1,)), ((), ())), preferred_element_type=F32)


def nn_dot(a, b):
    return lax.dot_general(a, b, (((1,), (0,)), ((), ())), preferred_element_type=F32)


def low_lanes(shape):
    return lax.broadcasted_iota(jnp.int32, shape, 1) < 64


def pair_low(a, b, low):
    return jnp.where(low, a, pltpu.roll(b, 64, 1))


def pair_high(a, b, low):
    return jnp.where(low, pltpu.roll(a, 64, 1), b)


def store_halves(ref, x):
    low = low_lanes((x.shape[0], 128))
    for p in range(x.shape[1] // 256):
        a, b = x[:, p * 256 : p * 256 + 128], x[:, p * 256 + 128 : (p + 1) * 256]
        ref[0, :, p * 128 : (p + 1) * 128] = pair_low(a, b, low).astype(BF16)
        ref[1, :, p * 128 : (p + 1) * 128] = pair_high(a, b, low).astype(BF16)


def block_bounds(len_ref, items, qpos, first, last, key_block):
    off = jnp.int32(0)
    start = jnp.zeros(qpos.shape, jnp.int32)
    s_first, s_last = jnp.int32(0), jnp.int32(0)
    for i in range(items):
        start = jnp.where(qpos >= off, off, start)
        s_first = jnp.where(first >= off, off, s_first)
        s_last = jnp.where(last >= off, off, s_last)
        off = off + len_ref[i]
    lo, hi = s_first // key_block, last // key_block + 1
    f0 = jnp.clip((s_last + key_block - 1) // key_block, lo, hi)
    f1 = jnp.clip((first + 1) // key_block, f0, hi)
    return start, lo, f0, f1, hi


def query_ends(i, chunks, half, core):
    first = i * chunks * 2 * half + core * half
    return first, first + (chunks - 1) * 2 * half + half - 1


def spread(packed, low, to_high):
    f = packed.astype(F32)
    other = pltpu.roll(f, 64, 1)
    zero = jnp.zeros_like(f)
    if to_high:
        return jnp.where(low, zero, other).astype(BF16), jnp.where(low, zero, f).astype(BF16)
    return jnp.where(low, f, zero).astype(BF16), jnp.where(low, other, zero).astype(BF16)


def mix_kernel(
    items, chunks, key_block,
    len_ref, core_ref, kv_ref, qp_ref, qpos_ref,
    out_t_ref, lse_ref, out_ref,
    kv_t, qz, acc, m_ref, l_ref,
):
    i = pl.program_id(0)
    half = 2 * qp_ref.shape[1]
    n = chunks * half
    core = core_ref[0]

    @pl.when(i == 0)
    def _():
        for c in range(kv_ref.shape[0] // 512):
            at = slice(c * 512, (c + 1) * 512)
            kv_t[:, at] = kv_ref[at, :].astype(F32).T.astype(BF16)

    low = low_lanes((half // 2, 128))
    for c in range(chunks):
        a, b = spread(qp_ref[c], low, False)
        qz[c * half : c * half + half // 2] = a
        qz[c * half + half // 2 : (c + 1) * half] = b
    qpos = qpos_ref[...] + core * half
    first, last = query_ends(i, chunks, half, core)
    start, lo, f0, f1, hi = block_bounds(len_ref, items, qpos, first, last, key_block)
    acc[...] = jnp.zeros_like(acc)
    m_ref[...] = jnp.full_like(m_ref, MASKED)
    l_ref[...] = jnp.zeros_like(l_ref)

    def step(j, masked):
        at = pl.ds(pl.multiple_of(j * key_block, key_block), key_block)
        s = nt_dot(kv_ref[at, :], qz[...]) * LOG2E
        if masked:
            kpos = j * key_block + lax.broadcasted_iota(jnp.int32, (key_block, 1), 0)
            s = jnp.where((kpos >= start) & (kpos <= qpos), s, MASKED)
        m_old = m_ref[...]
        m_new = jnp.maximum(m_old, jnp.max(s, axis=0, keepdims=True))
        p = jnp.exp2(s - m_new)
        alpha = jnp.exp2(m_old - m_new)
        m_ref[...] = m_new
        l_ref[...] = l_ref[...] * alpha + jnp.sum(p, axis=0, keepdims=True)
        acc[...] = acc[...] * alpha + nn_dot(kv_t[64:, at], p.astype(BF16))

    lax.fori_loop(lo, f0, lambda j, c: (step(j, True), c)[1], 0)
    lax.fori_loop(f0, f1, lambda j, c: (step(j, False), c)[1], 0)
    lax.fori_loop(f1, hi, lambda j, c: (step(j, True), c)[1], 0)
    out_t = acc[...] / l_ref[...]
    out_t_ref[...] = out_t
    lse_ref[...] = m_ref[...] + jnp.log2(l_ref[...])
    doubled = jnp.concatenate([out_t, out_t], axis=0).T
    for c in range(chunks):
        a = doubled[c * half : c * half + half // 2]
        b = doubled[c * half + half // 2 : (c + 1) * half]
        out_ref[c] = jnp.where(low, a, b).astype(BF16)


def mix(lengths, core, kv, qp, qpos, chunks=4, key_block=768):
    total = kv.shape[0]
    n_src, quarter = qp.shape[0], qp.shape[1]
    half = 2 * quarter
    n = chunks * half
    whole = lambda i, *_: (0, 0)
    return pl.pallas_call(
        functools.partial(mix_kernel, lengths.shape[0], chunks, key_block),
        grid_spec=pltpu.PrefetchScalarGridSpec(
            num_scalar_prefetch=2,
            grid=(n_src // chunks,),
            in_specs=[
                pl.BlockSpec((total, 128), whole),
                pl.BlockSpec((chunks, quarter, 128), lambda i, *_: (i, 0, 0)),
                pl.BlockSpec((1, n), lambda i, *_: (0, i)),
            ],
            out_specs=[
                pl.BlockSpec((64, n), lambda i, *_: (0, i)),
                pl.BlockSpec((1, n), lambda i, *_: (0, i)),
                pl.BlockSpec((chunks, quarter, 128), lambda i, *_: (i, 0, 0)),
            ],
            scratch_shapes=[
                pltpu.VMEM((128, total), BF16),
                pltpu.VMEM((n, 128), BF16),
                pltpu.VMEM((64, n), F32),
                pltpu.VMEM((1, n), F32),
                pltpu.VMEM((1, n), F32),
            ],
        ),
        out_shape=[
            jax.ShapeDtypeStruct((64, n_src * half), F32),
            jax.ShapeDtypeStruct((1, n_src * half), F32),
            jax.ShapeDtypeStruct((n_src, quarter, 128), BF16),
        ],
        compiler_params=pltpu.CompilerParams(vmem_limit_bytes=22 << 20),
        cost_estimate=pl.CostEstimate(flops=25_000_000_000, bytes_accessed=8 << 20, transcendentals=0),
        name="mix",
    )(lengths, core, kv, qp, qpos)


def back_kernel(
    items, chunks, key_block,
    len_ref, core_ref, kv_ref, qp_ref, dp_ref, qpos_ref, out_t_ref, lse_ref,
    dkv_ref, dq_ref,
    kv_t, qd, dq_acc,
):
    i = pl.program_id(0)
    half = 2 * qp_ref.shape[1]
    n = chunks * half
    core = core_ref[0]

    @pl.when(i == 0)
    def _():
        for c in range(kv_ref.shape[0] // 512):
            at = slice(c * 512, (c + 1) * 512)
            kv_t[:, at] = kv_ref[at, :].astype(F32).T.astype(BF16)
        dkv_ref[...] = jnp.zeros_like(dkv_ref)

    low = low_lanes((half // 2, 128))
    for c in range(chunks):
        a, b = spread(qp_ref[c], low, False)
        qd[c * half : c * half + half // 2] = a
        qd[c * half + half // 2 : (c + 1) * half] = b
        a, b = spread(dp_ref[c], low, True)
        qd[n + c * half : n + c * half + half // 2] = a
        qd[n + c * half + half // 2 : n + (c + 1) * half] = b
    do_t = qd[n:, :].astype(F32).T[64:]
    delta = jnp.sum(do_t * out_t_ref[...], axis=0, keepdims=True)
    lse = lse_ref[...]
    qpos = qpos_ref[...] + core * half
    first, last = query_ends(i, chunks, half, core)
    start, lo, f0, f1, hi = block_bounds(len_ref, items, qpos, first, last, key_block)
    dq_acc[...] = jnp.zeros_like(dq_acc)

    def step(j, masked):
        at = pl.ds(pl.multiple_of(j * key_block, key_block), key_block)
        both = nt_dot(kv_ref[at, :], qd[...])
        s = both[:, :n] * LOG2E
        if masked:
            kpos = j * key_block + lax.broadcasted_iota(jnp.int32, (key_block, 1), 0)
            s = jnp.where((kpos >= start) & (kpos <= qpos), s, MASKED)
        p = jnp.exp2(s - lse)
        ds = (p * (both[:, n:] - delta)).astype(BF16)
        dq_acc[...] += nn_dot(kv_t[:64, at], ds)
        dkv_ref[at, :] += nn_dot(ds, qd[:n, :]) + nn_dot(p.astype(BF16), qd[n:, :])

    lax.fori_loop(lo, f0, lambda j, c: (step(j, True), c)[1], 0)
    lax.fori_loop(f0, f1, lambda j, c: (step(j, False), c)[1], 0)
    lax.fori_loop(f1, hi, lambda j, c: (step(j, True), c)[1], 0)
    dq_t = dq_acc[...] * 0.125
    doubled = jnp.concatenate([dq_t, dq_t], axis=0).T
    for c in range(chunks):
        a = doubled[c * half : c * half + half // 2]
        b = doubled[c * half + half // 2 : (c + 1) * half]
        dq_ref[c] = jnp.where(low, a, b).astype(BF16)


def mix_back(lengths, core, kv, qp, dp, qpos, out_t, lse, chunks=4, key_block=768):
    total = kv.shape[0]
    n_src, quarter = qp.shape[0], qp.shape[1]
    half = 2 * quarter
    n = chunks * half
    whole = lambda i, *_: (0, 0)
    rows = lambda i, *_: (0, i)
    blocks = pl.BlockSpec((chunks, quarter, 128), lambda i, *_: (i, 0, 0))
    return pl.pallas_call(
        functools.partial(back_kernel, lengths.shape[0], chunks, key_block),
        grid_spec=pltpu.PrefetchScalarGridSpec(
            num_scalar_prefetch=2,
            grid=(n_src // chunks,),
            in_specs=[
                pl.BlockSpec((total, 128), whole),
                blocks,
                blocks,
                pl.BlockSpec((1, n), rows),
                pl.BlockSpec((64, n), rows),
                pl.BlockSpec((1, n), rows),
            ],
            out_specs=[pl.BlockSpec((total, 128), whole), blocks],
            scratch_shapes=[
                pltpu.VMEM((128, total), BF16),
                pltpu.VMEM((2 * n, 128), BF16),
                pltpu.VMEM((64, n), F32),
            ],
        ),
        out_shape=[
            jax.ShapeDtypeStruct((total, 128), F32),
            jax.ShapeDtypeStruct((n_src, quarter, 128), BF16),
        ],
        compiler_params=pltpu.CompilerParams(vmem_limit_bytes=22 << 20),
        cost_estimate=pl.CostEstimate(flops=40_000_000_000, bytes_accessed=8 << 20, transcendentals=0),
        name="mix_back",
    )(lengths, core, kv, qp, dp, qpos, out_t, lse)


def packed_positions(n_src, half):
    j = np.arange(n_src * half)
    return ((j // half) * 2 * half + j % half).astype(np.int32)[None]


def feed_kernel(
    blocks_ref, frames_ref, cot_ref, w_out_ref, gain_ref, w_up_ref, b_up_ref, w_down_ref, b_down_ref,
    out_ref, grad_mid_ref, grad_blocks_ref, hidden_ref, grad_before_ref, act2_ref, mixed_ref, low_ref, attn_ref,
    gain_grad_ref, b_up_grad_ref, b_down_grad_ref,
    mixed, act2, act_grad,
):
    i = pl.program_id(0)
    rows = frames_ref.shape[0]
    quarter = rows // 4
    low_q = low_lanes((quarter, 128))

    @pl.when(i == 0)
    def _():
        for zy in range(8):
            for s in range(2):
                a = blocks_ref[(zy * 2 + s) * 2].astype(F32)
                b = blocks_ref[(zy * 2 + s) * 2 + 1].astype(F32)
                at = slice(zy * 128, (zy + 1) * 128)
                first = 2 * s * quarter
                mixed[first : first + quarter, at] = pair_low(a, b, low_q)
                mixed[first + quarter : first + 2 * quarter, at] = pair_high(a, b, low_q)
        store_halves(mixed_ref, mixed[...])
        middle = frames_ref[...] + nn_dot(mixed[...].astype(BF16), w_out_ref[...])
        r = lax.rsqrt(jnp.mean(middle * middle, axis=-1, keepdims=True) + EPSILON)
        normed = middle * r * gain_ref[...]
        act2[...] = normed.astype(BF16)
        store_halves(act2_ref, normed)
        grad_mid_ref[...] = middle
        out_ref[...] = middle + b_down_ref[...]
        grad_low = cot_ref[...].astype(BF16)
        low_ref[...] = grad_low
        b_down_grad_ref[...] = jnp.sum(grad_low.astype(F32), axis=0, keepdims=True)
        act_grad[...] = jnp.zeros_like(act_grad)

    before = nn_dot(act2[...], w_up_ref[...]) + b_up_ref[...]
    cdf = 0.5 + 0.5 * lax.erf(before * 0.7071067811865476)
    pdf = jnp.exp(-0.5 * before * before) * 0.3989422804014327
    hidden = (before * cdf).astype(BF16)
    step = hidden.shape[1] // 2
    hidden_ref[0] = hidden[:, :step]
    hidden_ref[1] = hidden[:, step:]
    out_ref[...] += nn_dot(hidden, w_down_ref[...])
    grad_before = (nt_dot(low_ref[...], w_down_ref[...]) * (cdf + before * pdf)).astype(BF16)
    grad_before_ref[...] = grad_before
    b_up_grad_ref[...] = jnp.sum(grad_before.astype(F32), axis=0, keepdims=True)
    act_grad[...] += nt_dot(grad_before, w_up_ref[...])

    @pl.when(i == pl.num_programs(0) - 1)
    def _():
        middle = grad_mid_ref[...]
        r = lax.rsqrt(jnp.mean(middle * middle, axis=-1, keepdims=True) + EPSILON)
        n = middle * r
        g = act_grad[...]
        gain_grad_ref[...] = jnp.sum(g * n, axis=0, keepdims=True)
        g = g * gain_ref[...]
        grad_mid = cot_ref[...] + r * (g - n * jnp.mean(g * n, axis=-1, keepdims=True))
        grad_mid_ref[...] = grad_mid
        grad_attn = grad_mid.astype(BF16)
        attn_ref[...] = grad_attn
        grad_mixed = nt_dot(grad_attn, w_out_ref[...])
        for zy in range(8):
            for s in range(2):
                at = slice(zy * 128, (zy + 1) * 128)
                first = 2 * s * quarter
                a = grad_mixed[first : first + quarter, at]
                b = grad_mixed[first + quarter : first + 2 * quarter, at]
                grad_blocks_ref[(zy * 2 + s) * 2] = pair_low(a, b, low_q).astype(BF16)
                grad_blocks_ref[(zy * 2 + s) * 2 + 1] = pair_high(a, b, low_q).astype(BF16)


def feed(blocks, frames, cotangent, w_out, gain, w_up, b_up, w_down, b_down):
    rows, width = frames.shape
    ff = w_up.shape[1]
    steps = 8
    step = ff // steps
    fixed = lambda *shape: pl.BlockSpec(shape, lambda i: (0,) * len(shape))
    columns = lambda *shape: pl.BlockSpec(shape, lambda i: (0,) * (len(shape) - 1) + (i,))
    shape = jax.ShapeDtypeStruct
    return pl.pallas_call(
        feed_kernel,
        grid=(steps,),
        in_specs=[
            fixed(*blocks.shape),
            fixed(rows, width),
            fixed(rows, width),
            fixed(width, width),
            fixed(1, width),
            columns(width, step),
            columns(1, step),
            pl.BlockSpec((step, width), lambda i: (i, 0)),
            fixed(1, width),
        ],
        out_specs=[
            fixed(rows, width),
            fixed(rows, width),
            fixed(*blocks.shape),
            columns(2, rows, step // 2),
            columns(rows, step),
            fixed(2, rows, width // 2),
            fixed(2, rows, width // 2),
            fixed(rows, width),
            fixed(rows, width),
            fixed(1, width),
            columns(1, step),
            fixed(1, width),
        ],
        out_shape=[
            shape((rows, width), F32),
            shape((rows, width), F32),
            shape(blocks.shape, BF16),
            shape((2, rows, ff // 2), BF16),
            shape((rows, ff), BF16),
            shape((2, rows, width // 2), BF16),
            shape((2, rows, width // 2), BF16),
            shape((rows, width), BF16),
            shape((rows, width), BF16),
            shape((1, width), F32),
            shape((1, ff), F32),
            shape((1, width), F32),
        ],
        scratch_shapes=[
            pltpu.VMEM((rows, width), F32),
            pltpu.VMEM((rows, width), BF16),
            pltpu.VMEM((rows, width), F32),
        ],
        compiler_params=pltpu.CompilerParams(vmem_limit_bytes=28 << 20),
        name="feed",
    )(
        blocks, frames, cotangent, w_out, gain.reshape(1, width), w_up, b_up.reshape(1, ff), w_down,
        b_down.reshape(1, width),
    )


MESH = pl.DeviceIdType.MESH
ALL = ("blk", "grp")


def in_hbm(*arrays):
    return [pltpu.with_memory_space_constraint(x, pltpu.HBM) for x in arrays]


def in_vmem(*arrays):
    return [pltpu.with_memory_space_constraint(x, pltpu.VMEM) for x in arrays]


def place(index):
    return {"blk": lax.div(index, 2), "grp": lax.rem(index, 2)}


def head_of(index):
    blk, grp = lax.div(index, 2), lax.rem(index, 2)
    return lax.div(blk, 2) * 2 + grp, lax.rem(blk, 2)


def own_index():
    return lax.axis_index("blk") * 2 + lax.axis_index("grp")


def sibling_of(core):
    return {"blk": lax.axis_index("blk") + 1 - 2 * core, "grp": lax.axis_index("grp")}


def greet_all(me, n):
    barrier = pltpu.get_barrier_semaphore()

    @pl.loop(1, n)
    def _(i):
        pl.semaphore_signal(barrier, inc=1, device_id=place(lax.rem(me + i, n)), device_id_type=MESH)

    pl.semaphore_wait(barrier, n - 1)


def remote(src, dst, send_sem, recv_sem, device):
    return pltpu.make_async_remote_copy(
        src_ref=src, dst_ref=dst, send_sem=send_sem, recv_sem=recv_sem, device_id=device, device_id_type=MESH
    )


def to_heads_kernel(
    n, gain_in, frames_in, wq_in, wk_in, wv_in, kv_out, q_out, halves_out,
    gain, frames, act, halves, wq, wk, wv, kv_own, q_own, send, recv, local, fetched, pair,
):
    me = own_index()
    head, core = head_of(me)
    rows, width = frames.shape
    half = rows // 2
    weights = [
        pltpu.make_async_copy(src, dst, local.at[k])
        for k, (src, dst) in enumerate(
            ((gain_in, gain), (frames_in, frames), (halves, halves_out))
        )
    ]
    groups = width // 256

    def group_at(i):
        return lax.rem(lax.div(me, n // groups) + 1 + i, groups)

    def fetch(group):
        columns = pl.ds(pl.multiple_of(group * 256, 256), 256)
        return [
            pltpu.make_async_copy(src.at[:, columns], dst.at[:, columns], fetched.at[k, group])
            for k, (src, dst) in enumerate(((wq_in, wq), (wk_in, wk), (wv_in, wv)))
        ]

    for copy in weights[:2]:
        copy.start()

    @pl.loop(0, groups)
    def _(i):
        for copy in fetch(group_at(i)):
            copy.start()

    greet_all(me, n)
    weights[0].wait()
    weights[1].wait()
    x = frames[...]
    r = lax.rsqrt(jnp.mean(x * x, axis=-1, keepdims=True) + EPSILON)
    normed = x * r * gain[...]
    act[...] = normed.astype(BF16)
    store_halves(halves, normed)
    weights[2].start()

    def copies(other, src):
        h, c = head_of(other)
        kv_at = core if src is not me else c
        return (
            remote(kv_own.at[h, c], kv_out.at[src, kv_at], send.at[0, other], recv.at[0, src], place(other)),
            remote(q_own.at[h, c], q_out.at[src], send.at[1, other], recv.at[1, src], place(other)),
        )

    low = low_lanes((rows, 128))
    low_h = low_lanes((half // 2, 128))

    @pl.loop(0, groups)
    def _(i):
        group = group_at(i)
        for copy in fetch(group):
            copy.wait()
        columns = pl.ds(pl.multiple_of(group * 256, 256), 256)
        q = nn_dot(act[...], wq[:, columns]).astype(BF16).astype(F32) * 0.125
        k = nn_dot(act[...], wk[:, columns])
        v = nn_dot(act[...], wv[:, columns])
        for p in range(2):
            at = slice(p * 128, (p + 1) * 128)
            k2, v2, q2 = k[:, at], v[:, at], q[:, at]
            kv_a = pair_low(k2, v2, low).astype(BF16)
            kv_b = pair_high(k2, v2, low).astype(BF16)
            h = group * 4 + 2 * p
            for s in range(2):
                span = slice(s * half, (s + 1) * half)
                kv_own[h, s] = kv_a[span]
                kv_own[h + 1, s] = kv_b[span]
                top = q2[s * half : s * half + half // 2]
                bot = q2[s * half + half // 2 : (s + 1) * half]
                q_own[h, s] = pair_low(top, bot, low_h).astype(BF16)
                q_own[h + 1, s] = pair_high(top, bot, low_h).astype(BF16)

        @pl.loop(0, n // groups)
        def _(j):
            other = group * (n // groups) + j

            @pl.when(other != me)
            def _():
                for copy in copies(other, me):
                    copy.start()

    kv_out[me, core] = kv_own[head, core]
    q_out[me] = q_own[head, core]

    plane = n // groups
    swaps = []
    for t in range(groups):
        first = pl.multiple_of(lax.rem(lax.div(me, plane) + groups - 1 - t, groups) * plane, plane)

        @pl.loop(0, plane)
        def _(j):
            @pl.when(first + j != me)
            def _():
                for copy in copies(first + j, first + j):
                    copy.wait()

        at = pl.ds(first, plane)
        swap = remote(kv_out.at[at, core], kv_out.at[at, core], pair.at[0, t], pair.at[1, t], sibling_of(core))
        swap.start()
        swaps.append(swap)
    weights[2].wait()
    for swap in swaps:
        swap.wait()


def to_heads(frames, gain, w_query, w_key, w_value, n):
    rows, width = frames.shape
    half = rows // 2
    vmem = pl.BlockSpec(memory_space=pltpu.VMEM)
    hbm = pl.BlockSpec(memory_space=pltpu.HBM)
    return pl.pallas_call(
        functools.partial(to_heads_kernel, n),
        in_specs=[hbm] * 5,
        out_specs=[vmem, vmem, hbm],
        out_shape=[
            jax.ShapeDtypeStruct((n, 2, half, 128), BF16),
            jax.ShapeDtypeStruct((n, half // 2, 128), BF16),
            pltpu.HBM((2, rows, width // 2), BF16),
        ],
        scratch_shapes=[
            pltpu.VMEM((1, width), F32),
            pltpu.VMEM((rows, width), F32),
            pltpu.VMEM((rows, width), BF16),
            pltpu.VMEM((2, rows, width // 2), BF16),
            pltpu.VMEM((width, width), BF16),
            pltpu.VMEM((width, width), BF16),
            pltpu.VMEM((width, width), BF16),
            pltpu.VMEM((width // 64, 2, half, 128), BF16),
            pltpu.VMEM((width // 64, 2, half // 2, 128), BF16),
            pltpu.SemaphoreType.DMA((2, n)),
            pltpu.SemaphoreType.DMA((2, n)),
            pltpu.SemaphoreType.DMA((3,)),
            pltpu.SemaphoreType.DMA((3, 4)),
            pltpu.SemaphoreType.DMA((2, 4)),
        ],
        compiler_params=pltpu.CompilerParams(
            collective_id=0, has_side_effects=True, vmem_limit_bytes=16 << 20
        ),
        name="to_heads",
    )(*in_hbm(gain.reshape(1, width), frames, w_query, w_key, w_value))


def exchange_kernel(n, x_in, x_out, send, recv, local):
    me = own_index()
    greet_all(me, n)

    def copy_with(i, src):
        other = lax.rem(me + i, n)
        return remote(x_in.at[other], x_out.at[src], send.at[i], recv.at[src], place(other))

    @pl.loop(1, n)
    def _(i):
        copy_with(i, me).start()

    own = pltpu.make_async_copy(x_in.at[me], x_out.at[me], local)
    own.start()
    own.wait()

    @pl.loop(1, n)
    def _(i):
        copy_with(i, lax.rem(me + i, n)).wait()


def exchange(x, n, collective_id):
    vmem = pl.BlockSpec(memory_space=pltpu.VMEM)
    return pl.pallas_call(
        functools.partial(exchange_kernel, n),
        in_specs=[vmem],
        out_specs=vmem,
        out_shape=pltpu.VMEM(x.shape, x.dtype),
        scratch_shapes=[
            pltpu.SemaphoreType.DMA((n,)),
            pltpu.SemaphoreType.DMA((n,)),
            pltpu.SemaphoreType.DMA,
        ],
        compiler_params=pltpu.CompilerParams(collective_id=collective_id, has_side_effects=True, vmem_limit_bytes=8 << 20),
        name="exchange",
    )(*in_vmem(x))


BITS = {"core": 1, "y": 2, "z0": 4, "z1": 8}


def flipped(x, axis):
    if axis == "x":
        return lax.ppermute(x, "grp", [(0, 1), (1, 0)])
    return lax.ppermute(x, "blk", [(i, i ^ BITS[axis]) for i in range(lax.axis_size("blk"))])


def bit_of(axis):
    if axis == "x":
        return lax.axis_index("grp")
    return lax.rem(lax.div(lax.axis_index("blk"), BITS[axis]), 2)


def across(axis):
    blk, grp = lax.axis_index("blk"), lax.axis_index("grp")
    if axis == "x":
        return {"blk": blk, "grp": 1 - grp}
    bit = BITS[axis]
    return {"blk": blk + bit - 2 * bit * bit_of(axis), "grp": grp}


def tn_dot(a, b):
    return lax.dot_general(a, b, (((0,), (0,)), ((), ())), preferred_element_type=F32)


def share_kernel(
    n, blocks_in, hidden, grad_before, act2, mixed, low, attn,
    blocks_out, keep_a_out, send_a_out, keep_b_out, send_b_out, keep_c_out, send_c_out,
    keep_a, send_a, keep_b, send_b, keep_c, send_c, hidden2, before2, act2_2, mixed2, low2, attn2, tile, send, recv, local, out, pair_send, pair_recv,
):
    me = own_index()
    head, core = head_of(me)
    rows = low.shape[0]
    greet_all(me, n)
    sibling = sibling_of(core)
    theirs = pl.ds(rows, rows)
    pairs = [
        remote(src, dst.at[theirs], pair_send.at[k], pair_recv.at[k], sibling)
        for k, (src, dst) in enumerate(
            (
                (low, low2),
                (hidden.at[1 - core], hidden2),
                (act2.at[1 - core], act2_2),
                (grad_before, before2),
                (mixed.at[1 - core], mixed2),
                (attn, attn2),
            )
        )
    ]
    for copy in pairs:
        copy.start()

    def copy_with(i, src):
        other = lax.rem(me + i, n)
        return remote(blocks_in.at[other], blocks_out.at[src], send.at[i], recv.at[src], place(other))

    @pl.loop(1, n)
    def _(i):
        copy_with(i, me).start()

    own = pltpu.make_async_copy(blocks_in.at[me], blocks_out.at[me], local)
    own.start()
    low2[:rows] = low[...]
    hidden2[:rows] = hidden[core]
    act2_2[:rows] = act2[core]
    before2[:rows] = grad_before[...]
    mixed2[:rows] = mixed[core]
    attn2[:rows] = attn[...]

    x_mine, y_mine, z_mine = bit_of("x"), bit_of("y"), bit_of("z0")

    def put(keep, away, mine, bit, at, row, value):
        @pl.when(mine == bit)
        def _():
            keep[at, row : row + value.shape[0]] = value

        @pl.when(mine != bit)
        def _():
            away[at, row : row + value.shape[0]] = value

    flushes = []

    def flush(src, dst):
        flushes.append(pltpu.make_async_copy(src, dst, out.at[len(flushes)]))
        flushes[-1].start()

    pairs[0].wait()
    pairs[1].wait()

    @pl.loop(0, 8)
    def _(zy):
        columns = pl.ds(pl.multiple_of(zy * 256, 256), 256)
        value = tn_dot(hidden2[:, columns], low2[...]).astype(BF16)
        z1, z0, y = lax.div(zy, 4), lax.rem(lax.div(zy, 2), 2), lax.rem(zy, 2)
        for x in range(2):
            put(keep_a, send_a, x_mine, x, zy, 0, value[x * 128 : x * 128 + 96])
            put(keep_c, send_c, z_mine, z0, (z1 * 2 + y) * 2 + x, 0, value[x * 128 + 96 : (x + 1) * 128])

    def spread_rows(left, right, slab, to_b, row):
        tile[...] = tn_dot(left[...], right[:, slab * 1024 : (slab + 1) * 1024]).astype(BF16)

        @pl.loop(0, 16)
        def _(j):
            value = tile[pl.ds(pl.multiple_of(j * 32, 32), 32)]
            z1, z0 = lax.div(j, 8), lax.rem(lax.div(j, 4), 2)
            y, x = lax.rem(lax.div(j, 2), 2), lax.rem(j, 2)
            if to_b:
                put(keep_b, send_b, y_mine, y, (z1 * 2 + z0) * 2 + x, row, value)
            else:
                put(keep_c, send_c, z_mine, z0, (z1 * 2 + y) * 2 + x, row, value)

    flush(keep_a, keep_a_out)
    flush(send_a, send_a_out)
    pairs[2].wait()
    pairs[3].wait()
    for slab in range(3):
        spread_rows(act2_2, before2, slab, True, 32 * slab)
    flush(keep_b, keep_b_out)
    flush(send_b, send_b_out)
    spread_rows(act2_2, before2, 3, False, 32)
    pairs[4].wait()
    pairs[5].wait()
    spread_rows(mixed2, attn2, 0, False, 64)
    flush(keep_c, keep_c_out)
    flush(send_c, send_c_out)
    own.wait()

    @pl.loop(1, n)
    def _(i):
        copy_with(i, lax.rem(me + i, n)).wait()

    for copy in flushes:
        copy.wait()


def share(blocks, hidden, grad_before, act2, mixed, low, attn, n):
    rows, width = low.shape
    vmem = pl.BlockSpec(memory_space=pltpu.VMEM)
    hbm = pl.BlockSpec(memory_space=pltpu.HBM)
    shape = jax.ShapeDtypeStruct
    return pl.pallas_call(
        functools.partial(share_kernel, n),
        in_specs=[vmem] * 7,
        out_specs=[vmem] + [hbm] * 6,
        out_shape=[pltpu.VMEM(blocks.shape, BF16)] + [pltpu.HBM((8, 96, width), BF16)] * 6,
        scratch_shapes=[
            *[pltpu.VMEM((8, 96, width), BF16)] * 6,
            pltpu.VMEM((2 * rows, hidden.shape[2]), BF16),
            pltpu.VMEM((2 * rows, grad_before.shape[1]), BF16),
            pltpu.VMEM((2 * rows, width // 2), BF16),
            pltpu.VMEM((2 * rows, width // 2), BF16),
            pltpu.VMEM((2 * rows, width), BF16),
            pltpu.VMEM((2 * rows, width), BF16),
            pltpu.VMEM((width // 2, 1024), BF16),
            pltpu.SemaphoreType.DMA((n,)),
            pltpu.SemaphoreType.DMA((n,)),
            pltpu.SemaphoreType.DMA,
            pltpu.SemaphoreType.DMA((6,)),
            pltpu.SemaphoreType.DMA((6,)),
            pltpu.SemaphoreType.DMA((6,)),
        ],
        compiler_params=pltpu.CompilerParams(
            collective_id=3, has_side_effects=True, vmem_limit_bytes=26 << 20
        ),
        name="share",
    )(blocks, hidden, grad_before, act2, mixed, low, attn)


class Part:
    def __init__(self, total, dims, order, landing, send, recv):
        self.view, self.dims, self.order = total, list(dims), list(order)
        self.landing, self.send, self.recv = landing, send, recv
        self.stage, self.copy, self.kept = 0, None, None

    def start(self):
        axis = self.order[self.stage]
        at, mine = self.dims.index(axis), bit_of(axis)
        ahead = (slice(None),) * at
        self.copy = remote(
            self.view.at[ahead + (1 - mine,)],
            self.landing[self.stage],
            self.send.at[self.stage],
            self.recv.at[self.stage],
            across(axis),
        )
        self.copy.start()
        self.kept = self.view.at[ahead + (mine,)]
        self.dims.remove(axis)
        self.stage += 1

    def finish(self):
        self.copy.wait()
        got, kept = self.landing[self.stage - 1], self.kept
        lead = len(self.dims)

        @pl.loop(0, 2**lead)
        def _(k):
            at = tuple(lax.rem(lax.div(k, 2**d), 2) for d in reversed(range(lead)))
            kept[at] = (kept[at].astype(F32) + got[at].astype(F32)).astype(BF16)

        self.view = kept

    def last(self):
        self.copy.wait()
        return self.kept[...].astype(F32) + self.landing[self.stage - 1][...].astype(F32)


def finish_kernel(
    n, dkv_in, dq_in, gain2_grad, b_up_grad, b_down_grad,
    gain_in, act1, frames_in, grad_mid_in, wq_in, wk_in, wv_in, keep_a, keep_b, keep_c, got_a, got_b, got_c,
    frames_out, q_out, k_out, v_out, o_out, up_out, down_out, small_out,
    theirs, total, dkv_all, dq_all, gain, frames, grad_mid, wq, wk, wv, small_in, new_a, new_b, new_c,
    act1_2, qkv2, sum_a, sum_b, sum_c, sum_q, sum_k, sum_v,
    a2, a3, a4, b2, b3, b4, c2, c3, c4,
    q1, q2, q3, q4, k1, k2, k3, k4, v1, v2, v3, v4, small_all,
    early_send, early_recv, send, recv, dq_send, dq_recv, dkv_send, dkv_recv, small_send, small_recv, pair_send, pair_recv, local,
):
    me = own_index()
    head, core = head_of(me)
    rows, width = frames.shape
    quarter = rows // 4
    sums = [sum_a, sum_b, sum_c, sum_q, sum_k, sum_v]
    news = [new_a, new_b, new_c]
    fetches = [
        pltpu.make_async_copy(src, dst, local.at[k])
        for k, (src, dst) in enumerate(
            (
                (keep_a, sum_a), (got_a, new_a), (keep_b, sum_b), (got_b, new_b), (keep_c, sum_c), (got_c, new_c),
                (wq_in, wq), (wk_in, wk), (wv_in, wv), (gain_in, gain), (frames_in, frames), (grad_mid_in, grad_mid),
            )
        )
    ]
    for copy in fetches:
        copy.start()
    greet_all(me, n)
    sibling = sibling_of(core)
    swap = remote(dkv_in.at[:, 1 - core], theirs, pair_send.at[0], pair_recv.at[0], sibling)
    swap.start()
    act1_copy = remote(act1.at[1 - core], act1_2.at[pl.ds(rows, rows)], pair_send.at[1], pair_recv.at[1], sibling)

    def to_all(src_ref, dst_ref, sends, recvs):
        def copy_with(i, src):
            other = lax.rem(me + i, n)
            return remote(src_ref.at[other], dst_ref.at[src], sends.at[i], recvs.at[src], place(other))

        return copy_with

    dq_copy = to_all(dq_in, dq_all, dq_send, dq_recv)
    dkv_copy = to_all(total, dkv_all, dkv_send, dkv_recv)
    small_copy = to_all(small_in, small_all, small_send, small_recv)

    @pl.loop(1, n)
    def _(i):
        dq_copy(i, me).start()

    swap.wait()

    def add(j):
        return (dkv_in[j, core] + theirs[j]).astype(BF16)

    @pl.loop(1, n)
    def _(i):
        other = lax.rem(me + i, n)
        total[other] = add(other)
        dkv_copy(i, me).start()

    dkv_all[me] = add(me)
    dq_all[me] = dq_in[me]
    act1_copy.start()
    order = ("x", "y", "z0", "z1"), ("y", "x", "z0", "z1"), ("z0", "x", "y", "z1")
    landings = (q1, q2, q3, q4), (k1, k2, k3, k4), (v1, v2, v3, v4)
    late = [Part(sums[3 + k], ("z1", "z0", "y", "x"), order[k], landings[k], send.at[k], recv.at[k]) for k in range(3)]
    dims = ("z1", "z0", "y"), ("z1", "z0", "x"), ("z1", "y", "x")
    order = (
        (("y", "z0", "z1"),) * 3,
        (("x", "z0", "z1"), ("x", "z0", "z1"), ("z0", "x", "z1")),
        (("y", "x", "z1"), ("x", "y", "z1"), ("x", "y", "z1")),
    )
    landings = (a2, a3, a4), (b2, b3, b4), (c2, c3, c4)
    waves = []
    for u in range(3):
        band = slice(32 * u, 32 * u + 32)
        wave = []
        for k in range(3):
            wave.append(
                Part(
                    sums[k].at[:, :, :, band],
                    dims[k],
                    order[k][u],
                    [ref.at[(slice(None),) * lead + (band,)] for lead, ref in zip((2, 1, 0), landings[k])],
                    early_send.at[u, k],
                    early_recv.at[u, k],
                )
            )
        waves.append(wave)

    for u, wave in enumerate(waves):
        for k, part in enumerate(wave):
            whole, new = sums[k], news[k]
            if u == 0:
                fetches[2 * k].wait()
                fetches[2 * k + 1].wait()

            @pl.loop(0, 8)
            def _(j):
                at = (lax.div(j, 4), lax.rem(lax.div(j, 2), 2), lax.rem(j, 2), slice(32 * u, 32 * u + 32))
                whole[at] = (whole[at].astype(F32) + new[at].astype(F32)).astype(BF16)

            part.start()

    def advance(parts):
        for part in parts:
            part.finish()
            part.start()

    act1_own = pltpu.make_async_copy(act1.at[core], act1_2.at[pl.ds(0, rows)], local.at[12])
    act1_own.start()

    @pl.loop(1, n)
    def _(i):
        dq_copy(i, lax.rem(me + i, n)).wait()

    advance(waves[0])
    advance(waves[1])

    @pl.loop(1, n)
    def _(i):
        dkv_copy(i, lax.rem(me + i, n)).wait()

    advance(waves[0])
    advance(waves[2])
    def pair_with(k):
        columns = slice(k * width, (k + 1) * width)
        own, other = qkv2.at[pl.ds(0, rows), columns], qkv2.at[pl.ds(rows, rows), columns]
        return remote(own, other, pair_send.at[2 + k], pair_recv.at[2 + k], sibling)

    pairs = [pair_with(k) for k in range(3)]
    low_q, low_h = low_lanes((quarter, 128)), low_lanes((2 * quarter, 128))
    for zy in range(8):
        for s in range(2):
            j = (zy * 2 + s) * 2
            first = 2 * s * quarter
            a, b = dq_all[j].astype(F32), dq_all[j + 1].astype(F32)
            at = slice(zy * 128, (zy + 1) * 128)
            qkv2[first : first + quarter, at] = pair_low(a, b, low_q).astype(BF16)
            qkv2[first + quarter : first + 2 * quarter, at] = pair_high(a, b, low_q).astype(BF16)
    pairs[0].start()
    for zy in range(8):
        for s in range(2):
            j = (zy * 2 + s) * 2
            first = 2 * s * quarter
            a, b = dkv_all[j].astype(F32), dkv_all[j + 1].astype(F32)
            at = slice(width + zy * 128, width + (zy + 1) * 128)
            qkv2[first : first + 2 * quarter, at] = pair_low(a, b, low_h).astype(BF16)
            at = slice(2 * width + zy * 128, 2 * width + (zy + 1) * 128)
            qkv2[first : first + 2 * quarter, at] = pair_high(a, b, low_h).astype(BF16)
    pairs[1].start()
    pairs[2].start()
    advance(waves[1])
    act1_copy.wait()
    act1_own.wait()
    for k in range(3):
        pairs[k].wait()
        value = tn_dot(act1_2[...], qkv2[:, k * width : (k + 1) * width]).astype(BF16)
        for j in range(16):
            sums[3 + k][j // 8, j // 4 % 2, j // 2 % 2, j % 2] = value[j * 32 : (j + 1) * 32]
        late[k].start()

    for copy in fetches[6:]:
        copy.wait()
    g = nt_dot(qkv2[:rows, :width], wq[...])
    g += nt_dot(qkv2[:rows, width : 2 * width], wk[...])
    g += nt_dot(qkv2[:rows, 2 * width :], wv[...])
    advance(waves[2])

    x = frames[...]
    r = lax.rsqrt(jnp.mean(x * x, axis=-1, keepdims=True) + EPSILON)
    norm = x * r
    gain_grad = jnp.sum(g * norm, axis=0, keepdims=True)
    small_in[...] = jnp.zeros_like(small_in)
    for d in range(n):
        at = slice(d // 4 * 128, (d // 4 + 1) * 128)
        small_in[d, 0:1] = gain_grad[:, at]
        small_in[d, 1:2] = gain2_grad[:, at]
        small_in[d, 2:3] = b_down_grad[:, at]
        small_in[d, 3:4] = b_up_grad[:, d * 128 : (d + 1) * 128]

    @pl.loop(1, n)
    def _(i):
        small_copy(i, me).start()

    g = g * gain[...]
    frames_out[...] = grad_mid[...] + r * (g - norm * jnp.mean(g * norm, axis=-1, keepdims=True))
    small_all[me] = small_in[me]

    advance(late * 3)

    @pl.loop(1, n)
    def _(i):
        small_copy(i, lax.rem(me + i, n)).wait()

    small_out[...] = jnp.sum(small_all[...], axis=0)
    for u, wave in enumerate(waves):
        down_out[32 * u : 32 * u + 32] = wave[0].last()
        up_out[:, 1024 * u : 1024 * u + 1024] = wave[1].last()
    down_out[96:] = waves[0][2].last()
    up_out[:, 3072:] = waves[1][2].last()
    o_out[...] = waves[2][2].last()
    q_out[...] = late[0].last()
    k_out[...] = late[1].last()
    v_out[...] = late[2].last()


def finish(dkv, dq, act1, frames, grad_mid, gain, gain2_grad, b_up_grad, b_down_grad, weights, keeps, gots, n):
    rows, width = frames.shape
    keeps, gots = [[x.reshape(2, 2, 2, *x.shape[1:]) for x in xs] for xs in (keeps, gots)]
    half = dkv.shape[2]
    vmem = pl.BlockSpec(memory_space=pltpu.VMEM)
    hbm = pl.BlockSpec(memory_space=pltpu.HBM)
    shape = jax.ShapeDtypeStruct
    thin, wide = (32, width), (96, width)
    buffers = [pltpu.VMEM((2, 2, 2, *wide), BF16)] * 3 + [pltpu.VMEM((2, 2, 2, 2, *thin), BF16)] * 3
    buffers += [pltpu.VMEM((2,) * k + wide, BF16) for k in (2, 1, 0)] * 3
    buffers += [pltpu.VMEM((2,) * k + thin, BF16) for k in (3, 2, 1, 0)] * 3
    over_devices = [pltpu.SemaphoreType.DMA((n,))] * 6
    return pl.pallas_call(
        functools.partial(finish_kernel, n),
        in_specs=[vmem] * 5 + [hbm] * 13,
        out_specs=[vmem] * 8,
        out_shape=[pltpu.VMEM((rows, width), F32)]
        + [pltpu.VMEM(thin, F32)] * 4
        + [pltpu.VMEM((32, 4 * width), F32), pltpu.VMEM((128, width), F32), shape((8, 128), F32)],
        scratch_shapes=[
            pltpu.VMEM((n, half, 128), F32),
            pltpu.VMEM((n, half, 128), BF16),
            pltpu.VMEM((n, half, 128), BF16),
            pltpu.VMEM((n, half // 2, 128), BF16),
            pltpu.VMEM((1, width), F32),
            pltpu.VMEM((rows, width), F32),
            pltpu.VMEM((rows, width), F32),
            pltpu.VMEM((width, width), BF16),
            pltpu.VMEM((width, width), BF16),
            pltpu.VMEM((width, width), BF16),
            pltpu.VMEM((n, 8, 128), F32),
            *[pltpu.VMEM((2, 2, 2, *wide), BF16)] * 3,
            pltpu.VMEM((2 * rows, width // 2), BF16),
            pltpu.VMEM((2 * rows, 3 * width), BF16),
            *buffers,
            pltpu.VMEM((n, 8, 128), F32),
            pltpu.SemaphoreType.DMA((3, 3, 3)),
            pltpu.SemaphoreType.DMA((3, 3, 3)),
            pltpu.SemaphoreType.DMA((3, 4)),
            pltpu.SemaphoreType.DMA((3, 4)),
            *over_devices,
            pltpu.SemaphoreType.DMA((5,)),
            pltpu.SemaphoreType.DMA((5,)),
            pltpu.SemaphoreType.DMA((13,)),
        ],
        compiler_params=pltpu.CompilerParams(
            collective_id=4, has_side_effects=True, vmem_limit_bytes=40 << 20
        ),
        name="finish",
    )(
        *in_vmem(dkv, dq), gain2_grad, b_up_grad, b_down_grad,
        *in_hbm(gain.reshape(1, width), act1, frames, grad_mid, *weights, *keeps, *gots),
    )


def emit_kernel(n, *refs):
    sems = refs[-1]
    copies = [pltpu.make_async_copy(refs[k], refs[n + k], sems.at[k]) for k in range(n)]
    for copy in copies:
        copy.start()
    for copy in copies:
        copy.wait()


def emit(*arrays):
    n = len(arrays)
    return pl.pallas_call(
        functools.partial(emit_kernel, n),
        in_specs=[pl.BlockSpec(memory_space=pltpu.VMEM)] * n,
        out_specs=[pl.BlockSpec(memory_space=pltpu.HBM)] * n,
        out_shape=[pltpu.HBM(x.shape, x.dtype) for x in arrays],
        scratch_shapes=[pltpu.SemaphoreType.DMA((n,))],
        compiler_params=pltpu.CompilerParams(vmem_limit_bytes=8 << 20),
        name="emit",
    )(*in_vmem(*arrays))


def shards_heads(
    frames, lengths, norm1_gain, w_query, w_key, w_value, w_out, norm2_gain, w_up, b_up, w_down, b_down, cotangent
):
    rows, width = frames.shape
    n = lax.axis_size("blk") * lax.axis_size("grp")
    half = rows // 2
    core_word = bit_of("core").astype(jnp.int32).reshape(1)
    qpos = jnp.asarray(packed_positions(n, half))

    kv, q, act1 = to_heads(frames, norm1_gain, w_query, w_key, w_value, n)
    kv_rows = kv.reshape(n * rows, 128)
    out_t, lse, out_blocks = mix(lengths, core_word, kv_rows, q, qpos)
    mixed_blocks = exchange(out_blocks, n, 2)
    (
        layer_out, grad_middle, grad_blocks, hidden, grad_before, act2, mixed, grad_low, grad_attn,
        norm2_gain_grad, b_up_grad, b_down_grad,
    ) = feed(mixed_blocks, frames, cotangent, w_out, norm2_gain, w_up, b_up, w_down, b_down)
    grad_blocks, *parts = share(grad_blocks, hidden, grad_before, act2, mixed, grad_low, grad_attn, n)
    keeps = parts[0::2]
    gots = [flipped(part, axis) for part, axis in zip(parts[1::2], ("x", "y", "z0"))]
    dkv, dq = mix_back(lengths, core_word, kv_rows, q, *in_vmem(grad_blocks), qpos, out_t, lse)

    frames_grad, w_query_grad, w_key_grad, w_value_grad, w_out_grad, w_up_grad, w_down_grad, small = finish(
        dkv.reshape(n, 2, half, 128), dq, act1, frames, grad_middle, norm1_gain, norm2_gain_grad, b_up_grad,
        b_down_grad, (w_query, w_key, w_value), keeps, gots, n,
    )
    (
        layer_out, frames_grad, w_query_grad, w_key_grad, w_value_grad, w_out_grad, w_up_grad, w_down_grad
    ) = emit(
        layer_out, frames_grad, w_query_grad, w_key_grad, w_value_grad, w_out_grad, w_up_grad, w_down_grad
    )
    part = width // n
    turn = lax.rem(own_index(), 128 // part) * part
    vectors = lax.dynamic_slice(small, (0, turn), (3, part))
    return (
        layer_out,
        frames_grad,
        vectors[0],
        w_query_grad,
        w_key_grad,
        w_value_grad,
        w_out_grad,
        vectors[1],
        w_up_grad,
        small[3],
        w_down_grad,
        vectors[2],
    )


def solution(mesh):
    if mesh.shape["blk"] != 16 or mesh.shape["grp"] != 2:
        return solution_ring(mesh)
    split = P(ALL, None)
    return jax.shard_map(
        shards_heads,
        mesh=mesh,
        in_specs=(split, P(), P(), P(), P(), P(), P(), P(), P(), P(), P(), P(), split),
        out_specs=(split, split, P(ALL), split, split, split, split, P(ALL), split, P(ALL), split, P(ALL)),
        check_vma=False,
    )
```

```python
import functools

import jax
import jax.numpy as jnp
import numpy as np
from jax import lax
from jax.experimental import pallas as pl
from jax.experimental.pallas import tpu as pltpu
from jax.sharding import PartitionSpec as P

HEAD_DIM = 64
ITEM_MAX = 4096


EPSILON = 1e-05
MASKED = -1e30
SCALING = 0.125


def shortened(array):

    def short(part):
        return part.astype(jnp.bfloat16) if part.dtype == jnp.float32 else part

    return jax.tree.map(short, array)


def passed_along(block, axis, distance):
    devices = range(lax.axis_size(axis))
    route = [(i - distance, i) for i in devices if i - distance in devices]
    return lax.ppermute(block, axis, route)


def rms_norm(values, gain):
    return values * lax.rsqrt(jnp.mean(values * values, axis=-1, keepdims=True) + EPSILON) * gain


def gelu_exact(values):
    return jax.nn.gelu(values, approximate=False)


def item_starts(lengths, positions):
    ends = jnp.cumsum(lengths)
    offsets = ends - lengths
    before = offsets[None, :] <= positions[:, None]
    return jnp.max(jnp.where(before, offsets[None, :], 0), axis=1)


def live_mask(query_pos, query_start, key_first, key_count):
    key_pos = key_first + jnp.arange(key_count, dtype=jnp.int32)
    return (key_pos[None, :] >= query_start[:, None]) & (key_pos[None, :] <= query_pos[:, None])


def split_heads(matrix):
    return matrix.reshape(matrix.shape[0], matrix.shape[1] // HEAD_DIM, HEAD_DIM)


def merge_heads(tensor):
    return tensor.reshape(tensor.shape[0], tensor.shape[1] * tensor.shape[2])


def scores_of(queries3, keys_block, mask):
    raw = jnp.einsum(
        "qhd,khd->hqk", queries3, split_heads(keys_block), preferred_element_type=jnp.float32
    )
    return jnp.where(mask[None], raw * SCALING, MASKED)


def left_dot(left, right):
    return lax.dot_general(
        left, right, (((0,), (0,)), ((), ())), preferred_element_type=jnp.float32
    )


def right_dot(left, right):
    return lax.dot_general(
        left, right, (((1,), (1,)), ((), ())), preferred_element_type=jnp.float32
    )


def grad_parts(queries3, grad_out3, log_total, delta, keys_block, values_block, mask):
    probs = jnp.exp(scores_of(queries3, keys_block, mask) - log_total[:, :, None])
    grad_probs = jnp.einsum(
        "qhd,khd->hqk", grad_out3, split_heads(values_block), preferred_element_type=jnp.float32
    )
    grad_scores = (probs * (grad_probs - delta[:, :, None])).astype(jnp.bfloat16)
    return (probs.astype(jnp.bfloat16), grad_scores)


def key_terms(queries3, grad_out3, probs_low, grad_scores):
    grad_keys = jnp.einsum(
        "hqk,qhd->khd", grad_scores, queries3, preferred_element_type=jnp.float32
    )
    grad_values = jnp.einsum(
        "hqk,qhd->khd", probs_low, grad_out3, preferred_element_type=jnp.float32
    )
    return (merge_heads(grad_keys), merge_heads(grad_values))


def query_term(grad_scores, keys_block):
    return jnp.einsum(
        "hqk,khd->qhd", grad_scores, split_heads(keys_block), preferred_element_type=jnp.float32
    )


def shards_ring(
    frames,
    lengths,
    norm1_gain,
    w_query,
    w_key,
    w_value,
    w_out,
    norm2_gain,
    w_up,
    b_up,
    w_down,
    b_down,
    cotangent,
):
    row_count = frames.shape[0]
    width = frames.shape[1]
    heads = width // HEAD_DIM
    groups = lax.axis_size("grp")
    block_rows = row_count * groups
    span = (ITEM_MAX + block_rows - 2) // block_rows
    blk_index = lax.axis_index("blk")
    sub_index = lax.axis_index("grp")
    block_first = blk_index * block_rows
    query_pos = block_first + sub_index * row_count + jnp.arange(row_count, dtype=jnp.int32)
    query_start = item_starts(lengths, query_pos)
    back_steps = jnp.arange(span + 1, dtype=jnp.int32)
    normed1, norm1_back = jax.vjp(rms_norm, frames, norm1_gain)
    act1 = normed1.astype(jnp.bfloat16)
    queries = jnp.dot(act1, w_query, preferred_element_type=jnp.float32).astype(jnp.bfloat16)
    keys_own = jnp.dot(act1, w_key, preferred_element_type=jnp.float32).astype(jnp.bfloat16)
    values_own = jnp.dot(act1, w_value, preferred_element_type=jnp.float32).astype(jnp.bfloat16)
    queries3 = split_heads(queries)
    block_keys, block_values = (
        lax.all_gather(keys_own, "grp", axis=0, tiled=True),
        lax.all_gather(values_own, "grp", axis=0, tiled=True),
    )

    def cycle_step(carry, unused_input):
        moved = jax.tree.map(
            lambda part, own: part.astype(own.dtype),
            passed_along(shortened(carry), "blk", 1),
            carry,
        )
        return (moved, moved)

    unused_last, far_blocks = lax.scan(cycle_step, (block_keys, block_values), None, length=span)
    keys_all = jnp.concatenate([block_keys[None], far_blocks[0]], axis=0)
    values_all = jnp.concatenate([block_values[None], far_blocks[1]], axis=0)

    def mask_for(back):
        return live_mask(query_pos, query_start, block_first - back * block_rows, block_rows)

    def total_step(carry, inputs):
        run_max, run_sum = carry
        keys_block, back = inputs
        scores = scores_of(queries3, keys_block, mask_for(back))
        new_max = jnp.maximum(run_max, jnp.max(scores, axis=-1))
        run_sum = run_sum * jnp.exp(run_max - new_max) + jnp.sum(
            jnp.exp(scores - new_max[:, :, None]), axis=-1
        )
        return ((new_max, run_sum), None)

    start_max = jnp.full((heads, row_count), MASKED, jnp.float32)
    start_sum = jnp.zeros((heads, row_count), jnp.float32)
    (top_max, top_sum), unused_out = lax.scan(
        total_step, (start_max, start_sum), (keys_all, back_steps)
    )
    log_total = top_max + jnp.log(top_sum)

    def mix_step(total, inputs):
        keys_block, values_block, back = inputs
        probs = jnp.exp(
            scores_of(queries3, keys_block, mask_for(back)) - log_total[:, :, None]
        ).astype(jnp.bfloat16)
        return (
            total
            + jnp.einsum(
                "hqk,khd->qhd", probs, split_heads(values_block), preferred_element_type=jnp.float32
            ),
            None,
        )

    zero_query = jnp.zeros((row_count, heads, HEAD_DIM), jnp.float32)
    mixed_sum, unused_out = lax.scan(mix_step, zero_query, (keys_all, values_all, back_steps))
    mixed = merge_heads(mixed_sum).astype(jnp.bfloat16)
    middle = frames + jnp.dot(mixed, w_out, preferred_element_type=jnp.float32)
    normed2, norm2_back = jax.vjp(rms_norm, middle, norm2_gain)
    act2 = normed2.astype(jnp.bfloat16)
    before = jnp.dot(act2, w_up, preferred_element_type=jnp.float32) + b_up
    activated, gelu_back = jax.vjp(gelu_exact, before)
    hidden = activated.astype(jnp.bfloat16)
    layer_out = middle + jnp.dot(hidden, w_down, preferred_element_type=jnp.float32) + b_down
    grad_low = cotangent.astype(jnp.bfloat16)
    b_down_grad = jnp.sum(grad_low.astype(jnp.float32), axis=0)
    w_down_grad = left_dot(hidden, grad_low)
    grad_before = gelu_back(right_dot(grad_low, w_down))[0].astype(jnp.bfloat16)
    b_up_grad = jnp.sum(grad_before.astype(jnp.float32), axis=0)
    w_up_grad = left_dot(act2, grad_before)
    grad_mid_norm, norm2_gain_grad = norm2_back(right_dot(grad_before, w_up))
    grad_middle = cotangent + grad_mid_norm
    grad_attn = grad_middle.astype(jnp.bfloat16)
    w_out_grad = left_dot(mixed, grad_attn)
    grad_mixed = right_dot(grad_attn, w_out).astype(jnp.bfloat16)
    grad_out3 = split_heads(grad_mixed)

    def delta_step(total, inputs):
        keys_block, values_block, back = inputs
        probs = jnp.exp(scores_of(queries3, keys_block, mask_for(back)) - log_total[:, :, None])
        grad_probs = jnp.einsum(
            "qhd,khd->hqk", grad_out3, split_heads(values_block), preferred_element_type=jnp.float32
        )
        return (total + jnp.sum(probs * grad_probs, axis=-1), None)

    delta, unused_out = lax.scan(
        delta_step, jnp.zeros((heads, row_count), jnp.float32), (keys_all, values_all, back_steps)
    )
    zero_block = jnp.zeros((block_rows, width), jnp.float32)

    def return_step(carry, inputs):
        grad_q, travel = carry
        keys_block, values_block, back = inputs
        probs_low, grad_scores = grad_parts(
            queries3, grad_out3, log_total, delta, keys_block, values_block, mask_for(back)
        )
        grad_keys, grad_values = key_terms(queries3, grad_out3, probs_low, grad_scores)
        moved = (
            passed_along((travel[0] + grad_keys).astype(jnp.bfloat16), "blk", -1).astype(
                jnp.float32
            ),
            passed_along((travel[1] + grad_values).astype(jnp.bfloat16), "blk", -1).astype(
                jnp.float32
            ),
        )
        return ((grad_q + query_term(grad_scores, keys_block), moved), None)

    (grad_q, travel), unused_out = lax.scan(
        return_step,
        (zero_query, (zero_block, zero_block)),
        (far_blocks[0], far_blocks[1], back_steps[1:]),
        reverse=True,
    )
    probs_low, grad_scores = grad_parts(
        queries3, grad_out3, log_total, delta, block_keys, block_values, mask_for(0)
    )
    grad_keys, grad_values = key_terms(queries3, grad_out3, probs_low, grad_scores)
    grad_q = grad_q + query_term(grad_scores, block_keys)
    block_grad_keys = travel[0] + grad_keys
    block_grad_values = travel[1] + grad_values
    grad_keys_rows, grad_values_rows = (
        lax.psum_scatter(
            block_grad_keys.astype(jnp.bfloat16), "grp", scatter_dimension=0, tiled=True
        ).astype(jnp.float32),
        lax.psum_scatter(
            block_grad_values.astype(jnp.bfloat16), "grp", scatter_dimension=0, tiled=True
        ).astype(jnp.float32),
    )
    grad_keys_low = (grad_keys_rows * SCALING).astype(jnp.bfloat16)
    grad_values_low = grad_values_rows.astype(jnp.bfloat16)
    grad_queries_low = (merge_heads(grad_q) * SCALING).astype(jnp.bfloat16)
    w_query_grad = left_dot(act1, grad_queries_low)
    w_key_grad = left_dot(act1, grad_keys_low)
    w_value_grad = left_dot(act1, grad_values_low)
    grad_act1 = (
        right_dot(grad_queries_low, w_query)
        + right_dot(grad_keys_low, w_key)
        + right_dot(grad_values_low, w_value)
    )
    grad_frames_norm, norm1_gain_grad = norm1_back(grad_act1)
    frames_grad = grad_middle + grad_frames_norm
    shares = (
        lax.psum_scatter(norm1_gain_grad, ("blk", "grp"), scatter_dimension=0, tiled=True),
        lax.psum_scatter(w_query_grad, ("blk", "grp"), scatter_dimension=0, tiled=True),
        lax.psum_scatter(w_key_grad, ("blk", "grp"), scatter_dimension=0, tiled=True),
        lax.psum_scatter(w_value_grad, ("blk", "grp"), scatter_dimension=0, tiled=True),
        lax.psum_scatter(w_out_grad, ("blk", "grp"), scatter_dimension=0, tiled=True),
        lax.psum_scatter(norm2_gain_grad, ("blk", "grp"), scatter_dimension=0, tiled=True),
        lax.psum_scatter(w_up_grad, ("blk", "grp"), scatter_dimension=0, tiled=True),
        lax.psum_scatter(b_up_grad, ("blk", "grp"), scatter_dimension=0, tiled=True),
        lax.psum_scatter(w_down_grad, ("blk", "grp"), scatter_dimension=0, tiled=True),
        lax.psum_scatter(b_down_grad, ("blk", "grp"), scatter_dimension=0, tiled=True),
    )
    return (
        layer_out,
        frames_grad,
        shares[0],
        shares[1],
        shares[2],
        shares[3],
        shares[4],
        shares[5],
        shares[6],
        shares[7],
        shares[8],
        shares[9],
    )


def solution_ring(mesh):
    placed = (
        P(("blk", "grp"), None),
        P(),
        P(),
        P(),
        P(),
        P(),
        P(),
        P(),
        P(),
        P(),
        P(),
        P(),
        P(("blk", "grp"), None),
    )
    return jax.shard_map(
        shards_ring,
        mesh=mesh,
        in_specs=placed,
        out_specs=(
            P(("blk", "grp"), None),
            P(("blk", "grp"), None),
            P(("blk", "grp")),
            P(("blk", "grp"), None),
            P(("blk", "grp"), None),
            P(("blk", "grp"), None),
            P(("blk", "grp"), None),
            P(("blk", "grp")),
            P(("blk", "grp"), None),
            P(("blk", "grp")),
            P(("blk", "grp"), None),
            P(("blk", "grp")),
        ),
        check_vma=False,
    )


LOG2E = 1.4426950408889634
F32, BF16 = jnp.float32, jnp.bfloat16


def nt_dot(a, b):
    return lax.dot_general(a, b, (((1,), (1,)), ((), ())), preferred_element_type=F32)


def nn_dot(a, b):
    return lax.dot_general(a, b, (((1,), (0,)), ((), ())), preferred_element_type=F32)


def low_lanes(shape):
    return lax.broadcasted_iota(jnp.int32, shape, 1) < 64


def pair_low(a, b, low):
    return jnp.where(low, a, pltpu.roll(b, 64, 1))


def pair_high(a, b, low):
    return jnp.where(low, pltpu.roll(a, 64, 1), b)


def store_halves(ref, x):
    low = low_lanes((x.shape[0], 128))
    for p in range(x.shape[1] // 256):
        a, b = x[:, p * 256 : p * 256 + 128], x[:, p * 256 + 128 : (p + 1) * 256]
        ref[0, :, p * 128 : (p + 1) * 128] = pair_low(a, b, low).astype(BF16)
        ref[1, :, p * 128 : (p + 1) * 128] = pair_high(a, b, low).astype(BF16)


def block_bounds(len_ref, items, qpos, first, last, key_block):
    off = jnp.int32(0)
    start = jnp.zeros(qpos.shape, jnp.int32)
    s_first, s_last = jnp.int32(0), jnp.int32(0)
    for i in range(items):
        start = jnp.where(qpos >= off, off, start)
        s_first = jnp.where(first >= off, off, s_first)
        s_last = jnp.where(last >= off, off, s_last)
        off = off + len_ref[i]
    lo, hi = s_first // key_block, last // key_block + 1
    f0 = jnp.clip((s_last + key_block - 1) // key_block, lo, hi)
    f1 = jnp.clip((first + 1) // key_block, f0, hi)
    return start, lo, f0, f1, hi


def query_ends(i, chunks, half, core):
    first = i * chunks * 2 * half + core * half
    return first, first + (chunks - 1) * 2 * half + half - 1


def spread(packed, low, to_high):
    f = packed.astype(F32)
    other = pltpu.roll(f, 64, 1)
    zero = jnp.zeros_like(f)
    if to_high:
        return jnp.where(low, zero, other).astype(BF16), jnp.where(low, zero, f).astype(BF16)
    return jnp.where(low, f, zero).astype(BF16), jnp.where(low, other, zero).astype(BF16)


def mix_kernel(
    items, chunks, key_block,
    len_ref, core_ref, kv_ref, qp_ref, qpos_ref,
    out_t_ref, lse_ref, out_ref,
    kv_t, qz, acc, m_ref, l_ref,
):
    i = pl.program_id(0)
    half = 2 * qp_ref.shape[1]
    n = chunks * half
    core = core_ref[0]

    @pl.when(i == 0)
    def _():
        for c in range(kv_ref.shape[0] // 512):
            at = slice(c * 512, (c + 1) * 512)
            kv_t[:, at] = kv_ref[at, :].astype(F32).T.astype(BF16)

    low = low_lanes((half // 2, 128))
    for c in range(chunks):
        a, b = spread(qp_ref[c], low, False)
        qz[c * half : c * half + half // 2] = a
        qz[c * half + half // 2 : (c + 1) * half] = b
    qpos = qpos_ref[...] + core * half
    first, last = query_ends(i, chunks, half, core)
    start, lo, f0, f1, hi = block_bounds(len_ref, items, qpos, first, last, key_block)
    acc[...] = jnp.zeros_like(acc)
    m_ref[...] = jnp.full_like(m_ref, MASKED)
    l_ref[...] = jnp.zeros_like(l_ref)

    def step(j, masked):
        at = pl.ds(pl.multiple_of(j * key_block, key_block), key_block)
        s = nt_dot(kv_ref[at, :], qz[...]) * LOG2E
        if masked:
            kpos = j * key_block + lax.broadcasted_iota(jnp.int32, (key_block, 1), 0)
            s = jnp.where((kpos >= start) & (kpos <= qpos), s, MASKED)
        m_old = m_ref[...]
        m_new = jnp.maximum(m_old, jnp.max(s, axis=0, keepdims=True))
        p = jnp.exp2(s - m_new)
        alpha = jnp.exp2(m_old - m_new)
        m_ref[...] = m_new
        l_ref[...] = l_ref[...] * alpha + jnp.sum(p, axis=0, keepdims=True)
        acc[...] = acc[...] * alpha + nn_dot(kv_t[64:, at], p.astype(BF16))

    lax.fori_loop(lo, f0, lambda j, c: (step(j, True), c)[1], 0)
    lax.fori_loop(f0, f1, lambda j, c: (step(j, False), c)[1], 0)
    lax.fori_loop(f1, hi, lambda j, c: (step(j, True), c)[1], 0)
    out_t = acc[...] / l_ref[...]
    out_t_ref[...] = out_t
    lse_ref[...] = m_ref[...] + jnp.log2(l_ref[...])
    doubled = jnp.concatenate([out_t, out_t], axis=0).T
    for c in range(chunks):
        a = doubled[c * half : c * half + half // 2]
        b = doubled[c * half + half // 2 : (c + 1) * half]
        out_ref[c] = jnp.where(low, a, b).astype(BF16)


def mix(lengths, core, kv, qp, qpos, chunks=4, key_block=768):
    total = kv.shape[0]
    n_src, quarter = qp.shape[0], qp.shape[1]
    half = 2 * quarter
    n = chunks * half
    whole = lambda i, *_: (0, 0)
    return pl.pallas_call(
        functools.partial(mix_kernel, lengths.shape[0], chunks, key_block),
        grid_spec=pltpu.PrefetchScalarGridSpec(
            num_scalar_prefetch=2,
            grid=(n_src // chunks,),
            in_specs=[
                pl.BlockSpec((total, 128), whole),
                pl.BlockSpec((chunks, quarter, 128), lambda i, *_: (i, 0, 0)),
                pl.BlockSpec((1, n), lambda i, *_: (0, i)),
            ],
            out_specs=[
                pl.BlockSpec((64, n), lambda i, *_: (0, i)),
                pl.BlockSpec((1, n), lambda i, *_: (0, i)),
                pl.BlockSpec((chunks, quarter, 128), lambda i, *_: (i, 0, 0)),
            ],
            scratch_shapes=[
                pltpu.VMEM((128, total), BF16),
                pltpu.VMEM((n, 128), BF16),
                pltpu.VMEM((64, n), F32),
                pltpu.VMEM((1, n), F32),
                pltpu.VMEM((1, n), F32),
            ],
        ),
        out_shape=[
            jax.ShapeDtypeStruct((64, n_src * half), F32),
            jax.ShapeDtypeStruct((1, n_src * half), F32),
            jax.ShapeDtypeStruct((n_src, quarter, 128), BF16),
        ],
        compiler_params=pltpu.CompilerParams(vmem_limit_bytes=22 << 20),
        cost_estimate=pl.CostEstimate(flops=25_000_000_000, bytes_accessed=8 << 20, transcendentals=0),
        name="mix",
    )(lengths, core, kv, qp, qpos)


def back_kernel(
    items, chunks, key_block,
    len_ref, core_ref, kv_ref, qp_ref, dp_ref, qpos_ref, out_t_ref, lse_ref,
    dkv_ref, dq_ref,
    kv_t, qd, dq_acc,
):
    i = pl.program_id(0)
    half = 2 * qp_ref.shape[1]
    n = chunks * half
    core = core_ref[0]

    @pl.when(i == 0)
    def _():
        for c in range(kv_ref.shape[0] // 512):
            at = slice(c * 512, (c + 1) * 512)
            kv_t[:, at] = kv_ref[at, :].astype(F32).T.astype(BF16)
        dkv_ref[...] = jnp.zeros_like(dkv_ref)

    low = low_lanes((half // 2, 128))
    for c in range(chunks):
        a, b = spread(qp_ref[c], low, False)
        qd[c * half : c * half + half // 2] = a
        qd[c * half + half // 2 : (c + 1) * half] = b
        a, b = spread(dp_ref[c], low, True)
        qd[n + c * half : n + c * half + half // 2] = a
        qd[n + c * half + half // 2 : n + (c + 1) * half] = b
    do_t = qd[n:, :].astype(F32).T[64:]
    delta = jnp.sum(do_t * out_t_ref[...], axis=0, keepdims=True)
    lse = lse_ref[...]
    qpos = qpos_ref[...] + core * half
    first, last = query_ends(i, chunks, half, core)
    start, lo, f0, f1, hi = block_bounds(len_ref, items, qpos, first, last, key_block)
    dq_acc[...] = jnp.zeros_like(dq_acc)

    def step(j, masked):
        at = pl.ds(pl.multiple_of(j * key_block, key_block), key_block)
        both = nt_dot(kv_ref[at, :], qd[...])
        s = both[:, :n] * LOG2E
        if masked:
            kpos = j * key_block + lax.broadcasted_iota(jnp.int32, (key_block, 1), 0)
            s = jnp.where((kpos >= start) & (kpos <= qpos), s, MASKED)
        p = jnp.exp2(s - lse)
        ds = (p * (both[:, n:] - delta)).astype(BF16)
        dq_acc[...] += nn_dot(kv_t[:64, at], ds)
        dkv_ref[at, :] += nn_dot(ds, qd[:n, :]) + nn_dot(p.astype(BF16), qd[n:, :])

    lax.fori_loop(lo, f0, lambda j, c: (step(j, True), c)[1], 0)
    lax.fori_loop(f0, f1, lambda j, c: (step(j, False), c)[1], 0)
    lax.fori_loop(f1, hi, lambda j, c: (step(j, True), c)[1], 0)
    dq_t = dq_acc[...] * 0.125
    doubled = jnp.concatenate([dq_t, dq_t], axis=0).T
    for c in range(chunks):
        a = doubled[c * half : c * half + half // 2]
        b = doubled[c * half + half // 2 : (c + 1) * half]
        dq_ref[c] = jnp.where(low, a, b).astype(BF16)


def mix_back(lengths, core, kv, qp, dp, qpos, out_t, lse, chunks=4, key_block=768):
    total = kv.shape[0]
    n_src, quarter = qp.shape[0], qp.shape[1]
    half = 2 * quarter
    n = chunks * half
    whole = lambda i, *_: (0, 0)
    rows = lambda i, *_: (0, i)
    blocks = pl.BlockSpec((chunks, quarter, 128), lambda i, *_: (i, 0, 0))
    return pl.pallas_call(
        functools.partial(back_kernel, lengths.shape[0], chunks, key_block),
        grid_spec=pltpu.PrefetchScalarGridSpec(
            num_scalar_prefetch=2,
            grid=(n_src // chunks,),
            in_specs=[
                pl.BlockSpec((total, 128), whole),
                blocks,
                blocks,
                pl.BlockSpec((1, n), rows),
                pl.BlockSpec((64, n), rows),
                pl.BlockSpec((1, n), rows),
            ],
            out_specs=[pl.BlockSpec((total, 128), whole), blocks],
            scratch_shapes=[
                pltpu.VMEM((128, total), BF16),
                pltpu.VMEM((2 * n, 128), BF16),
                pltpu.VMEM((64, n), F32),
            ],
        ),
        out_shape=[
            jax.ShapeDtypeStruct((total, 128), F32),
            jax.ShapeDtypeStruct((n_src, quarter, 128), BF16),
        ],
        compiler_params=pltpu.CompilerParams(vmem_limit_bytes=22 << 20),
        cost_estimate=pl.CostEstimate(flops=40_000_000_000, bytes_accessed=8 << 20, transcendentals=0),
        name="mix_back",
    )(lengths, core, kv, qp, dp, qpos, out_t, lse)


def packed_positions(n_src, half):
    j = np.arange(n_src * half)
    return ((j // half) * 2 * half + j % half).astype(np.int32)[None]


def feed_kernel(
    blocks_ref, frames_ref, cot_ref, w_out_ref, gain_ref, w_up_ref, b_up_ref, w_down_ref, b_down_ref,
    out_ref, grad_mid_ref, grad_blocks_ref, hidden_ref, grad_before_ref, act2_ref, mixed_ref, low_ref, attn_ref,
    gain_grad_ref, b_up_grad_ref, b_down_grad_ref,
    mixed, act2, act_grad,
):
    i = pl.program_id(0)
    rows = frames_ref.shape[0]
    quarter = rows // 4
    low_q = low_lanes((quarter, 128))

    @pl.when(i == 0)
    def _():
        for zy in range(8):
            for s in range(2):
                a = blocks_ref[(zy * 2 + s) * 2].astype(F32)
                b = blocks_ref[(zy * 2 + s) * 2 + 1].astype(F32)
                at = slice(zy * 128, (zy + 1) * 128)
                first = 2 * s * quarter
                mixed[first : first + quarter, at] = pair_low(a, b, low_q)
                mixed[first + quarter : first + 2 * quarter, at] = pair_high(a, b, low_q)
        store_halves(mixed_ref, mixed[...])
        middle = frames_ref[...] + nn_dot(mixed[...].astype(BF16), w_out_ref[...])
        r = lax.rsqrt(jnp.mean(middle * middle, axis=-1, keepdims=True) + EPSILON)
        normed = middle * r * gain_ref[...]
        act2[...] = normed.astype(BF16)
        store_halves(act2_ref, normed)
        grad_mid_ref[...] = middle
        out_ref[...] = middle + b_down_ref[...]
        grad_low = cot_ref[...].astype(BF16)
        low_ref[...] = grad_low
        b_down_grad_ref[...] = jnp.sum(grad_low.astype(F32), axis=0, keepdims=True)
        act_grad[...] = jnp.zeros_like(act_grad)

    before = nn_dot(act2[...], w_up_ref[...]) + b_up_ref[...]
    cdf = 0.5 + 0.5 * lax.erf(before * 0.7071067811865476)
    pdf = jnp.exp(-0.5 * before * before) * 0.3989422804014327
    hidden = (before * cdf).astype(BF16)
    step = hidden.shape[1] // 2
    hidden_ref[0] = hidden[:, :step]
    hidden_ref[1] = hidden[:, step:]
    out_ref[...] += nn_dot(hidden, w_down_ref[...])
    grad_before = (nt_dot(low_ref[...], w_down_ref[...]) * (cdf + before * pdf)).astype(BF16)
    grad_before_ref[...] = grad_before
    b_up_grad_ref[...] = jnp.sum(grad_before.astype(F32), axis=0, keepdims=True)
    act_grad[...] += nt_dot(grad_before, w_up_ref[...])

    @pl.when(i == pl.num_programs(0) - 1)
    def _():
        middle = grad_mid_ref[...]
        r = lax.rsqrt(jnp.mean(middle * middle, axis=-1, keepdims=True) + EPSILON)
        n = middle * r
        g = act_grad[...]
        gain_grad_ref[...] = jnp.sum(g * n, axis=0, keepdims=True)
        g = g * gain_ref[...]
        grad_mid = cot_ref[...] + r * (g - n * jnp.mean(g * n, axis=-1, keepdims=True))
        grad_mid_ref[...] = grad_mid
        grad_attn = grad_mid.astype(BF16)
        attn_ref[...] = grad_attn
        grad_mixed = nt_dot(grad_attn, w_out_ref[...])
        for zy in range(8):
            for s in range(2):
                at = slice(zy * 128, (zy + 1) * 128)
                first = 2 * s * quarter
                a = grad_mixed[first : first + quarter, at]
                b = grad_mixed[first + quarter : first + 2 * quarter, at]
                grad_blocks_ref[(zy * 2 + s) * 2] = pair_low(a, b, low_q).astype(BF16)
                grad_blocks_ref[(zy * 2 + s) * 2 + 1] = pair_high(a, b, low_q).astype(BF16)


def feed(blocks, frames, cotangent, w_out, gain, w_up, b_up, w_down, b_down):
    rows, width = frames.shape
    ff = w_up.shape[1]
    steps = 8
    step = ff // steps
    fixed = lambda *shape: pl.BlockSpec(shape, lambda i: (0,) * len(shape))
    columns = lambda *shape: pl.BlockSpec(shape, lambda i: (0,) * (len(shape) - 1) + (i,))
    shape = jax.ShapeDtypeStruct
    return pl.pallas_call(
        feed_kernel,
        grid=(steps,),
        in_specs=[
            fixed(*blocks.shape),
            fixed(rows, width),
            fixed(rows, width),
            fixed(width, width),
            fixed(1, width),
            columns(width, step),
            columns(1, step),
            pl.BlockSpec((step, width), lambda i: (i, 0)),
            fixed(1, width),
        ],
        out_specs=[
            fixed(rows, width),
            fixed(rows, width),
            fixed(*blocks.shape),
            columns(2, rows, step // 2),
            columns(rows, step),
            fixed(2, rows, width // 2),
            fixed(2, rows, width // 2),
            fixed(rows, width),
            fixed(rows, width),
            fixed(1, width),
            columns(1, step),
            fixed(1, width),
        ],
        out_shape=[
            shape((rows, width), F32),
            pltpu.HBM((rows, width), F32),
            shape(blocks.shape, BF16),
            shape((2, rows, ff // 2), BF16),
            shape((rows, ff), BF16),
            shape((2, rows, width // 2), BF16),
            shape((2, rows, width // 2), BF16),
            shape((rows, width), BF16),
            shape((rows, width), BF16),
            pltpu.VMEM((1, width), F32),
            pltpu.VMEM((1, ff), F32),
            pltpu.VMEM((1, width), F32),
        ],
        scratch_shapes=[
            pltpu.VMEM((rows, width), F32),
            pltpu.VMEM((rows, width), BF16),
            pltpu.VMEM((rows, width), F32),
        ],
        compiler_params=pltpu.CompilerParams(vmem_limit_bytes=28 << 20),
        name="feed",
    )(
        blocks, frames, cotangent, w_out, gain.reshape(1, width), w_up, b_up.reshape(1, ff), w_down,
        b_down.reshape(1, width),
    )


MESH = pl.DeviceIdType.MESH
ALL = ("blk", "grp")


def in_hbm(*arrays):
    return [pltpu.with_memory_space_constraint(x, pltpu.HBM) for x in arrays]


def in_vmem(*arrays):
    return [pltpu.with_memory_space_constraint(x, pltpu.VMEM) for x in arrays]


def place(index):
    return {"blk": lax.div(index, 2), "grp": lax.rem(index, 2)}


def head_of(index):
    blk, grp = lax.div(index, 2), lax.rem(index, 2)
    return lax.div(blk, 2) * 2 + grp, lax.rem(blk, 2)


def own_index():
    return lax.axis_index("blk") * 2 + lax.axis_index("grp")


def sibling_of(core):
    return {"blk": lax.axis_index("blk") + 1 - 2 * core, "grp": lax.axis_index("grp")}


def greet_all(me, n):
    barrier = pltpu.get_barrier_semaphore()

    @pl.loop(1, n)
    def _(i):
        pl.semaphore_signal(barrier, inc=1, device_id=place(lax.rem(me + i, n)), device_id_type=MESH)

    pl.semaphore_wait(barrier, n - 1)


def remote(src, dst, send_sem, recv_sem, device):
    return pltpu.make_async_remote_copy(
        src_ref=src, dst_ref=dst, send_sem=send_sem, recv_sem=recv_sem, device_id=device, device_id_type=MESH
    )


def to_heads_kernel(
    n, gain_in, frames_in, wq_in, wk_in, wv_in, kv_out, q_out, halves_out,
    gain, frames, act, halves, wq, wk, wv, kv_own, q_own, send, recv, local, fetched, pair,
):
    me = own_index()
    head, core = head_of(me)
    rows, width = frames.shape
    half = rows // 2
    weights = [
        pltpu.make_async_copy(src, dst, local.at[k])
        for k, (src, dst) in enumerate(
            ((gain_in, gain), (frames_in, frames), (halves, halves_out))
        )
    ]
    groups = width // 256

    def group_at(i):
        return lax.rem(lax.div(me, n // groups) + 1 + i, groups)

    def fetch(group):
        columns = pl.ds(pl.multiple_of(group * 256, 256), 256)
        return [
            pltpu.make_async_copy(src.at[:, columns], dst.at[:, columns], fetched.at[k, group])
            for k, (src, dst) in enumerate(((wq_in, wq), (wk_in, wk), (wv_in, wv)))
        ]

    for copy in weights[:2]:
        copy.start()

    @pl.loop(0, groups)
    def _(i):
        for copy in fetch(group_at(i)):
            copy.start()

    greet_all(me, n)
    weights[0].wait()
    weights[1].wait()
    x = frames[...]
    r = lax.rsqrt(jnp.mean(x * x, axis=-1, keepdims=True) + EPSILON)
    normed = x * r * gain[...]
    act[...] = normed.astype(BF16)
    store_halves(halves, normed)
    weights[2].start()

    def copies(other, src):
        h, c = head_of(other)
        kv_at = core if src is not me else c
        return (
            remote(kv_own.at[h, c], kv_out.at[src, kv_at], send.at[0, other], recv.at[0, src], place(other)),
            remote(q_own.at[h, c], q_out.at[src], send.at[1, other], recv.at[1, src], place(other)),
        )

    low = low_lanes((rows, 128))
    low_h = low_lanes((half // 2, 128))

    @pl.loop(0, groups)
    def _(i):
        group = group_at(i)
        for copy in fetch(group):
            copy.wait()
        columns = pl.ds(pl.multiple_of(group * 256, 256), 256)
        q = nn_dot(act[...], wq[:, columns]).astype(BF16).astype(F32) * 0.125
        k = nn_dot(act[...], wk[:, columns])
        v = nn_dot(act[...], wv[:, columns])
        for p in range(2):
            at = slice(p * 128, (p + 1) * 128)
            k2, v2, q2 = k[:, at], v[:, at], q[:, at]
            kv_a = pair_low(k2, v2, low).astype(BF16)
            kv_b = pair_high(k2, v2, low).astype(BF16)
            h = group * 4 + 2 * p
            for s in range(2):
                span = slice(s * half, (s + 1) * half)
                kv_own[h, s] = kv_a[span]
                kv_own[h + 1, s] = kv_b[span]
                top = q2[s * half : s * half + half // 2]
                bot = q2[s * half + half // 2 : (s + 1) * half]
                q_own[h, s] = pair_low(top, bot, low_h).astype(BF16)
                q_own[h + 1, s] = pair_high(top, bot, low_h).astype(BF16)

        @pl.loop(0, n // groups)
        def _(j):
            other = group * (n // groups) + j

            @pl.when(other != me)
            def _():
                for copy in copies(other, me):
                    copy.start()

    kv_out[me, core] = kv_own[head, core]
    q_out[me] = q_own[head, core]

    plane = n // groups
    swaps = []
    for t in range(groups):
        first = pl.multiple_of(lax.rem(lax.div(me, plane) + groups - 1 - t, groups) * plane, plane)

        @pl.loop(0, plane)
        def _(j):
            @pl.when(first + j != me)
            def _():
                for copy in copies(first + j, first + j):
                    copy.wait()

        at = pl.ds(first, plane)
        swap = remote(kv_out.at[at, core], kv_out.at[at, core], pair.at[0, t], pair.at[1, t], sibling_of(core))
        swap.start()
        swaps.append(swap)
    weights[2].wait()
    for swap in swaps:
        swap.wait()


def to_heads(frames, gain, w_query, w_key, w_value, n):
    rows, width = frames.shape
    half = rows // 2
    vmem = pl.BlockSpec(memory_space=pltpu.VMEM)
    hbm = pl.BlockSpec(memory_space=pltpu.HBM)
    return pl.pallas_call(
        functools.partial(to_heads_kernel, n),
        in_specs=[hbm] * 5,
        out_specs=[vmem, vmem, hbm],
        out_shape=[
            jax.ShapeDtypeStruct((n, 2, half, 128), BF16),
            jax.ShapeDtypeStruct((n, half // 2, 128), BF16),
            pltpu.HBM((2, rows, width // 2), BF16),
        ],
        scratch_shapes=[
            pltpu.VMEM((1, width), F32),
            pltpu.VMEM((rows, width), F32),
            pltpu.VMEM((rows, width), BF16),
            pltpu.VMEM((2, rows, width // 2), BF16),
            pltpu.VMEM((width, width), BF16),
            pltpu.VMEM((width, width), BF16),
            pltpu.VMEM((width, width), BF16),
            pltpu.VMEM((width // 64, 2, half, 128), BF16),
            pltpu.VMEM((width // 64, 2, half // 2, 128), BF16),
            pltpu.SemaphoreType.DMA((2, n)),
            pltpu.SemaphoreType.DMA((2, n)),
            pltpu.SemaphoreType.DMA((3,)),
            pltpu.SemaphoreType.DMA((3, 4)),
            pltpu.SemaphoreType.DMA((2, 4)),
        ],
        compiler_params=pltpu.CompilerParams(
            collective_id=0, has_side_effects=True, vmem_limit_bytes=16 << 20
        ),
        name="to_heads",
    )(*in_hbm(gain.reshape(1, width), frames, w_query, w_key, w_value))


def exchange_kernel(n, x_in, x_out, send, recv, local):
    me = own_index()
    greet_all(me, n)

    def copy_with(i, src):
        other = lax.rem(me + i, n)
        return remote(x_in.at[other], x_out.at[src], send.at[i], recv.at[src], place(other))

    @pl.loop(1, n)
    def _(i):
        copy_with(i, me).start()

    own = pltpu.make_async_copy(x_in.at[me], x_out.at[me], local)
    own.start()
    own.wait()

    @pl.loop(1, n)
    def _(i):
        copy_with(i, lax.rem(me + i, n)).wait()


def exchange(x, n, collective_id):
    vmem = pl.BlockSpec(memory_space=pltpu.VMEM)
    return pl.pallas_call(
        functools.partial(exchange_kernel, n),
        in_specs=[vmem],
        out_specs=vmem,
        out_shape=pltpu.VMEM(x.shape, x.dtype),
        scratch_shapes=[
            pltpu.SemaphoreType.DMA((n,)),
            pltpu.SemaphoreType.DMA((n,)),
            pltpu.SemaphoreType.DMA,
        ],
        compiler_params=pltpu.CompilerParams(collective_id=collective_id, has_side_effects=True, vmem_limit_bytes=8 << 20),
        name="exchange",
    )(*in_vmem(x))


BITS = {"core": 1, "y": 2, "z0": 4, "z1": 8}


def flipped(x, axis):
    if axis == "x":
        return lax.ppermute(x, "grp", [(0, 1), (1, 0)])
    return lax.ppermute(x, "blk", [(i, i ^ BITS[axis]) for i in range(lax.axis_size("blk"))])


def bit_of(axis):
    if axis == "x":
        return lax.axis_index("grp")
    return lax.rem(lax.div(lax.axis_index("blk"), BITS[axis]), 2)


def across(axis):
    blk, grp = lax.axis_index("blk"), lax.axis_index("grp")
    if axis == "x":
        return {"blk": blk, "grp": 1 - grp}
    bit = BITS[axis]
    return {"blk": blk + bit - 2 * bit * bit_of(axis), "grp": grp}


def tn_dot(a, b):
    return lax.dot_general(a, b, (((0,), (0,)), ((), ())), preferred_element_type=F32)


def share_kernel(
    n, blocks_in, hidden, grad_before, act2, mixed, low, attn,
    blocks_out, keep_a_out, send_a_out, keep_b_out, send_b_out, keep_c_out, send_c_out,
    keep_a, send_a, keep_b, send_b, keep_c, send_c, hidden2, before2, act2_2, mixed2, low2, attn2, tile, send, recv, local, out, pair_send, pair_recv,
):
    me = own_index()
    head, core = head_of(me)
    rows = low.shape[0]
    greet_all(me, n)
    sibling = sibling_of(core)
    theirs = pl.ds(rows, rows)
    pairs = [
        remote(src, dst.at[theirs], pair_send.at[k], pair_recv.at[k], sibling)
        for k, (src, dst) in enumerate(
            (
                (low, low2),
                (hidden.at[1 - core], hidden2),
                (act2.at[1 - core], act2_2),
                (grad_before, before2),
                (mixed.at[1 - core], mixed2),
                (attn, attn2),
            )
        )
    ]
    for copy in pairs:
        copy.start()

    def copy_with(i, src):
        other = lax.rem(me + i, n)
        return remote(blocks_in.at[other], blocks_out.at[src], send.at[i], recv.at[src], place(other))

    @pl.loop(1, n)
    def _(i):
        copy_with(i, me).start()

    own = pltpu.make_async_copy(blocks_in.at[me], blocks_out.at[me], local)
    own.start()
    low2[:rows] = low[...]
    hidden2[:rows] = hidden[core]
    act2_2[:rows] = act2[core]
    before2[:rows] = grad_before[...]
    mixed2[:rows] = mixed[core]
    attn2[:rows] = attn[...]

    x_mine, y_mine, z_mine = bit_of("x"), bit_of("y"), bit_of("z0")

    def put(keep, away, mine, bit, at, row, value):
        @pl.when(mine == bit)
        def _():
            keep[at, row : row + value.shape[0]] = value

        @pl.when(mine != bit)
        def _():
            away[at, row : row + value.shape[0]] = value

    flushes = []

    def flush(src, dst):
        flushes.append(pltpu.make_async_copy(src, dst, out.at[len(flushes)]))
        flushes[-1].start()

    pairs[0].wait()
    pairs[1].wait()

    @pl.loop(0, 8)
    def _(zy):
        columns = pl.ds(pl.multiple_of(zy * 256, 256), 256)
        value = tn_dot(hidden2[:, columns], low2[...]).astype(BF16)
        z1, z0, y = lax.div(zy, 4), lax.rem(lax.div(zy, 2), 2), lax.rem(zy, 2)
        for x in range(2):
            put(keep_a, send_a, x_mine, x, zy, 0, value[x * 128 : x * 128 + 96])
            put(keep_c, send_c, z_mine, z0, (z1 * 2 + y) * 2 + x, 0, value[x * 128 + 96 : (x + 1) * 128])

    def spread_rows(left, right, slab, to_b, row):
        tile[...] = tn_dot(left[...], right[:, slab * 1024 : (slab + 1) * 1024]).astype(BF16)

        @pl.loop(0, 16)
        def _(j):
            value = tile[pl.ds(pl.multiple_of(j * 32, 32), 32)]
            z1, z0 = lax.div(j, 8), lax.rem(lax.div(j, 4), 2)
            y, x = lax.rem(lax.div(j, 2), 2), lax.rem(j, 2)
            if to_b:
                put(keep_b, send_b, y_mine, y, (z1 * 2 + z0) * 2 + x, row, value)
            else:
                put(keep_c, send_c, z_mine, z0, (z1 * 2 + y) * 2 + x, row, value)

    flush(keep_a, keep_a_out)
    flush(send_a, send_a_out)
    pairs[2].wait()
    pairs[3].wait()
    for slab in range(3):
        spread_rows(act2_2, before2, slab, True, 32 * slab)
    flush(keep_b, keep_b_out)
    flush(send_b, send_b_out)
    spread_rows(act2_2, before2, 3, False, 32)
    pairs[4].wait()
    pairs[5].wait()
    spread_rows(mixed2, attn2, 0, False, 64)
    flush(keep_c, keep_c_out)
    flush(send_c, send_c_out)
    own.wait()

    @pl.loop(1, n)
    def _(i):
        copy_with(i, lax.rem(me + i, n)).wait()

    for copy in flushes:
        copy.wait()


def share(blocks, hidden, grad_before, act2, mixed, low, attn, n):
    rows, width = low.shape
    vmem = pl.BlockSpec(memory_space=pltpu.VMEM)
    hbm = pl.BlockSpec(memory_space=pltpu.HBM)
    shape = jax.ShapeDtypeStruct
    return pl.pallas_call(
        functools.partial(share_kernel, n),
        in_specs=[vmem] * 7,
        out_specs=[vmem] + [hbm] * 6,
        out_shape=[pltpu.VMEM(blocks.shape, BF16)] + [pltpu.HBM((8, 96, width), BF16)] * 6,
        scratch_shapes=[
            *[pltpu.VMEM((8, 96, width), BF16)] * 6,
            pltpu.VMEM((2 * rows, hidden.shape[2]), BF16),
            pltpu.VMEM((2 * rows, grad_before.shape[1]), BF16),
            pltpu.VMEM((2 * rows, width // 2), BF16),
            pltpu.VMEM((2 * rows, width // 2), BF16),
            pltpu.VMEM((2 * rows, width), BF16),
            pltpu.VMEM((2 * rows, width), BF16),
            pltpu.VMEM((width // 2, 1024), BF16),
            pltpu.SemaphoreType.DMA((n,)),
            pltpu.SemaphoreType.DMA((n,)),
            pltpu.SemaphoreType.DMA,
            pltpu.SemaphoreType.DMA((6,)),
            pltpu.SemaphoreType.DMA((6,)),
            pltpu.SemaphoreType.DMA((6,)),
        ],
        compiler_params=pltpu.CompilerParams(
            collective_id=3, has_side_effects=True, vmem_limit_bytes=26 << 20
        ),
        name="share",
    )(blocks, hidden, grad_before, act2, mixed, low, attn)


class Part:
    def __init__(self, total, dims, order, landing, send, recv):
        self.view, self.dims, self.order = total, list(dims), list(order)
        self.landing, self.send, self.recv = landing, send, recv
        self.stage, self.copy, self.kept = 0, None, None

    def start(self):
        axis = self.order[self.stage]
        at, mine = self.dims.index(axis), bit_of(axis)
        ahead = (slice(None),) * at
        self.copy = remote(
            self.view.at[ahead + (1 - mine,)],
            self.landing[self.stage],
            self.send.at[self.stage],
            self.recv.at[self.stage],
            across(axis),
        )
        self.copy.start()
        self.kept = self.view.at[ahead + (mine,)]
        self.dims.remove(axis)
        self.stage += 1

    def finish(self):
        self.copy.wait()
        got, kept = self.landing[self.stage - 1], self.kept
        lead = len(self.dims)

        @pl.loop(0, 2**lead)
        def _(k):
            at = tuple(lax.rem(lax.div(k, 2**d), 2) for d in reversed(range(lead)))
            kept[at] = (kept[at].astype(F32) + got[at].astype(F32)).astype(BF16)

        self.view = kept

    def last(self):
        self.copy.wait()
        return self.kept[...].astype(F32) + self.landing[self.stage - 1][...].astype(F32)


def finish_kernel(
    n, dkv_in, dq_in, gain2_grad, b_up_grad, b_down_grad, got_a, got_b, got_c,
    gain_in, act1, frames_in, grad_mid_in, wq_in, wk_in, wv_in, keep_a, keep_b, keep_c,
    frames_out, q_out, k_out, v_out, o_out, up_out, down_out, small_out,
    theirs, total, dkv_all, dq_all, gain, frames, grad_mid, wq, wk, wv, small_in,
    act1_2, qkv2, sum_a, sum_b, sum_c, sum_q, sum_k, sum_v,
    a2, a3, a4, b2, b3, b4, c2, c3, c4,
    q1, q2, q3, q4, k1, k2, k3, k4, v1, v2, v3, v4, small_all,
    early_send, early_recv, send, recv, dq_send, dq_recv, dkv_send, dkv_recv, small_send, small_recv, pair_send, pair_recv, local,
):
    me = own_index()
    head, core = head_of(me)
    rows, width = frames.shape
    quarter = rows // 4
    sums = [sum_a, sum_b, sum_c, sum_q, sum_k, sum_v]
    news = [got_a, got_b, got_c]
    fetches = [
        pltpu.make_async_copy(src, dst, local.at[k])
        for k, (src, dst) in enumerate(
            (
                (keep_a, sum_a), (keep_b, sum_b), (keep_c, sum_c),
                (wq_in, wq), (wk_in, wk), (wv_in, wv), (gain_in, gain), (frames_in, frames), (grad_mid_in, grad_mid),
            )
        )
    ]
    for copy in fetches:
        copy.start()
    greet_all(me, n)
    sibling = sibling_of(core)
    swap = remote(dkv_in.at[:, 1 - core], theirs, pair_send.at[0], pair_recv.at[0], sibling)
    swap.start()
    act1_copy = remote(act1.at[1 - core], act1_2.at[pl.ds(rows, rows)], pair_send.at[1], pair_recv.at[1], sibling)

    def to_all(src_ref, dst_ref, sends, recvs):
        def copy_with(i, src):
            other = lax.rem(me + i, n)
            return remote(src_ref.at[other], dst_ref.at[src], sends.at[i], recvs.at[src], place(other))

        return copy_with

    dq_copy = to_all(dq_in, dq_all, dq_send, dq_recv)
    dkv_copy = to_all(total, dkv_all, dkv_send, dkv_recv)
    small_copy = to_all(small_in, small_all, small_send, small_recv)

    @pl.loop(1, n)
    def _(i):
        dq_copy(i, me).start()

    swap.wait()

    def add(j):
        return (dkv_in[j, core] + theirs[j]).astype(BF16)

    @pl.loop(1, n)
    def _(i):
        other = lax.rem(me + i, n)
        total[other] = add(other)
        dkv_copy(i, me).start()

    dkv_all[me] = add(me)
    dq_all[me] = dq_in[me]
    act1_copy.start()
    order = ("x", "y", "z0", "z1"), ("y", "x", "z0", "z1"), ("z0", "x", "y", "z1")
    landings = (q1, q2, q3, q4), (k1, k2, k3, k4), (v1, v2, v3, v4)
    late = [Part(sums[3 + k], ("z1", "z0", "y", "x"), order[k], landings[k], send.at[k], recv.at[k]) for k in range(3)]
    dims = ("z1", "z0", "y"), ("z1", "z0", "x"), ("z1", "y", "x")
    order = (
        (("y", "z0", "z1"),) * 3,
        (("x", "z0", "z1"), ("x", "z0", "z1"), ("z0", "x", "z1")),
        (("x", "y", "z1"), ("y", "x", "z1"), ("x", "y", "z1")),
    )
    landings = (a2, a3, a4), (b2, b3, b4), (c2, c3, c4)
    waves = []
    for u in range(3):
        band = slice(32 * u, 32 * u + 32)
        wave = []
        for k in range(3):
            wave.append(
                Part(
                    sums[k].at[:, :, :, band],
                    dims[k],
                    order[k][u],
                    [ref.at[(slice(None),) * lead + (band,)] for lead, ref in zip((2, 1, 0), landings[k])],
                    early_send.at[u, k],
                    early_recv.at[u, k],
                )
            )
        waves.append(wave)

    for u, wave in enumerate(waves):
        for k, part in enumerate(wave):
            whole, new = sums[k], news[k]
            if u == 0:
                fetches[k].wait()

            @pl.loop(0, 8)
            def _(j):
                at = (lax.div(j, 4), lax.rem(lax.div(j, 2), 2), lax.rem(j, 2), slice(32 * u, 32 * u + 32))
                whole[at] = (whole[at].astype(F32) + new[at].astype(F32)).astype(BF16)

            part.start()

    def advance(parts):
        for part in parts:
            part.finish()
            part.start()

    act1_own = pltpu.make_async_copy(act1.at[core], act1_2.at[pl.ds(0, rows)], local.at[9])
    act1_own.start()

    @pl.loop(1, n)
    def _(i):
        dq_copy(i, lax.rem(me + i, n)).wait()

    advance(waves[0])
    advance(waves[1])

    @pl.loop(1, n)
    def _(i):
        dkv_copy(i, lax.rem(me + i, n)).wait()

    advance(waves[0])
    advance(waves[2])
    def pair_with(k):
        columns = slice(k * width, (k + 1) * width)
        own, other = qkv2.at[pl.ds(0, rows), columns], qkv2.at[pl.ds(rows, rows), columns]
        return remote(own, other, pair_send.at[2 + k], pair_recv.at[2 + k], sibling)

    pairs = [pair_with(k) for k in range(3)]
    low_q, low_h = low_lanes((quarter, 128)), low_lanes((2 * quarter, 128))
    for zy in range(8):
        for s in range(2):
            j = (zy * 2 + s) * 2
            first = 2 * s * quarter
            a, b = dq_all[j].astype(F32), dq_all[j + 1].astype(F32)
            at = slice(zy * 128, (zy + 1) * 128)
            qkv2[first : first + quarter, at] = pair_low(a, b, low_q).astype(BF16)
            qkv2[first + quarter : first + 2 * quarter, at] = pair_high(a, b, low_q).astype(BF16)
    pairs[0].start()
    for zy in range(8):
        for s in range(2):
            j = (zy * 2 + s) * 2
            first = 2 * s * quarter
            a, b = dkv_all[j].astype(F32), dkv_all[j + 1].astype(F32)
            at = slice(width + zy * 128, width + (zy + 1) * 128)
            qkv2[first : first + 2 * quarter, at] = pair_low(a, b, low_h).astype(BF16)
            at = slice(2 * width + zy * 128, 2 * width + (zy + 1) * 128)
            qkv2[first : first + 2 * quarter, at] = pair_high(a, b, low_h).astype(BF16)
    pairs[1].start()
    pairs[2].start()
    advance(waves[1])
    act1_copy.wait()
    act1_own.wait()
    for k in range(3):
        pairs[k].wait()
        value = tn_dot(act1_2[...], qkv2[:, k * width : (k + 1) * width]).astype(BF16)
        for j in range(16):
            sums[3 + k][j // 8, j // 4 % 2, j // 2 % 2, j % 2] = value[j * 32 : (j + 1) * 32]
        late[k].start()

    for copy in fetches[3:]:
        copy.wait()
    g = nt_dot(qkv2[:rows, :width], wq[...])
    g += nt_dot(qkv2[:rows, width : 2 * width], wk[...])
    g += nt_dot(qkv2[:rows, 2 * width :], wv[...])
    advance(waves[2])

    x = frames[...]
    r = lax.rsqrt(jnp.mean(x * x, axis=-1, keepdims=True) + EPSILON)
    norm = x * r
    gain_grad = jnp.sum(g * norm, axis=0, keepdims=True)
    small_in[...] = jnp.zeros_like(small_in)
    for d in range(n):
        at = slice(d // 4 * 128, (d // 4 + 1) * 128)
        small_in[d, 0:1] = gain_grad[:, at]
        small_in[d, 1:2] = gain2_grad[:, at]
        small_in[d, 2:3] = b_down_grad[:, at]
        small_in[d, 3:4] = b_up_grad[:, d * 128 : (d + 1) * 128]

    @pl.loop(1, n)
    def _(i):
        small_copy(i, me).start()

    g = g * gain[...]
    frames_out[...] = grad_mid[...] + r * (g - norm * jnp.mean(g * norm, axis=-1, keepdims=True))
    small_all[me] = small_in[me]

    advance(late * 3)

    @pl.loop(1, n)
    def _(i):
        small_copy(i, lax.rem(me + i, n)).wait()

    part = width // n
    small_out[...] = pltpu.roll(jnp.sum(small_all[...], axis=0), lax.rem(128 - lax.rem(me, 128 // part) * part, 128), 1)
    small_out[3:4] = jnp.sum(small_all[:, 3:4], axis=0)
    for u, wave in enumerate(waves):
        down_out[32 * u : 32 * u + 32] = wave[0].last()
        up_out[:, 1024 * u : 1024 * u + 1024] = wave[1].last()
    down_out[96:] = waves[0][2].last()
    up_out[:, 3072:] = waves[1][2].last()
    o_out[...] = waves[2][2].last()
    q_out[...] = late[0].last()
    k_out[...] = late[1].last()
    v_out[...] = late[2].last()


def finish(dkv, dq, act1, frames, grad_mid, gain, gain2_grad, b_up_grad, b_down_grad, weights, keeps, gots, n):
    rows, width = frames.shape
    keeps, gots = [[x.reshape(2, 2, 2, *x.shape[1:]) for x in xs] for xs in (keeps, gots)]
    half = dkv.shape[2]
    vmem = pl.BlockSpec(memory_space=pltpu.VMEM)
    hbm = pl.BlockSpec(memory_space=pltpu.HBM)
    shape = jax.ShapeDtypeStruct
    thin, wide = (32, width), (96, width)
    buffers = [pltpu.VMEM((2, 2, 2, *wide), BF16)] * 3 + [pltpu.VMEM((2, 2, 2, 2, *thin), BF16)] * 3
    buffers += [pltpu.VMEM((2,) * k + wide, BF16) for k in (2, 1, 0)] * 3
    buffers += [pltpu.VMEM((2,) * k + thin, BF16) for k in (3, 2, 1, 0)] * 3
    over_devices = [pltpu.SemaphoreType.DMA((n,))] * 6
    return pl.pallas_call(
        functools.partial(finish_kernel, n),
        in_specs=[vmem] * 8 + [hbm] * 10,
        out_specs=[vmem] * 8,
        out_shape=[pltpu.VMEM((rows, width), F32)]
        + [pltpu.VMEM(thin, F32)] * 4
        + [pltpu.VMEM((32, 4 * width), F32), pltpu.VMEM((128, width), F32), pltpu.VMEM((8, 128), F32)],
        scratch_shapes=[
            pltpu.VMEM((n, half, 128), F32),
            pltpu.VMEM((n, half, 128), BF16),
            pltpu.VMEM((n, half, 128), BF16),
            pltpu.VMEM((n, half // 2, 128), BF16),
            pltpu.VMEM((1, width), F32),
            pltpu.VMEM((rows, width), F32),
            pltpu.VMEM((rows, width), F32),
            pltpu.VMEM((width, width), BF16),
            pltpu.VMEM((width, width), BF16),
            pltpu.VMEM((width, width), BF16),
            pltpu.VMEM((n, 8, 128), F32),
            pltpu.VMEM((2 * rows, width // 2), BF16),
            pltpu.VMEM((2 * rows, 3 * width), BF16),
            *buffers,
            pltpu.VMEM((n, 8, 128), F32),
            pltpu.SemaphoreType.DMA((3, 3, 3)),
            pltpu.SemaphoreType.DMA((3, 3, 3)),
            pltpu.SemaphoreType.DMA((3, 4)),
            pltpu.SemaphoreType.DMA((3, 4)),
            *over_devices,
            pltpu.SemaphoreType.DMA((5,)),
            pltpu.SemaphoreType.DMA((5,)),
            pltpu.SemaphoreType.DMA((10,)),
        ],
        compiler_params=pltpu.CompilerParams(
            collective_id=4, has_side_effects=True, vmem_limit_bytes=36 << 20
        ),
        name="finish",
    )(
        *in_vmem(dkv, dq, gain2_grad, b_up_grad, b_down_grad, *gots),
        *in_hbm(gain.reshape(1, width), act1, frames, grad_mid, *weights, *keeps),
    )


def emit_kernel(n, small, *refs):
    sems = refs[-1]
    copies = [pltpu.make_async_copy(refs[k], refs[n + k], sems.at[k]) for k in range(n)]
    for copy in copies:
        copy.start()
    for row, out in enumerate(refs[2 * n : -1]):
        out[...] = small[row : row + 1, : out.shape[1]]
    for copy in copies:
        copy.wait()


def emit(small, widths, *arrays):
    n = len(arrays)
    vmem = pl.BlockSpec(memory_space=pltpu.VMEM)
    return pl.pallas_call(
        functools.partial(emit_kernel, n),
        in_specs=[vmem] * (n + 1),
        out_specs=[pl.BlockSpec(memory_space=pltpu.HBM)] * n + [vmem] * len(widths),
        out_shape=[pltpu.HBM(x.shape, x.dtype) for x in arrays]
        + [jax.ShapeDtypeStruct((1, width), F32) for width in widths],
        scratch_shapes=[pltpu.SemaphoreType.DMA((n,))],
        compiler_params=pltpu.CompilerParams(vmem_limit_bytes=8 << 20),
        name="emit",
    )(*in_vmem(small, *arrays))


def shards_heads(
    frames, lengths, norm1_gain, w_query, w_key, w_value, w_out, norm2_gain, w_up, b_up, w_down, b_down, cotangent
):
    rows, width = frames.shape
    n = lax.axis_size("blk") * lax.axis_size("grp")
    half = rows // 2
    core_word = bit_of("core").astype(jnp.int32).reshape(1)
    qpos = jnp.asarray(packed_positions(n, half))

    kv, q, act1 = to_heads(frames, norm1_gain, w_query, w_key, w_value, n)
    kv_rows = kv.reshape(n * rows, 128)
    out_t, lse, out_blocks = mix(lengths, core_word, kv_rows, q, qpos)
    mixed_blocks = exchange(out_blocks, n, 2)
    (
        layer_out, grad_middle, grad_blocks, hidden, grad_before, act2, mixed, grad_low, grad_attn,
        norm2_gain_grad, b_up_grad, b_down_grad,
    ) = feed(mixed_blocks, frames, cotangent, w_out, norm2_gain, w_up, b_up, w_down, b_down)
    grad_blocks, *parts = share(grad_blocks, hidden, grad_before, act2, mixed, grad_low, grad_attn, n)
    keeps = parts[0::2]
    gots = [flipped(part, axis) for part, axis in zip(parts[1::2], ("x", "y", "z0"))]
    dkv, dq = mix_back(lengths, core_word, kv_rows, q, *in_vmem(grad_blocks), qpos, out_t, lse)

    frames_grad, w_query_grad, w_key_grad, w_value_grad, w_out_grad, w_up_grad, w_down_grad, small = finish(
        dkv.reshape(n, 2, half, 128), dq, act1, frames, grad_middle, norm1_gain, norm2_gain_grad, b_up_grad,
        b_down_grad, (w_query, w_key, w_value), keeps, gots, n,
    )
    part = width // n
    (
        layer_out, frames_grad, w_query_grad, w_key_grad, w_value_grad, w_out_grad, w_up_grad, w_down_grad, *vectors
    ) = emit(
        small, (part, part, part, b_up.shape[0] // n),
        layer_out, frames_grad, w_query_grad, w_key_grad, w_value_grad, w_out_grad, w_up_grad, w_down_grad,
    )
    return (
        layer_out,
        frames_grad,
        vectors[0].reshape(-1),
        w_query_grad,
        w_key_grad,
        w_value_grad,
        w_out_grad,
        vectors[1].reshape(-1),
        w_up_grad,
        vectors[3].reshape(-1),
        w_down_grad,
        vectors[2].reshape(-1),
    )


def solution(mesh):
    if mesh.shape["blk"] != 16 or mesh.shape["grp"] != 2:
        return solution_ring(mesh)
    split = P(ALL, None)
    return jax.shard_map(
        shards_heads,
        mesh=mesh,
        in_specs=(split, P(), P(), P(), P(), P(), P(), P(), P(), P(), P(), P(), split),
        out_specs=(split, split, P(ALL), split, split, split, split, P(ALL), split, P(ALL), split, P(ALL)),
        check_vma=False,
    )
```

```python
import functools

import jax
import jax.numpy as jnp
import numpy as np
from jax import lax
from jax.experimental import pallas as pl
from jax.experimental.pallas import tpu as pltpu
from jax.sharding import PartitionSpec as P

HEAD_DIM = 64
ITEM_MAX = 4096


EPSILON = 1e-05
MASKED = -1e30
SCALING = 0.125


def shortened(array):

    def short(part):
        return part.astype(jnp.bfloat16) if part.dtype == jnp.float32 else part

    return jax.tree.map(short, array)


def passed_along(block, axis, distance):
    devices = range(lax.axis_size(axis))
    route = [(i - distance, i) for i in devices if i - distance in devices]
    return lax.ppermute(block, axis, route)


def rms_norm(values, gain):
    return values * lax.rsqrt(jnp.mean(values * values, axis=-1, keepdims=True) + EPSILON) * gain


def gelu_exact(values):
    return jax.nn.gelu(values, approximate=False)


def item_starts(lengths, positions):
    ends = jnp.cumsum(lengths)
    offsets = ends - lengths
    before = offsets[None, :] <= positions[:, None]
    return jnp.max(jnp.where(before, offsets[None, :], 0), axis=1)


def live_mask(query_pos, query_start, key_first, key_count):
    key_pos = key_first + jnp.arange(key_count, dtype=jnp.int32)
    return (key_pos[None, :] >= query_start[:, None]) & (key_pos[None, :] <= query_pos[:, None])


def split_heads(matrix):
    return matrix.reshape(matrix.shape[0], matrix.shape[1] // HEAD_DIM, HEAD_DIM)


def merge_heads(tensor):
    return tensor.reshape(tensor.shape[0], tensor.shape[1] * tensor.shape[2])


def scores_of(queries3, keys_block, mask):
    raw = jnp.einsum(
        "qhd,khd->hqk", queries3, split_heads(keys_block), preferred_element_type=jnp.float32
    )
    return jnp.where(mask[None], raw * SCALING, MASKED)


def left_dot(left, right):
    return lax.dot_general(
        left, right, (((0,), (0,)), ((), ())), preferred_element_type=jnp.float32
    )


def right_dot(left, right):
    return lax.dot_general(
        left, right, (((1,), (1,)), ((), ())), preferred_element_type=jnp.float32
    )


def grad_parts(queries3, grad_out3, log_total, delta, keys_block, values_block, mask):
    probs = jnp.exp(scores_of(queries3, keys_block, mask) - log_total[:, :, None])
    grad_probs = jnp.einsum(
        "qhd,khd->hqk", grad_out3, split_heads(values_block), preferred_element_type=jnp.float32
    )
    grad_scores = (probs * (grad_probs - delta[:, :, None])).astype(jnp.bfloat16)
    return (probs.astype(jnp.bfloat16), grad_scores)


def key_terms(queries3, grad_out3, probs_low, grad_scores):
    grad_keys = jnp.einsum(
        "hqk,qhd->khd", grad_scores, queries3, preferred_element_type=jnp.float32
    )
    grad_values = jnp.einsum(
        "hqk,qhd->khd", probs_low, grad_out3, preferred_element_type=jnp.float32
    )
    return (merge_heads(grad_keys), merge_heads(grad_values))


def query_term(grad_scores, keys_block):
    return jnp.einsum(
        "hqk,khd->qhd", grad_scores, split_heads(keys_block), preferred_element_type=jnp.float32
    )


def shards_ring(
    frames,
    lengths,
    norm1_gain,
    w_query,
    w_key,
    w_value,
    w_out,
    norm2_gain,
    w_up,
    b_up,
    w_down,
    b_down,
    cotangent,
):
    row_count = frames.shape[0]
    width = frames.shape[1]
    heads = width // HEAD_DIM
    groups = lax.axis_size("grp")
    block_rows = row_count * groups
    span = (ITEM_MAX + block_rows - 2) // block_rows
    blk_index = lax.axis_index("blk")
    sub_index = lax.axis_index("grp")
    block_first = blk_index * block_rows
    query_pos = block_first + sub_index * row_count + jnp.arange(row_count, dtype=jnp.int32)
    query_start = item_starts(lengths, query_pos)
    back_steps = jnp.arange(span + 1, dtype=jnp.int32)
    normed1, norm1_back = jax.vjp(rms_norm, frames, norm1_gain)
    act1 = normed1.astype(jnp.bfloat16)
    queries = jnp.dot(act1, w_query, preferred_element_type=jnp.float32).astype(jnp.bfloat16)
    keys_own = jnp.dot(act1, w_key, preferred_element_type=jnp.float32).astype(jnp.bfloat16)
    values_own = jnp.dot(act1, w_value, preferred_element_type=jnp.float32).astype(jnp.bfloat16)
    queries3 = split_heads(queries)
    block_keys, block_values = (
        lax.all_gather(keys_own, "grp", axis=0, tiled=True),
        lax.all_gather(values_own, "grp", axis=0, tiled=True),
    )

    def cycle_step(carry, unused_input):
        moved = jax.tree.map(
            lambda part, own: part.astype(own.dtype),
            passed_along(shortened(carry), "blk", 1),
            carry,
        )
        return (moved, moved)

    unused_last, far_blocks = lax.scan(cycle_step, (block_keys, block_values), None, length=span)
    keys_all = jnp.concatenate([block_keys[None], far_blocks[0]], axis=0)
    values_all = jnp.concatenate([block_values[None], far_blocks[1]], axis=0)

    def mask_for(back):
        return live_mask(query_pos, query_start, block_first - back * block_rows, block_rows)

    def total_step(carry, inputs):
        run_max, run_sum = carry
        keys_block, back = inputs
        scores = scores_of(queries3, keys_block, mask_for(back))
        new_max = jnp.maximum(run_max, jnp.max(scores, axis=-1))
        run_sum = run_sum * jnp.exp(run_max - new_max) + jnp.sum(
            jnp.exp(scores - new_max[:, :, None]), axis=-1
        )
        return ((new_max, run_sum), None)

    start_max = jnp.full((heads, row_count), MASKED, jnp.float32)
    start_sum = jnp.zeros((heads, row_count), jnp.float32)
    (top_max, top_sum), unused_out = lax.scan(
        total_step, (start_max, start_sum), (keys_all, back_steps)
    )
    log_total = top_max + jnp.log(top_sum)

    def mix_step(total, inputs):
        keys_block, values_block, back = inputs
        probs = jnp.exp(
            scores_of(queries3, keys_block, mask_for(back)) - log_total[:, :, None]
        ).astype(jnp.bfloat16)
        return (
            total
            + jnp.einsum(
                "hqk,khd->qhd", probs, split_heads(values_block), preferred_element_type=jnp.float32
            ),
            None,
        )

    zero_query = jnp.zeros((row_count, heads, HEAD_DIM), jnp.float32)
    mixed_sum, unused_out = lax.scan(mix_step, zero_query, (keys_all, values_all, back_steps))
    mixed = merge_heads(mixed_sum).astype(jnp.bfloat16)
    middle = frames + jnp.dot(mixed, w_out, preferred_element_type=jnp.float32)
    normed2, norm2_back = jax.vjp(rms_norm, middle, norm2_gain)
    act2 = normed2.astype(jnp.bfloat16)
    before = jnp.dot(act2, w_up, preferred_element_type=jnp.float32) + b_up
    activated, gelu_back = jax.vjp(gelu_exact, before)
    hidden = activated.astype(jnp.bfloat16)
    layer_out = middle + jnp.dot(hidden, w_down, preferred_element_type=jnp.float32) + b_down
    grad_low = cotangent.astype(jnp.bfloat16)
    b_down_grad = jnp.sum(grad_low.astype(jnp.float32), axis=0)
    w_down_grad = left_dot(hidden, grad_low)
    grad_before = gelu_back(right_dot(grad_low, w_down))[0].astype(jnp.bfloat16)
    b_up_grad = jnp.sum(grad_before.astype(jnp.float32), axis=0)
    w_up_grad = left_dot(act2, grad_before)
    grad_mid_norm, norm2_gain_grad = norm2_back(right_dot(grad_before, w_up))
    grad_middle = cotangent + grad_mid_norm
    grad_attn = grad_middle.astype(jnp.bfloat16)
    w_out_grad = left_dot(mixed, grad_attn)
    grad_mixed = right_dot(grad_attn, w_out).astype(jnp.bfloat16)
    grad_out3 = split_heads(grad_mixed)

    def delta_step(total, inputs):
        keys_block, values_block, back = inputs
        probs = jnp.exp(scores_of(queries3, keys_block, mask_for(back)) - log_total[:, :, None])
        grad_probs = jnp.einsum(
            "qhd,khd->hqk", grad_out3, split_heads(values_block), preferred_element_type=jnp.float32
        )
        return (total + jnp.sum(probs * grad_probs, axis=-1), None)

    delta, unused_out = lax.scan(
        delta_step, jnp.zeros((heads, row_count), jnp.float32), (keys_all, values_all, back_steps)
    )
    zero_block = jnp.zeros((block_rows, width), jnp.float32)

    def return_step(carry, inputs):
        grad_q, travel = carry
        keys_block, values_block, back = inputs
        probs_low, grad_scores = grad_parts(
            queries3, grad_out3, log_total, delta, keys_block, values_block, mask_for(back)
        )
        grad_keys, grad_values = key_terms(queries3, grad_out3, probs_low, grad_scores)
        moved = (
            passed_along((travel[0] + grad_keys).astype(jnp.bfloat16), "blk", -1).astype(
                jnp.float32
            ),
            passed_along((travel[1] + grad_values).astype(jnp.bfloat16), "blk", -1).astype(
                jnp.float32
            ),
        )
        return ((grad_q + query_term(grad_scores, keys_block), moved), None)

    (grad_q, travel), unused_out = lax.scan(
        return_step,
        (zero_query, (zero_block, zero_block)),
        (far_blocks[0], far_blocks[1], back_steps[1:]),
        reverse=True,
    )
    probs_low, grad_scores = grad_parts(
        queries3, grad_out3, log_total, delta, block_keys, block_values, mask_for(0)
    )
    grad_keys, grad_values = key_terms(queries3, grad_out3, probs_low, grad_scores)
    grad_q = grad_q + query_term(grad_scores, block_keys)
    block_grad_keys = travel[0] + grad_keys
    block_grad_values = travel[1] + grad_values
    grad_keys_rows, grad_values_rows = (
        lax.psum_scatter(
            block_grad_keys.astype(jnp.bfloat16), "grp", scatter_dimension=0, tiled=True
        ).astype(jnp.float32),
        lax.psum_scatter(
            block_grad_values.astype(jnp.bfloat16), "grp", scatter_dimension=0, tiled=True
        ).astype(jnp.float32),
    )
    grad_keys_low = (grad_keys_rows * SCALING).astype(jnp.bfloat16)
    grad_values_low = grad_values_rows.astype(jnp.bfloat16)
    grad_queries_low = (merge_heads(grad_q) * SCALING).astype(jnp.bfloat16)
    w_query_grad = left_dot(act1, grad_queries_low)
    w_key_grad = left_dot(act1, grad_keys_low)
    w_value_grad = left_dot(act1, grad_values_low)
    grad_act1 = (
        right_dot(grad_queries_low, w_query)
        + right_dot(grad_keys_low, w_key)
        + right_dot(grad_values_low, w_value)
    )
    grad_frames_norm, norm1_gain_grad = norm1_back(grad_act1)
    frames_grad = grad_middle + grad_frames_norm
    shares = (
        lax.psum_scatter(norm1_gain_grad, ("blk", "grp"), scatter_dimension=0, tiled=True),
        lax.psum_scatter(w_query_grad, ("blk", "grp"), scatter_dimension=0, tiled=True),
        lax.psum_scatter(w_key_grad, ("blk", "grp"), scatter_dimension=0, tiled=True),
        lax.psum_scatter(w_value_grad, ("blk", "grp"), scatter_dimension=0, tiled=True),
        lax.psum_scatter(w_out_grad, ("blk", "grp"), scatter_dimension=0, tiled=True),
        lax.psum_scatter(norm2_gain_grad, ("blk", "grp"), scatter_dimension=0, tiled=True),
        lax.psum_scatter(w_up_grad, ("blk", "grp"), scatter_dimension=0, tiled=True),
        lax.psum_scatter(b_up_grad, ("blk", "grp"), scatter_dimension=0, tiled=True),
        lax.psum_scatter(w_down_grad, ("blk", "grp"), scatter_dimension=0, tiled=True),
        lax.psum_scatter(b_down_grad, ("blk", "grp"), scatter_dimension=0, tiled=True),
    )
    return (
        layer_out,
        frames_grad,
        shares[0],
        shares[1],
        shares[2],
        shares[3],
        shares[4],
        shares[5],
        shares[6],
        shares[7],
        shares[8],
        shares[9],
    )


def solution_ring(mesh):
    placed = (
        P(("blk", "grp"), None),
        P(),
        P(),
        P(),
        P(),
        P(),
        P(),
        P(),
        P(),
        P(),
        P(),
        P(),
        P(("blk", "grp"), None),
    )
    return jax.shard_map(
        shards_ring,
        mesh=mesh,
        in_specs=placed,
        out_specs=(
            P(("blk", "grp"), None),
            P(("blk", "grp"), None),
            P(("blk", "grp")),
            P(("blk", "grp"), None),
            P(("blk", "grp"), None),
            P(("blk", "grp"), None),
            P(("blk", "grp"), None),
            P(("blk", "grp")),
            P(("blk", "grp"), None),
            P(("blk", "grp")),
            P(("blk", "grp"), None),
            P(("blk", "grp")),
        ),
        check_vma=False,
    )


LOG2E = 1.4426950408889634
F32, BF16 = jnp.float32, jnp.bfloat16


def nt_dot(a, b):
    return lax.dot_general(a, b, (((1,), (1,)), ((), ())), preferred_element_type=F32)


def nn_dot(a, b):
    return lax.dot_general(a, b, (((1,), (0,)), ((), ())), preferred_element_type=F32)


def low_lanes(shape):
    return lax.broadcasted_iota(jnp.int32, shape, 1) < 64


def pair_low(a, b, low):
    return jnp.where(low, a, pltpu.roll(b, 64, 1))


def pair_high(a, b, low):
    return jnp.where(low, pltpu.roll(a, 64, 1), b)


def store_halves(ref, x):
    low = low_lanes((x.shape[0], 128))
    for p in range(x.shape[1] // 256):
        a, b = x[:, p * 256 : p * 256 + 128], x[:, p * 256 + 128 : (p + 1) * 256]
        ref[0, :, p * 128 : (p + 1) * 128] = pair_low(a, b, low).astype(BF16)
        ref[1, :, p * 128 : (p + 1) * 128] = pair_high(a, b, low).astype(BF16)


def block_bounds(len_ref, items, qpos, first, last, key_block):
    off = jnp.int32(0)
    start = jnp.zeros(qpos.shape, jnp.int32)
    s_first, s_last = jnp.int32(0), jnp.int32(0)
    for i in range(items):
        start = jnp.where(qpos >= off, off, start)
        s_first = jnp.where(first >= off, off, s_first)
        s_last = jnp.where(last >= off, off, s_last)
        off = off + len_ref[i]
    lo, hi = s_first // key_block, last // key_block + 1
    f0 = jnp.clip((s_last + key_block - 1) // key_block, lo, hi)
    f1 = jnp.clip((first + 1) // key_block, f0, hi)
    return start, lo, f0, f1, hi


def query_ends(i, chunks, half, core):
    first = i * chunks * 2 * half + core * half
    return first, first + (chunks - 1) * 2 * half + half - 1


def spread(packed, low, to_high):
    f = packed.astype(F32)
    other = pltpu.roll(f, 64, 1)
    zero = jnp.zeros_like(f)
    if to_high:
        return jnp.where(low, zero, other).astype(BF16), jnp.where(low, zero, f).astype(BF16)
    return jnp.where(low, f, zero).astype(BF16), jnp.where(low, other, zero).astype(BF16)


def mix_kernel(
    items, chunks, key_block,
    len_ref, core_ref, kv_ref, qp_ref, qpos_ref,
    out_t_ref, lse_ref, out_ref,
    kv_t, qz, acc, m_ref, l_ref,
):
    i = pl.program_id(0)
    half = 2 * qp_ref.shape[1]
    n = chunks * half
    core = core_ref[0]

    @pl.when(i == 0)
    def _():
        for c in range(kv_ref.shape[0] // 512):
            at = slice(c * 512, (c + 1) * 512)
            kv_t[:, at] = kv_ref[at, :].astype(F32).T.astype(BF16)

    low = low_lanes((half // 2, 128))
    for c in range(chunks):
        a, b = spread(qp_ref[c], low, False)
        qz[c * half : c * half + half // 2] = a
        qz[c * half + half // 2 : (c + 1) * half] = b
    qpos = qpos_ref[...] + core * half
    first, last = query_ends(i, chunks, half, core)
    start, lo, f0, f1, hi = block_bounds(len_ref, items, qpos, first, last, key_block)
    acc[...] = jnp.zeros_like(acc)
    m_ref[...] = jnp.full_like(m_ref, MASKED)
    l_ref[...] = jnp.zeros_like(l_ref)

    def step(j, masked):
        at = pl.ds(pl.multiple_of(j * key_block, key_block), key_block)
        s = nt_dot(kv_ref[at, :], qz[...]) * LOG2E
        if masked:
            kpos = j * key_block + lax.broadcasted_iota(jnp.int32, (key_block, 1), 0)
            s = jnp.where((kpos >= start) & (kpos <= qpos), s, MASKED)
        m_old = m_ref[...]
        m_new = jnp.maximum(m_old, jnp.max(s, axis=0, keepdims=True))
        p = jnp.exp2(s - m_new)
        alpha = jnp.exp2(m_old - m_new)
        m_ref[...] = m_new
        l_ref[...] = l_ref[...] * alpha + jnp.sum(p, axis=0, keepdims=True)
        acc[...] = acc[...] * alpha + nn_dot(kv_t[64:, at], p.astype(BF16))

    lax.fori_loop(lo, f0, lambda j, c: (step(j, True), c)[1], 0)
    lax.fori_loop(f0, f1, lambda j, c: (step(j, False), c)[1], 0)
    lax.fori_loop(f1, hi, lambda j, c: (step(j, True), c)[1], 0)
    out_t = acc[...] / l_ref[...]
    out_t_ref[...] = out_t
    lse_ref[...] = m_ref[...] + jnp.log2(l_ref[...])
    doubled = jnp.concatenate([out_t, out_t], axis=0).T
    for c in range(chunks):
        a = doubled[c * half : c * half + half // 2]
        b = doubled[c * half + half // 2 : (c + 1) * half]
        out_ref[c] = jnp.where(low, a, b).astype(BF16)


def mix(lengths, core, kv, qp, qpos, chunks=4, key_block=768):
    total = kv.shape[0]
    n_src, quarter = qp.shape[0], qp.shape[1]
    half = 2 * quarter
    n = chunks * half
    whole = lambda i, *_: (0, 0)
    return pl.pallas_call(
        functools.partial(mix_kernel, lengths.shape[0], chunks, key_block),
        grid_spec=pltpu.PrefetchScalarGridSpec(
            num_scalar_prefetch=2,
            grid=(n_src // chunks,),
            in_specs=[
                pl.BlockSpec((total, 128), whole),
                pl.BlockSpec((chunks, quarter, 128), lambda i, *_: (i, 0, 0)),
                pl.BlockSpec((1, n), lambda i, *_: (0, i)),
            ],
            out_specs=[
                pl.BlockSpec((64, n), lambda i, *_: (0, i)),
                pl.BlockSpec((1, n), lambda i, *_: (0, i)),
                pl.BlockSpec((chunks, quarter, 128), lambda i, *_: (i, 0, 0)),
            ],
            scratch_shapes=[
                pltpu.VMEM((128, total), BF16),
                pltpu.VMEM((n, 128), BF16),
                pltpu.VMEM((64, n), F32),
                pltpu.VMEM((1, n), F32),
                pltpu.VMEM((1, n), F32),
            ],
        ),
        out_shape=[
            jax.ShapeDtypeStruct((64, n_src * half), F32),
            jax.ShapeDtypeStruct((1, n_src * half), F32),
            jax.ShapeDtypeStruct((n_src, quarter, 128), BF16),
        ],
        compiler_params=pltpu.CompilerParams(vmem_limit_bytes=22 << 20),
        cost_estimate=pl.CostEstimate(flops=25_000_000_000, bytes_accessed=8 << 20, transcendentals=0),
        name="mix",
    )(lengths, core, kv, qp, qpos)


def back_kernel(
    items, chunks, key_block,
    len_ref, core_ref, kv_ref, qp_ref, dp_ref, qpos_ref, out_t_ref, lse_ref,
    dkv_ref, dq_ref,
    kv_t, qd, dq_acc,
):
    i = pl.program_id(0)
    half = 2 * qp_ref.shape[1]
    n = chunks * half
    core = core_ref[0]

    @pl.when(i == 0)
    def _():
        for c in range(kv_ref.shape[0] // 512):
            at = slice(c * 512, (c + 1) * 512)
            kv_t[:, at] = kv_ref[at, :].astype(F32).T.astype(BF16)
        dkv_ref[...] = jnp.zeros_like(dkv_ref)

    low = low_lanes((half // 2, 128))
    for c in range(chunks):
        a, b = spread(qp_ref[c], low, False)
        qd[c * half : c * half + half // 2] = a
        qd[c * half + half // 2 : (c + 1) * half] = b
        a, b = spread(dp_ref[c], low, True)
        qd[n + c * half : n + c * half + half // 2] = a
        qd[n + c * half + half // 2 : n + (c + 1) * half] = b
    do_t = qd[n:, :].astype(F32).T[64:]
    delta = jnp.sum(do_t * out_t_ref[...], axis=0, keepdims=True)
    lse = lse_ref[...]
    qpos = qpos_ref[...] + core * half
    first, last = query_ends(i, chunks, half, core)
    start, lo, f0, f1, hi = block_bounds(len_ref, items, qpos, first, last, key_block)
    dq_acc[...] = jnp.zeros_like(dq_acc)

    def step(j, masked):
        at = pl.ds(pl.multiple_of(j * key_block, key_block), key_block)
        both = nt_dot(kv_ref[at, :], qd[...])
        s = both[:, :n] * LOG2E
        if masked:
            kpos = j * key_block + lax.broadcasted_iota(jnp.int32, (key_block, 1), 0)
            s = jnp.where((kpos >= start) & (kpos <= qpos), s, MASKED)
        p = jnp.exp2(s - lse)
        ds = (p * (both[:, n:] - delta)).astype(BF16)
        dq_acc[...] += nn_dot(kv_t[:64, at], ds)
        dkv_ref[at, :] += nn_dot(ds, qd[:n, :]) + nn_dot(p.astype(BF16), qd[n:, :])

    lax.fori_loop(lo, f0, lambda j, c: (step(j, True), c)[1], 0)
    lax.fori_loop(f0, f1, lambda j, c: (step(j, False), c)[1], 0)
    lax.fori_loop(f1, hi, lambda j, c: (step(j, True), c)[1], 0)
    dq_t = dq_acc[...] * 0.125
    doubled = jnp.concatenate([dq_t, dq_t], axis=0).T
    for c in range(chunks):
        a = doubled[c * half : c * half + half // 2]
        b = doubled[c * half + half // 2 : (c + 1) * half]
        dq_ref[c] = jnp.where(low, a, b).astype(BF16)


def mix_back(lengths, core, kv, qp, dp, qpos, out_t, lse, chunks=4, key_block=768):
    total = kv.shape[0]
    n_src, quarter = qp.shape[0], qp.shape[1]
    half = 2 * quarter
    n = chunks * half
    whole = lambda i, *_: (0, 0)
    rows = lambda i, *_: (0, i)
    blocks = pl.BlockSpec((chunks, quarter, 128), lambda i, *_: (i, 0, 0))
    return pl.pallas_call(
        functools.partial(back_kernel, lengths.shape[0], chunks, key_block),
        grid_spec=pltpu.PrefetchScalarGridSpec(
            num_scalar_prefetch=2,
            grid=(n_src // chunks,),
            in_specs=[
                pl.BlockSpec((total, 128), whole),
                blocks,
                blocks,
                pl.BlockSpec((1, n), rows),
                pl.BlockSpec((64, n), rows),
                pl.BlockSpec((1, n), rows),
            ],
            out_specs=[pl.BlockSpec((total, 128), whole), blocks],
            scratch_shapes=[
                pltpu.VMEM((128, total), BF16),
                pltpu.VMEM((2 * n, 128), BF16),
                pltpu.VMEM((64, n), F32),
            ],
        ),
        out_shape=[
            jax.ShapeDtypeStruct((total, 128), F32),
            jax.ShapeDtypeStruct((n_src, quarter, 128), BF16),
        ],
        compiler_params=pltpu.CompilerParams(vmem_limit_bytes=22 << 20),
        cost_estimate=pl.CostEstimate(flops=40_000_000_000, bytes_accessed=8 << 20, transcendentals=0),
        name="mix_back",
    )(lengths, core, kv, qp, dp, qpos, out_t, lse)


def packed_positions(n_src, half):
    j = np.arange(n_src * half)
    return ((j // half) * 2 * half + j % half).astype(np.int32)[None]


def feed_kernel(
    blocks_ref, frames_ref, cot_ref, w_out_ref, gain_ref, w_up_ref, b_up_ref, w_down_ref, b_down_ref,
    out_ref, grad_mid_ref, grad_blocks_ref, hidden_ref, grad_before_ref, act2_ref, mixed_ref, low_ref, attn_ref,
    gain_grad_ref, b_up_grad_ref, b_down_grad_ref,
    mixed, act2, act_grad,
):
    i = pl.program_id(0)
    rows = frames_ref.shape[0]
    quarter = rows // 4
    low_q = low_lanes((quarter, 128))

    @pl.when(i == 0)
    def _():
        for zy in range(8):
            for s in range(2):
                a = blocks_ref[(zy * 2 + s) * 2].astype(F32)
                b = blocks_ref[(zy * 2 + s) * 2 + 1].astype(F32)
                at = slice(zy * 128, (zy + 1) * 128)
                first = 2 * s * quarter
                mixed[first : first + quarter, at] = pair_low(a, b, low_q)
                mixed[first + quarter : first + 2 * quarter, at] = pair_high(a, b, low_q)
        store_halves(mixed_ref, mixed[...])
        middle = frames_ref[...] + nn_dot(mixed[...].astype(BF16), w_out_ref[...])
        r = lax.rsqrt(jnp.mean(middle * middle, axis=-1, keepdims=True) + EPSILON)
        normed = middle * r * gain_ref[...]
        act2[...] = normed.astype(BF16)
        store_halves(act2_ref, normed)
        grad_mid_ref[...] = middle
        out_ref[...] = middle + b_down_ref[...]
        grad_low = cot_ref[...].astype(BF16)
        low_ref[...] = grad_low
        b_down_grad_ref[...] = jnp.sum(grad_low.astype(F32), axis=0, keepdims=True)
        act_grad[...] = jnp.zeros_like(act_grad)

    before = nn_dot(act2[...], w_up_ref[...]) + b_up_ref[...]
    cdf = 0.5 + 0.5 * lax.erf(before * 0.7071067811865476)
    pdf = jnp.exp(-0.5 * before * before) * 0.3989422804014327
    hidden = (before * cdf).astype(BF16)
    step = hidden.shape[1] // 2
    hidden_ref[0] = hidden[:, :step]
    hidden_ref[1] = hidden[:, step:]
    out_ref[...] += nn_dot(hidden, w_down_ref[...])
    grad_before = (nt_dot(low_ref[...], w_down_ref[...]) * (cdf + before * pdf)).astype(BF16)
    grad_before_ref[...] = grad_before
    b_up_grad_ref[...] = jnp.sum(grad_before.astype(F32), axis=0, keepdims=True)
    act_grad[...] += nt_dot(grad_before, w_up_ref[...])

    @pl.when(i == pl.num_programs(0) - 1)
    def _():
        middle = grad_mid_ref[...]
        r = lax.rsqrt(jnp.mean(middle * middle, axis=-1, keepdims=True) + EPSILON)
        n = middle * r
        g = act_grad[...]
        gain_grad_ref[...] = jnp.sum(g * n, axis=0, keepdims=True)
        g = g * gain_ref[...]
        grad_mid = cot_ref[...] + r * (g - n * jnp.mean(g * n, axis=-1, keepdims=True))
        grad_mid_ref[...] = grad_mid
        grad_attn = grad_mid.astype(BF16)
        attn_ref[...] = grad_attn
        grad_mixed = nt_dot(grad_attn, w_out_ref[...])
        for zy in range(8):
            for s in range(2):
                at = slice(zy * 128, (zy + 1) * 128)
                first = 2 * s * quarter
                a = grad_mixed[first : first + quarter, at]
                b = grad_mixed[first + quarter : first + 2 * quarter, at]
                grad_blocks_ref[(zy * 2 + s) * 2] = pair_low(a, b, low_q).astype(BF16)
                grad_blocks_ref[(zy * 2 + s) * 2 + 1] = pair_high(a, b, low_q).astype(BF16)


def feed(blocks, frames, cotangent, w_out, gain, w_up, b_up, w_down, b_down):
    rows, width = frames.shape
    ff = w_up.shape[1]
    steps = 8
    step = ff // steps
    fixed = lambda *shape: pl.BlockSpec(shape, lambda i: (0,) * len(shape))
    columns = lambda *shape: pl.BlockSpec(shape, lambda i: (0,) * (len(shape) - 1) + (i,))
    shape = jax.ShapeDtypeStruct
    return pl.pallas_call(
        feed_kernel,
        grid=(steps,),
        in_specs=[
            fixed(*blocks.shape),
            fixed(rows, width),
            fixed(rows, width),
            fixed(width, width),
            fixed(1, width),
            columns(width, step),
            columns(1, step),
            pl.BlockSpec((step, width), lambda i: (i, 0)),
            fixed(1, width),
        ],
        out_specs=[
            fixed(rows, width),
            fixed(rows, width),
            fixed(*blocks.shape),
            columns(2, rows, step // 2),
            columns(rows, step),
            fixed(2, rows, width // 2),
            fixed(2, rows, width // 2),
            fixed(rows, width),
            fixed(rows, width),
            fixed(1, width),
            columns(1, step),
            fixed(1, width),
        ],
        out_shape=[
            shape((rows, width), F32),
            pltpu.HBM((rows, width), F32),
            shape(blocks.shape, BF16),
            shape((2, rows, ff // 2), BF16),
            shape((rows, ff), BF16),
            shape((2, rows, width // 2), BF16),
            shape((2, rows, width // 2), BF16),
            shape((rows, width), BF16),
            shape((rows, width), BF16),
            pltpu.VMEM((1, width), F32),
            pltpu.VMEM((1, ff), F32),
            pltpu.VMEM((1, width), F32),
        ],
        scratch_shapes=[
            pltpu.VMEM((rows, width), F32),
            pltpu.VMEM((rows, width), BF16),
            pltpu.VMEM((rows, width), F32),
        ],
        compiler_params=pltpu.CompilerParams(vmem_limit_bytes=28 << 20),
        name="feed",
    )(
        blocks, frames, cotangent, w_out, gain.reshape(1, width), w_up, b_up.reshape(1, ff), w_down,
        b_down.reshape(1, width),
    )


MESH = pl.DeviceIdType.MESH
ALL = ("blk", "grp")


def in_hbm(*arrays):
    return [pltpu.with_memory_space_constraint(x, pltpu.HBM) for x in arrays]


def in_vmem(*arrays):
    return [pltpu.with_memory_space_constraint(x, pltpu.VMEM) for x in arrays]


def place(index):
    return {"blk": lax.div(index, 2), "grp": lax.rem(index, 2)}


def head_of(index):
    blk, grp = lax.div(index, 2), lax.rem(index, 2)
    return lax.div(blk, 2) * 2 + grp, lax.rem(blk, 2)


def own_index():
    return lax.axis_index("blk") * 2 + lax.axis_index("grp")


def plane_at(z, turn):
    high = lax.rem(lax.div(z, 2) + jnp.where(turn < 2, 1, 0), 2)
    low = lax.rem(z + jnp.where((turn == 1) | (turn == 2), 1, 0), 2)
    return high * 2 + low


def peer_at(i, n):
    me, plane = own_index(), n // 4
    return plane_at(lax.div(me, plane), lax.div(i, plane)) * plane + lax.rem(me + i, plane)


def each_peer(n, body):
    @pl.loop(0, n)
    def _(i):
        other = peer_at(i, n)

        @pl.when(other != own_index())
        def _():
            body(i, other)


def sibling_of(core):
    return {"blk": lax.axis_index("blk") + 1 - 2 * core, "grp": lax.axis_index("grp")}


def greet_all(me, n):
    barrier = pltpu.get_barrier_semaphore()

    @pl.loop(1, n)
    def _(i):
        pl.semaphore_signal(barrier, inc=1, device_id=place(lax.rem(me + i, n)), device_id_type=MESH)

    pl.semaphore_wait(barrier, n - 1)


def remote(src, dst, send_sem, recv_sem, device):
    return pltpu.make_async_remote_copy(
        src_ref=src, dst_ref=dst, send_sem=send_sem, recv_sem=recv_sem, device_id=device, device_id_type=MESH
    )


def to_heads_kernel(
    n, gain_in, frames_in, wq_in, wk_in, wv_in, kv_out, q_out, halves_out,
    gain, frames, act, halves, wq, wk, wv, kv_own, q_own, send, recv, local, fetched, pair,
):
    me = own_index()
    head, core = head_of(me)
    rows, width = frames.shape
    half = rows // 2
    weights = [
        pltpu.make_async_copy(src, dst, local.at[k])
        for k, (src, dst) in enumerate(
            ((gain_in, gain), (frames_in, frames), (halves, halves_out))
        )
    ]
    groups = width // 256

    def group_at(i):
        return plane_at(lax.div(me, n // groups), i)

    def fetch(group):
        columns = pl.ds(pl.multiple_of(group * 256, 256), 256)
        return [
            pltpu.make_async_copy(src.at[:, columns], dst.at[:, columns], fetched.at[k, group])
            for k, (src, dst) in enumerate(((wq_in, wq), (wk_in, wk), (wv_in, wv)))
        ]

    for copy in weights[:2]:
        copy.start()

    @pl.loop(0, groups)
    def _(i):
        for copy in fetch(group_at(i)):
            copy.start()

    greet_all(me, n)
    weights[0].wait()
    weights[1].wait()
    x = frames[...]
    r = lax.rsqrt(jnp.mean(x * x, axis=-1, keepdims=True) + EPSILON)
    normed = x * r * gain[...]
    act[...] = normed.astype(BF16)
    store_halves(halves, normed)
    weights[2].start()

    def copies(other, src):
        h, c = head_of(other)
        kv_at = core if src is not me else c
        return (
            remote(kv_own.at[h, c], kv_out.at[src, kv_at], send.at[0, other], recv.at[0, src], place(other)),
            remote(q_own.at[h, c], q_out.at[src], send.at[1, other], recv.at[1, src], place(other)),
        )

    low = low_lanes((rows, 128))
    low_h = low_lanes((half // 2, 128))

    @pl.loop(0, groups)
    def _(i):
        group = group_at(i)
        for copy in fetch(group):
            copy.wait()
        columns = pl.ds(pl.multiple_of(group * 256, 256), 256)
        q = nn_dot(act[...], wq[:, columns]).astype(BF16).astype(F32) * 0.125
        k = nn_dot(act[...], wk[:, columns])
        v = nn_dot(act[...], wv[:, columns])
        for p in range(2):
            at = slice(p * 128, (p + 1) * 128)
            k2, v2, q2 = k[:, at], v[:, at], q[:, at]
            kv_a = pair_low(k2, v2, low).astype(BF16)
            kv_b = pair_high(k2, v2, low).astype(BF16)
            h = group * 4 + 2 * p
            for s in range(2):
                span = slice(s * half, (s + 1) * half)
                kv_own[h, s] = kv_a[span]
                kv_own[h + 1, s] = kv_b[span]
                top = q2[s * half : s * half + half // 2]
                bot = q2[s * half + half // 2 : (s + 1) * half]
                q_own[h, s] = pair_low(top, bot, low_h).astype(BF16)
                q_own[h + 1, s] = pair_high(top, bot, low_h).astype(BF16)

        @pl.loop(0, n // groups)
        def _(j):
            other = group * (n // groups) + j

            @pl.when(other != me)
            def _():
                for copy in copies(other, me):
                    copy.start()

    kv_out[me, core] = kv_own[head, core]
    q_out[me] = q_own[head, core]

    plane = n // groups
    swaps = []
    for t in range(groups):
        first = pl.multiple_of(group_at(t) * plane, plane)

        @pl.loop(0, plane)
        def _(j):
            @pl.when(first + j != me)
            def _():
                for copy in copies(first + j, first + j):
                    copy.wait()

        at = pl.ds(first, plane)
        swap = remote(kv_out.at[at, core], kv_out.at[at, core], pair.at[0, t], pair.at[1, t], sibling_of(core))
        swap.start()
        swaps.append(swap)
    weights[2].wait()
    for swap in swaps:
        swap.wait()


def to_heads(frames, gain, w_query, w_key, w_value, n):
    rows, width = frames.shape
    half = rows // 2
    vmem = pl.BlockSpec(memory_space=pltpu.VMEM)
    hbm = pl.BlockSpec(memory_space=pltpu.HBM)
    return pl.pallas_call(
        functools.partial(to_heads_kernel, n),
        in_specs=[hbm] * 5,
        out_specs=[vmem, vmem, hbm],
        out_shape=[
            jax.ShapeDtypeStruct((n, 2, half, 128), BF16),
            jax.ShapeDtypeStruct((n, half // 2, 128), BF16),
            pltpu.HBM((2, rows, width // 2), BF16),
        ],
        scratch_shapes=[
            pltpu.VMEM((1, width), F32),
            pltpu.VMEM((rows, width), F32),
            pltpu.VMEM((rows, width), BF16),
            pltpu.VMEM((2, rows, width // 2), BF16),
            pltpu.VMEM((width, width), BF16),
            pltpu.VMEM((width, width), BF16),
            pltpu.VMEM((width, width), BF16),
            pltpu.VMEM((width // 64, 2, half, 128), BF16),
            pltpu.VMEM((width // 64, 2, half // 2, 128), BF16),
            pltpu.SemaphoreType.DMA((2, n)),
            pltpu.SemaphoreType.DMA((2, n)),
            pltpu.SemaphoreType.DMA((3,)),
            pltpu.SemaphoreType.DMA((3, 4)),
            pltpu.SemaphoreType.DMA((2, 4)),
        ],
        compiler_params=pltpu.CompilerParams(
            collective_id=0, has_side_effects=True, vmem_limit_bytes=16 << 20
        ),
        name="to_heads",
    )(*in_hbm(gain.reshape(1, width), frames, w_query, w_key, w_value))


def exchange_kernel(n, x_in, x_out, send, recv, local):
    me = own_index()
    greet_all(me, n)

    def copy_with(i, src):
        other = peer_at(i, n)
        return remote(x_in.at[other], x_out.at[src], send.at[i], recv.at[src], place(other))

    each_peer(n, lambda i, other: copy_with(i, me).start())

    own = pltpu.make_async_copy(x_in.at[me], x_out.at[me], local)
    own.start()
    own.wait()

    each_peer(n, lambda i, other: copy_with(i, other).wait())


def exchange(x, n, collective_id):
    vmem = pl.BlockSpec(memory_space=pltpu.VMEM)
    return pl.pallas_call(
        functools.partial(exchange_kernel, n),
        in_specs=[vmem],
        out_specs=vmem,
        out_shape=pltpu.VMEM(x.shape, x.dtype),
        scratch_shapes=[
            pltpu.SemaphoreType.DMA((n,)),
            pltpu.SemaphoreType.DMA((n,)),
            pltpu.SemaphoreType.DMA,
        ],
        compiler_params=pltpu.CompilerParams(collective_id=collective_id, has_side_effects=True, vmem_limit_bytes=8 << 20),
        name="exchange",
    )(*in_vmem(x))


BITS = {"core": 1, "y": 2, "z0": 4, "z1": 8}


def flipped(x, axis):
    if axis == "x":
        return lax.ppermute(x, "grp", [(0, 1), (1, 0)])
    return lax.ppermute(x, "blk", [(i, i ^ BITS[axis]) for i in range(lax.axis_size("blk"))])


def bit_of(axis):
    if axis == "x":
        return lax.axis_index("grp")
    return lax.rem(lax.div(lax.axis_index("blk"), BITS[axis]), 2)


def across(axis):
    blk, grp = lax.axis_index("blk"), lax.axis_index("grp")
    if axis == "x":
        return {"blk": blk, "grp": 1 - grp}
    bit = BITS[axis]
    return {"blk": blk + bit - 2 * bit * bit_of(axis), "grp": grp}


def tn_dot(a, b):
    return lax.dot_general(a, b, (((0,), (0,)), ((), ())), preferred_element_type=F32)


def share_kernel(
    n, blocks_in, hidden, grad_before, act2, mixed, low, attn,
    blocks_out, keep_a_out, send_a_out, keep_b_out, send_b_out, keep_c_out, send_c_out,
    keep_a, send_a, keep_b, send_b, keep_c, send_c, hidden2, before2, act2_2, mixed2, low2, attn2, tile, send, recv, local, out, pair_send, pair_recv,
):
    me = own_index()
    head, core = head_of(me)
    rows = low.shape[0]
    greet_all(me, n)
    sibling = sibling_of(core)
    theirs = pl.ds(rows, rows)
    pairs = [
        remote(src, dst.at[theirs], pair_send.at[k], pair_recv.at[k], sibling)
        for k, (src, dst) in enumerate(
            (
                (low, low2),
                (hidden.at[1 - core], hidden2),
                (act2.at[1 - core], act2_2),
                (grad_before, before2),
                (mixed.at[1 - core], mixed2),
                (attn, attn2),
            )
        )
    ]
    for copy in pairs:
        copy.start()

    def copy_with(i, src):
        other = peer_at(i, n)
        return remote(blocks_in.at[other], blocks_out.at[src], send.at[i], recv.at[src], place(other))

    each_peer(n, lambda i, other: copy_with(i, me).start())

    own = pltpu.make_async_copy(blocks_in.at[me], blocks_out.at[me], local)
    own.start()
    low2[:rows] = low[...]
    hidden2[:rows] = hidden[core]
    act2_2[:rows] = act2[core]
    before2[:rows] = grad_before[...]
    mixed2[:rows] = mixed[core]
    attn2[:rows] = attn[...]

    x_mine, y_mine, z_mine = bit_of("x"), bit_of("y"), bit_of("z0")

    def put(keep, away, mine, bit, at, row, value):
        @pl.when(mine == bit)
        def _():
            keep[at, row : row + value.shape[0]] = value

        @pl.when(mine != bit)
        def _():
            away[at, row : row + value.shape[0]] = value

    flushes = []

    def flush(src, dst):
        flushes.append(pltpu.make_async_copy(src, dst, out.at[len(flushes)]))
        flushes[-1].start()

    pairs[0].wait()
    pairs[1].wait()

    @pl.loop(0, 8)
    def _(zy):
        columns = pl.ds(pl.multiple_of(zy * 256, 256), 256)
        value = tn_dot(hidden2[:, columns], low2[...]).astype(BF16)
        z1, z0, y = lax.div(zy, 4), lax.rem(lax.div(zy, 2), 2), lax.rem(zy, 2)
        for x in range(2):
            put(keep_a, send_a, x_mine, x, zy, 0, value[x * 128 : x * 128 + 96])
            put(keep_c, send_c, z_mine, z0, (z1 * 2 + y) * 2 + x, 0, value[x * 128 + 96 : (x + 1) * 128])

    def spread_rows(left, right, slab, to_b, row):
        tile[...] = tn_dot(left[...], right[:, slab * 1024 : (slab + 1) * 1024]).astype(BF16)

        @pl.loop(0, 16)
        def _(j):
            value = tile[pl.ds(pl.multiple_of(j * 32, 32), 32)]
            z1, z0 = lax.div(j, 8), lax.rem(lax.div(j, 4), 2)
            y, x = lax.rem(lax.div(j, 2), 2), lax.rem(j, 2)
            if to_b:
                put(keep_b, send_b, y_mine, y, (z1 * 2 + z0) * 2 + x, row, value)
            else:
                put(keep_c, send_c, z_mine, z0, (z1 * 2 + y) * 2 + x, row, value)

    flush(keep_a, keep_a_out)
    flush(send_a, send_a_out)
    pairs[2].wait()
    pairs[3].wait()
    for slab in range(3):
        spread_rows(act2_2, before2, slab, True, 32 * slab)
    flush(keep_b, keep_b_out)
    flush(send_b, send_b_out)
    spread_rows(act2_2, before2, 3, False, 32)
    pairs[4].wait()
    pairs[5].wait()
    spread_rows(mixed2, attn2, 0, False, 64)
    flush(keep_c, keep_c_out)
    flush(send_c, send_c_out)
    own.wait()

    each_peer(n, lambda i, other: copy_with(i, other).wait())

    for copy in flushes:
        copy.wait()


def share(blocks, hidden, grad_before, act2, mixed, low, attn, n):
    rows, width = low.shape
    vmem = pl.BlockSpec(memory_space=pltpu.VMEM)
    hbm = pl.BlockSpec(memory_space=pltpu.HBM)
    shape = jax.ShapeDtypeStruct
    return pl.pallas_call(
        functools.partial(share_kernel, n),
        in_specs=[vmem] * 7,
        out_specs=[vmem] + [hbm] * 6,
        out_shape=[pltpu.VMEM(blocks.shape, BF16)] + [pltpu.HBM((8, 96, width), BF16)] * 6,
        scratch_shapes=[
            *[pltpu.VMEM((8, 96, width), BF16)] * 6,
            pltpu.VMEM((2 * rows, hidden.shape[2]), BF16),
            pltpu.VMEM((2 * rows, grad_before.shape[1]), BF16),
            pltpu.VMEM((2 * rows, width // 2), BF16),
            pltpu.VMEM((2 * rows, width // 2), BF16),
            pltpu.VMEM((2 * rows, width), BF16),
            pltpu.VMEM((2 * rows, width), BF16),
            pltpu.VMEM((width // 2, 1024), BF16),
            pltpu.SemaphoreType.DMA((n,)),
            pltpu.SemaphoreType.DMA((n,)),
            pltpu.SemaphoreType.DMA,
            pltpu.SemaphoreType.DMA((6,)),
            pltpu.SemaphoreType.DMA((6,)),
            pltpu.SemaphoreType.DMA((6,)),
        ],
        compiler_params=pltpu.CompilerParams(
            collective_id=3, has_side_effects=True, vmem_limit_bytes=26 << 20
        ),
        name="share",
    )(blocks, hidden, grad_before, act2, mixed, low, attn)


class Part:
    def __init__(self, total, dims, order, landing, send, recv):
        self.view, self.dims, self.order = total, list(dims), list(order)
        self.landing, self.send, self.recv = landing, send, recv
        self.stage, self.copy, self.kept = 0, None, None

    def start(self):
        axis = self.order[self.stage]
        at, mine = self.dims.index(axis), bit_of(axis)
        ahead = (slice(None),) * at
        self.copy = remote(
            self.view.at[ahead + (1 - mine,)],
            self.landing[self.stage],
            self.send.at[self.stage],
            self.recv.at[self.stage],
            across(axis),
        )
        self.copy.start()
        self.kept = self.view.at[ahead + (mine,)]
        self.dims.remove(axis)
        self.stage += 1

    def finish(self):
        self.copy.wait()
        got, kept = self.landing[self.stage - 1], self.kept
        lead = len(self.dims)

        @pl.loop(0, 2**lead)
        def _(k):
            at = tuple(lax.rem(lax.div(k, 2**d), 2) for d in reversed(range(lead)))
            kept[at] = (kept[at].astype(F32) + got[at].astype(F32)).astype(BF16)

        self.view = kept

    def last(self):
        self.copy.wait()
        return self.kept[...].astype(F32) + self.landing[self.stage - 1][...].astype(F32)


def finish_kernel(
    n, dkv_in, dq_in, gain2_grad, b_up_grad, b_down_grad, got_a, got_b, got_c,
    gain_in, act1, frames_in, grad_mid_in, wq_in, wk_in, wv_in, keep_a, keep_b, keep_c,
    frames_out, q_out, k_out, v_out, o_out, up_out, down_out, small_out,
    theirs, total, dkv_all, dq_all, gain, frames, grad_mid, wq, wk, wv, small_in,
    act1_2, qkv2, sum_a, sum_b, sum_c, sum_q, sum_k, sum_v,
    a2, a3, a4, b2, b3, b4, c2, c3, c4,
    q1, q2, q3, q4, k1, k2, k3, k4, v1, v2, v3, v4, small_all,
    early_send, early_recv, send, recv, dq_send, dq_recv, dkv_send, dkv_recv, small_send, small_recv, pair_send, pair_recv, local,
):
    me = own_index()
    head, core = head_of(me)
    rows, width = frames.shape
    quarter = rows // 4
    sums = [sum_a, sum_b, sum_c, sum_q, sum_k, sum_v]
    news = [got_a, got_b, got_c]
    fetches = [
        pltpu.make_async_copy(src, dst, local.at[k])
        for k, (src, dst) in enumerate(
            (
                (keep_a, sum_a), (keep_b, sum_b), (keep_c, sum_c),
                (wq_in, wq), (wk_in, wk), (wv_in, wv), (gain_in, gain), (frames_in, frames), (grad_mid_in, grad_mid),
            )
        )
    ]
    for copy in fetches:
        copy.start()
    greet_all(me, n)
    sibling = sibling_of(core)
    swap = remote(dkv_in.at[:, 1 - core], theirs, pair_send.at[0], pair_recv.at[0], sibling)
    swap.start()
    act1_copy = remote(act1.at[1 - core], act1_2.at[pl.ds(rows, rows)], pair_send.at[1], pair_recv.at[1], sibling)

    def to_all(src_ref, dst_ref, sends, recvs):
        def copy_with(i, src):
            other = peer_at(i, n)
            return remote(src_ref.at[other], dst_ref.at[src], sends.at[i], recvs.at[src], place(other))

        return copy_with

    dq_copy = to_all(dq_in, dq_all, dq_send, dq_recv)
    dkv_copy = to_all(total, dkv_all, dkv_send, dkv_recv)
    small_copy = to_all(small_in, small_all, small_send, small_recv)

    each_peer(n, lambda i, other: dq_copy(i, me).start())

    swap.wait()

    def add(j):
        return (dkv_in[j, core] + theirs[j]).astype(BF16)

    def add_and_send(i, other):
        total[other] = add(other)
        dkv_copy(i, me).start()

    each_peer(n, add_and_send)

    dkv_all[me] = add(me)
    dq_all[me] = dq_in[me]
    act1_copy.start()
    order = ("x", "y", "z0", "z1"), ("y", "x", "z0", "z1"), ("z0", "x", "y", "z1")
    landings = (q1, q2, q3, q4), (k1, k2, k3, k4), (v1, v2, v3, v4)
    late = [Part(sums[3 + k], ("z1", "z0", "y", "x"), order[k], landings[k], send.at[k], recv.at[k]) for k in range(3)]
    dims = ("z1", "z0", "y"), ("z1", "z0", "x"), ("z1", "y", "x")
    order = (
        (("y", "z0", "z1"),) * 3,
        (("x", "z0", "z1"), ("x", "z0", "z1"), ("z0", "x", "z1")),
        (("x", "y", "z1"), ("y", "x", "z1"), ("x", "y", "z1")),
    )
    landings = (a2, a3, a4), (b2, b3, b4), (c2, c3, c4)
    waves = []
    for u in range(3):
        band = slice(32 * u, 32 * u + 32)
        wave = []
        for k in range(3):
            wave.append(
                Part(
                    sums[k].at[:, :, :, band],
                    dims[k],
                    order[k][u],
                    [ref.at[(slice(None),) * lead + (band,)] for lead, ref in zip((2, 1, 0), landings[k])],
                    early_send.at[u, k],
                    early_recv.at[u, k],
                )
            )
        waves.append(wave)

    for u, wave in enumerate(waves):
        for k, part in enumerate(wave):
            whole, new = sums[k], news[k]
            if u == 0:
                fetches[k].wait()

            @pl.loop(0, 8)
            def _(j):
                at = (lax.div(j, 4), lax.rem(lax.div(j, 2), 2), lax.rem(j, 2), slice(32 * u, 32 * u + 32))
                whole[at] = (whole[at].astype(F32) + new[at].astype(F32)).astype(BF16)

            part.start()

    def advance(parts):
        for part in parts:
            part.finish()
            part.start()

    act1_own = pltpu.make_async_copy(act1.at[core], act1_2.at[pl.ds(0, rows)], local.at[9])
    act1_own.start()

    each_peer(n, lambda i, other: dq_copy(i, other).wait())

    advance(waves[0])
    advance(waves[1])

    each_peer(n, lambda i, other: dkv_copy(i, other).wait())

    advance(waves[0])
    advance(waves[2])
    def pair_with(k):
        columns = slice(k * width, (k + 1) * width)
        own, other = qkv2.at[pl.ds(0, rows), columns], qkv2.at[pl.ds(rows, rows), columns]
        return remote(own, other, pair_send.at[2 + k], pair_recv.at[2 + k], sibling)

    pairs = [pair_with(k) for k in range(3)]
    low_q, low_h = low_lanes((quarter, 128)), low_lanes((2 * quarter, 128))
    for zy in range(8):
        for s in range(2):
            j = (zy * 2 + s) * 2
            first = 2 * s * quarter
            a, b = dq_all[j].astype(F32), dq_all[j + 1].astype(F32)
            at = slice(zy * 128, (zy + 1) * 128)
            qkv2[first : first + quarter, at] = pair_low(a, b, low_q).astype(BF16)
            qkv2[first + quarter : first + 2 * quarter, at] = pair_high(a, b, low_q).astype(BF16)
    pairs[0].start()
    for zy in range(8):
        for s in range(2):
            j = (zy * 2 + s) * 2
            first = 2 * s * quarter
            a, b = dkv_all[j].astype(F32), dkv_all[j + 1].astype(F32)
            at = slice(width + zy * 128, width + (zy + 1) * 128)
            qkv2[first : first + 2 * quarter, at] = pair_low(a, b, low_h).astype(BF16)
            at = slice(2 * width + zy * 128, 2 * width + (zy + 1) * 128)
            qkv2[first : first + 2 * quarter, at] = pair_high(a, b, low_h).astype(BF16)
    pairs[1].start()
    pairs[2].start()
    advance(waves[1])
    act1_copy.wait()
    act1_own.wait()
    for k in range(3):
        pairs[k].wait()
        value = tn_dot(act1_2[...], qkv2[:, k * width : (k + 1) * width]).astype(BF16)
        for j in range(16):
            sums[3 + k][j // 8, j // 4 % 2, j // 2 % 2, j % 2] = value[j * 32 : (j + 1) * 32]
        late[k].start()

    for copy in fetches[3:]:
        copy.wait()
    g = nt_dot(qkv2[:rows, :width], wq[...])
    g += nt_dot(qkv2[:rows, width : 2 * width], wk[...])
    g += nt_dot(qkv2[:rows, 2 * width :], wv[...])
    advance(waves[2])

    x = frames[...]
    r = lax.rsqrt(jnp.mean(x * x, axis=-1, keepdims=True) + EPSILON)
    norm = x * r
    gain_grad = jnp.sum(g * norm, axis=0, keepdims=True)
    small_in[...] = jnp.zeros_like(small_in)
    for d in range(n):
        at = slice(d // 4 * 128, (d // 4 + 1) * 128)
        small_in[d, 0:1] = gain_grad[:, at]
        small_in[d, 1:2] = gain2_grad[:, at]
        small_in[d, 2:3] = b_down_grad[:, at]
        small_in[d, 3:4] = b_up_grad[:, d * 128 : (d + 1) * 128]

    each_peer(n, lambda i, other: small_copy(i, me).start())

    g = g * gain[...]
    frames_out[...] = grad_mid[...] + r * (g - norm * jnp.mean(g * norm, axis=-1, keepdims=True))
    small_all[me] = small_in[me]

    advance(late * 3)

    each_peer(n, lambda i, other: small_copy(i, other).wait())

    part = width // n
    small_out[...] = pltpu.roll(jnp.sum(small_all[...], axis=0), lax.rem(128 - lax.rem(me, 128 // part) * part, 128), 1)
    small_out[3:4] = jnp.sum(small_all[:, 3:4], axis=0)
    for u, wave in enumerate(waves):
        down_out[32 * u : 32 * u + 32] = wave[0].last()
        up_out[:, 1024 * u : 1024 * u + 1024] = wave[1].last()
    down_out[96:] = waves[0][2].last()
    up_out[:, 3072:] = waves[1][2].last()
    o_out[...] = waves[2][2].last()
    q_out[...] = late[0].last()
    k_out[...] = late[1].last()
    v_out[...] = late[2].last()


def finish(dkv, dq, act1, frames, grad_mid, gain, gain2_grad, b_up_grad, b_down_grad, weights, keeps, gots, n):
    rows, width = frames.shape
    keeps, gots = [[x.reshape(2, 2, 2, *x.shape[1:]) for x in xs] for xs in (keeps, gots)]
    half = dkv.shape[2]
    vmem = pl.BlockSpec(memory_space=pltpu.VMEM)
    hbm = pl.BlockSpec(memory_space=pltpu.HBM)
    shape = jax.ShapeDtypeStruct
    thin, wide = (32, width), (96, width)
    buffers = [pltpu.VMEM((2, 2, 2, *wide), BF16)] * 3 + [pltpu.VMEM((2, 2, 2, 2, *thin), BF16)] * 3
    buffers += [pltpu.VMEM((2,) * k + wide, BF16) for k in (2, 1, 0)] * 3
    buffers += [pltpu.VMEM((2,) * k + thin, BF16) for k in (3, 2, 1, 0)] * 3
    over_devices = [pltpu.SemaphoreType.DMA((n,))] * 6
    return pl.pallas_call(
        functools.partial(finish_kernel, n),
        in_specs=[vmem] * 8 + [hbm] * 10,
        out_specs=[vmem] * 8,
        out_shape=[pltpu.VMEM((rows, width), F32)]
        + [pltpu.VMEM(thin, F32)] * 4
        + [pltpu.VMEM((32, 4 * width), F32), pltpu.VMEM((128, width), F32), pltpu.VMEM((8, 128), F32)],
        scratch_shapes=[
            pltpu.VMEM((n, half, 128), F32),
            pltpu.VMEM((n, half, 128), BF16),
            pltpu.VMEM((n, half, 128), BF16),
            pltpu.VMEM((n, half // 2, 128), BF16),
            pltpu.VMEM((1, width), F32),
            pltpu.VMEM((rows, width), F32),
            pltpu.VMEM((rows, width), F32),
            pltpu.VMEM((width, width), BF16),
            pltpu.VMEM((width, width), BF16),
            pltpu.VMEM((width, width), BF16),
            pltpu.VMEM((n, 8, 128), F32),
            pltpu.VMEM((2 * rows, width // 2), BF16),
            pltpu.VMEM((2 * rows, 3 * width), BF16),
            *buffers,
            pltpu.VMEM((n, 8, 128), F32),
            pltpu.SemaphoreType.DMA((3, 3, 3)),
            pltpu.SemaphoreType.DMA((3, 3, 3)),
            pltpu.SemaphoreType.DMA((3, 4)),
            pltpu.SemaphoreType.DMA((3, 4)),
            *over_devices,
            pltpu.SemaphoreType.DMA((5,)),
            pltpu.SemaphoreType.DMA((5,)),
            pltpu.SemaphoreType.DMA((10,)),
        ],
        compiler_params=pltpu.CompilerParams(
            collective_id=4, has_side_effects=True, vmem_limit_bytes=36 << 20
        ),
        name="finish",
    )(
        *in_vmem(dkv, dq, gain2_grad, b_up_grad, b_down_grad, *gots),
        *in_hbm(gain.reshape(1, width), act1, frames, grad_mid, *weights, *keeps),
    )


def emit_kernel(n, small, *refs):
    sems = refs[-1]
    copies = [pltpu.make_async_copy(refs[k], refs[n + k], sems.at[k]) for k in range(n)]
    for copy in copies:
        copy.start()
    for row, out in enumerate(refs[2 * n : -1]):
        out[...] = small[row : row + 1, : out.shape[1]]
    for copy in copies:
        copy.wait()


def emit(small, widths, *arrays):
    n = len(arrays)
    vmem = pl.BlockSpec(memory_space=pltpu.VMEM)
    return pl.pallas_call(
        functools.partial(emit_kernel, n),
        in_specs=[vmem] * (n + 1),
        out_specs=[pl.BlockSpec(memory_space=pltpu.HBM)] * n + [vmem] * len(widths),
        out_shape=[pltpu.HBM(x.shape, x.dtype) for x in arrays]
        + [jax.ShapeDtypeStruct((1, width), F32) for width in widths],
        scratch_shapes=[pltpu.SemaphoreType.DMA((n,))],
        compiler_params=pltpu.CompilerParams(vmem_limit_bytes=8 << 20),
        name="emit",
    )(*in_vmem(small, *arrays))


def shards_heads(
    frames, lengths, norm1_gain, w_query, w_key, w_value, w_out, norm2_gain, w_up, b_up, w_down, b_down, cotangent
):
    rows, width = frames.shape
    n = lax.axis_size("blk") * lax.axis_size("grp")
    half = rows // 2
    core_word = bit_of("core").astype(jnp.int32).reshape(1)
    qpos = jnp.asarray(packed_positions(n, half))

    kv, q, act1 = to_heads(frames, norm1_gain, w_query, w_key, w_value, n)
    kv_rows = kv.reshape(n * rows, 128)
    out_t, lse, out_blocks = mix(lengths, core_word, kv_rows, q, qpos)
    mixed_blocks = exchange(out_blocks, n, 2)
    (
        layer_out, grad_middle, grad_blocks, hidden, grad_before, act2, mixed, grad_low, grad_attn,
        norm2_gain_grad, b_up_grad, b_down_grad,
    ) = feed(mixed_blocks, frames, cotangent, w_out, norm2_gain, w_up, b_up, w_down, b_down)
    grad_blocks, *parts = share(grad_blocks, hidden, grad_before, act2, mixed, grad_low, grad_attn, n)
    keeps = parts[0::2]
    gots = [flipped(part, axis) for part, axis in zip(parts[1::2], ("x", "y", "z0"))]
    dkv, dq = mix_back(lengths, core_word, kv_rows, q, *in_vmem(grad_blocks), qpos, out_t, lse)

    frames_grad, w_query_grad, w_key_grad, w_value_grad, w_out_grad, w_up_grad, w_down_grad, small = finish(
        dkv.reshape(n, 2, half, 128), dq, act1, frames, grad_middle, norm1_gain, norm2_gain_grad, b_up_grad,
        b_down_grad, (w_query, w_key, w_value), keeps, gots, n,
    )
    part = width // n
    (
        layer_out, frames_grad, w_query_grad, w_key_grad, w_value_grad, w_out_grad, w_up_grad, w_down_grad, *vectors
    ) = emit(
        small, (part, part, part, b_up.shape[0] // n),
        layer_out, frames_grad, w_query_grad, w_key_grad, w_value_grad, w_out_grad, w_up_grad, w_down_grad,
    )
    return (
        layer_out,
        frames_grad,
        vectors[0].reshape(-1),
        w_query_grad,
        w_key_grad,
        w_value_grad,
        w_out_grad,
        vectors[1].reshape(-1),
        w_up_grad,
        vectors[3].reshape(-1),
        w_down_grad,
        vectors[2].reshape(-1),
    )


def solution(mesh):
    if mesh.shape["blk"] != 16 or mesh.shape["grp"] != 2:
        return solution_ring(mesh)
    split = P(ALL, None)
    return jax.shard_map(
        shards_heads,
        mesh=mesh,
        in_specs=(split, P(), P(), P(), P(), P(), P(), P(), P(), P(), P(), P(), split),
        out_specs=(split, split, P(ALL), split, split, split, split, P(ALL), split, P(ALL), split, P(ALL)),
        check_vma=False,
    )
```

```python
import functools

import jax
import jax.numpy as jnp
import numpy as np
from jax import lax
from jax.experimental import pallas as pl
from jax.experimental.pallas import tpu as pltpu
from jax.sharding import PartitionSpec as P

HEAD_DIM = 64
ITEM_MAX = 4096


EPSILON = 1e-05
MASKED = -1e30
SCALING = 0.125


def shortened(array):

    def short(part):
        return part.astype(jnp.bfloat16) if part.dtype == jnp.float32 else part

    return jax.tree.map(short, array)


def passed_along(block, axis, distance):
    devices = range(lax.axis_size(axis))
    route = [(i - distance, i) for i in devices if i - distance in devices]
    return lax.ppermute(block, axis, route)


def rms_norm(values, gain):
    return values * lax.rsqrt(jnp.mean(values * values, axis=-1, keepdims=True) + EPSILON) * gain


def gelu_exact(values):
    return jax.nn.gelu(values, approximate=False)


def item_starts(lengths, positions):
    ends = jnp.cumsum(lengths)
    offsets = ends - lengths
    before = offsets[None, :] <= positions[:, None]
    return jnp.max(jnp.where(before, offsets[None, :], 0), axis=1)


def live_mask(query_pos, query_start, key_first, key_count):
    key_pos = key_first + jnp.arange(key_count, dtype=jnp.int32)
    return (key_pos[None, :] >= query_start[:, None]) & (key_pos[None, :] <= query_pos[:, None])


def split_heads(matrix):
    return matrix.reshape(matrix.shape[0], matrix.shape[1] // HEAD_DIM, HEAD_DIM)


def merge_heads(tensor):
    return tensor.reshape(tensor.shape[0], tensor.shape[1] * tensor.shape[2])


def scores_of(queries3, keys_block, mask):
    raw = jnp.einsum(
        "qhd,khd->hqk", queries3, split_heads(keys_block), preferred_element_type=jnp.float32
    )
    return jnp.where(mask[None], raw * SCALING, MASKED)


def left_dot(left, right):
    return lax.dot_general(
        left, right, (((0,), (0,)), ((), ())), preferred_element_type=jnp.float32
    )


def right_dot(left, right):
    return lax.dot_general(
        left, right, (((1,), (1,)), ((), ())), preferred_element_type=jnp.float32
    )


def grad_parts(queries3, grad_out3, log_total, delta, keys_block, values_block, mask):
    probs = jnp.exp(scores_of(queries3, keys_block, mask) - log_total[:, :, None])
    grad_probs = jnp.einsum(
        "qhd,khd->hqk", grad_out3, split_heads(values_block), preferred_element_type=jnp.float32
    )
    grad_scores = (probs * (grad_probs - delta[:, :, None])).astype(jnp.bfloat16)
    return (probs.astype(jnp.bfloat16), grad_scores)


def key_terms(queries3, grad_out3, probs_low, grad_scores):
    grad_keys = jnp.einsum(
        "hqk,qhd->khd", grad_scores, queries3, preferred_element_type=jnp.float32
    )
    grad_values = jnp.einsum(
        "hqk,qhd->khd", probs_low, grad_out3, preferred_element_type=jnp.float32
    )
    return (merge_heads(grad_keys), merge_heads(grad_values))


def query_term(grad_scores, keys_block):
    return jnp.einsum(
        "hqk,khd->qhd", grad_scores, split_heads(keys_block), preferred_element_type=jnp.float32
    )


def shards_ring(
    frames,
    lengths,
    norm1_gain,
    w_query,
    w_key,
    w_value,
    w_out,
    norm2_gain,
    w_up,
    b_up,
    w_down,
    b_down,
    cotangent,
):
    row_count = frames.shape[0]
    width = frames.shape[1]
    heads = width // HEAD_DIM
    groups = lax.axis_size("grp")
    block_rows = row_count * groups
    span = (ITEM_MAX + block_rows - 2) // block_rows
    blk_index = lax.axis_index("blk")
    sub_index = lax.axis_index("grp")
    block_first = blk_index * block_rows
    query_pos = block_first + sub_index * row_count + jnp.arange(row_count, dtype=jnp.int32)
    query_start = item_starts(lengths, query_pos)
    back_steps = jnp.arange(span + 1, dtype=jnp.int32)
    normed1, norm1_back = jax.vjp(rms_norm, frames, norm1_gain)
    act1 = normed1.astype(jnp.bfloat16)
    queries = jnp.dot(act1, w_query, preferred_element_type=jnp.float32).astype(jnp.bfloat16)
    keys_own = jnp.dot(act1, w_key, preferred_element_type=jnp.float32).astype(jnp.bfloat16)
    values_own = jnp.dot(act1, w_value, preferred_element_type=jnp.float32).astype(jnp.bfloat16)
    queries3 = split_heads(queries)
    block_keys, block_values = (
        lax.all_gather(keys_own, "grp", axis=0, tiled=True),
        lax.all_gather(values_own, "grp", axis=0, tiled=True),
    )

    def cycle_step(carry, unused_input):
        moved = jax.tree.map(
            lambda part, own: part.astype(own.dtype),
            passed_along(shortened(carry), "blk", 1),
            carry,
        )
        return (moved, moved)

    unused_last, far_blocks = lax.scan(cycle_step, (block_keys, block_values), None, length=span)
    keys_all = jnp.concatenate([block_keys[None], far_blocks[0]], axis=0)
    values_all = jnp.concatenate([block_values[None], far_blocks[1]], axis=0)

    def mask_for(back):
        return live_mask(query_pos, query_start, block_first - back * block_rows, block_rows)

    def total_step(carry, inputs):
        run_max, run_sum = carry
        keys_block, back = inputs
        scores = scores_of(queries3, keys_block, mask_for(back))
        new_max = jnp.maximum(run_max, jnp.max(scores, axis=-1))
        run_sum = run_sum * jnp.exp(run_max - new_max) + jnp.sum(
            jnp.exp(scores - new_max[:, :, None]), axis=-1
        )
        return ((new_max, run_sum), None)

    start_max = jnp.full((heads, row_count), MASKED, jnp.float32)
    start_sum = jnp.zeros((heads, row_count), jnp.float32)
    (top_max, top_sum), unused_out = lax.scan(
        total_step, (start_max, start_sum), (keys_all, back_steps)
    )
    log_total = top_max + jnp.log(top_sum)

    def mix_step(total, inputs):
        keys_block, values_block, back = inputs
        probs = jnp.exp(
            scores_of(queries3, keys_block, mask_for(back)) - log_total[:, :, None]
        ).astype(jnp.bfloat16)
        return (
            total
            + jnp.einsum(
                "hqk,khd->qhd", probs, split_heads(values_block), preferred_element_type=jnp.float32
            ),
            None,
        )

    zero_query = jnp.zeros((row_count, heads, HEAD_DIM), jnp.float32)
    mixed_sum, unused_out = lax.scan(mix_step, zero_query, (keys_all, values_all, back_steps))
    mixed = merge_heads(mixed_sum).astype(jnp.bfloat16)
    middle = frames + jnp.dot(mixed, w_out, preferred_element_type=jnp.float32)
    normed2, norm2_back = jax.vjp(rms_norm, middle, norm2_gain)
    act2 = normed2.astype(jnp.bfloat16)
    before = jnp.dot(act2, w_up, preferred_element_type=jnp.float32) + b_up
    activated, gelu_back = jax.vjp(gelu_exact, before)
    hidden = activated.astype(jnp.bfloat16)
    layer_out = middle + jnp.dot(hidden, w_down, preferred_element_type=jnp.float32) + b_down
    grad_low = cotangent.astype(jnp.bfloat16)
    b_down_grad = jnp.sum(grad_low.astype(jnp.float32), axis=0)
    w_down_grad = left_dot(hidden, grad_low)
    grad_before = gelu_back(right_dot(grad_low, w_down))[0].astype(jnp.bfloat16)
    b_up_grad = jnp.sum(grad_before.astype(jnp.float32), axis=0)
    w_up_grad = left_dot(act2, grad_before)
    grad_mid_norm, norm2_gain_grad = norm2_back(right_dot(grad_before, w_up))
    grad_middle = cotangent + grad_mid_norm
    grad_attn = grad_middle.astype(jnp.bfloat16)
    w_out_grad = left_dot(mixed, grad_attn)
    grad_mixed = right_dot(grad_attn, w_out).astype(jnp.bfloat16)
    grad_out3 = split_heads(grad_mixed)

    def delta_step(total, inputs):
        keys_block, values_block, back = inputs
        probs = jnp.exp(scores_of(queries3, keys_block, mask_for(back)) - log_total[:, :, None])
        grad_probs = jnp.einsum(
            "qhd,khd->hqk", grad_out3, split_heads(values_block), preferred_element_type=jnp.float32
        )
        return (total + jnp.sum(probs * grad_probs, axis=-1), None)

    delta, unused_out = lax.scan(
        delta_step, jnp.zeros((heads, row_count), jnp.float32), (keys_all, values_all, back_steps)
    )
    zero_block = jnp.zeros((block_rows, width), jnp.float32)

    def return_step(carry, inputs):
        grad_q, travel = carry
        keys_block, values_block, back = inputs
        probs_low, grad_scores = grad_parts(
            queries3, grad_out3, log_total, delta, keys_block, values_block, mask_for(back)
        )
        grad_keys, grad_values = key_terms(queries3, grad_out3, probs_low, grad_scores)
        moved = (
            passed_along((travel[0] + grad_keys).astype(jnp.bfloat16), "blk", -1).astype(
                jnp.float32
            ),
            passed_along((travel[1] + grad_values).astype(jnp.bfloat16), "blk", -1).astype(
                jnp.float32
            ),
        )
        return ((grad_q + query_term(grad_scores, keys_block), moved), None)

    (grad_q, travel), unused_out = lax.scan(
        return_step,
        (zero_query, (zero_block, zero_block)),
        (far_blocks[0], far_blocks[1], back_steps[1:]),
        reverse=True,
    )
    probs_low, grad_scores = grad_parts(
        queries3, grad_out3, log_total, delta, block_keys, block_values, mask_for(0)
    )
    grad_keys, grad_values = key_terms(queries3, grad_out3, probs_low, grad_scores)
    grad_q = grad_q + query_term(grad_scores, block_keys)
    block_grad_keys = travel[0] + grad_keys
    block_grad_values = travel[1] + grad_values
    grad_keys_rows, grad_values_rows = (
        lax.psum_scatter(
            block_grad_keys.astype(jnp.bfloat16), "grp", scatter_dimension=0, tiled=True
        ).astype(jnp.float32),
        lax.psum_scatter(
            block_grad_values.astype(jnp.bfloat16), "grp", scatter_dimension=0, tiled=True
        ).astype(jnp.float32),
    )
    grad_keys_low = (grad_keys_rows * SCALING).astype(jnp.bfloat16)
    grad_values_low = grad_values_rows.astype(jnp.bfloat16)
    grad_queries_low = (merge_heads(grad_q) * SCALING).astype(jnp.bfloat16)
    w_query_grad = left_dot(act1, grad_queries_low)
    w_key_grad = left_dot(act1, grad_keys_low)
    w_value_grad = left_dot(act1, grad_values_low)
    grad_act1 = (
        right_dot(grad_queries_low, w_query)
        + right_dot(grad_keys_low, w_key)
        + right_dot(grad_values_low, w_value)
    )
    grad_frames_norm, norm1_gain_grad = norm1_back(grad_act1)
    frames_grad = grad_middle + grad_frames_norm
    shares = (
        lax.psum_scatter(norm1_gain_grad, ("blk", "grp"), scatter_dimension=0, tiled=True),
        lax.psum_scatter(w_query_grad, ("blk", "grp"), scatter_dimension=0, tiled=True),
        lax.psum_scatter(w_key_grad, ("blk", "grp"), scatter_dimension=0, tiled=True),
        lax.psum_scatter(w_value_grad, ("blk", "grp"), scatter_dimension=0, tiled=True),
        lax.psum_scatter(w_out_grad, ("blk", "grp"), scatter_dimension=0, tiled=True),
        lax.psum_scatter(norm2_gain_grad, ("blk", "grp"), scatter_dimension=0, tiled=True),
        lax.psum_scatter(w_up_grad, ("blk", "grp"), scatter_dimension=0, tiled=True),
        lax.psum_scatter(b_up_grad, ("blk", "grp"), scatter_dimension=0, tiled=True),
        lax.psum_scatter(w_down_grad, ("blk", "grp"), scatter_dimension=0, tiled=True),
        lax.psum_scatter(b_down_grad, ("blk", "grp"), scatter_dimension=0, tiled=True),
    )
    return (
        layer_out,
        frames_grad,
        shares[0],
        shares[1],
        shares[2],
        shares[3],
        shares[4],
        shares[5],
        shares[6],
        shares[7],
        shares[8],
        shares[9],
    )


def solution_ring(mesh):
    placed = (
        P(("blk", "grp"), None),
        P(),
        P(),
        P(),
        P(),
        P(),
        P(),
        P(),
        P(),
        P(),
        P(),
        P(),
        P(("blk", "grp"), None),
    )
    return jax.shard_map(
        shards_ring,
        mesh=mesh,
        in_specs=placed,
        out_specs=(
            P(("blk", "grp"), None),
            P(("blk", "grp"), None),
            P(("blk", "grp")),
            P(("blk", "grp"), None),
            P(("blk", "grp"), None),
            P(("blk", "grp"), None),
            P(("blk", "grp"), None),
            P(("blk", "grp")),
            P(("blk", "grp"), None),
            P(("blk", "grp")),
            P(("blk", "grp"), None),
            P(("blk", "grp")),
        ),
        check_vma=False,
    )


LOG2E = 1.4426950408889634
F32, BF16 = jnp.float32, jnp.bfloat16


def nt_dot(a, b):
    return lax.dot_general(a, b, (((1,), (1,)), ((), ())), preferred_element_type=F32)


def nn_dot(a, b):
    return lax.dot_general(a, b, (((1,), (0,)), ((), ())), preferred_element_type=F32)


def low_lanes(shape):
    return lax.broadcasted_iota(jnp.int32, shape, 1) < 64


def pair_low(a, b, low):
    return jnp.where(low, a, pltpu.roll(b, 64, 1))


def pair_high(a, b, low):
    return jnp.where(low, pltpu.roll(a, 64, 1), b)


def store_halves(ref, x):
    low = low_lanes((x.shape[0], 128))
    for p in range(x.shape[1] // 256):
        a, b = x[:, p * 256 : p * 256 + 128], x[:, p * 256 + 128 : (p + 1) * 256]
        ref[0, :, p * 128 : (p + 1) * 128] = pair_low(a, b, low).astype(BF16)
        ref[1, :, p * 128 : (p + 1) * 128] = pair_high(a, b, low).astype(BF16)


def block_bounds(len_ref, items, qpos, first, last, key_block):
    off = jnp.int32(0)
    start = jnp.zeros(qpos.shape, jnp.int32)
    s_first, s_last = jnp.int32(0), jnp.int32(0)
    for i in range(items):
        start = jnp.where(qpos >= off, off, start)
        s_first = jnp.where(first >= off, off, s_first)
        s_last = jnp.where(last >= off, off, s_last)
        off = off + len_ref[i]
    lo, hi = s_first // key_block, last // key_block + 1
    f0 = jnp.clip((s_last + key_block - 1) // key_block, lo, hi)
    f1 = jnp.clip((first + 1) // key_block, f0, hi)
    return start, lo, f0, f1, hi


def query_ends(i, chunks, half, core):
    first = i * chunks * 2 * half + core * half
    return first, first + (chunks - 1) * 2 * half + half - 1


def spread(packed, low, to_high):
    f = packed.astype(F32)
    other = pltpu.roll(f, 64, 1)
    zero = jnp.zeros_like(f)
    if to_high:
        return jnp.where(low, zero, other).astype(BF16), jnp.where(low, zero, f).astype(BF16)
    return jnp.where(low, f, zero).astype(BF16), jnp.where(low, other, zero).astype(BF16)


def mix_kernel(
    items, chunks, key_block,
    len_ref, core_ref, kv_ref, qp_ref, qpos_ref,
    out_t_ref, lse_ref, out_ref,
    kv_t, qz, acc, m_ref, l_ref,
):
    i = pl.program_id(0)
    half = 2 * qp_ref.shape[1]
    n = chunks * half
    core = core_ref[0]

    @pl.when(i == 0)
    def _():
        for c in range(kv_ref.shape[0] // 512):
            at = slice(c * 512, (c + 1) * 512)
            kv_t[:, at] = kv_ref[at, :].astype(F32).T.astype(BF16)

    low = low_lanes((half // 2, 128))
    for c in range(chunks):
        a, b = spread(qp_ref[c], low, False)
        qz[c * half : c * half + half // 2] = a
        qz[c * half + half // 2 : (c + 1) * half] = b
    qpos = qpos_ref[...] + core * half
    first, last = query_ends(i, chunks, half, core)
    start, lo, f0, f1, hi = block_bounds(len_ref, items, qpos, first, last, key_block)
    acc[...] = jnp.zeros_like(acc)
    m_ref[...] = jnp.full_like(m_ref, MASKED)
    l_ref[...] = jnp.zeros_like(l_ref)

    def step(j, masked):
        at = pl.ds(pl.multiple_of(j * key_block, key_block), key_block)
        s = nt_dot(kv_ref[at, :], qz[...]) * LOG2E
        if masked:
            kpos = j * key_block + lax.broadcasted_iota(jnp.int32, (key_block, 1), 0)
            s = jnp.where((kpos >= start) & (kpos <= qpos), s, MASKED)
        m_old = m_ref[...]
        m_new = jnp.maximum(m_old, jnp.max(s, axis=0, keepdims=True))
        p = jnp.exp2(s - m_new)
        alpha = jnp.exp2(m_old - m_new)
        m_ref[...] = m_new
        l_ref[...] = l_ref[...] * alpha + jnp.sum(p, axis=0, keepdims=True)
        acc[...] = acc[...] * alpha + nn_dot(kv_t[64:, at], p.astype(BF16))

    lax.fori_loop(lo, f0, lambda j, c: (step(j, True), c)[1], 0)
    lax.fori_loop(f0, f1, lambda j, c: (step(j, False), c)[1], 0)
    lax.fori_loop(f1, hi, lambda j, c: (step(j, True), c)[1], 0)
    out_t = acc[...] / l_ref[...]
    out_t_ref[...] = out_t
    lse_ref[...] = m_ref[...] + jnp.log2(l_ref[...])
    doubled = jnp.concatenate([out_t, out_t], axis=0).T
    for c in range(chunks):
        a = doubled[c * half : c * half + half // 2]
        b = doubled[c * half + half // 2 : (c + 1) * half]
        out_ref[c] = jnp.where(low, a, b).astype(BF16)


def mix(lengths, core, kv, qp, qpos, chunks=4, key_block=768):
    total = kv.shape[0]
    n_src, quarter = qp.shape[0], qp.shape[1]
    half = 2 * quarter
    n = chunks * half
    whole = lambda i, *_: (0, 0)
    return pl.pallas_call(
        functools.partial(mix_kernel, lengths.shape[0], chunks, key_block),
        grid_spec=pltpu.PrefetchScalarGridSpec(
            num_scalar_prefetch=2,
            grid=(n_src // chunks,),
            in_specs=[
                pl.BlockSpec((total, 128), whole),
                pl.BlockSpec((chunks, quarter, 128), lambda i, *_: (i, 0, 0)),
                pl.BlockSpec((1, n), lambda i, *_: (0, i)),
            ],
            out_specs=[
                pl.BlockSpec((64, n), lambda i, *_: (0, i)),
                pl.BlockSpec((1, n), lambda i, *_: (0, i)),
                pl.BlockSpec((chunks, quarter, 128), lambda i, *_: (i, 0, 0)),
            ],
            scratch_shapes=[
                pltpu.VMEM((128, total), BF16),
                pltpu.VMEM((n, 128), BF16),
                pltpu.VMEM((64, n), F32),
                pltpu.VMEM((1, n), F32),
                pltpu.VMEM((1, n), F32),
            ],
        ),
        out_shape=[
            jax.ShapeDtypeStruct((64, n_src * half), F32),
            jax.ShapeDtypeStruct((1, n_src * half), F32),
            jax.ShapeDtypeStruct((n_src, quarter, 128), BF16),
        ],
        compiler_params=pltpu.CompilerParams(vmem_limit_bytes=22 << 20),
        cost_estimate=pl.CostEstimate(flops=25_000_000_000, bytes_accessed=8 << 20, transcendentals=0),
        name="mix",
    )(lengths, core, kv, qp, qpos)


def back_kernel(
    items, chunks, key_block,
    len_ref, core_ref, kv_ref, qp_ref, dp_ref, qpos_ref, out_t_ref, lse_ref,
    dkv_ref, dq_ref,
    kv_t, qd, dq_acc,
):
    i = pl.program_id(0)
    half = 2 * qp_ref.shape[1]
    n = chunks * half
    core = core_ref[0]

    @pl.when(i == 0)
    def _():
        for c in range(kv_ref.shape[0] // 512):
            at = slice(c * 512, (c + 1) * 512)
            kv_t[:, at] = kv_ref[at, :].astype(F32).T.astype(BF16)
        dkv_ref[...] = jnp.zeros_like(dkv_ref)

    low = low_lanes((half // 2, 128))
    for c in range(chunks):
        a, b = spread(qp_ref[c], low, False)
        qd[c * half : c * half + half // 2] = a
        qd[c * half + half // 2 : (c + 1) * half] = b
        a, b = spread(dp_ref[c], low, True)
        qd[n + c * half : n + c * half + half // 2] = a
        qd[n + c * half + half // 2 : n + (c + 1) * half] = b
    do_t = qd[n:, :].astype(F32).T[64:]
    delta = jnp.sum(do_t * out_t_ref[...], axis=0, keepdims=True)
    lse = lse_ref[...]
    qpos = qpos_ref[...] + core * half
    first, last = query_ends(i, chunks, half, core)
    start, lo, f0, f1, hi = block_bounds(len_ref, items, qpos, first, last, key_block)
    dq_acc[...] = jnp.zeros_like(dq_acc)

    def step(j, masked):
        at = pl.ds(pl.multiple_of(j * key_block, key_block), key_block)
        both = nt_dot(kv_ref[at, :], qd[...])
        s = both[:, :n] * LOG2E
        if masked:
            kpos = j * key_block + lax.broadcasted_iota(jnp.int32, (key_block, 1), 0)
            s = jnp.where((kpos >= start) & (kpos <= qpos), s, MASKED)
        p = jnp.exp2(s - lse)
        ds = (p * (both[:, n:] - delta)).astype(BF16)
        dq_acc[...] += nn_dot(kv_t[:64, at], ds)
        dkv_ref[at, :] += nn_dot(ds, qd[:n, :]) + nn_dot(p.astype(BF16), qd[n:, :])

    lax.fori_loop(lo, f0, lambda j, c: (step(j, True), c)[1], 0)
    lax.fori_loop(f0, f1, lambda j, c: (step(j, False), c)[1], 0)
    lax.fori_loop(f1, hi, lambda j, c: (step(j, True), c)[1], 0)
    dq_t = dq_acc[...] * 0.125
    doubled = jnp.concatenate([dq_t, dq_t], axis=0).T
    for c in range(chunks):
        a = doubled[c * half : c * half + half // 2]
        b = doubled[c * half + half // 2 : (c + 1) * half]
        dq_ref[c] = jnp.where(low, a, b).astype(BF16)


def mix_back(lengths, core, kv, qp, dp, qpos, out_t, lse, chunks=4, key_block=768):
    total = kv.shape[0]
    n_src, quarter = qp.shape[0], qp.shape[1]
    half = 2 * quarter
    n = chunks * half
    whole = lambda i, *_: (0, 0)
    rows = lambda i, *_: (0, i)
    blocks = pl.BlockSpec((chunks, quarter, 128), lambda i, *_: (i, 0, 0))
    return pl.pallas_call(
        functools.partial(back_kernel, lengths.shape[0], chunks, key_block),
        grid_spec=pltpu.PrefetchScalarGridSpec(
            num_scalar_prefetch=2,
            grid=(n_src // chunks,),
            in_specs=[
                pl.BlockSpec((total, 128), whole),
                blocks,
                blocks,
                pl.BlockSpec((1, n), rows),
                pl.BlockSpec((64, n), rows),
                pl.BlockSpec((1, n), rows),
            ],
            out_specs=[pl.BlockSpec((total, 128), whole), blocks],
            scratch_shapes=[
                pltpu.VMEM((128, total), BF16),
                pltpu.VMEM((2 * n, 128), BF16),
                pltpu.VMEM((64, n), F32),
            ],
        ),
        out_shape=[
            jax.ShapeDtypeStruct((total, 128), F32),
            jax.ShapeDtypeStruct((n_src, quarter, 128), BF16),
        ],
        compiler_params=pltpu.CompilerParams(vmem_limit_bytes=22 << 20),
        cost_estimate=pl.CostEstimate(flops=40_000_000_000, bytes_accessed=8 << 20, transcendentals=0),
        name="mix_back",
    )(lengths, core, kv, qp, dp, qpos, out_t, lse)


def packed_positions(n_src, half):
    j = np.arange(n_src * half)
    return ((j // half) * 2 * half + j % half).astype(np.int32)[None]


def feed_kernel(
    blocks_ref, frames_ref, cot_ref, w_out_ref, gain_ref, w_up_ref, b_up_ref, w_down_ref, b_down_ref,
    out_ref, grad_mid_ref, grad_blocks_ref, hidden_ref, grad_before_ref, act2_ref, mixed_ref, low_ref, attn_ref,
    gain_grad_ref, b_up_grad_ref, b_down_grad_ref,
    mixed, act2, act_grad,
):
    i = pl.program_id(0)
    rows = frames_ref.shape[0]
    quarter = rows // 4
    low_q = low_lanes((quarter, 128))

    @pl.when(i == 0)
    def _():
        for zy in range(8):
            for s in range(2):
                a = blocks_ref[(zy * 2 + s) * 2].astype(F32)
                b = blocks_ref[(zy * 2 + s) * 2 + 1].astype(F32)
                at = slice(zy * 128, (zy + 1) * 128)
                first = 2 * s * quarter
                mixed[first : first + quarter, at] = pair_low(a, b, low_q)
                mixed[first + quarter : first + 2 * quarter, at] = pair_high(a, b, low_q)
        store_halves(mixed_ref, mixed[...])
        middle = frames_ref[...] + nn_dot(mixed[...].astype(BF16), w_out_ref[...])
        r = lax.rsqrt(jnp.mean(middle * middle, axis=-1, keepdims=True) + EPSILON)
        normed = middle * r * gain_ref[...]
        act2[...] = normed.astype(BF16)
        store_halves(act2_ref, normed)
        grad_mid_ref[...] = middle
        out_ref[...] = middle + b_down_ref[...]
        grad_low = cot_ref[...].astype(BF16)
        low_ref[...] = grad_low
        b_down_grad_ref[...] = jnp.sum(grad_low.astype(F32), axis=0, keepdims=True)
        act_grad[...] = jnp.zeros_like(act_grad)

    before = nn_dot(act2[...], w_up_ref[...]) + b_up_ref[...]
    cdf = 0.5 + 0.5 * lax.erf(before * 0.7071067811865476)
    pdf = jnp.exp(-0.5 * before * before) * 0.3989422804014327
    hidden = (before * cdf).astype(BF16)
    step = hidden.shape[1] // 2
    hidden_ref[0] = hidden[:, :step]
    hidden_ref[1] = hidden[:, step:]
    out_ref[...] += nn_dot(hidden, w_down_ref[...])
    grad_before = (nt_dot(low_ref[...], w_down_ref[...]) * (cdf + before * pdf)).astype(BF16)
    grad_before_ref[...] = grad_before
    b_up_grad_ref[...] = jnp.sum(grad_before.astype(F32), axis=0, keepdims=True)
    act_grad[...] += nt_dot(grad_before, w_up_ref[...])

    @pl.when(i == pl.num_programs(0) - 1)
    def _():
        middle = grad_mid_ref[...]
        r = lax.rsqrt(jnp.mean(middle * middle, axis=-1, keepdims=True) + EPSILON)
        n = middle * r
        g = act_grad[...]
        gain_grad_ref[...] = jnp.sum(g * n, axis=0, keepdims=True)
        g = g * gain_ref[...]
        grad_mid = cot_ref[...] + r * (g - n * jnp.mean(g * n, axis=-1, keepdims=True))
        grad_mid_ref[...] = grad_mid
        grad_attn = grad_mid.astype(BF16)
        attn_ref[...] = grad_attn
        grad_mixed = nt_dot(grad_attn, w_out_ref[...])
        for zy in range(8):
            for s in range(2):
                at = slice(zy * 128, (zy + 1) * 128)
                first = 2 * s * quarter
                a = grad_mixed[first : first + quarter, at]
                b = grad_mixed[first + quarter : first + 2 * quarter, at]
                grad_blocks_ref[(zy * 2 + s) * 2] = pair_low(a, b, low_q).astype(BF16)
                grad_blocks_ref[(zy * 2 + s) * 2 + 1] = pair_high(a, b, low_q).astype(BF16)


def feed(blocks, frames, cotangent, w_out, gain, w_up, b_up, w_down, b_down):
    rows, width = frames.shape
    ff = w_up.shape[1]
    steps = 8
    step = ff // steps
    fixed = lambda *shape: pl.BlockSpec(shape, lambda i: (0,) * len(shape))
    columns = lambda *shape: pl.BlockSpec(shape, lambda i: (0,) * (len(shape) - 1) + (i,))
    shape = jax.ShapeDtypeStruct
    return pl.pallas_call(
        feed_kernel,
        grid=(steps,),
        in_specs=[
            fixed(*blocks.shape),
            fixed(rows, width),
            fixed(rows, width),
            fixed(width, width),
            fixed(1, width),
            columns(width, step),
            columns(1, step),
            pl.BlockSpec((step, width), lambda i: (i, 0)),
            fixed(1, width),
        ],
        out_specs=[
            fixed(rows, width),
            fixed(rows, width),
            fixed(*blocks.shape),
            columns(2, rows, step // 2),
            columns(rows, step),
            fixed(2, rows, width // 2),
            fixed(2, rows, width // 2),
            fixed(rows, width),
            fixed(rows, width),
            fixed(1, width),
            columns(1, step),
            fixed(1, width),
        ],
        out_shape=[
            shape((rows, width), F32),
            pltpu.HBM((rows, width), F32),
            shape(blocks.shape, BF16),
            shape((2, rows, ff // 2), BF16),
            shape((rows, ff), BF16),
            shape((2, rows, width // 2), BF16),
            shape((2, rows, width // 2), BF16),
            shape((rows, width), BF16),
            shape((rows, width), BF16),
            pltpu.VMEM((1, width), F32),
            pltpu.VMEM((1, ff), F32),
            pltpu.VMEM((1, width), F32),
        ],
        scratch_shapes=[
            pltpu.VMEM((rows, width), F32),
            pltpu.VMEM((rows, width), BF16),
            pltpu.VMEM((rows, width), F32),
        ],
        compiler_params=pltpu.CompilerParams(vmem_limit_bytes=28 << 20),
        name="feed",
    )(
        blocks, frames, cotangent, w_out, gain.reshape(1, width), w_up, b_up.reshape(1, ff), w_down,
        b_down.reshape(1, width),
    )


MESH = pl.DeviceIdType.MESH
ALL = ("blk", "grp")


def in_hbm(*arrays):
    return [pltpu.with_memory_space_constraint(x, pltpu.HBM) for x in arrays]


def in_vmem(*arrays):
    return [pltpu.with_memory_space_constraint(x, pltpu.VMEM) for x in arrays]


def place(index):
    return {"blk": lax.div(index, 2), "grp": lax.rem(index, 2)}


def head_of(index):
    blk, grp = lax.div(index, 2), lax.rem(index, 2)
    return lax.div(blk, 2) * 2 + grp, lax.rem(blk, 2)


def own_index():
    return lax.axis_index("blk") * 2 + lax.axis_index("grp")


def plane_at(z, turn):
    high = lax.rem(lax.div(z, 2) + jnp.where(turn < 2, 1, 0), 2)
    low = lax.rem(z + jnp.where((turn == 1) | (turn == 2), 1, 0), 2)
    return high * 2 + low


def peer_at(i, n):
    me, plane = own_index(), n // 4
    return plane_at(lax.div(me, plane), lax.div(i, plane)) * plane + lax.rem(me + i, plane)


def each_peer(n, body):
    @pl.loop(0, n)
    def _(i):
        other = peer_at(i, n)

        @pl.when(other != own_index())
        def _():
            body(i, other)


def sibling_of(core):
    return {"blk": lax.axis_index("blk") + 1 - 2 * core, "grp": lax.axis_index("grp")}


def greet_all(me, n):
    barrier = pltpu.get_barrier_semaphore()

    @pl.loop(1, n)
    def _(i):
        pl.semaphore_signal(barrier, inc=1, device_id=place(lax.rem(me + i, n)), device_id_type=MESH)

    pl.semaphore_wait(barrier, n - 1)


def remote(src, dst, send_sem, recv_sem, device):
    return pltpu.make_async_remote_copy(
        src_ref=src, dst_ref=dst, send_sem=send_sem, recv_sem=recv_sem, device_id=device, device_id_type=MESH
    )


def to_heads_kernel(
    n, gain_in, frames_in, wq_in, wk_in, wv_in, kv_out, q_out, halves_out,
    gain, frames, act, halves, wq, wk, wv, kv_own, q_own, send, recv, local, fetched, pair,
):
    me = own_index()
    head, core = head_of(me)
    rows, width = frames.shape
    half = rows // 2
    weights = [
        pltpu.make_async_copy(src, dst, local.at[k])
        for k, (src, dst) in enumerate(
            ((gain_in, gain), (frames_in, frames), (halves, halves_out))
        )
    ]
    groups = width // 256

    def group_at(i):
        return plane_at(lax.div(me, n // groups), i)

    def fetch(group):
        columns = pl.ds(pl.multiple_of(group * 256, 256), 256)
        return [
            pltpu.make_async_copy(src.at[:, columns], dst.at[:, columns], fetched.at[k, group])
            for k, (src, dst) in enumerate(((wq_in, wq), (wk_in, wk), (wv_in, wv)))
        ]

    for copy in weights[:2]:
        copy.start()

    @pl.loop(0, groups)
    def _(i):
        for copy in fetch(group_at(i)):
            copy.start()

    greet_all(me, n)
    weights[0].wait()
    weights[1].wait()
    x = frames[...]
    r = lax.rsqrt(jnp.mean(x * x, axis=-1, keepdims=True) + EPSILON)
    normed = x * r * gain[...]
    act[...] = normed.astype(BF16)
    store_halves(halves, normed)
    weights[2].start()

    def copies(other, src):
        h, c = head_of(other)
        kv_at = core if src is not me else c
        return (
            remote(kv_own.at[h, c], kv_out.at[src, kv_at], send.at[0, other], recv.at[0, src], place(other)),
            remote(q_own.at[h, c], q_out.at[src], send.at[1, other], recv.at[1, src], place(other)),
        )

    low = low_lanes((rows, 128))
    low_h = low_lanes((half // 2, 128))

    @pl.loop(0, groups)
    def _(i):
        group = group_at(i)
        for copy in fetch(group):
            copy.wait()
        columns = pl.ds(pl.multiple_of(group * 256, 256), 256)
        q = nn_dot(act[...], wq[:, columns]).astype(BF16).astype(F32) * 0.125
        k = nn_dot(act[...], wk[:, columns])
        v = nn_dot(act[...], wv[:, columns])
        for p in range(2):
            at = slice(p * 128, (p + 1) * 128)
            k2, v2, q2 = k[:, at], v[:, at], q[:, at]
            kv_a = pair_low(k2, v2, low).astype(BF16)
            kv_b = pair_high(k2, v2, low).astype(BF16)
            h = group * 4 + 2 * p
            for s in range(2):
                span = slice(s * half, (s + 1) * half)
                kv_own[h, s] = kv_a[span]
                kv_own[h + 1, s] = kv_b[span]
                top = q2[s * half : s * half + half // 2]
                bot = q2[s * half + half // 2 : (s + 1) * half]
                q_own[h, s] = pair_low(top, bot, low_h).astype(BF16)
                q_own[h + 1, s] = pair_high(top, bot, low_h).astype(BF16)

        @pl.loop(0, n // groups)
        def _(j):
            other = group * (n // groups) + j

            @pl.when(other != me)
            def _():
                for copy in copies(other, me):
                    copy.start()

    kv_out[me, core] = kv_own[head, core]
    q_out[me] = q_own[head, core]

    plane = n // groups
    swaps = []
    for t in range(groups):
        first = pl.multiple_of(group_at(t) * plane, plane)

        @pl.loop(0, plane)
        def _(j):
            @pl.when(first + j != me)
            def _():
                for copy in copies(first + j, first + j):
                    copy.wait()

        at = pl.ds(first, plane)
        swap = remote(kv_out.at[at, core], kv_out.at[at, core], pair.at[0, t], pair.at[1, t], sibling_of(core))
        swap.start()
        swaps.append(swap)
    weights[2].wait()
    for swap in swaps:
        swap.wait()


def to_heads(frames, gain, w_query, w_key, w_value, n):
    rows, width = frames.shape
    half = rows // 2
    vmem = pl.BlockSpec(memory_space=pltpu.VMEM)
    hbm = pl.BlockSpec(memory_space=pltpu.HBM)
    return pl.pallas_call(
        functools.partial(to_heads_kernel, n),
        in_specs=[hbm] * 5,
        out_specs=[vmem, vmem, hbm],
        out_shape=[
            jax.ShapeDtypeStruct((n, 2, half, 128), BF16),
            jax.ShapeDtypeStruct((n, half // 2, 128), BF16),
            pltpu.HBM((2, rows, width // 2), BF16),
        ],
        scratch_shapes=[
            pltpu.VMEM((1, width), F32),
            pltpu.VMEM((rows, width), F32),
            pltpu.VMEM((rows, width), BF16),
            pltpu.VMEM((2, rows, width // 2), BF16),
            pltpu.VMEM((width, width), BF16),
            pltpu.VMEM((width, width), BF16),
            pltpu.VMEM((width, width), BF16),
            pltpu.VMEM((width // 64, 2, half, 128), BF16),
            pltpu.VMEM((width // 64, 2, half // 2, 128), BF16),
            pltpu.SemaphoreType.DMA((2, n)),
            pltpu.SemaphoreType.DMA((2, n)),
            pltpu.SemaphoreType.DMA((3,)),
            pltpu.SemaphoreType.DMA((3, 4)),
            pltpu.SemaphoreType.DMA((2, 4)),
        ],
        compiler_params=pltpu.CompilerParams(
            collective_id=0, has_side_effects=True, vmem_limit_bytes=16 << 20
        ),
        name="to_heads",
    )(*in_hbm(gain.reshape(1, width), frames, w_query, w_key, w_value))


def exchange_kernel(n, x_in, x_out, send, recv, local):
    me = own_index()
    greet_all(me, n)

    def copy_with(i, src):
        other = peer_at(i, n)
        return remote(x_in.at[other], x_out.at[src], send.at[i], recv.at[src], place(other))

    each_peer(n, lambda i, other: copy_with(i, me).start())

    own = pltpu.make_async_copy(x_in.at[me], x_out.at[me], local)
    own.start()
    own.wait()

    each_peer(n, lambda i, other: copy_with(i, other).wait())


def exchange(x, n, collective_id):
    vmem = pl.BlockSpec(memory_space=pltpu.VMEM)
    return pl.pallas_call(
        functools.partial(exchange_kernel, n),
        in_specs=[vmem],
        out_specs=vmem,
        out_shape=pltpu.VMEM(x.shape, x.dtype),
        scratch_shapes=[
            pltpu.SemaphoreType.DMA((n,)),
            pltpu.SemaphoreType.DMA((n,)),
            pltpu.SemaphoreType.DMA,
        ],
        compiler_params=pltpu.CompilerParams(collective_id=collective_id, has_side_effects=True, vmem_limit_bytes=8 << 20),
        name="exchange",
    )(*in_vmem(x))


BITS = {"core": 1, "y": 2, "z0": 4, "z1": 8}


def flipped(x, axis):
    if axis == "x":
        return lax.ppermute(x, "grp", [(0, 1), (1, 0)])
    return lax.ppermute(x, "blk", [(i, i ^ BITS[axis]) for i in range(lax.axis_size("blk"))])


def bit_of(axis):
    if axis == "x":
        return lax.axis_index("grp")
    return lax.rem(lax.div(lax.axis_index("blk"), BITS[axis]), 2)


def across(axis):
    blk, grp = lax.axis_index("blk"), lax.axis_index("grp")
    if axis == "x":
        return {"blk": blk, "grp": 1 - grp}
    bit = BITS[axis]
    return {"blk": blk + bit - 2 * bit * bit_of(axis), "grp": grp}


def tn_dot(a, b):
    return lax.dot_general(a, b, (((0,), (0,)), ((), ())), preferred_element_type=F32)


def share_kernel(
    n, blocks_in, hidden, grad_before, act2, mixed, low, attn,
    blocks_out, keep_a_out, send_a_out, keep_b_out, send_b_out, keep_c_out, send_c_out,
    keep_a, send_a, keep_b, send_b, keep_c, send_c, hidden2, before2, act2_2, mixed2, low2, attn2, tile, send, recv, local, out, pair_send, pair_recv,
):
    me = own_index()
    head, core = head_of(me)
    rows = low.shape[0]
    greet_all(me, n)
    sibling = sibling_of(core)
    theirs = pl.ds(rows, rows)
    pairs = [
        remote(src, dst.at[theirs], pair_send.at[k], pair_recv.at[k], sibling)
        for k, (src, dst) in enumerate(
            (
                (low, low2),
                (hidden.at[1 - core], hidden2),
                (act2.at[1 - core], act2_2),
                (grad_before, before2),
                (mixed.at[1 - core], mixed2),
                (attn, attn2),
            )
        )
    ]
    for copy in pairs:
        copy.start()

    def copy_with(i, src):
        other = peer_at(i, n)
        return remote(blocks_in.at[other], blocks_out.at[src], send.at[i], recv.at[src], place(other))

    each_peer(n, lambda i, other: copy_with(i, me).start())

    own = pltpu.make_async_copy(blocks_in.at[me], blocks_out.at[me], local)
    own.start()
    low2[:rows] = low[...]
    hidden2[:rows] = hidden[core]
    act2_2[:rows] = act2[core]
    before2[:rows] = grad_before[...]
    mixed2[:rows] = mixed[core]
    attn2[:rows] = attn[...]

    x_mine, y_mine, z_mine = bit_of("x"), bit_of("y"), bit_of("z0")

    def put(keep, away, mine, bit, at, row, value):
        @pl.when(mine == bit)
        def _():
            keep[at, row : row + value.shape[0]] = value

        @pl.when(mine != bit)
        def _():
            away[at, row : row + value.shape[0]] = value

    flushes = []

    def flush(src, dst):
        flushes.append(pltpu.make_async_copy(src, dst, out.at[len(flushes)]))
        flushes[-1].start()

    pairs[0].wait()
    pairs[1].wait()

    @pl.loop(0, 8)
    def _(zy):
        columns = pl.ds(pl.multiple_of(zy * 256, 256), 256)
        value = tn_dot(hidden2[:, columns], low2[...]).astype(BF16)
        z1, z0, y = lax.div(zy, 4), lax.rem(lax.div(zy, 2), 2), lax.rem(zy, 2)
        for x in range(2):
            put(keep_a, send_a, x_mine, x, zy, 0, value[x * 128 : x * 128 + 96])
            put(keep_c, send_c, z_mine, z0, (z1 * 2 + y) * 2 + x, 0, value[x * 128 + 96 : (x + 1) * 128])

    def spread_rows(left, right, slab, to_b, row):
        tile[...] = tn_dot(left[...], right[:, slab * 1024 : (slab + 1) * 1024]).astype(BF16)

        @pl.loop(0, 16)
        def _(j):
            value = tile[pl.ds(pl.multiple_of(j * 32, 32), 32)]
            z1, z0 = lax.div(j, 8), lax.rem(lax.div(j, 4), 2)
            y, x = lax.rem(lax.div(j, 2), 2), lax.rem(j, 2)
            if to_b:
                put(keep_b, send_b, y_mine, y, (z1 * 2 + z0) * 2 + x, row, value)
            else:
                put(keep_c, send_c, z_mine, z0, (z1 * 2 + y) * 2 + x, row, value)

    flush(keep_a, keep_a_out)
    flush(send_a, send_a_out)
    pairs[2].wait()
    pairs[3].wait()
    for slab in range(3):
        spread_rows(act2_2, before2, slab, True, 32 * slab)
    flush(keep_b, keep_b_out)
    flush(send_b, send_b_out)
    spread_rows(act2_2, before2, 3, False, 32)
    pairs[4].wait()
    pairs[5].wait()
    spread_rows(mixed2, attn2, 0, False, 64)
    flush(keep_c, keep_c_out)
    flush(send_c, send_c_out)
    own.wait()

    each_peer(n, lambda i, other: copy_with(i, other).wait())

    for copy in flushes:
        copy.wait()


def share(blocks, hidden, grad_before, act2, mixed, low, attn, n):
    rows, width = low.shape
    vmem = pl.BlockSpec(memory_space=pltpu.VMEM)
    hbm = pl.BlockSpec(memory_space=pltpu.HBM)
    shape = jax.ShapeDtypeStruct
    return pl.pallas_call(
        functools.partial(share_kernel, n),
        in_specs=[vmem] * 7,
        out_specs=[vmem] + [hbm] * 6,
        out_shape=[pltpu.VMEM(blocks.shape, BF16)] + [pltpu.HBM((8, 96, width), BF16)] * 6,
        scratch_shapes=[
            *[pltpu.VMEM((8, 96, width), BF16)] * 6,
            pltpu.VMEM((2 * rows, hidden.shape[2]), BF16),
            pltpu.VMEM((2 * rows, grad_before.shape[1]), BF16),
            pltpu.VMEM((2 * rows, width // 2), BF16),
            pltpu.VMEM((2 * rows, width // 2), BF16),
            pltpu.VMEM((2 * rows, width), BF16),
            pltpu.VMEM((2 * rows, width), BF16),
            pltpu.VMEM((width // 2, 1024), BF16),
            pltpu.SemaphoreType.DMA((n,)),
            pltpu.SemaphoreType.DMA((n,)),
            pltpu.SemaphoreType.DMA,
            pltpu.SemaphoreType.DMA((6,)),
            pltpu.SemaphoreType.DMA((6,)),
            pltpu.SemaphoreType.DMA((6,)),
        ],
        compiler_params=pltpu.CompilerParams(
            collective_id=3, has_side_effects=True, vmem_limit_bytes=26 << 20
        ),
        name="share",
    )(blocks, hidden, grad_before, act2, mixed, low, attn)


class Part:
    def __init__(self, total, dims, order, landing, send, recv):
        self.view, self.dims, self.order = total, list(dims), list(order)
        self.landing, self.send, self.recv = landing, send, recv
        self.stage, self.copy, self.kept = 0, None, None

    def start(self):
        axis = self.order[self.stage]
        at, mine = self.dims.index(axis), bit_of(axis)
        ahead = (slice(None),) * at
        self.copy = remote(
            self.view.at[ahead + (1 - mine,)],
            self.landing[self.stage],
            self.send.at[self.stage],
            self.recv.at[self.stage],
            across(axis),
        )
        self.copy.start()
        self.kept = self.view.at[ahead + (mine,)]
        self.dims.remove(axis)
        self.stage += 1

    def finish(self):
        self.copy.wait()
        got, kept = self.landing[self.stage - 1], self.kept
        lead = len(self.dims)

        @pl.loop(0, 2**lead)
        def _(k):
            at = tuple(lax.rem(lax.div(k, 2**d), 2) for d in reversed(range(lead)))
            kept[at] = (kept[at].astype(F32) + got[at].astype(F32)).astype(BF16)

        self.view = kept

    def last(self):
        self.copy.wait()
        return self.kept[...].astype(F32) + self.landing[self.stage - 1][...].astype(F32)


def finish_kernel(
    n, dkv_in, dq_in, gain2_grad, b_up_grad, b_down_grad, got_a, got_b, got_c,
    gain_in, act1, frames_in, grad_mid_in, wq_in, wk_in, wv_in, keep_a, keep_b, keep_c,
    frames_out, q_out, k_out, v_out, o_out, up_out, down_out, small_out,
    theirs, total, dkv_all, dq_all, gain, frames, grad_mid, wq, wk, wv, small_in,
    act1_2, qkv2, sum_a, sum_b, sum_c, sum_q, sum_k, sum_v,
    a2, a3, a4, b2, b3, b4, c2, c3, c4,
    q1, q2, q3, q4, k1, k2, k3, k4, v1, v2, v3, v4, small_all,
    early_send, early_recv, send, recv, dq_send, dq_recv, dkv_send, dkv_recv, small_send, small_recv, pair_send, pair_recv, local,
):
    me = own_index()
    head, core = head_of(me)
    rows, width = frames.shape
    quarter = rows // 4
    sums = [sum_a, sum_b, sum_c, sum_q, sum_k, sum_v]
    news = [got_a, got_b, got_c]
    fetches = [
        pltpu.make_async_copy(src, dst, local.at[k])
        for k, (src, dst) in enumerate(
            (
                (keep_a, sum_a), (keep_b, sum_b), (keep_c, sum_c),
                (wq_in, wq), (wk_in, wk), (wv_in, wv), (gain_in, gain), (frames_in, frames), (grad_mid_in, grad_mid),
            )
        )
    ]
    for copy in fetches:
        copy.start()
    greet_all(me, n)
    sibling = sibling_of(core)
    swap = remote(dkv_in.at[:, 1 - core], theirs, pair_send.at[0], pair_recv.at[0], sibling)
    swap.start()
    act1_copy = remote(act1.at[1 - core], act1_2.at[pl.ds(rows, rows)], pair_send.at[1], pair_recv.at[1], sibling)

    def to_all(src_ref, dst_ref, sends, recvs):
        def copy_with(i, src):
            other = peer_at(i, n)
            return remote(src_ref.at[other], dst_ref.at[src], sends.at[i], recvs.at[src], place(other))

        return copy_with

    dq_copy = to_all(dq_in, dq_all, dq_send, dq_recv)
    dkv_copy = to_all(total, dkv_all, dkv_send, dkv_recv)
    small_copy = to_all(small_in, small_all, small_send, small_recv)

    each_peer(n, lambda i, other: dq_copy(i, me).start())

    swap.wait()

    def add(j):
        return (dkv_in[j, core] + theirs[j]).astype(BF16)

    def add_and_send(i, other):
        total[other] = add(other)
        dkv_copy(i, me).start()

    each_peer(n, add_and_send)

    dkv_all[me] = add(me)
    dq_all[me] = dq_in[me]
    act1_copy.start()
    order = ("x", "y", "z0", "z1"), ("y", "x", "z0", "z1"), ("z0", "x", "y", "z1")
    landings = (q1, q2, q3, q4), (k1, k2, k3, k4), (v1, v2, v3, v4)
    late = [Part(sums[3 + k], ("z1", "z0", "y", "x"), order[k], landings[k], send.at[k], recv.at[k]) for k in range(3)]
    dims = ("z1", "z0", "y"), ("z1", "z0", "x"), ("z1", "y", "x")
    order = (
        (("y", "z0", "z1"),) * 3,
        (("x", "z0", "z1"), ("x", "z0", "z1"), ("z0", "x", "z1")),
        (("x", "y", "z1"), ("y", "x", "z1"), ("x", "y", "z1")),
    )
    landings = (a2, a3, a4), (b2, b3, b4), (c2, c3, c4)
    waves = []
    for u in range(3):
        band = slice(32 * u, 32 * u + 32)
        wave = []
        for k in range(3):
            wave.append(
                Part(
                    sums[k].at[:, :, :, band],
                    dims[k],
                    order[k][u],
                    [ref.at[(slice(None),) * lead + (band,)] for lead, ref in zip((2, 1, 0), landings[k])],
                    early_send.at[u, k],
                    early_recv.at[u, k],
                )
            )
        waves.append(wave)

    for u, wave in enumerate(waves):
        for k, part in enumerate(wave):
            whole, new = sums[k], news[k]
            if u == 0:
                fetches[k].wait()

            @pl.loop(0, 8)
            def _(j):
                at = (lax.div(j, 4), lax.rem(lax.div(j, 2), 2), lax.rem(j, 2), slice(32 * u, 32 * u + 32))
                whole[at] = (whole[at].astype(F32) + new[at].astype(F32)).astype(BF16)

            part.start()

    def advance(parts):
        for part in parts:
            part.finish()
            part.start()

    act1_own = pltpu.make_async_copy(act1.at[core], act1_2.at[pl.ds(0, rows)], local.at[9])
    act1_own.start()

    each_peer(n, lambda i, other: dq_copy(i, other).wait())

    def pair_with(k):
        columns = slice(k * width, (k + 1) * width)
        own, other = qkv2.at[pl.ds(0, rows), columns], qkv2.at[pl.ds(rows, rows), columns]
        return remote(own, other, pair_send.at[2 + k], pair_recv.at[2 + k], sibling)

    pairs = [pair_with(k) for k in range(3)]
    low_q, low_h = low_lanes((quarter, 128)), low_lanes((2 * quarter, 128))
    for zy in range(8):
        for s in range(2):
            j = (zy * 2 + s) * 2
            first = 2 * s * quarter
            a, b = dq_all[j].astype(F32), dq_all[j + 1].astype(F32)
            at = slice(zy * 128, (zy + 1) * 128)
            qkv2[first : first + quarter, at] = pair_low(a, b, low_q).astype(BF16)
            qkv2[first + quarter : first + 2 * quarter, at] = pair_high(a, b, low_q).astype(BF16)
    pairs[0].start()
    def product(k):
        pairs[k].wait()
        value = tn_dot(act1_2[...], qkv2[:, k * width : (k + 1) * width]).astype(BF16)
        for j in range(16):
            sums[3 + k][j // 8, j // 4 % 2, j // 2 % 2, j % 2] = value[j * 32 : (j + 1) * 32]
        late[k].start()

    advance(waves[0])
    act1_copy.wait()
    act1_own.wait()
    product(0)
    advance(waves[1])

    each_peer(n, lambda i, other: dkv_copy(i, other).wait())

    advance(waves[0])
    advance(waves[2])
    for zy in range(8):
        for s in range(2):
            j = (zy * 2 + s) * 2
            first = 2 * s * quarter
            a, b = dkv_all[j].astype(F32), dkv_all[j + 1].astype(F32)
            at = slice(width + zy * 128, width + (zy + 1) * 128)
            qkv2[first : first + 2 * quarter, at] = pair_low(a, b, low_h).astype(BF16)
            at = slice(2 * width + zy * 128, 2 * width + (zy + 1) * 128)
            qkv2[first : first + 2 * quarter, at] = pair_high(a, b, low_h).astype(BF16)
    pairs[1].start()
    pairs[2].start()
    advance(waves[1])
    product(1)
    product(2)
    for copy in fetches[3:]:
        copy.wait()
    g = nt_dot(qkv2[:rows, :width], wq[...])
    g += nt_dot(qkv2[:rows, width : 2 * width], wk[...])
    g += nt_dot(qkv2[:rows, 2 * width :], wv[...])
    advance(waves[2])

    x = frames[...]
    r = lax.rsqrt(jnp.mean(x * x, axis=-1, keepdims=True) + EPSILON)
    norm = x * r
    gain_grad = jnp.sum(g * norm, axis=0, keepdims=True)
    small_in[...] = jnp.zeros_like(small_in)
    for d in range(n):
        at = slice(d // 4 * 128, (d // 4 + 1) * 128)
        small_in[d, 0:1] = gain_grad[:, at]
        small_in[d, 1:2] = gain2_grad[:, at]
        small_in[d, 2:3] = b_down_grad[:, at]
        small_in[d, 3:4] = b_up_grad[:, d * 128 : (d + 1) * 128]

    each_peer(n, lambda i, other: small_copy(i, me).start())

    g = g * gain[...]
    frames_out[...] = grad_mid[...] + r * (g - norm * jnp.mean(g * norm, axis=-1, keepdims=True))
    small_all[me] = small_in[me]

    advance(late * 3)

    each_peer(n, lambda i, other: small_copy(i, other).wait())

    part = width // n
    small_out[...] = pltpu.roll(jnp.sum(small_all[...], axis=0), lax.rem(128 - lax.rem(me, 128 // part) * part, 128), 1)
    small_out[3:4] = jnp.sum(small_all[:, 3:4], axis=0)
    for u, wave in enumerate(waves):
        down_out[32 * u : 32 * u + 32] = wave[0].last()
        up_out[:, 1024 * u : 1024 * u + 1024] = wave[1].last()
    down_out[96:] = waves[0][2].last()
    up_out[:, 3072:] = waves[1][2].last()
    o_out[...] = waves[2][2].last()
    q_out[...] = late[0].last()
    k_out[...] = late[1].last()
    v_out[...] = late[2].last()


def finish(dkv, dq, act1, frames, grad_mid, gain, gain2_grad, b_up_grad, b_down_grad, weights, keeps, gots, n):
    rows, width = frames.shape
    keeps, gots = [[x.reshape(2, 2, 2, *x.shape[1:]) for x in xs] for xs in (keeps, gots)]
    half = dkv.shape[2]
    vmem = pl.BlockSpec(memory_space=pltpu.VMEM)
    hbm = pl.BlockSpec(memory_space=pltpu.HBM)
    shape = jax.ShapeDtypeStruct
    thin, wide = (32, width), (96, width)
    buffers = [pltpu.VMEM((2, 2, 2, *wide), BF16)] * 3 + [pltpu.VMEM((2, 2, 2, 2, *thin), BF16)] * 3
    buffers += [pltpu.VMEM((2,) * k + wide, BF16) for k in (2, 1, 0)] * 3
    buffers += [pltpu.VMEM((2,) * k + thin, BF16) for k in (3, 2, 1, 0)] * 3
    over_devices = [pltpu.SemaphoreType.DMA((n,))] * 6
    return pl.pallas_call(
        functools.partial(finish_kernel, n),
        in_specs=[vmem] * 8 + [hbm] * 10,
        out_specs=[vmem] * 8,
        out_shape=[pltpu.VMEM((rows, width), F32)]
        + [pltpu.VMEM(thin, F32)] * 4
        + [pltpu.VMEM((32, 4 * width), F32), pltpu.VMEM((128, width), F32), pltpu.VMEM((8, 128), F32)],
        scratch_shapes=[
            pltpu.VMEM((n, half, 128), F32),
            pltpu.VMEM((n, half, 128), BF16),
            pltpu.VMEM((n, half, 128), BF16),
            pltpu.VMEM((n, half // 2, 128), BF16),
            pltpu.VMEM((1, width), F32),
            pltpu.VMEM((rows, width), F32),
            pltpu.VMEM((rows, width), F32),
            pltpu.VMEM((width, width), BF16),
            pltpu.VMEM((width, width), BF16),
            pltpu.VMEM((width, width), BF16),
            pltpu.VMEM((n, 8, 128), F32),
            pltpu.VMEM((2 * rows, width // 2), BF16),
            pltpu.VMEM((2 * rows, 3 * width), BF16),
            *buffers,
            pltpu.VMEM((n, 8, 128), F32),
            pltpu.SemaphoreType.DMA((3, 3, 3)),
            pltpu.SemaphoreType.DMA((3, 3, 3)),
            pltpu.SemaphoreType.DMA((3, 4)),
            pltpu.SemaphoreType.DMA((3, 4)),
            *over_devices,
            pltpu.SemaphoreType.DMA((5,)),
            pltpu.SemaphoreType.DMA((5,)),
            pltpu.SemaphoreType.DMA((10,)),
        ],
        compiler_params=pltpu.CompilerParams(
            collective_id=4, has_side_effects=True, vmem_limit_bytes=36 << 20
        ),
        name="finish",
    )(
        *in_vmem(dkv, dq, gain2_grad, b_up_grad, b_down_grad, *gots),
        *in_hbm(gain.reshape(1, width), act1, frames, grad_mid, *weights, *keeps),
    )


def emit_kernel(n, small, *refs):
    sems = refs[-1]
    copies = [pltpu.make_async_copy(refs[k], refs[n + k], sems.at[k]) for k in range(n)]
    for copy in copies:
        copy.start()
    for row, out in enumerate(refs[2 * n : -1]):
        out[...] = small[row : row + 1, : out.shape[1]]
    for copy in copies:
        copy.wait()


def emit(small, widths, *arrays):
    n = len(arrays)
    vmem = pl.BlockSpec(memory_space=pltpu.VMEM)
    return pl.pallas_call(
        functools.partial(emit_kernel, n),
        in_specs=[vmem] * (n + 1),
        out_specs=[pl.BlockSpec(memory_space=pltpu.HBM)] * n + [vmem] * len(widths),
        out_shape=[pltpu.HBM(x.shape, x.dtype) for x in arrays]
        + [jax.ShapeDtypeStruct((1, width), F32) for width in widths],
        scratch_shapes=[pltpu.SemaphoreType.DMA((n,))],
        compiler_params=pltpu.CompilerParams(vmem_limit_bytes=8 << 20),
        name="emit",
    )(*in_vmem(small, *arrays))


def shards_heads(
    frames, lengths, norm1_gain, w_query, w_key, w_value, w_out, norm2_gain, w_up, b_up, w_down, b_down, cotangent
):
    rows, width = frames.shape
    n = lax.axis_size("blk") * lax.axis_size("grp")
    half = rows // 2
    core_word = bit_of("core").astype(jnp.int32).reshape(1)
    qpos = jnp.asarray(packed_positions(n, half))

    kv, q, act1 = to_heads(frames, norm1_gain, w_query, w_key, w_value, n)
    kv_rows = kv.reshape(n * rows, 128)
    out_t, lse, out_blocks = mix(lengths, core_word, kv_rows, q, qpos)
    mixed_blocks = exchange(out_blocks, n, 2)
    (
        layer_out, grad_middle, grad_blocks, hidden, grad_before, act2, mixed, grad_low, grad_attn,
        norm2_gain_grad, b_up_grad, b_down_grad,
    ) = feed(mixed_blocks, frames, cotangent, w_out, norm2_gain, w_up, b_up, w_down, b_down)
    grad_blocks, *parts = share(grad_blocks, hidden, grad_before, act2, mixed, grad_low, grad_attn, n)
    keeps = parts[0::2]
    gots = [flipped(part, axis) for part, axis in zip(parts[1::2], ("x", "y", "z0"))]
    dkv, dq = mix_back(lengths, core_word, kv_rows, q, *in_vmem(grad_blocks), qpos, out_t, lse)

    frames_grad, w_query_grad, w_key_grad, w_value_grad, w_out_grad, w_up_grad, w_down_grad, small = finish(
        dkv.reshape(n, 2, half, 128), dq, act1, frames, grad_middle, norm1_gain, norm2_gain_grad, b_up_grad,
        b_down_grad, (w_query, w_key, w_value), keeps, gots, n,
    )
    part = width // n
    (
        layer_out, frames_grad, w_query_grad, w_key_grad, w_value_grad, w_out_grad, w_up_grad, w_down_grad, *vectors
    ) = emit(
        small, (part, part, part, b_up.shape[0] // n),
        layer_out, frames_grad, w_query_grad, w_key_grad, w_value_grad, w_out_grad, w_up_grad, w_down_grad,
    )
    return (
        layer_out,
        frames_grad,
        vectors[0].reshape(-1),
        w_query_grad,
        w_key_grad,
        w_value_grad,
        w_out_grad,
        vectors[1].reshape(-1),
        w_up_grad,
        vectors[3].reshape(-1),
        w_down_grad,
        vectors[2].reshape(-1),
    )


def solution(mesh):
    if mesh.shape["blk"] != 16 or mesh.shape["grp"] != 2:
        return solution_ring(mesh)
    split = P(ALL, None)
    return jax.shard_map(
        shards_heads,
        mesh=mesh,
        in_specs=(split, P(), P(), P(), P(), P(), P(), P(), P(), P(), P(), P(), split),
        out_specs=(split, split, P(ALL), split, split, split, split, P(ALL), split, P(ALL), split, P(ALL)),
        check_vma=False,
    )
```
